32 devices in a mesh: dp: 8 (over y, x, core), mp: 4 (over z).
Axes of the slice: x: 2, y: 2, z: 4, core: 2. Of those that a mesh axis runs over, the one named last changes fastest.
Arguments:
- points: bfloat16 [8192, 1024], P(('dp', 'mp')), may hold values from -6 to 6
- members: int32 [32, 256], P(('dp', 'mp')), may hold values from -1 to 255, as said below
- cotangent: bfloat16 [8192, 1024], P(('dp', 'mp')), may hold values from -6 to 6
- project_weight: bfloat16 [1024, 3, 1024], P(None, None, 'mp'), may hold values from -0.1875 to 0.1875
- output_weight: bfloat16 [1024, 1024], P('mp'), may hold values from -1.5 to 1.5
- upward_weight: bfloat16 [1024, 4096], P(None, 'mp'), may hold values from -0.1875 to 0.1875
- downward_weight: bfloat16 [4096, 1024], P('mp'), may hold values from -0.09375 to 0.09375
- layer_norms: float32 [4, 1024], replicated, may hold values from -0.9 to 1.75
- project_master: float32 [1024, 3, 1024], P('dp', None, 'mp'), may hold values from -0.1875 to 0.1875
- project_first: float32 [1024, 3, 1024], P('dp', None, 'mp'), may hold values from -96 to 96
- project_second: float32 [1024, 3, 1024], P('dp', None, 'mp'), may hold values from 966.656 to 3874.816
- output_master: float32 [1024, 1024], P('mp', 'dp'), may hold values from -1.5 to 1.5
- output_first: float32 [1024, 1024], P('mp', 'dp'), may hold values from -6 to 6
- output_second: float32 [1024, 1024], P('mp', 'dp'), may hold values from 6.22592 to 24.82176
- upward_master: float32 [1024, 4096], P('dp', 'mp'), may hold values from -0.1875 to 0.1875
- upward_first: float32 [1024, 4096], P('dp', 'mp'), may hold values from -16 to 16
- upward_second: float32 [1024, 4096], P('dp', 'mp'), may hold values from 38.5024 to 155.648
- downward_master: float32 [4096, 1024], P('mp', 'dp'), may hold values from -0.09375 to 0.09375
- downward_first: float32 [4096, 1024], P('mp', 'dp'), may hold values from -28 to 28
- downward_second: float32 [4096, 1024], P('mp', 'dp'), may hold values from 87.6544 to 352.256
- norm_first: float32 [4, 1024], P(None, 'dp'), may hold values from -64 to 64
- norm_second: float32 [4, 1024], P(None, 'dp'), may hold values from 430.8992 to 1720.32
Outputs:
- latents: float32 [8192, 1024], P(('dp', 'mp'))
- point_gradient: float32 [8192, 1024], P(('dp', 'mp'))
- project_gradient: float32 [1024, 3, 1024], P('dp', None, 'mp')
- project_updated: float32 [1024, 3, 1024], P('dp', None, 'mp')
- project_moment_one: float32 [1024, 3, 1024], P('dp', None, 'mp')
- project_moment_two: float32 [1024, 3, 1024], P('dp', None, 'mp')
- project_copy: bfloat16 [1024, 3, 1024], P('dp', None, 'mp')
- output_gradient: float32 [1024, 1024], P('mp', 'dp')
- output_updated: float32 [1024, 1024], P('mp', 'dp')
- output_moment_one: float32 [1024, 1024], P('mp', 'dp')
- output_moment_two: float32 [1024, 1024], P('mp', 'dp')
- output_copy: bfloat16 [1024, 1024], P('mp', 'dp')
- upward_gradient: float32 [1024, 4096], P('dp', 'mp')
- upward_updated: float32 [1024, 4096], P('dp', 'mp')
- upward_moment_one: float32 [1024, 4096], P('dp', 'mp')
- upward_moment_two: float32 [1024, 4096], P('dp', 'mp')
- upward_copy: bfloat16 [1024, 4096], P('dp', 'mp')
- downward_gradient: float32 [4096, 1024], P('mp', 'dp')
- downward_updated: float32 [4096, 1024], P('mp', 'dp')
- downward_moment_one: float32 [4096, 1024], P('mp', 'dp')
- downward_moment_two: float32 [4096, 1024], P('mp', 'dp')
- downward_copy: bfloat16 [4096, 1024], P('mp', 'dp')
- norm_gradient: float32 [4, 1024], P(None, 'dp')
- norm_updated: float32 [4, 1024], P(None, 'dp')
- norm_moment_one: float32 [4, 1024], P(None, 'dp')
- norm_moment_two: float32 [4, 1024], P(None, 'dp')
The draws below stay inside these ranges and needn't reach their ends.
Inputs may be any that keep to these rules, and one draw needn't show every extreme that they name: members[g, j] names row g * 256 + members[g, j] of points, or is -1 for a padded slot; in each row every value of 0 to 255 stands at most once, and at most 64 entries are -1.
All inputs are finite; a program needn't handle non-finite values.
Results may differ from the reference program's by a relative error of at most 0.014.
The reference program's roundings to bfloat16 on the way count: a program that leaves them out, or rounds other values in their place, can miss the bound.
Values may be sent and summed in bfloat16 or wider, within the bound.
A program may use at most 128 MiB of HBM per device.

```python
import math
import jax
import jax.numpy as jnp
from jax import lax

D = 1024
HEADS = 8
HEAD_DIM = 128
FF = 4096
LAT = 256
ADAM_STEP = 10
GROUPS = 32
ROWS = 8192


def draw_members(key, part):
    group_keys = jax.random.split(jax.random.fold_in(key, 11), GROUPS)
    orders = jax.vmap(lambda single_key: jax.random.permutation(single_key, LAT))(group_keys).astype(jnp.int32)
    pad_counts = jax.random.randint(jax.random.fold_in(key, 12), (GROUPS,), 0, LAT // 4 + 1).astype(jnp.int32)
    group_ids = jnp.arange(GROUPS, dtype=jnp.int32)
    pad_counts = jnp.where(group_ids % 4 == 0, 0, jnp.where(group_ids % 4 == 1, LAT // 4, pad_counts))
    return jnp.where(orders >= LAT - pad_counts[:, None], -1, orders).astype(jnp.int32)


def draw_layer_norms(key, part):
    noise = jnp.clip(jax.random.normal(jax.random.fold_in(key, 21), (4, D), jnp.float32), -3.0, 3.0)
    is_gain = (jnp.arange(4) % 2 == 0)[:, None]
    return jnp.where(is_gain, 1.0 + 0.25 * noise, 0.3 * noise).astype(jnp.float32)


def block_levels(stream_key, extent, cuts, low, top_value):
    def one(dim, parts):
        draws = jax.random.uniform(jax.random.fold_in(jax.random.fold_in(stream_key, 6), dim), (parts,), jnp.float32, low / len(cuts), top_value / len(cuts))
        return jnp.repeat(jnp.exp(draws), extent[dim] // parts).reshape((-1,) + (1,) * (len(extent) - dim - 1))

    factor_of = one(*cuts[0])
    for cut in cuts[1:]:
        factor_of = factor_of * one(*cut)
    return factor_of


def bell_draw(key, extent, width, limit, cuts=(), held_as=jnp.bfloat16):
    result = width * jax.random.normal(key, extent, jnp.float32)
    if cuts:
        result = result * block_levels(key, extent, cuts, -0.22, 0.18)
    return jnp.clip(result, -limit, limit).astype(held_as)


def setup_inputs(seed: int = 0) -> dict:
    key_of = jax.random.split(jax.random.key(seed), 23)
    points = bell_draw(key_of[0], (ROWS, D), 1.0, 6.0, ((0, 32),))
    members = draw_members(jax.random.fold_in(key_of[22], 71), 0)
    cotangent = bell_draw(key_of[2], (ROWS, D), 1.0, 6.0, ((0, 32),))
    project_weight = bell_draw(key_of[3], (D, 3, D), D ** -0.5, 0.1875, ((2, 4),))
    output_weight = bell_draw(key_of[4], (D, D), (max(1, D * 4 // LAT)) ** -0.5, 1.5, ((0, 4),))
    upward_weight = bell_draw(key_of[5], (D, FF), D ** -0.5, 0.1875, ((1, 4),))
    downward_weight = bell_draw(key_of[6], (FF, D), FF ** -0.5, 0.09375, ((0, 4),))
    layer_norms = draw_layer_norms(jax.random.fold_in(key_of[22], 71), 0)
    project_master = bell_draw(key_of[8], (D, 3, D), D ** -0.5, 0.1875, ((0, 8), (2, 4)), jnp.float32)
    project_first = bell_draw(key_of[9], (D, 3, D), (0.165 * ROWS ** 0.5), 96.0, ((0, 8), (2, 4)), jnp.float32)
    project_second = jnp.clip(jnp.exp(math.log(3874.816) - 1.3884107 * jax.random.uniform(key_of[10], (D, 3, D), jnp.float32) ** block_levels(key_of[10], (D, 3, D), ((0, 8), (2, 4)), -0.2, 0.2)), 966.656, 3874.816)
    output_master = bell_draw(key_of[11], (D, D), (max(1, D * 4 // LAT)) ** -0.5, 1.5, ((0, 4), (1, 8)), jnp.float32)
    output_first = bell_draw(key_of[12], (D, D), (0.0132 * ROWS ** 0.5), 6.0, ((0, 4), (1, 8)), jnp.float32)
    output_second = jnp.clip(jnp.exp(math.log(24.82176) - 1.3829994 * jax.random.uniform(key_of[13], (D, D), jnp.float32) ** block_levels(key_of[13], (D, D), ((0, 4), (1, 8)), -0.2, 0.2)), 6.22592, 24.82176)
    upward_master = bell_draw(key_of[14], (D, FF), D ** -0.5, 0.1875, ((0, 8), (1, 4)), jnp.float32)
    upward_first = bell_draw(key_of[15], (D, FF), (0.033 * ROWS ** 0.5), 16.0, ((0, 8), (1, 4)), jnp.float32)
    upward_second = jnp.clip(jnp.exp(math.log(155.648) - 1.3968765 * jax.random.uniform(key_of[16], (D, FF), jnp.float32) ** block_levels(key_of[16], (D, FF), ((0, 8), (1, 4)), -0.2, 0.2)), 38.5024, 155.648)
    downward_master = bell_draw(key_of[17], (FF, D), FF ** -0.5, 0.09375, ((0, 4), (1, 8)), jnp.float32)
    downward_first = bell_draw(key_of[18], (FF, D), (0.05 * ROWS ** 0.5), 28.0, ((0, 4), (1, 8)), jnp.float32)
    downward_second = jnp.clip(jnp.exp(math.log(352.256) - 1.3909564 * jax.random.uniform(key_of[19], (FF, D), jnp.float32) ** block_levels(key_of[19], (FF, D), ((0, 4), (1, 8)), -0.2, 0.2)), 87.6544, 352.256)
    norm_first = bell_draw(key_of[20], (4, D), (0.11 * ROWS ** 0.5), 64.0, ((1, 8),), jnp.float32)
    norm_second = jnp.clip(jnp.exp(math.log(1720.32) - 1.3843914 * jax.random.uniform(key_of[21], (4, D), jnp.float32) ** block_levels(key_of[21], (4, D), ((1, 8),), -0.2, 0.2)), 430.8992, 1720.32)
    return {"points": points, "members": members, "cotangent": cotangent, "project_weight": project_weight, "output_weight": output_weight, "upward_weight": upward_weight, "downward_weight": downward_weight, "layer_norms": layer_norms, "project_master": project_master, "project_first": project_first, "project_second": project_second, "output_master": output_master, "output_first": output_first, "output_second": output_second, "upward_master": upward_master, "upward_first": upward_first, "upward_second": upward_second, "downward_master": downward_master, "downward_first": downward_first, "downward_second": downward_second, "norm_first": norm_first, "norm_second": norm_second}


@jax.custom_vjp
def low(v):
    return lax.optimization_barrier(v.astype(jnp.bfloat16)).astype(jnp.float32)

@jax.custom_vjp
def low_back(v):
    return v

def low_keep(v):
    return (low(v), None)

def low_pass(kept, grad):
    return (grad,)

def back_keep(v):
    return (v, None)

def back_low(kept, grad):
    return (low(grad),)
low.defvjp(low_keep, low_pass)
low_back.defvjp(back_keep, back_low)
highest_mode = lax.Precision.HIGHEST
norm_epsilon = 1e-05
beta_one = 0.9
beta_two = 0.95
adam_epsilon = 1e-08
weight_decay = 0.1
masked_score = -1e+30

def layer_norm(values, norm_gain, norm_shift):
    center = values - lax.optimization_barrier(jnp.mean(values, axis=-1, keepdims=True))
    spread = lax.optimization_barrier(jnp.mean(center * center, axis=-1, keepdims=True))
    return center * lax.rsqrt(spread + norm_epsilon) * norm_gain + norm_shift

def pick_rows(source_rows, row_index):
    return source_rows[row_index]

def adamw_step(weight, gradient, moment_one, moment_two, step_rate):
    one_new = beta_one * moment_one + (1.0 - beta_one) * gradient
    two_new = beta_two * moment_two + (1.0 - beta_two) * gradient * gradient
    corrected_one = one_new / (1.0 - beta_one ** ADAM_STEP)
    corrected_two = two_new / (1.0 - beta_two ** ADAM_STEP)
    updated = weight - step_rate * (corrected_one / (jnp.sqrt(corrected_two) + adam_epsilon) + weight_decay * weight)
    return (updated, one_new, two_new)

def forward(points_float, project_float, output_float, upward_float, downward_float, norms_float, members_block):
    groups_block = members_block.shape[0]
    grouped = points_float.reshape(groups_block, LAT, D)
    slot_index = jnp.maximum(members_block, 0)
    key_live = members_block >= 0
    picked = jax.vmap(pick_rows)(grouped, slot_index)
    inputs = jnp.where(key_live[:, :, None], picked, 0.0).reshape(groups_block * LAT, D)
    entering = low(layer_norm(inputs, norms_float[0], norms_float[1]))
    projected = low(low_back(jnp.einsum('rd,dcf->rcf', entering, project_float, precision=highest_mode)))
    heads_view = projected.reshape(groups_block, LAT, 3, HEADS, HEAD_DIM)
    queries = heads_view[:, :, 0]
    keys_all = heads_view[:, :, 1]
    values_all = heads_view[:, :, 2]
    scores = jnp.einsum('gqhe,gkhe->ghqk', queries, keys_all, precision=highest_mode) * HEAD_DIM ** (-0.5)
    scores = low_back(jnp.where(key_live[:, None, None, :], scores, masked_score))
    weights_low = low(jax.nn.softmax(scores, axis=-1))
    attended = low(low_back(jnp.einsum('ghqk,gkhe->gqhe', weights_low, values_all, precision=highest_mode)))
    attended = attended.reshape(groups_block * LAT, D)
    branch = low_back(jnp.dot(attended, output_float, precision=highest_mode))
    residual = inputs + branch
    entering_two = low(layer_norm(residual, norms_float[2], norms_float[3]))
    upward = low_back(jnp.dot(entering_two, upward_float, precision=highest_mode))
    activated = low(jax.nn.gelu(upward))
    return residual + jnp.dot(activated, downward_float, precision=highest_mode)

def reference(points, members, cotangent, project_weight, output_weight, upward_weight, downward_weight, layer_norms, project_master, project_first, project_second, output_master, output_first, output_second, upward_master, upward_first, upward_second, downward_master, downward_first, downward_second, norm_first, norm_second):
    parameters = (project_weight.astype(jnp.float32), output_weight.astype(jnp.float32), upward_weight.astype(jnp.float32), downward_weight.astype(jnp.float32), layer_norms)
    block_groups = 16
    blocks = GROUPS // block_groups
    block_rows = block_groups * LAT
    points_blocks = points.astype(jnp.float32).reshape(blocks, block_rows, D)
    members_blocks = members.reshape(blocks, block_groups, LAT)
    cotangent_blocks = cotangent.astype(jnp.float32).reshape(blocks, block_rows, D)

    def accumulate(totals, block_inputs):
        points_block, members_block, cotangent_block = block_inputs

        def local(points_float, project_float, output_float, upward_float, downward_float, norms_float):
            return forward(points_float, project_float, output_float, upward_float, downward_float, norms_float, members_block)
        latent_block, pullback = jax.vjp(local, points_block, parameters[0], parameters[1], parameters[2], parameters[3], parameters[4])
        gradients = pullback(cotangent_block)
        summed = tuple((total + extra for total, extra in zip(totals, gradients[1:])))
        return (summed, (latent_block, gradients[0]))
    initial = tuple((jnp.zeros_like(weight) for weight in parameters))
    totals, outputs_scan = lax.scan(accumulate, initial, (points_blocks, members_blocks, cotangent_blocks))
    latents = outputs_scan[0].reshape(ROWS, D)
    point_gradient = outputs_scan[1].reshape(ROWS, D)
    project_gradient, output_gradient, upward_gradient, downward_gradient, norm_gradient = totals
    project_new = adamw_step(project_master, project_gradient, project_first, project_second, D ** (-0.5))
    output_new = adamw_step(output_master, output_gradient, output_first, output_second, max(1, D * 4 // LAT) ** (-0.5))
    upward_new = adamw_step(upward_master, upward_gradient, upward_first, upward_second, D ** (-0.5))
    downward_new = adamw_step(downward_master, downward_gradient, downward_first, downward_second, FF ** (-0.5))
    norm_new = adamw_step(layer_norms, norm_gradient, norm_first, norm_second, 0.2)
    return (latents, point_gradient, project_gradient, project_new[0], project_new[1], project_new[2], project_new[0].astype(jnp.bfloat16), output_gradient, output_new[0], output_new[1], output_new[2], output_new[0].astype(jnp.bfloat16), upward_gradient, upward_new[0], upward_new[1], upward_new[2], upward_new[0].astype(jnp.bfloat16), downward_gradient, downward_new[0], downward_new[1], downward_new[2], downward_new[0].astype(jnp.bfloat16), norm_gradient, norm_new[0], norm_new[1], norm_new[2])
```

```python
import functools

import jax
import jax.numpy as jnp
from jax import lax
from jax.experimental import pallas as pl
from jax.experimental.pallas import tpu as pltpu
from jax.sharding import PartitionSpec as P

D = 1024
HEAD_DIM = 128
FF = 4096
LAT = 256
ADAM_STEP = 10


norm_epsilon = 1e-05
beta_one = 0.9
beta_two = 0.95
adam_epsilon = 1e-08
weight_decay = 0.1
masked_score = -1e30


def layer_norm(values, norm_gain, norm_shift):
    center = values - jnp.mean(values, axis=-1, keepdims=True)
    spread = jnp.mean(center * center, axis=-1, keepdims=True)
    return center * lax.rsqrt(spread + norm_epsilon) * norm_gain + norm_shift


def pick_rows(source_rows, row_index):
    return source_rows[row_index]


def adamw_step(weight, gradient, moment_one, moment_two, step_rate):
    one_new = beta_one * moment_one + (1.0 - beta_one) * gradient
    two_new = beta_two * moment_two + (1.0 - beta_two) * gradient * gradient
    corrected_one = one_new / (1.0 - beta_one**ADAM_STEP)
    corrected_two = two_new / (1.0 - beta_two**ADAM_STEP)
    updated = weight - step_rate * (
        corrected_one / (jnp.sqrt(corrected_two) + adam_epsilon) + weight_decay * weight
    )
    return (updated, one_new, two_new)


def masked_scores(queries, keys_all, key_mask, score_scale):
    raw_scores = (
        jnp.einsum("gqhe,gkhe->ghqk", queries, keys_all, preferred_element_type=jnp.float32)
        * score_scale
    )
    return jnp.where(key_mask, raw_scores, masked_score)


def on_device_any(
    points,
    members,
    cotangent,
    project_weight,
    output_weight,
    upward_weight,
    downward_weight,
    layer_norms,
    project_master,
    project_first,
    project_second,
    output_master,
    output_first,
    output_second,
    upward_master,
    upward_first,
    upward_second,
    downward_master,
    downward_first,
    downward_second,
    norm_first,
    norm_second,
):
    groups_here = members.shape[0]
    shard_rows = points.shape[0]
    model_width = points.shape[1]
    heads_here = project_weight.shape[2] // HEAD_DIM
    score_scale = HEAD_DIM ** (-0.5)
    grouped = points.reshape(groups_here, LAT, model_width)
    slot_index = jnp.maximum(members, 0)
    key_live = members >= 0
    picked = jax.vmap(pick_rows)(grouped, slot_index)
    inputs = jnp.where(key_live[:, :, None], picked.astype(jnp.float32), 0.0).reshape(
        shard_rows, model_width
    )
    normed, norm_back_one = jax.vjp(layer_norm, inputs, layer_norms[0], layer_norms[1])
    gathered, live_all = (
        lax.all_gather(normed.astype(jnp.bfloat16), "mp", axis=0, tiled=True),
        lax.all_gather(key_live.astype(jnp.bfloat16), "mp", axis=0, tiled=True),
    )
    total_rows = gathered.shape[0]
    total_groups = live_all.shape[0]
    key_mask = (live_all > 0)[:, None, None, :]
    projected = jnp.einsum(
        "rd,dcf->rcf", gathered, project_weight, preferred_element_type=jnp.float32
    ).astype(jnp.bfloat16)
    heads_view = projected.reshape(total_groups, LAT, 3, heads_here, HEAD_DIM)
    queries = heads_view[:, :, 0]
    keys_all = heads_view[:, :, 1]
    values_all = heads_view[:, :, 2]
    scores = masked_scores(queries, keys_all, key_mask, score_scale)
    row_top = jnp.max(scores, axis=-1, keepdims=True)
    exponent = jnp.exp(scores - row_top)
    row_total = jnp.sum(exponent, axis=-1, keepdims=True)
    attention_weights = exponent / row_total
    log_total = row_top + jnp.log(row_total)
    weights_low = attention_weights.astype(jnp.bfloat16)
    attended = jnp.einsum(
        "ghqk,gkhe->gqhe", weights_low, values_all, preferred_element_type=jnp.float32
    ).astype(jnp.bfloat16)
    attended = attended.reshape(total_rows, heads_here * HEAD_DIM)
    branch = lax.psum_scatter(
        jnp.dot(attended, output_weight, preferred_element_type=jnp.float32),
        "mp",
        scatter_dimension=0,
        tiled=True,
    )
    residual = inputs + branch
    normed_two, norm_back_two = jax.vjp(layer_norm, residual, layer_norms[2], layer_norms[3])
    gathered_two = lax.all_gather(normed_two.astype(jnp.bfloat16), "mp", axis=0, tiled=True)
    upward = jnp.dot(gathered_two, upward_weight, preferred_element_type=jnp.float32)
    activated_float, gelu_back = jax.vjp(jax.nn.gelu, upward)
    activated = activated_float.astype(jnp.bfloat16)
    latents = residual + lax.psum_scatter(
        jnp.dot(activated, downward_weight, preferred_element_type=jnp.float32).astype(
            jnp.bfloat16
        ),
        "mp",
        scatter_dimension=0,
        tiled=True,
    ).astype(jnp.float32)
    cotangent_all = lax.all_gather(cotangent, "mp", axis=0, tiled=True)
    downward_local = jnp.einsum(
        "rf,rd->fd", activated, cotangent_all, preferred_element_type=jnp.float32
    )
    activated_grad = jnp.einsum(
        "rd,fd->rf", cotangent_all, downward_weight, preferred_element_type=jnp.float32
    )
    upward_grad = gelu_back(activated_grad)[0].astype(jnp.bfloat16)
    upward_local = jnp.einsum(
        "rd,rf->df", gathered_two, upward_grad, preferred_element_type=jnp.float32
    )
    normed_two_grad = lax.psum_scatter(
        jnp.einsum("rf,df->rd", upward_grad, upward_weight, preferred_element_type=jnp.float32),
        "mp",
        scatter_dimension=0,
        tiled=True,
    )
    residual_part, gain_two_grad, shift_two_grad = norm_back_two(normed_two_grad)
    residual_grad = residual_part + cotangent.astype(jnp.float32)
    norm_two_local = jnp.stack([gain_two_grad, shift_two_grad])
    branch_grad = lax.all_gather(residual_grad.astype(jnp.bfloat16), "mp", axis=0, tiled=True)
    output_local = jnp.einsum(
        "rh,rd->hd", attended, branch_grad, preferred_element_type=jnp.float32
    )
    attended_grad = jnp.einsum(
        "rd,hd->rh", branch_grad, output_weight, preferred_element_type=jnp.float32
    ).astype(jnp.bfloat16)
    attended_grad = attended_grad.reshape(total_groups, LAT, heads_here, HEAD_DIM)
    scores_again = masked_scores(queries, keys_all, key_mask, score_scale)
    weights_again = jnp.exp(scores_again - log_total)
    weights_again_low = weights_again.astype(jnp.bfloat16)
    value_grad = jnp.einsum(
        "ghqk,gqhe->gkhe", weights_again_low, attended_grad, preferred_element_type=jnp.float32
    ).astype(jnp.bfloat16)
    weight_grad = jnp.einsum(
        "gqhe,gkhe->ghqk", attended_grad, values_all, preferred_element_type=jnp.float32
    )
    score_grad = (
        weights_again * (weight_grad - jnp.sum(weights_again * weight_grad, axis=-1, keepdims=True))
    ).astype(jnp.bfloat16)
    query_grad = (
        jnp.einsum("ghqk,gkhe->gqhe", score_grad, keys_all, preferred_element_type=jnp.float32)
        * score_scale
    ).astype(jnp.bfloat16)
    key_grad = (
        jnp.einsum("ghqk,gqhe->gkhe", score_grad, queries, preferred_element_type=jnp.float32)
        * score_scale
    ).astype(jnp.bfloat16)
    projected_grad = jnp.stack([query_grad, key_grad, value_grad], axis=2).reshape(
        total_rows, 3, heads_here * HEAD_DIM
    )
    project_local = jnp.einsum(
        "rd,rcf->dcf", gathered, projected_grad, preferred_element_type=jnp.float32
    )
    normed_grad = lax.psum_scatter(
        jnp.einsum(
            "rcf,dcf->rd", projected_grad, project_weight, preferred_element_type=jnp.float32
        ).astype(jnp.bfloat16),
        "mp",
        scatter_dimension=0,
        tiled=True,
    ).astype(jnp.float32)
    input_part, gain_one_grad, shift_one_grad = norm_back_one(normed_grad)
    input_grad = input_part + residual_grad
    norm_one_local = jnp.stack([gain_one_grad, shift_one_grad])
    matches = members[:, :, None] == jnp.arange(LAT, dtype=jnp.int32)[None, None, :]
    slot_of = jnp.argmax(matches, axis=1)
    point_used = jnp.any(matches, axis=1)
    grouped_grad = input_grad.reshape(groups_here, LAT, model_width)
    point_gradient = jnp.where(
        point_used[:, :, None], jax.vmap(pick_rows)(grouped_grad, slot_of), 0.0
    ).reshape(shard_rows, model_width)
    (
        project_summed,
        output_summed,
        upward_summed,
        downward_summed,
        norm_one_summed,
        norm_two_summed,
    ) = (
        lax.psum_scatter(project_local, "dp", scatter_dimension=0, tiled=True),
        lax.psum_scatter(output_local, "dp", scatter_dimension=1, tiled=True),
        lax.psum_scatter(upward_local, "dp", scatter_dimension=0, tiled=True),
        lax.psum_scatter(downward_local, "dp", scatter_dimension=1, tiled=True),
        lax.psum_scatter(norm_one_local, "dp", scatter_dimension=1, tiled=True),
        lax.psum_scatter(norm_two_local, "dp", scatter_dimension=1, tiled=True),
    )
    norm_gradient = lax.psum(jnp.concatenate([norm_one_summed, norm_two_summed], axis=0), "mp")
    data_index = lax.axis_index("dp")
    norm_columns = norm_first.shape[1]
    norm_current = lax.dynamic_slice_in_dim(layer_norms, data_index * norm_columns, norm_columns, 1)
    project_new = adamw_step(
        project_master, project_summed, project_first, project_second, D ** (-0.5)
    )
    output_new = adamw_step(
        output_master, output_summed, output_first, output_second, max(1, D * 4 // LAT) ** (-0.5)
    )
    upward_new = adamw_step(upward_master, upward_summed, upward_first, upward_second, D ** (-0.5))
    downward_new = adamw_step(
        downward_master, downward_summed, downward_first, downward_second, FF ** (-0.5)
    )
    norm_new = adamw_step(norm_current, norm_gradient, norm_first, norm_second, 0.2)
    return (
        latents,
        point_gradient,
        project_summed,
        project_new[0],
        project_new[1],
        project_new[2],
        project_new[0].astype(jnp.bfloat16),
        output_summed,
        output_new[0],
        output_new[1],
        output_new[2],
        output_new[0].astype(jnp.bfloat16),
        upward_summed,
        upward_new[0],
        upward_new[1],
        upward_new[2],
        upward_new[0].astype(jnp.bfloat16),
        downward_summed,
        downward_new[0],
        downward_new[1],
        downward_new[2],
        downward_new[0].astype(jnp.bfloat16),
        norm_gradient,
        norm_new[0],
        norm_new[1],
        norm_new[2],
    )


MESH = pl.DeviceIdType.MESH
PLANES = 4
OWNERS = 8


def place():
    dp = lax.axis_index("dp")
    return dp // 4, (dp // 2) % 2, dp % 2, lax.axis_index("mp")


def device(y, x, c, z):
    return (y * 4 + x * 2 + c, z)


def greet(y, x, c, z):
    barrier = pltpu.get_barrier_semaphore()
    partners = [device(1 - y, x, c, z), device(y, 1 - x, c, z), device(y, x, 1 - c, z)]
    partners += [device(y, x, c, (z + d) % PLANES) for d in (1, 2, 3)]
    for partner in partners:
        pl.semaphore_signal(barrier, inc=1, device_id=partner, device_id_type=MESH)
    pl.semaphore_wait(barrier, len(partners))


def gather_kernel(*refs):
    shards, fulls = refs[0:4], refs[4:8]
    own_sem, z_send, z_recv, a_send, a_recv, b_send, b_recv, c_send, c_recv = refs[8:]
    y, x, c, z = place()
    greet(y, x, c, z)

    def view(ref, lead, rows):
        index = (rows, slice(None))
        if len(ref.shape) - len(lead) == 3:
            index = (slice(None),) + index
        return ref.at[lead + index]

    def row_count(w):
        return shards[w].shape[-2]

    def block(w, half, first, count):
        size = row_count(w) // 16
        start = pl.multiple_of(half * (row_count(w) // 2) + first * size, size)
        return pl.ds(start, count * size)

    spot = (c * 4 + y * 2 + x, c * 4 + x * 2 + y)
    pair = (c * 4 + y * 2, c * 4 + x * 2)
    quad = (c * 4, c * 4)
    first_hop = (device(y, 1 - x, c, z), device(1 - y, x, c, z))
    second_hop = (device(1 - y, x, c, z), device(y, 1 - x, c, z))

    def z_copy(w, d, half):
        rows = block(w, half, spot[half], 1)
        return pltpu.make_async_remote_copy(
            src_ref=view(shards[w], (), rows),
            dst_ref=view(fulls[w], (z,), rows),
            send_sem=z_send.at[w, d - 1, half],
            recv_sem=z_recv.at[w, d - 1, half],
            device_id=device(y, x, c, (z + d) % PLANES),
            device_id_type=MESH,
        )

    def plane_copy(w, d, half, first, count, target, send, recv):
        shard = (z - d + PLANES) % PLANES
        rows = block(w, half, first, count)
        return pltpu.make_async_remote_copy(
            src_ref=view(fulls[w], (shard,), rows),
            dst_ref=view(fulls[w], (shard,), rows),
            send_sem=send.at[w, d - 1, half],
            recv_sem=recv.at[w, d - 1, half],
            device_id=target,
            device_id_type=MESH,
        )

    def a_copy(w, d, half):
        return plane_copy(w, d, half, spot[half], 1, first_hop[half], a_send, a_recv)

    def b_copy(w, d, half):
        return plane_copy(w, d, half, pair[half], 2, second_hop[half], b_send, b_recv)

    def c_copy(w, d, half):
        return plane_copy(w, d, half, quad[half], 4, device(y, x, 1 - c, z), c_send, c_recv)

    stages = (z_copy, a_copy, b_copy, c_copy)
    chunks = [(w, d) for w in range(4) for d in (1, 2, 3)]
    locals_ = [
        pltpu.make_async_copy(shards[w], fulls[w].at[z], own_sem.at[w]) for w in range(4)
    ]
    lag = (0, 2, 3, 4, 5)
    for step in range(len(chunks) + lag[-1]):
        if step < len(chunks):
            for half in (0, 1):
                z_copy(*chunks[step], half).start()
        if step < 4:
            locals_[step].start()
        for stage in range(1, 5):
            at = step - lag[stage]
            if 0 <= at < len(chunks):
                for half in (0, 1):
                    stages[stage - 1](*chunks[at], half).wait_recv()
                    if stage < 4:
                        stages[stage](*chunks[at], half).start()
    for w, d in chunks:
        for half in (0, 1):
            for make in stages:
                make(w, d, half).wait_send()
    for copy in locals_:
        copy.wait()


def gather_weights(*shards):
    sems = pltpu.SemaphoreType.DMA((4, 3, 2))
    return pl.pallas_call(
        gather_kernel,
        out_shape=[jax.ShapeDtypeStruct((PLANES,) + s.shape, s.dtype) for s in shards],
        in_specs=[pl.BlockSpec(memory_space=pl.ANY)] * 4,
        out_specs=[pl.BlockSpec(memory_space=pl.ANY)] * 4,
        scratch_shapes=[pltpu.SemaphoreType.DMA((4,))] + [sems] * 8,
        name="gather_weights",
        compiler_params=pltpu.CompilerParams(collective_id=0, has_side_effects=True),
    )(*shards)


BLOCKS = ((1024, 128), (128, 1024), (256, 128), (384, 256))
STRIPS = (128, 16, 128, 64)


def owner_view(ref, w, plane, owner):
    if w in (0, 2):
        return ref.at[plane, :, pl.ds(pl.multiple_of(owner * 128, 128), 128)]
    return ref.at[plane, pl.ds(pl.multiple_of(owner * BLOCKS[w][0], BLOCKS[w][0]), BLOCKS[w][0]), :]


def reduce_kernel(*refs):
    grads, norm_part = refs[0:4], refs[4]
    outs, norm_out = refs[5:9], refs[9]
    own, pair_in, one_in, two_in, z_in = (refs[10 + 4 * k : 14 + 4 * k] for k in range(5))
    norm_own, norm_in, norm_planes = refs[30:33]
    load_sem, c_send, c_recv, one_send, one_recv, two_send, two_recv, z_send, z_recv = refs[33:42]
    norm_send, norm_recv = refs[42:44]
    y, x, c, z = place()
    greet(y, x, c, z)
    sibling = device(y, x, 1 - c, z)
    over_x, over_y = device(y, 1 - x, c, z), device(1 - y, x, c, z)

    def plane_of(i):
        return (z + 1 + i) % PLANES

    def remote(src, dst, send, recv, target):
        return pltpu.make_async_remote_copy(
            src_ref=src, dst_ref=dst, send_sem=send, recv_sem=recv, device_id=target, device_id_type=MESH
        )

    def load(w, i, k):
        return pltpu.make_async_copy(
            owner_view(grads[w], w, plane_of(i), k * 2 + c), own[w].at[i, k // 2, k % 2], load_sem.at[w, i, k]
        )

    def pair_copy(w, i, k):
        return remote(
            owner_view(grads[w], w, plane_of(i), k * 2 + 1 - c),
            pair_in[w].at[i, k // 2, k % 2],
            c_send.at[w, i, k],
            c_recv.at[w, i, k],
            sibling,
        )

    def half_rows(w, half):
        size = BLOCKS[w][0] // 2
        return pl.ds(half * size, size)

    def one_copy(w, i, half):
        rows = half_rows(w, half)
        src = own[w].at[i, 1 - y, :, rows] if half == 0 else own[w].at[i, :, 1 - x, rows]
        return remote(
            src, one_in[w].at[i, half], one_send.at[w, i, half], one_recv.at[w, i, half], (over_y, over_x)[half]
        )

    def two_copy(w, i, half):
        rows = half_rows(w, half)
        src = own[w].at[i, y, 1 - x, rows] if half == 0 else own[w].at[i, 1 - y, x, rows]
        return remote(
            src, two_in[w].at[i, half], two_send.at[w, i, half], two_recv.at[w, i, half], (over_x, over_y)[half]
        )

    def z_copy(w, i):
        return remote(
            own[w].at[i, y, x], z_in[w].at[i], z_send.at[w, i], z_recv.at[w, i], device(y, x, c, plane_of(i))
        )

    def add_rows(target, source, count, strip):
        def body(r, carry):
            rows = pl.ds(pl.multiple_of(r * strip, strip), strip)
            total = target[rows].astype(jnp.float32) + source[rows].astype(jnp.float32)
            target[rows] = total.astype(target.dtype)
            return carry

        lax.fori_loop(0, count // strip, body, 0)

    def start_unit(w, i):
        for k in range(4):
            pair_copy(w, i, k).start()
            load(w, i, k).start()

    def after_pair(w, i):
        for k in range(4):
            load(w, i, k).wait()
            pair_copy(w, i, k).wait_recv()
            add_rows(own[w].at[i, k // 2, k % 2], pair_in[w].at[i, k // 2, k % 2], BLOCKS[w][0], STRIPS[w])
        for half in (0, 1):
            one_copy(w, i, half).start()

    def after_one(w, i):
        size = BLOCKS[w][0] // 2
        for half in (0, 1):
            one_copy(w, i, half).wait()
            rows = half_rows(w, half)
            for k in (0, 1):
                target = own[w].at[i, y, k, rows] if half == 0 else own[w].at[i, k, x, rows]
                add_rows(target, one_in[w].at[i, half, k], size, min(size, STRIPS[w]))
            two_copy(w, i, half).start()

    def after_two(w, i):
        size = BLOCKS[w][0] // 2
        for half in (0, 1):
            two_copy(w, i, half).wait()
            add_rows(own[w].at[i, y, x, half_rows(w, half)], two_in[w].at[i, half], size, min(size, STRIPS[w]))
        if i < PLANES - 1:
            z_copy(w, i).start()

    def finish(w):
        for i in range(PLANES - 1):
            z_copy(w, i).wait()

        def body(r, carry):
            rows = pl.ds(pl.multiple_of(r * STRIPS[w], STRIPS[w]), STRIPS[w])
            total = own[w].at[PLANES - 1, y, x][rows].astype(jnp.float32)
            for i in range(PLANES - 1):
                total = total + z_in[w].at[i][rows].astype(jnp.float32)
            outs[w][rows] = total
            return carry

        lax.fori_loop(0, BLOCKS[w][0] // STRIPS[w], body, 0)

    def norm_step(k):
        return remote(
            norm_own.at[k], norm_in.at[k], norm_send.at[k], norm_recv.at[k], (sibling, over_x, over_y)[k]
        )

    def norm_plane(d):
        return remote(
            norm_own.at[3],
            norm_planes.at[z],
            norm_send.at[2 + d],
            norm_recv.at[2 + d],
            device(y, x, c, (z + d) % PLANES),
        )

    norm_own[0] = norm_part[...]
    norm_step(0).start()

    units = [(w, i) for w in range(4) for i in range(PLANES)]
    ahead = 2
    for unit in units[:ahead]:
        start_unit(*unit)
    for step in range(len(units) + 4):
        if step + ahead < len(units):
            start_unit(*units[step + ahead])
        if step < len(units):
            after_pair(*units[step])
        if 0 <= step - 1 < len(units):
            after_one(*units[step - 1])
        if 0 <= step - 2 < len(units):
            after_two(*units[step - 2])
        if step < 3:
            norm_step(step).wait()
            norm_own[step + 1] = norm_own[step] + norm_in[step]
            if step < 2:
                norm_step(step + 1).start()
            else:
                norm_planes[z] = norm_own[3]
                for d in (1, 2, 3):
                    norm_plane(d).start()
        if step >= 4 and (step - 4) % PLANES == PLANES - 1:
            finish((step - 4) // PLANES)
    for d in (1, 2, 3):
        norm_plane(d).wait()
    norm_out[...] = (norm_planes[0] + norm_planes[1]) + (norm_planes[2] + norm_planes[3])
    for w, i in units:
        for k in range(4):
            pair_copy(w, i, k).wait_send()


def reduce_gradients(grads, norm_part):
    bf16 = jnp.bfloat16
    halves = [(b[0] // 2, b[1]) for b in BLOCKS]
    scratch = [pltpu.VMEM((4, 2, 2) + b, bf16) for b in BLOCKS]
    scratch += [pltpu.VMEM((4, 2, 2) + b, bf16) for b in BLOCKS]
    scratch += [pltpu.VMEM((4, 2, 2) + h, bf16) for h in halves]
    scratch += [pltpu.VMEM((4, 2) + h, bf16) for h in halves]
    scratch += [pltpu.VMEM((3,) + b, bf16) for b in BLOCKS]
    scratch += [
        pltpu.VMEM((4,) + norm_part.shape, jnp.float32),
        pltpu.VMEM((3,) + norm_part.shape, jnp.float32),
        pltpu.VMEM((4,) + norm_part.shape, jnp.float32),
    ]
    dma = pltpu.SemaphoreType.DMA
    scratch += [dma((4, 4, 4)), dma((4, 4, 4)), dma((4, 4, 4)), dma((4, 4, 2)), dma((4, 4, 2))]
    scratch += [dma((4, 4, 2)), dma((4, 4, 2)), dma((4, 3)), dma((4, 3)), dma((6,)), dma((6,))]
    vmem = pl.BlockSpec(memory_space=pltpu.VMEM)
    result = pl.pallas_call(
        reduce_kernel,
        out_shape=[jax.ShapeDtypeStruct(b, jnp.float32) for b in BLOCKS]
        + [jax.ShapeDtypeStruct(norm_part.shape, jnp.float32)],
        in_specs=[pl.BlockSpec(memory_space=pl.ANY)] * 4 + [vmem],
        out_specs=[vmem] * 5,
        scratch_shapes=scratch,
        name="reduce_gradients",
        compiler_params=pltpu.CompilerParams(
            collective_id=1, has_side_effects=True, vmem_limit_bytes=48 << 20
        ),
    )(*grads, norm_part)
    return result[:4], result[4]


def on_device_cube(
    points,
    members,
    cotangent,
    project_weight,
    output_weight,
    upward_weight,
    downward_weight,
    layer_norms,
    project_master,
    project_first,
    project_second,
    output_master,
    output_first,
    output_second,
    upward_master,
    upward_first,
    upward_second,
    downward_master,
    downward_first,
    downward_second,
    norm_first,
    norm_second,
):
    f32, bf16 = jnp.float32, jnp.bfloat16
    score_scale = HEAD_DIM ** (-0.5)
    project_full, output_full, upward_full, downward_full = gather_weights(
        jnp.transpose(project_weight, (1, 0, 2)), output_weight, upward_weight, downward_weight
    )
    rows = points.shape[0]
    slots = members[0]
    live = slots >= 0
    inputs = jnp.where(live[:, None], points[jnp.maximum(slots, 0)].astype(f32), 0.0)
    normed, norm_back_one = jax.vjp(layer_norm, inputs, layer_norms[0], layer_norms[1])
    entering_one = normed.astype(bf16)
    projected = jnp.einsum("rd,sjdf->sjrf", entering_one, project_full, preferred_element_type=f32).astype(bf16)
    heads_view = projected.reshape(PLANES, 3, rows, 2, HEAD_DIM)
    queries, keys_all, values_all = heads_view[:, 0], heads_view[:, 1], heads_view[:, 2]
    scores = jnp.einsum("sqhe,skhe->shqk", queries, keys_all, preferred_element_type=f32) * score_scale
    scores = jnp.where(live[None, None, None, :], scores, masked_score)
    probs = jax.nn.softmax(scores, axis=-1)
    probs_low = probs.astype(bf16)
    attended = jnp.einsum("shqk,skhe->sqhe", probs_low, values_all, preferred_element_type=f32).astype(bf16)
    attended = attended.reshape(PLANES, rows, 2 * HEAD_DIM)
    residual = inputs + jnp.einsum("srh,shd->rd", attended, output_full, preferred_element_type=f32)
    normed_two, norm_back_two = jax.vjp(layer_norm, residual, layer_norms[2], layer_norms[3])
    entering_two = normed_two.astype(bf16)
    upward = jnp.einsum("rd,sdf->srf", entering_two, upward_full, preferred_element_type=f32)
    activated_float, gelu_back = jax.vjp(jax.nn.gelu, upward)
    activated = activated_float.astype(bf16)
    latents = residual + jnp.einsum("srf,sfd->rd", activated, downward_full, preferred_element_type=f32)
    downward_part = jnp.einsum("srf,rd->sfd", activated, cotangent, preferred_element_type=f32).astype(bf16)
    activated_grad = jnp.einsum("rd,sfd->srf", cotangent, downward_full, preferred_element_type=f32)
    upward_grad = gelu_back(activated_grad)[0].astype(bf16)
    upward_part = jnp.einsum("rd,srf->sdf", entering_two, upward_grad, preferred_element_type=f32).astype(bf16)
    normed_two_grad = jnp.einsum("srf,sdf->rd", upward_grad, upward_full, preferred_element_type=f32)
    residual_part, gain_two_grad, shift_two_grad = norm_back_two(normed_two_grad)
    residual_grad = residual_part + cotangent.astype(f32)
    branch_grad = residual_grad.astype(bf16)
    output_part = jnp.einsum("srh,rd->shd", attended, branch_grad, preferred_element_type=f32).astype(bf16)
    attended_grad = jnp.einsum("rd,shd->srh", branch_grad, output_full, preferred_element_type=f32).astype(bf16)
    attended_grad = attended_grad.reshape(PLANES, rows, 2, HEAD_DIM)
    value_grad = jnp.einsum("shqk,sqhe->skhe", probs_low, attended_grad, preferred_element_type=f32).astype(bf16)
    prob_grad = jnp.einsum("sqhe,skhe->shqk", attended_grad, values_all, preferred_element_type=f32)
    score_grad = (probs * (prob_grad - jnp.sum(probs * prob_grad, axis=-1, keepdims=True))).astype(bf16)
    query_grad = jnp.einsum("shqk,skhe->sqhe", score_grad, keys_all, preferred_element_type=f32) * score_scale
    key_grad = jnp.einsum("shqk,sqhe->skhe", score_grad, queries, preferred_element_type=f32) * score_scale
    projected_grad = jnp.stack([query_grad.astype(bf16), key_grad.astype(bf16), value_grad], axis=1)
    projected_grad = projected_grad.reshape(PLANES, 3, rows, 2 * HEAD_DIM)
    project_part = jnp.einsum(
        "rod,sjrf->sojdf",
        entering_one.reshape(rows, OWNERS, D // OWNERS),
        projected_grad,
        preferred_element_type=f32,
    ).astype(bf16)
    normed_grad = jnp.einsum("sjrf,sjdf->rd", projected_grad, project_full, preferred_element_type=f32)
    input_part, gain_one_grad, shift_one_grad = norm_back_one(normed_grad)
    input_grad = input_part + residual_grad
    norm_part = jnp.stack([gain_one_grad, shift_one_grad, gain_two_grad, shift_two_grad])
    matches = slots[:, None] == jnp.arange(LAT, dtype=jnp.int32)[None, :]
    slot_of = jnp.argmax(matches, axis=0)
    point_gradient = jnp.where(jnp.any(matches, axis=0)[:, None], input_grad[slot_of], 0.0)
    (downward_summed, upward_summed, output_summed, project_blocks), norm_summed = reduce_gradients(
        (downward_part, upward_part, output_part, project_part.reshape(PLANES, OWNERS * 384, 256)), norm_part
    )
    project_summed = jnp.transpose(project_blocks.reshape(3, D // OWNERS, 256), (1, 0, 2))
    data_index = lax.axis_index("dp")
    norm_columns = norm_first.shape[1]
    norm_gradient = lax.dynamic_slice_in_dim(norm_summed, data_index * norm_columns, norm_columns, 1)
    norm_current = lax.dynamic_slice_in_dim(layer_norms, data_index * norm_columns, norm_columns, 1)
    results = [latents, point_gradient]
    for master, summed, first, second, rate in (
        (project_master, project_summed, project_first, project_second, D ** (-0.5)),
        (output_master, output_summed, output_first, output_second, max(1, D * 4 // LAT) ** (-0.5)),
        (upward_master, upward_summed, upward_first, upward_second, D ** (-0.5)),
        (downward_master, downward_summed, downward_first, downward_second, FF ** (-0.5)),
    ):
        updated, one_new, two_new = adamw_step(master, summed, first, second, rate)
        results += [summed, updated, one_new, two_new, updated.astype(bf16)]
    norm_new = adamw_step(norm_current, norm_gradient, norm_first, norm_second, 0.2)
    results += [norm_gradient, *norm_new]
    return tuple(results)


def solution(mesh):
    return jax.shard_map(
        on_device_cube if dict(mesh.shape) == {"dp": 8, "mp": 4} else on_device_any,
        mesh=mesh,
        in_specs=(
            P(("dp", "mp"), None),
            P(("dp", "mp"), None),
            P(("dp", "mp"), None),
            P(None, None, "mp"),
            P("mp", None),
            P(None, "mp"),
            P("mp", None),
            P(),
            P("dp", None, "mp"),
            P("dp", None, "mp"),
            P("dp", None, "mp"),
            P("mp", "dp"),
            P("mp", "dp"),
            P("mp", "dp"),
            P("dp", "mp"),
            P("dp", "mp"),
            P("dp", "mp"),
            P("mp", "dp"),
            P("mp", "dp"),
            P("mp", "dp"),
            P(None, "dp"),
            P(None, "dp"),
        ),
        out_specs=(
            P(("dp", "mp"), None),
            P(("dp", "mp"), None),
            P("dp", None, "mp"),
            P("dp", None, "mp"),
            P("dp", None, "mp"),
            P("dp", None, "mp"),
            P("dp", None, "mp"),
            P("mp", "dp"),
            P("mp", "dp"),
            P("mp", "dp"),
            P("mp", "dp"),
            P("mp", "dp"),
            P("dp", "mp"),
            P("dp", "mp"),
            P("dp", "mp"),
            P("dp", "mp"),
            P("dp", "mp"),
            P("mp", "dp"),
            P("mp", "dp"),
            P("mp", "dp"),
            P("mp", "dp"),
            P("mp", "dp"),
            P(None, "dp"),
            P(None, "dp"),
            P(None, "dp"),
            P(None, "dp"),
        ),
        check_vma=False,
    )
```

```python
import functools

import jax
import jax.numpy as jnp
from jax import lax
from jax.experimental import pallas as pl
from jax.experimental.pallas import tpu as pltpu
from jax.sharding import PartitionSpec as P

D = 1024
HEAD_DIM = 128
FF = 4096
LAT = 256
ADAM_STEP = 10


norm_epsilon = 1e-05
beta_one = 0.9
beta_two = 0.95
adam_epsilon = 1e-08
weight_decay = 0.1
masked_score = -1e30


def layer_norm(values, norm_gain, norm_shift):
    center = values - jnp.mean(values, axis=-1, keepdims=True)
    spread = jnp.mean(center * center, axis=-1, keepdims=True)
    return center * lax.rsqrt(spread + norm_epsilon) * norm_gain + norm_shift


def pick_rows(source_rows, row_index):
    return source_rows[row_index]


def adamw_step(weight, gradient, moment_one, moment_two, step_rate):
    one_new = beta_one * moment_one + (1.0 - beta_one) * gradient
    two_new = beta_two * moment_two + (1.0 - beta_two) * gradient * gradient
    corrected_one = one_new / (1.0 - beta_one**ADAM_STEP)
    corrected_two = two_new / (1.0 - beta_two**ADAM_STEP)
    updated = weight - step_rate * (
        corrected_one / (jnp.sqrt(corrected_two) + adam_epsilon) + weight_decay * weight
    )
    return (updated, one_new, two_new)


def masked_scores(queries, keys_all, key_mask, score_scale):
    raw_scores = (
        jnp.einsum("gqhe,gkhe->ghqk", queries, keys_all, preferred_element_type=jnp.float32)
        * score_scale
    )
    return jnp.where(key_mask, raw_scores, masked_score)


def on_device_any(
    points,
    members,
    cotangent,
    project_weight,
    output_weight,
    upward_weight,
    downward_weight,
    layer_norms,
    project_master,
    project_first,
    project_second,
    output_master,
    output_first,
    output_second,
    upward_master,
    upward_first,
    upward_second,
    downward_master,
    downward_first,
    downward_second,
    norm_first,
    norm_second,
):
    groups_here = members.shape[0]
    shard_rows = points.shape[0]
    model_width = points.shape[1]
    heads_here = project_weight.shape[2] // HEAD_DIM
    score_scale = HEAD_DIM ** (-0.5)
    grouped = points.reshape(groups_here, LAT, model_width)
    slot_index = jnp.maximum(members, 0)
    key_live = members >= 0
    picked = jax.vmap(pick_rows)(grouped, slot_index)
    inputs = jnp.where(key_live[:, :, None], picked.astype(jnp.float32), 0.0).reshape(
        shard_rows, model_width
    )
    normed, norm_back_one = jax.vjp(layer_norm, inputs, layer_norms[0], layer_norms[1])
    gathered, live_all = (
        lax.all_gather(normed.astype(jnp.bfloat16), "mp", axis=0, tiled=True),
        lax.all_gather(key_live.astype(jnp.bfloat16), "mp", axis=0, tiled=True),
    )
    total_rows = gathered.shape[0]
    total_groups = live_all.shape[0]
    key_mask = (live_all > 0)[:, None, None, :]
    projected = jnp.einsum(
        "rd,dcf->rcf", gathered, project_weight, preferred_element_type=jnp.float32
    ).astype(jnp.bfloat16)
    heads_view = projected.reshape(total_groups, LAT, 3, heads_here, HEAD_DIM)
    queries = heads_view[:, :, 0]
    keys_all = heads_view[:, :, 1]
    values_all = heads_view[:, :, 2]
    scores = masked_scores(queries, keys_all, key_mask, score_scale)
    row_top = jnp.max(scores, axis=-1, keepdims=True)
    exponent = jnp.exp(scores - row_top)
    row_total = jnp.sum(exponent, axis=-1, keepdims=True)
    attention_weights = exponent / row_total
    log_total = row_top + jnp.log(row_total)
    weights_low = attention_weights.astype(jnp.bfloat16)
    attended = jnp.einsum(
        "ghqk,gkhe->gqhe", weights_low, values_all, preferred_element_type=jnp.float32
    ).astype(jnp.bfloat16)
    attended = attended.reshape(total_rows, heads_here * HEAD_DIM)
    branch = lax.psum_scatter(
        jnp.dot(attended, output_weight, preferred_element_type=jnp.float32),
        "mp",
        scatter_dimension=0,
        tiled=True,
    )
    residual = inputs + branch
    normed_two, norm_back_two = jax.vjp(layer_norm, residual, layer_norms[2], layer_norms[3])
    gathered_two = lax.all_gather(normed_two.astype(jnp.bfloat16), "mp", axis=0, tiled=True)
    upward = jnp.dot(gathered_two, upward_weight, preferred_element_type=jnp.float32)
    activated_float, gelu_back = jax.vjp(jax.nn.gelu, upward)
    activated = activated_float.astype(jnp.bfloat16)
    latents = residual + lax.psum_scatter(
        jnp.dot(activated, downward_weight, preferred_element_type=jnp.float32).astype(
            jnp.bfloat16
        ),
        "mp",
        scatter_dimension=0,
        tiled=True,
    ).astype(jnp.float32)
    cotangent_all = lax.all_gather(cotangent, "mp", axis=0, tiled=True)
    downward_local = jnp.einsum(
        "rf,rd->fd", activated, cotangent_all, preferred_element_type=jnp.float32
    )
    activated_grad = jnp.einsum(
        "rd,fd->rf", cotangent_all, downward_weight, preferred_element_type=jnp.float32
    )
    upward_grad = gelu_back(activated_grad)[0].astype(jnp.bfloat16)
    upward_local = jnp.einsum(
        "rd,rf->df", gathered_two, upward_grad, preferred_element_type=jnp.float32
    )
    normed_two_grad = lax.psum_scatter(
        jnp.einsum("rf,df->rd", upward_grad, upward_weight, preferred_element_type=jnp.float32),
        "mp",
        scatter_dimension=0,
        tiled=True,
    )
    residual_part, gain_two_grad, shift_two_grad = norm_back_two(normed_two_grad)
    residual_grad = residual_part + cotangent.astype(jnp.float32)
    norm_two_local = jnp.stack([gain_two_grad, shift_two_grad])
    branch_grad = lax.all_gather(residual_grad.astype(jnp.bfloat16), "mp", axis=0, tiled=True)
    output_local = jnp.einsum(
        "rh,rd->hd", attended, branch_grad, preferred_element_type=jnp.float32
    )
    attended_grad = jnp.einsum(
        "rd,hd->rh", branch_grad, output_weight, preferred_element_type=jnp.float32
    ).astype(jnp.bfloat16)
    attended_grad = attended_grad.reshape(total_groups, LAT, heads_here, HEAD_DIM)
    scores_again = masked_scores(queries, keys_all, key_mask, score_scale)
    weights_again = jnp.exp(scores_again - log_total)
    weights_again_low = weights_again.astype(jnp.bfloat16)
    value_grad = jnp.einsum(
        "ghqk,gqhe->gkhe", weights_again_low, attended_grad, preferred_element_type=jnp.float32
    ).astype(jnp.bfloat16)
    weight_grad = jnp.einsum(
        "gqhe,gkhe->ghqk", attended_grad, values_all, preferred_element_type=jnp.float32
    )
    score_grad = (
        weights_again * (weight_grad - jnp.sum(weights_again * weight_grad, axis=-1, keepdims=True))
    ).astype(jnp.bfloat16)
    query_grad = (
        jnp.einsum("ghqk,gkhe->gqhe", score_grad, keys_all, preferred_element_type=jnp.float32)
        * score_scale
    ).astype(jnp.bfloat16)
    key_grad = (
        jnp.einsum("ghqk,gqhe->gkhe", score_grad, queries, preferred_element_type=jnp.float32)
        * score_scale
    ).astype(jnp.bfloat16)
    projected_grad = jnp.stack([query_grad, key_grad, value_grad], axis=2).reshape(
        total_rows, 3, heads_here * HEAD_DIM
    )
    project_local = jnp.einsum(
        "rd,rcf->dcf", gathered, projected_grad, preferred_element_type=jnp.float32
    )
    normed_grad = lax.psum_scatter(
        jnp.einsum(
            "rcf,dcf->rd", projected_grad, project_weight, preferred_element_type=jnp.float32
        ).astype(jnp.bfloat16),
        "mp",
        scatter_dimension=0,
        tiled=True,
    ).astype(jnp.float32)
    input_part, gain_one_grad, shift_one_grad = norm_back_one(normed_grad)
    input_grad = input_part + residual_grad
    norm_one_local = jnp.stack([gain_one_grad, shift_one_grad])
    matches = members[:, :, None] == jnp.arange(LAT, dtype=jnp.int32)[None, None, :]
    slot_of = jnp.argmax(matches, axis=1)
    point_used = jnp.any(matches, axis=1)
    grouped_grad = input_grad.reshape(groups_here, LAT, model_width)
    point_gradient = jnp.where(
        point_used[:, :, None], jax.vmap(pick_rows)(grouped_grad, slot_of), 0.0
    ).reshape(shard_rows, model_width)
    (
        project_summed,
        output_summed,
        upward_summed,
        downward_summed,
        norm_one_summed,
        norm_two_summed,
    ) = (
        lax.psum_scatter(project_local, "dp", scatter_dimension=0, tiled=True),
        lax.psum_scatter(output_local, "dp", scatter_dimension=1, tiled=True),
        lax.psum_scatter(upward_local, "dp", scatter_dimension=0, tiled=True),
        lax.psum_scatter(downward_local, "dp", scatter_dimension=1, tiled=True),
        lax.psum_scatter(norm_one_local, "dp", scatter_dimension=1, tiled=True),
        lax.psum_scatter(norm_two_local, "dp", scatter_dimension=1, tiled=True),
    )
    norm_gradient = lax.psum(jnp.concatenate([norm_one_summed, norm_two_summed], axis=0), "mp")
    data_index = lax.axis_index("dp")
    norm_columns = norm_first.shape[1]
    norm_current = lax.dynamic_slice_in_dim(layer_norms, data_index * norm_columns, norm_columns, 1)
    project_new = adamw_step(
        project_master, project_summed, project_first, project_second, D ** (-0.5)
    )
    output_new = adamw_step(
        output_master, output_summed, output_first, output_second, max(1, D * 4 // LAT) ** (-0.5)
    )
    upward_new = adamw_step(upward_master, upward_summed, upward_first, upward_second, D ** (-0.5))
    downward_new = adamw_step(
        downward_master, downward_summed, downward_first, downward_second, FF ** (-0.5)
    )
    norm_new = adamw_step(norm_current, norm_gradient, norm_first, norm_second, 0.2)
    return (
        latents,
        point_gradient,
        project_summed,
        project_new[0],
        project_new[1],
        project_new[2],
        project_new[0].astype(jnp.bfloat16),
        output_summed,
        output_new[0],
        output_new[1],
        output_new[2],
        output_new[0].astype(jnp.bfloat16),
        upward_summed,
        upward_new[0],
        upward_new[1],
        upward_new[2],
        upward_new[0].astype(jnp.bfloat16),
        downward_summed,
        downward_new[0],
        downward_new[1],
        downward_new[2],
        downward_new[0].astype(jnp.bfloat16),
        norm_gradient,
        norm_new[0],
        norm_new[1],
        norm_new[2],
    )


MESH = pl.DeviceIdType.MESH
PLANES = 4
OWNERS = 8
ROWS = LAT
HALVES = (0, 1)
SHARDS = ((3, D, 256), (256, D), (D, D), (D, D))


def place():
    dp = lax.axis_index("dp")
    return dp // 4, (dp // 2) % 2, dp % 2, lax.axis_index("mp")


def device(y, x, c, z):
    return (y * 4 + x * 2 + c, z)


def greet(y, x, c, z):
    barrier = pltpu.get_barrier_semaphore()
    partners = [device(1 - y, x, c, z), device(y, 1 - x, c, z), device(y, x, 1 - c, z)]
    partners += [device(y, x, c, (z + d) % PLANES) for d in (1, 2, 3)]
    for partner in partners:
        pl.semaphore_signal(barrier, inc=1, device_id=partner, device_id_type=MESH)
    pl.semaphore_wait(barrier, len(partners))


def arrival(z, k):
    return (z + 1 - 2 * (z % 2), 2 - z // 2, 3 - 3 * (z // 2))[k]


def dot(a, b, contract):
    return lax.dot_general(a, b, (contract, ((), ())), preferred_element_type=jnp.float32)


NN = ((1,), (0,))
NT = ((1,), (1,))
TN = ((0,), (0,))


def tiles(count, size, body):
    def step(n, carry):
        body(pl.ds(pl.multiple_of(n * size, size), size))
        return carry

    lax.fori_loop(0, count, step, 0)


def norm_rows(source, target, gain, shift, strip=64):
    def step(n, carry):
        rows = pl.ds(pl.multiple_of(n * strip, strip), strip)
        target[rows, :] = layer_norm(source[rows, :], gain, shift).astype(target.dtype)
        return carry

    lax.fori_loop(0, ROWS // strip, step, 0)


def forward_kernel(*refs):
    shards, (points, members, norms) = refs[0:4], refs[4:7]
    fulls_out, saved_out, latents_out = refs[7:11], refs[11:19], refs[19]
    fulls, saved, latents = refs[20:24], refs[24:32], refs[32]
    inputs, entering_one, projected, attended, residual, entering_two, activated, slope = saved
    own_sem, z_send, z_recv, a_send, a_recv, b_send, b_recv, c_send, c_recv = refs[33:42]
    weight_sem, saved_sem, latents_sem = refs[42:45]
    y, x, c, z = place()
    greet(y, x, c, z)
    is_mid = jnp.logical_or(z == 1, z == 2)
    sibling = device(y, x, 1 - c, z)
    over_x, over_y = device(y, 1 - x, c, z), device(1 - y, x, c, z)
    beside, across = device(y, x, c, arrival(z, 0)), device(y, x, c, 3 - z)

    def view(w, plane, rows):
        return fulls[w].at[plane, :, rows, :] if w == 0 else fulls[w].at[plane, rows, :]

    def block(w, half, first, count):
        height = SHARDS[w][-2]
        start = pl.multiple_of(half * (height // 2) + first * (height // 16), height // 16)
        return pl.ds(start, count * (height // 16))

    spot = (c * 4 + y * 2 + x, c * 4 + x * 2 + y)
    pair = (c * 4 + y * 2, c * 4 + x * 2)

    def remote(w, plane, rows, send, recv, target):
        return pltpu.make_async_remote_copy(
            src_ref=view(w, plane, rows),
            dst_ref=view(w, plane, rows),
            send_sem=send,
            recv_sem=recv,
            device_id=target,
            device_id_type=MESH,
        )

    def z_copy(w, plane, half, lane, k, target):
        rows = block(w, half, spot[half], 1)
        return remote(w, plane, rows, z_send.at[w, lane, half], z_recv.at[w, k, half], target)

    def z_own(w, half):
        return z_copy(w, z, half, 0, 0, beside)

    def z_own_across(w, half):
        return z_copy(w, z, half, 1, 1, across)

    def z_pass(w, k, half):
        lane, target, slot = ((2, across, 2), (3, beside, 1), (4, beside, 2))[k]
        return z_copy(w, arrival(z, k), half, lane, slot, target)

    def z_arrived(w, k, half):
        return z_copy(w, arrival(z, k), half, 0, k, beside)

    def a_copy(w, k, half):
        rows = block(w, half, spot[half], 1)
        return remote(
            w, arrival(z, k), rows, a_send.at[w, k, half], a_recv.at[w, k, half], (over_x, over_y)[half]
        )

    def b_copy(w, k, half):
        rows = block(w, half, pair[half], 2)
        return remote(
            w, arrival(z, k), rows, b_send.at[w, k, half], b_recv.at[w, k, half], (over_y, over_x)[half]
        )

    def c_copy(w, k, half):
        rows = block(w, half, c * 4, 4)
        return remote(w, arrival(z, k), rows, c_send.at[w, k, half], c_recv.at[w, k, half], sibling)

    def own_load(w):
        return pltpu.make_async_copy(shards[w], fulls[w].at[z], own_sem.at[w])

    def keep_weight(w, k):
        plane = z if k is None else arrival(z, k)
        slot = 3 if k is None else k
        return pltpu.make_async_copy(fulls[w].at[plane], fulls_out[w].at[plane], weight_sem.at[w, slot])

    def keep(n):
        return pltpu.make_async_copy(saved[n], saved_out[n], saved_sem.at[n])

    def enter():
        slot_of = lax.broadcasted_iota(jnp.int32, (ROWS, ROWS), 0) == members[...]
        chosen = slot_of.astype(jnp.float32).astype(jnp.bfloat16)

        def pick(columns):
            inputs[:, columns] = dot(chosen, points[:, columns], TN)

        tiles(4, 256, pick)
        norm_rows(inputs, entering_one, norms[0:1, :], norms[1:2, :])
        residual[...] = inputs[...]

    def project(plane):
        for part in range(3):
            projected[plane, part] = dot(entering_one[...], fulls[0][plane, part], NN).astype(jnp.bfloat16)

    def attend(plane):
        live = members[...] >= 0
        for head in range(2):
            span = slice(head * HEAD_DIM, (head + 1) * HEAD_DIM)
            queries, keys_all, values_all = (projected[plane, part, :, span] for part in range(3))
            scores = jnp.where(live, dot(queries, keys_all, NT) * HEAD_DIM ** (-0.5), masked_score)
            exponent = jnp.exp(scores - jnp.max(scores, axis=-1, keepdims=True))
            probs = exponent * (1.0 / jnp.sum(exponent, axis=-1, keepdims=True))
            attended[plane, :, span] = dot(probs.astype(jnp.bfloat16), values_all, NN).astype(jnp.bfloat16)

    def branch(plane):
        def body(columns):
            residual[:, columns] += dot(attended[plane], fulls[1][plane, :, columns], NN)

        tiles(4, 256, body)

    def enter_two():
        norm_rows(residual, entering_two, norms[2:3, :], norms[3:4, :])
        latents[...] = residual[...]

    def widen(plane):
        def body(columns):
            u = dot(entering_two[...], fulls[2][plane, :, columns], NN)
            square = u * u
            bend = jnp.tanh(0.7978845608028654 * u * (1.0 + 0.044715 * square))
            activated[plane, :, columns] = (0.5 * u * (1.0 + bend)).astype(jnp.bfloat16)
            slope[plane, :, columns] = 0.5 * (1.0 + bend) + 0.5 * u * (1.0 - bend * bend) * (
                0.7978845608028654 * (1.0 + 3.0 * 0.044715 * square)
            )

        tiles(4, 256, body)

    def narrow(plane):
        def body(columns):
            latents[:, columns] += dot(activated[plane], fulls[3][plane, :, columns], NN)

        tiles(4, 256, body)

    def compute(w, k):
        plane = z if k is None else arrival(z, k)
        if w == 0:
            project(plane)
            attend(plane)
        elif w == 1:
            branch(plane)
        elif w == 2:
            widen(plane)
        else:
            narrow(plane)

    chunks = [(w, k) for w in range(4) for k in range(3)]
    lag = (1, 3, 5, 7)

    for w in range(4):
        own_load(w).start()
    for step in range(len(chunks) + lag[3]):
        for w in range(4):
            if step == max(0, 3 * w - 3):
                own_load(w).wait()
                keep_weight(w, None).start()
                for half in HALVES:
                    z_own(w, half).start()

                @pl.when(is_mid)
                def _():
                    for half in HALVES:
                        z_own_across(w, half).start()

        if 0 <= step - lag[0] < len(chunks):
            w, k = chunks[step - lag[0]]
            for half in HALVES:
                z_arrived(w, k, half).wait_recv()
                a_copy(w, k, half).start()

            @pl.when(is_mid)
            def _():
                for half in HALVES:
                    z_pass(w, k, half).start()

        if 0 <= step - lag[1] < len(chunks):
            w, k = chunks[step - lag[1]]
            for half in HALVES:
                a_copy(w, k, half).wait_recv()
                b_copy(w, k, half).start()
        if 0 <= step - lag[2] < len(chunks):
            w, k = chunks[step - lag[2]]
            for half in HALVES:
                b_copy(w, k, half).wait_recv()
                c_copy(w, k, half).start()
        if step == 0:
            enter()
            keep(0).start()
            keep(1).start()
            compute(0, None)
        if 0 <= step - lag[3] < len(chunks):
            w, k = chunks[step - lag[3]]
            for half in HALVES:
                c_copy(w, k, half).wait_recv()
            keep_weight(w, k).start()
            if k == 0 and w > 0:
                compute(w, None)
            compute(w, k)
            if k == 2:
                if w == 0:
                    keep(2).start()
                    keep(3).start()
                elif w == 1:
                    keep(4).start()
                    enter_two()
                    keep(5).start()
                elif w == 2:
                    keep(6).start()
                    keep(7).start()
    out = pltpu.make_async_copy(latents, latents_out, latents_sem)
    out.start()
    for w in range(4):
        for half in HALVES:
            z_own(w, half).wait_send()
            for k in range(3):
                a_copy(w, k, half).wait_send()
                b_copy(w, k, half).wait_send()
                c_copy(w, k, half).wait_send()

    @pl.when(is_mid)
    def _():
        for w in range(4):
            for half in HALVES:
                z_own_across(w, half).wait_send()
                for k in range(3):
                    z_pass(w, k, half).wait_send()

    for w in range(4):
        for k in (None, 0, 1, 2):
            keep_weight(w, k).wait()
    for n in range(8):
        keep(n).wait()
    out.wait()


def run_forward(shards, points, members, layer_norms):
    f32, bf16 = jnp.float32, jnp.bfloat16
    saved = [
        ((ROWS, D), f32),
        ((ROWS, D), bf16),
        ((PLANES, 3, ROWS, 256), bf16),
        ((PLANES, ROWS, 256), bf16),
        ((ROWS, D), f32),
        ((ROWS, D), bf16),
        ((PLANES, ROWS, D), bf16),
        ((PLANES, ROWS, D), f32),
    ]
    anywhere, vmem = pl.BlockSpec(memory_space=pl.ANY), pl.BlockSpec(memory_space=pltpu.VMEM)
    fulls = [((PLANES,) + s, bf16) for s in SHARDS]
    dma = pltpu.SemaphoreType.DMA
    result = pl.pallas_call(
        forward_kernel,
        out_shape=[jax.ShapeDtypeStruct(*a) for a in fulls + saved + [((ROWS, D), f32)]],
        in_specs=[anywhere] * 4 + [vmem] * 3,
        out_specs=[anywhere] * 13,
        scratch_shapes=[pltpu.VMEM(*a) for a in fulls + saved + [((ROWS, D), f32)]]
        + [dma((4,)), dma((4, 5, 2))]
        + [dma((4, 3, 2))] * 7
        + [dma((4, 4)), dma((8,)), dma],
        name="forward",
        compiler_params=pltpu.CompilerParams(
            collective_id=0, has_side_effects=True, vmem_limit_bytes=52 << 20
        ),
    )(*shards, points, members, layer_norms)
    return result[:4], result[4:12], result[12]


BLOCKS = ((1024, 128), (128, 1024), (256, 128), (384, 256))
STRIPS = (128, 16, 128, 64)


def owner_view(ref, w, plane, owner):
    if w in (0, 2):
        return ref.at[plane, :, pl.ds(pl.multiple_of(owner * 128, 128), 128)]
    return ref.at[plane, pl.ds(pl.multiple_of(owner * BLOCKS[w][0], BLOCKS[w][0]), BLOCKS[w][0]), :]


def reduce_kernel(*refs):
    grads, norm_part = refs[0:4], refs[4]
    outs, norm_out = refs[5:9], refs[9]
    own, pair_in, one_in, two_in, z_in = (refs[10 + 4 * k : 14 + 4 * k] for k in range(5))
    norm_own, norm_in, norm_planes = refs[30:33]
    load_sem, c_send, c_recv, one_send, one_recv, two_send, two_recv, z_send, z_recv = refs[33:42]
    norm_send, norm_recv = refs[42:44]
    y, x, c, z = place()
    greet(y, x, c, z)
    sibling = device(y, x, 1 - c, z)
    over_x, over_y = device(y, 1 - x, c, z), device(1 - y, x, c, z)

    def plane_of(i):
        return (z + 1 + i) % PLANES

    def remote(src, dst, send, recv, target):
        return pltpu.make_async_remote_copy(
            src_ref=src, dst_ref=dst, send_sem=send, recv_sem=recv, device_id=target, device_id_type=MESH
        )

    def load(w, i, k):
        return pltpu.make_async_copy(
            owner_view(grads[w], w, plane_of(i), k * 2 + c), own[w].at[i, k // 2, k % 2], load_sem.at[w, i, k]
        )

    def pair_copy(w, i, k):
        return remote(
            owner_view(grads[w], w, plane_of(i), k * 2 + 1 - c),
            pair_in[w].at[i, k // 2, k % 2],
            c_send.at[w, i, k],
            c_recv.at[w, i, k],
            sibling,
        )

    def half_rows(w, half):
        size = BLOCKS[w][0] // 2
        return pl.ds(half * size, size)

    def one_copy(w, i, half):
        rows = half_rows(w, half)
        src = own[w].at[i, 1 - y, :, rows] if half == 0 else own[w].at[i, :, 1 - x, rows]
        return remote(
            src, one_in[w].at[i, half], one_send.at[w, i, half], one_recv.at[w, i, half], (over_y, over_x)[half]
        )

    def two_copy(w, i, half):
        rows = half_rows(w, half)
        src = own[w].at[i, y, 1 - x, rows] if half == 0 else own[w].at[i, 1 - y, x, rows]
        return remote(
            src, two_in[w].at[i, half], two_send.at[w, i, half], two_recv.at[w, i, half], (over_x, over_y)[half]
        )

    def z_copy(w, i):
        return remote(
            own[w].at[i, y, x], z_in[w].at[i], z_send.at[w, i], z_recv.at[w, i], device(y, x, c, plane_of(i))
        )

    def add_rows(target, source, count, strip):
        def body(r, carry):
            rows = pl.ds(pl.multiple_of(r * strip, strip), strip)
            total = target[rows].astype(jnp.float32) + source[rows].astype(jnp.float32)
            target[rows] = total.astype(target.dtype)
            return carry

        lax.fori_loop(0, count // strip, body, 0)

    def start_unit(w, i):
        for k in range(4):
            pair_copy(w, i, k).start()
            load(w, i, k).start()

    def after_pair(w, i):
        for k in range(4):
            load(w, i, k).wait()
            pair_copy(w, i, k).wait_recv()
            add_rows(own[w].at[i, k // 2, k % 2], pair_in[w].at[i, k // 2, k % 2], BLOCKS[w][0], STRIPS[w])
        for half in (0, 1):
            one_copy(w, i, half).start()

    def after_one(w, i):
        size = BLOCKS[w][0] // 2
        for half in (0, 1):
            one_copy(w, i, half).wait()
            rows = half_rows(w, half)
            for k in (0, 1):
                target = own[w].at[i, y, k, rows] if half == 0 else own[w].at[i, k, x, rows]
                add_rows(target, one_in[w].at[i, half, k], size, min(size, STRIPS[w]))
            two_copy(w, i, half).start()

    def after_two(w, i):
        size = BLOCKS[w][0] // 2
        for half in (0, 1):
            two_copy(w, i, half).wait()
            add_rows(own[w].at[i, y, x, half_rows(w, half)], two_in[w].at[i, half], size, min(size, STRIPS[w]))
        if i < PLANES - 1:
            z_copy(w, i).start()

    def finish(w):
        for i in range(PLANES - 1):
            z_copy(w, i).wait()

        def body(r, carry):
            rows = pl.ds(pl.multiple_of(r * STRIPS[w], STRIPS[w]), STRIPS[w])
            total = own[w].at[PLANES - 1, y, x][rows].astype(jnp.float32)
            for i in range(PLANES - 1):
                total = total + z_in[w].at[i][rows].astype(jnp.float32)
            outs[w][rows] = total
            return carry

        lax.fori_loop(0, BLOCKS[w][0] // STRIPS[w], body, 0)

    def norm_step(k):
        return remote(
            norm_own.at[k], norm_in.at[k], norm_send.at[k], norm_recv.at[k], (sibling, over_x, over_y)[k]
        )

    def norm_plane(d):
        return remote(
            norm_own.at[3],
            norm_planes.at[z],
            norm_send.at[2 + d],
            norm_recv.at[2 + d],
            device(y, x, c, (z + d) % PLANES),
        )

    norm_own[0] = norm_part[...]
    norm_step(0).start()

    units = [(w, i) for w in range(4) for i in range(PLANES)]
    ahead = 2
    for unit in units[:ahead]:
        start_unit(*unit)
    for step in range(len(units) + 4):
        if step + ahead < len(units):
            start_unit(*units[step + ahead])
        if step < len(units):
            after_pair(*units[step])
        if 0 <= step - 1 < len(units):
            after_one(*units[step - 1])
        if 0 <= step - 2 < len(units):
            after_two(*units[step - 2])
        if step < 3:
            norm_step(step).wait()
            norm_own[step + 1] = norm_own[step] + norm_in[step]
            if step < 2:
                norm_step(step + 1).start()
            else:
                norm_planes[z] = norm_own[3]
                for d in (1, 2, 3):
                    norm_plane(d).start()
        if step >= 4 and (step - 4) % PLANES == PLANES - 1:
            finish((step - 4) // PLANES)
    for d in (1, 2, 3):
        norm_plane(d).wait()
    norm_out[...] = (norm_planes[0] + norm_planes[1]) + (norm_planes[2] + norm_planes[3])
    for w, i in units:
        for k in range(4):
            pair_copy(w, i, k).wait_send()


def reduce_gradients(grads, norm_part):
    bf16 = jnp.bfloat16
    halves = [(b[0] // 2, b[1]) for b in BLOCKS]
    scratch = [pltpu.VMEM((4, 2, 2) + b, bf16) for b in BLOCKS]
    scratch += [pltpu.VMEM((4, 2, 2) + b, bf16) for b in BLOCKS]
    scratch += [pltpu.VMEM((4, 2, 2) + h, bf16) for h in halves]
    scratch += [pltpu.VMEM((4, 2) + h, bf16) for h in halves]
    scratch += [pltpu.VMEM((3,) + b, bf16) for b in BLOCKS]
    scratch += [
        pltpu.VMEM((4,) + norm_part.shape, jnp.float32),
        pltpu.VMEM((3,) + norm_part.shape, jnp.float32),
        pltpu.VMEM((4,) + norm_part.shape, jnp.float32),
    ]
    dma = pltpu.SemaphoreType.DMA
    scratch += [dma((4, 4, 4)), dma((4, 4, 4)), dma((4, 4, 4)), dma((4, 4, 2)), dma((4, 4, 2))]
    scratch += [dma((4, 4, 2)), dma((4, 4, 2)), dma((4, 3)), dma((4, 3)), dma((6,)), dma((6,))]
    vmem = pl.BlockSpec(memory_space=pltpu.VMEM)
    result = pl.pallas_call(
        reduce_kernel,
        out_shape=[jax.ShapeDtypeStruct(b, jnp.float32) for b in BLOCKS]
        + [jax.ShapeDtypeStruct(norm_part.shape, jnp.float32)],
        in_specs=[pl.BlockSpec(memory_space=pl.ANY)] * 4 + [vmem],
        out_specs=[vmem] * 5,
        scratch_shapes=scratch,
        name="reduce_gradients",
        compiler_params=pltpu.CompilerParams(
            collective_id=1, has_side_effects=True, vmem_limit_bytes=48 << 20
        ),
    )(*grads, norm_part)
    return result[:4], result[4]


def on_device_cube(
    points,
    members,
    cotangent,
    project_weight,
    output_weight,
    upward_weight,
    downward_weight,
    layer_norms,
    project_master,
    project_first,
    project_second,
    output_master,
    output_first,
    output_second,
    upward_master,
    upward_first,
    upward_second,
    downward_master,
    downward_first,
    downward_second,
    norm_first,
    norm_second,
):
    f32, bf16 = jnp.float32, jnp.bfloat16
    score_scale = HEAD_DIM ** (-0.5)
    fulls, saved, latents = run_forward(
        (jnp.transpose(project_weight, (1, 0, 2)), output_weight, upward_weight, downward_weight),
        points,
        members,
        layer_norms,
    )
    project_full, output_full, upward_full, downward_full = fulls
    inputs, entering_one, projected, attended, residual, entering_two, activated, slope = saved
    rows = points.shape[0]
    slots = members[0]
    live = slots >= 0
    norm_back_one = jax.vjp(layer_norm, inputs, layer_norms[0], layer_norms[1])[1]
    norm_back_two = jax.vjp(layer_norm, residual, layer_norms[2], layer_norms[3])[1]
    heads_view = projected.reshape(PLANES, 3, rows, 2, HEAD_DIM)
    queries, keys_all, values_all = heads_view[:, 0], heads_view[:, 1], heads_view[:, 2]
    scores = jnp.einsum("sqhe,skhe->shqk", queries, keys_all, preferred_element_type=f32) * score_scale
    scores = jnp.where(live[None, None, None, :], scores, masked_score)
    probs = jax.nn.softmax(scores, axis=-1)
    probs_low = probs.astype(bf16)
    downward_part = jnp.einsum("srf,rd->sfd", activated, cotangent, preferred_element_type=f32).astype(bf16)
    activated_grad = jnp.einsum("rd,sfd->srf", cotangent, downward_full, preferred_element_type=f32)
    upward_grad = (activated_grad * slope).astype(bf16)
    upward_part = jnp.einsum("rd,srf->sdf", entering_two, upward_grad, preferred_element_type=f32).astype(bf16)
    normed_two_grad = jnp.einsum("srf,sdf->rd", upward_grad, upward_full, preferred_element_type=f32)
    residual_part, gain_two_grad, shift_two_grad = norm_back_two(normed_two_grad)
    residual_grad = residual_part + cotangent.astype(f32)
    branch_grad = residual_grad.astype(bf16)
    output_part = jnp.einsum("srh,rd->shd", attended, branch_grad, preferred_element_type=f32).astype(bf16)
    attended_grad = jnp.einsum("rd,shd->srh", branch_grad, output_full, preferred_element_type=f32).astype(bf16)
    attended_grad = attended_grad.reshape(PLANES, rows, 2, HEAD_DIM)
    value_grad = jnp.einsum("shqk,sqhe->skhe", probs_low, attended_grad, preferred_element_type=f32).astype(bf16)
    prob_grad = jnp.einsum("sqhe,skhe->shqk", attended_grad, values_all, preferred_element_type=f32)
    score_grad = (probs * (prob_grad - jnp.sum(probs * prob_grad, axis=-1, keepdims=True))).astype(bf16)
    query_grad = jnp.einsum("shqk,skhe->sqhe", score_grad, keys_all, preferred_element_type=f32) * score_scale
    key_grad = jnp.einsum("shqk,sqhe->skhe", score_grad, queries, preferred_element_type=f32) * score_scale
    projected_grad = jnp.stack([query_grad.astype(bf16), key_grad.astype(bf16), value_grad], axis=1)
    projected_grad = projected_grad.reshape(PLANES, 3, rows, 2 * HEAD_DIM)
    project_part = jnp.einsum(
        "rod,sjrf->sojdf",
        entering_one.reshape(rows, OWNERS, D // OWNERS),
        projected_grad,
        preferred_element_type=f32,
    ).astype(bf16)
    normed_grad = jnp.einsum("sjrf,sjdf->rd", projected_grad, project_full, preferred_element_type=f32)
    input_part, gain_one_grad, shift_one_grad = norm_back_one(normed_grad)
    input_grad = input_part + residual_grad
    norm_part = jnp.stack([gain_one_grad, shift_one_grad, gain_two_grad, shift_two_grad])
    matches = slots[:, None] == jnp.arange(LAT, dtype=jnp.int32)[None, :]
    slot_of = jnp.argmax(matches, axis=0)
    point_gradient = jnp.where(jnp.any(matches, axis=0)[:, None], input_grad[slot_of], 0.0)
    (downward_summed, upward_summed, output_summed, project_blocks), norm_summed = reduce_gradients(
        (downward_part, upward_part, output_part, project_part.reshape(PLANES, OWNERS * 384, 256)), norm_part
    )
    project_summed = jnp.transpose(project_blocks.reshape(3, D // OWNERS, 256), (1, 0, 2))
    data_index = lax.axis_index("dp")
    norm_columns = norm_first.shape[1]
    norm_gradient = lax.dynamic_slice_in_dim(norm_summed, data_index * norm_columns, norm_columns, 1)
    norm_current = lax.dynamic_slice_in_dim(layer_norms, data_index * norm_columns, norm_columns, 1)
    results = [latents, point_gradient]
    for master, summed, first, second, rate in (
        (project_master, project_summed, project_first, project_second, D ** (-0.5)),
        (output_master, output_summed, output_first, output_second, max(1, D * 4 // LAT) ** (-0.5)),
        (upward_master, upward_summed, upward_first, upward_second, D ** (-0.5)),
        (downward_master, downward_summed, downward_first, downward_second, FF ** (-0.5)),
    ):
        updated, one_new, two_new = adamw_step(master, summed, first, second, rate)
        results += [summed, updated, one_new, two_new, updated.astype(bf16)]
    norm_new = adamw_step(norm_current, norm_gradient, norm_first, norm_second, 0.2)
    results += [norm_gradient, *norm_new]
    return tuple(results)


def solution(mesh):
    return jax.shard_map(
        on_device_cube if dict(mesh.shape) == {"dp": 8, "mp": 4} else on_device_any,
        mesh=mesh,
        in_specs=(
            P(("dp", "mp"), None),
            P(("dp", "mp"), None),
            P(("dp", "mp"), None),
            P(None, None, "mp"),
            P("mp", None),
            P(None, "mp"),
            P("mp", None),
            P(),
            P("dp", None, "mp"),
            P("dp", None, "mp"),
            P("dp", None, "mp"),
            P("mp", "dp"),
            P("mp", "dp"),
            P("mp", "dp"),
            P("dp", "mp"),
            P("dp", "mp"),
            P("dp", "mp"),
            P("mp", "dp"),
            P("mp", "dp"),
            P("mp", "dp"),
            P(None, "dp"),
            P(None, "dp"),
        ),
        out_specs=(
            P(("dp", "mp"), None),
            P(("dp", "mp"), None),
            P("dp", None, "mp"),
            P("dp", None, "mp"),
            P("dp", None, "mp"),
            P("dp", None, "mp"),
            P("dp", None, "mp"),
            P("mp", "dp"),
            P("mp", "dp"),
            P("mp", "dp"),
            P("mp", "dp"),
            P("mp", "dp"),
            P("dp", "mp"),
            P("dp", "mp"),
            P("dp", "mp"),
            P("dp", "mp"),
            P("dp", "mp"),
            P("mp", "dp"),
            P("mp", "dp"),
            P("mp", "dp"),
            P("mp", "dp"),
            P("mp", "dp"),
            P(None, "dp"),
            P(None, "dp"),
            P(None, "dp"),
            P(None, "dp"),
        ),
        check_vma=False,
    )
```

```python
import jax
import jax.numpy as jnp
from jax import lax
from jax.experimental import pallas as pl
from jax.experimental.pallas import tpu as pltpu
from jax.sharding import PartitionSpec as P

D = 1024
HEAD_DIM = 128
FF = 4096
LAT = 256
ADAM_STEP = 10


norm_epsilon = 1e-05
beta_one = 0.9
beta_two = 0.95
adam_epsilon = 1e-08
weight_decay = 0.1
masked_score = -1e30


def layer_norm(values, norm_gain, norm_shift):
    center = values - jnp.mean(values, axis=-1, keepdims=True)
    spread = jnp.mean(center * center, axis=-1, keepdims=True)
    return center * lax.rsqrt(spread + norm_epsilon) * norm_gain + norm_shift


def pick_rows(source_rows, row_index):
    return source_rows[row_index]


def adamw_step(weight, gradient, moment_one, moment_two, step_rate):
    one_new = beta_one * moment_one + (1.0 - beta_one) * gradient
    two_new = beta_two * moment_two + (1.0 - beta_two) * gradient * gradient
    corrected_one = one_new / (1.0 - beta_one**ADAM_STEP)
    corrected_two = two_new / (1.0 - beta_two**ADAM_STEP)
    updated = weight - step_rate * (
        corrected_one / (jnp.sqrt(corrected_two) + adam_epsilon) + weight_decay * weight
    )
    return (updated, one_new, two_new)


def masked_scores(queries, keys_all, key_mask, score_scale):
    raw_scores = (
        jnp.einsum("gqhe,gkhe->ghqk", queries, keys_all, preferred_element_type=jnp.float32)
        * score_scale
    )
    return jnp.where(key_mask, raw_scores, masked_score)


def on_device_any(
    points,
    members,
    cotangent,
    project_weight,
    output_weight,
    upward_weight,
    downward_weight,
    layer_norms,
    project_master,
    project_first,
    project_second,
    output_master,
    output_first,
    output_second,
    upward_master,
    upward_first,
    upward_second,
    downward_master,
    downward_first,
    downward_second,
    norm_first,
    norm_second,
):
    groups_here = members.shape[0]
    shard_rows = points.shape[0]
    model_width = points.shape[1]
    heads_here = project_weight.shape[2] // HEAD_DIM
    score_scale = HEAD_DIM ** (-0.5)
    grouped = points.reshape(groups_here, LAT, model_width)
    slot_index = jnp.maximum(members, 0)
    key_live = members >= 0
    picked = jax.vmap(pick_rows)(grouped, slot_index)
    inputs = jnp.where(key_live[:, :, None], picked.astype(jnp.float32), 0.0).reshape(
        shard_rows, model_width
    )
    normed, norm_back_one = jax.vjp(layer_norm, inputs, layer_norms[0], layer_norms[1])
    gathered, live_all = (
        lax.all_gather(normed.astype(jnp.bfloat16), "mp", axis=0, tiled=True),
        lax.all_gather(key_live.astype(jnp.bfloat16), "mp", axis=0, tiled=True),
    )
    total_rows = gathered.shape[0]
    total_groups = live_all.shape[0]
    key_mask = (live_all > 0)[:, None, None, :]
    projected = jnp.einsum(
        "rd,dcf->rcf", gathered, project_weight, preferred_element_type=jnp.float32
    ).astype(jnp.bfloat16)
    heads_view = projected.reshape(total_groups, LAT, 3, heads_here, HEAD_DIM)
    queries = heads_view[:, :, 0]
    keys_all = heads_view[:, :, 1]
    values_all = heads_view[:, :, 2]
    scores = masked_scores(queries, keys_all, key_mask, score_scale)
    row_top = jnp.max(scores, axis=-1, keepdims=True)
    exponent = jnp.exp(scores - row_top)
    row_total = jnp.sum(exponent, axis=-1, keepdims=True)
    attention_weights = exponent / row_total
    log_total = row_top + jnp.log(row_total)
    weights_low = attention_weights.astype(jnp.bfloat16)
    attended = jnp.einsum(
        "ghqk,gkhe->gqhe", weights_low, values_all, preferred_element_type=jnp.float32
    ).astype(jnp.bfloat16)
    attended = attended.reshape(total_rows, heads_here * HEAD_DIM)
    branch = lax.psum_scatter(
        jnp.dot(attended, output_weight, preferred_element_type=jnp.float32),
        "mp",
        scatter_dimension=0,
        tiled=True,
    )
    residual = inputs + branch
    normed_two, norm_back_two = jax.vjp(layer_norm, residual, layer_norms[2], layer_norms[3])
    gathered_two = lax.all_gather(normed_two.astype(jnp.bfloat16), "mp", axis=0, tiled=True)
    upward = jnp.dot(gathered_two, upward_weight, preferred_element_type=jnp.float32)
    activated_float, gelu_back = jax.vjp(jax.nn.gelu, upward)
    activated = activated_float.astype(jnp.bfloat16)
    latents = residual + lax.psum_scatter(
        jnp.dot(activated, downward_weight, preferred_element_type=jnp.float32).astype(
            jnp.bfloat16
        ),
        "mp",
        scatter_dimension=0,
        tiled=True,
    ).astype(jnp.float32)
    cotangent_all = lax.all_gather(cotangent, "mp", axis=0, tiled=True)
    downward_local = jnp.einsum(
        "rf,rd->fd", activated, cotangent_all, preferred_element_type=jnp.float32
    )
    activated_grad = jnp.einsum(
        "rd,fd->rf", cotangent_all, downward_weight, preferred_element_type=jnp.float32
    )
    upward_grad = gelu_back(activated_grad)[0].astype(jnp.bfloat16)
    upward_local = jnp.einsum(
        "rd,rf->df", gathered_two, upward_grad, preferred_element_type=jnp.float32
    )
    normed_two_grad = lax.psum_scatter(
        jnp.einsum("rf,df->rd", upward_grad, upward_weight, preferred_element_type=jnp.float32),
        "mp",
        scatter_dimension=0,
        tiled=True,
    )
    residual_part, gain_two_grad, shift_two_grad = norm_back_two(normed_two_grad)
    residual_grad = residual_part + cotangent.astype(jnp.float32)
    norm_two_local = jnp.stack([gain_two_grad, shift_two_grad])
    branch_grad = lax.all_gather(residual_grad.astype(jnp.bfloat16), "mp", axis=0, tiled=True)
    output_local = jnp.einsum(
        "rh,rd->hd", attended, branch_grad, preferred_element_type=jnp.float32
    )
    attended_grad = jnp.einsum(
        "rd,hd->rh", branch_grad, output_weight, preferred_element_type=jnp.float32
    ).astype(jnp.bfloat16)
    attended_grad = attended_grad.reshape(total_groups, LAT, heads_here, HEAD_DIM)
    scores_again = masked_scores(queries, keys_all, key_mask, score_scale)
    weights_again = jnp.exp(scores_again - log_total)
    weights_again_low = weights_again.astype(jnp.bfloat16)
    value_grad = jnp.einsum(
        "ghqk,gqhe->gkhe", weights_again_low, attended_grad, preferred_element_type=jnp.float32
    ).astype(jnp.bfloat16)
    weight_grad = jnp.einsum(
        "gqhe,gkhe->ghqk", attended_grad, values_all, preferred_element_type=jnp.float32
    )
    score_grad = (
        weights_again * (weight_grad - jnp.sum(weights_again * weight_grad, axis=-1, keepdims=True))
    ).astype(jnp.bfloat16)
    query_grad = (
        jnp.einsum("ghqk,gkhe->gqhe", score_grad, keys_all, preferred_element_type=jnp.float32)
        * score_scale
    ).astype(jnp.bfloat16)
    key_grad = (
        jnp.einsum("ghqk,gqhe->gkhe", score_grad, queries, preferred_element_type=jnp.float32)
        * score_scale
    ).astype(jnp.bfloat16)
    projected_grad = jnp.stack([query_grad, key_grad, value_grad], axis=2).reshape(
        total_rows, 3, heads_here * HEAD_DIM
    )
    project_local = jnp.einsum(
        "rd,rcf->dcf", gathered, projected_grad, preferred_element_type=jnp.float32
    )
    normed_grad = lax.psum_scatter(
        jnp.einsum(
            "rcf,dcf->rd", projected_grad, project_weight, preferred_element_type=jnp.float32
        ).astype(jnp.bfloat16),
        "mp",
        scatter_dimension=0,
        tiled=True,
    ).astype(jnp.float32)
    input_part, gain_one_grad, shift_one_grad = norm_back_one(normed_grad)
    input_grad = input_part + residual_grad
    norm_one_local = jnp.stack([gain_one_grad, shift_one_grad])
    matches = members[:, :, None] == jnp.arange(LAT, dtype=jnp.int32)[None, None, :]
    slot_of = jnp.argmax(matches, axis=1)
    point_used = jnp.any(matches, axis=1)
    grouped_grad = input_grad.reshape(groups_here, LAT, model_width)
    point_gradient = jnp.where(
        point_used[:, :, None], jax.vmap(pick_rows)(grouped_grad, slot_of), 0.0
    ).reshape(shard_rows, model_width)
    (
        project_summed,
        output_summed,
        upward_summed,
        downward_summed,
        norm_one_summed,
        norm_two_summed,
    ) = (
        lax.psum_scatter(project_local, "dp", scatter_dimension=0, tiled=True),
        lax.psum_scatter(output_local, "dp", scatter_dimension=1, tiled=True),
        lax.psum_scatter(upward_local, "dp", scatter_dimension=0, tiled=True),
        lax.psum_scatter(downward_local, "dp", scatter_dimension=1, tiled=True),
        lax.psum_scatter(norm_one_local, "dp", scatter_dimension=1, tiled=True),
        lax.psum_scatter(norm_two_local, "dp", scatter_dimension=1, tiled=True),
    )
    norm_gradient = lax.psum(jnp.concatenate([norm_one_summed, norm_two_summed], axis=0), "mp")
    data_index = lax.axis_index("dp")
    norm_columns = norm_first.shape[1]
    norm_current = lax.dynamic_slice_in_dim(layer_norms, data_index * norm_columns, norm_columns, 1)
    project_new = adamw_step(
        project_master, project_summed, project_first, project_second, D ** (-0.5)
    )
    output_new = adamw_step(
        output_master, output_summed, output_first, output_second, max(1, D * 4 // LAT) ** (-0.5)
    )
    upward_new = adamw_step(upward_master, upward_summed, upward_first, upward_second, D ** (-0.5))
    downward_new = adamw_step(
        downward_master, downward_summed, downward_first, downward_second, FF ** (-0.5)
    )
    norm_new = adamw_step(norm_current, norm_gradient, norm_first, norm_second, 0.2)
    return (
        latents,
        point_gradient,
        project_summed,
        project_new[0],
        project_new[1],
        project_new[2],
        project_new[0].astype(jnp.bfloat16),
        output_summed,
        output_new[0],
        output_new[1],
        output_new[2],
        output_new[0].astype(jnp.bfloat16),
        upward_summed,
        upward_new[0],
        upward_new[1],
        upward_new[2],
        upward_new[0].astype(jnp.bfloat16),
        downward_summed,
        downward_new[0],
        downward_new[1],
        downward_new[2],
        downward_new[0].astype(jnp.bfloat16),
        norm_gradient,
        norm_new[0],
        norm_new[1],
        norm_new[2],
    )


MESH = pl.DeviceIdType.MESH
PLANES = 4
OWNERS = 8
ROWS = LAT
HALVES = (0, 1)
SHARDS = ((3, D, 256), (256, D), (D, D), (D, D))


def place():
    dp = lax.axis_index("dp")
    return dp // 4, (dp // 2) % 2, dp % 2, lax.axis_index("mp")


def device(y, x, c, z):
    return (y * 4 + x * 2 + c, z)


def greet(y, x, c, z):
    barrier = pltpu.get_barrier_semaphore()
    partners = [device(1 - y, x, c, z), device(y, 1 - x, c, z), device(y, x, 1 - c, z)]
    partners += [device(y, x, c, (z + d) % PLANES) for d in (1, 2, 3)]
    for partner in partners:
        pl.semaphore_signal(barrier, inc=1, device_id=partner, device_id_type=MESH)
    pl.semaphore_wait(barrier, len(partners))


def arrival(z, k):
    return (z + 1 - 2 * (z % 2), 2 - z // 2, 3 - 3 * (z // 2))[k]


def dot(a, b, contract):
    return lax.dot_general(a, b, (contract, ((), ())), preferred_element_type=jnp.float32)


NN = ((1,), (0,))
NT = ((1,), (1,))
TN = ((0,), (0,))


def tiles(count, size, body):
    def step(n, carry):
        body(pl.ds(pl.multiple_of(n * size, size), size))
        return carry

    lax.fori_loop(0, count, step, 0)


def norm_rows(source, target, gain, shift, strip=64):
    def step(n, carry):
        rows = pl.ds(pl.multiple_of(n * strip, strip), strip)
        target[rows, :] = layer_norm(source[rows, :], gain, shift).astype(target.dtype)
        return carry

    lax.fori_loop(0, ROWS // strip, step, 0)


def forward_kernel(*refs):
    shards, (points, members, norms) = refs[0:4], refs[4:7]
    fulls_out, saved_out, latents_out = refs[7:11], refs[11:19], refs[19]
    fulls, saved, latents = refs[20:24], refs[24:32], refs[32]
    inputs, entering_one, projected, attended, residual, entering_two, activated, slope = saved
    own_sem, z_send, z_recv, a_send, a_recv, b_send, b_recv, c_send, c_recv = refs[33:42]
    weight_sem, saved_sem, latents_sem = refs[42:45]
    y, x, c, z = place()
    greet(y, x, c, z)
    is_mid = jnp.logical_or(z == 1, z == 2)
    sibling = device(y, x, 1 - c, z)
    over_x, over_y = device(y, 1 - x, c, z), device(1 - y, x, c, z)
    beside, across = device(y, x, c, arrival(z, 0)), device(y, x, c, 3 - z)

    def view(w, plane, rows):
        return fulls[w].at[plane, :, rows, :] if w == 0 else fulls[w].at[plane, rows, :]

    def block(w, half, first, count):
        height = SHARDS[w][-2]
        start = pl.multiple_of(half * (height // 2) + first * (height // 16), height // 16)
        return pl.ds(start, count * (height // 16))

    spot = (c * 4 + y * 2 + x, c * 4 + x * 2 + y)
    pair = (c * 4 + y * 2, c * 4 + x * 2)

    def remote(w, plane, rows, send, recv, target):
        return pltpu.make_async_remote_copy(
            src_ref=view(w, plane, rows),
            dst_ref=view(w, plane, rows),
            send_sem=send,
            recv_sem=recv,
            device_id=target,
            device_id_type=MESH,
        )

    def z_copy(w, plane, half, lane, k, target):
        rows = block(w, half, spot[half], 1)
        return remote(w, plane, rows, z_send.at[w, lane, half], z_recv.at[w, k, half], target)

    def z_own(w, half):
        return z_copy(w, z, half, 0, 0, beside)

    def z_own_across(w, half):
        return z_copy(w, z, half, 1, 1, across)

    def z_pass(w, k, half):
        lane, target, slot = ((2, across, 2), (3, beside, 1), (4, beside, 2))[k]
        return z_copy(w, arrival(z, k), half, lane, slot, target)

    def z_arrived(w, k, half):
        return z_copy(w, arrival(z, k), half, 0, k, beside)

    def a_copy(w, k, half):
        rows = block(w, half, spot[half], 1)
        return remote(
            w, arrival(z, k), rows, a_send.at[w, k, half], a_recv.at[w, k, half], (over_x, over_y)[half]
        )

    def b_copy(w, k, half):
        rows = block(w, half, pair[half], 2)
        return remote(
            w, arrival(z, k), rows, b_send.at[w, k, half], b_recv.at[w, k, half], (over_y, over_x)[half]
        )

    def c_copy(w, k, half):
        rows = block(w, half, c * 4, 4)
        return remote(w, arrival(z, k), rows, c_send.at[w, k, half], c_recv.at[w, k, half], sibling)

    def own_load(w):
        return pltpu.make_async_copy(shards[w], fulls[w].at[z], own_sem.at[w])

    def keep_weight(w, k):
        plane = z if k is None else arrival(z, k)
        slot = 3 if k is None else k
        return pltpu.make_async_copy(fulls[w].at[plane], fulls_out[w].at[plane], weight_sem.at[w, slot])

    def keep(n):
        return pltpu.make_async_copy(saved[n], saved_out[n], saved_sem.at[n])

    def enter():
        slot_of = lax.broadcasted_iota(jnp.int32, (ROWS, ROWS), 0) == members[...]
        chosen = slot_of.astype(jnp.float32).astype(jnp.bfloat16)

        def pick(columns):
            inputs[:, columns] = dot(chosen, points[:, columns], TN)

        tiles(4, 256, pick)
        norm_rows(inputs, entering_one, norms[0:1, :], norms[1:2, :])
        residual[...] = inputs[...]

    def project(plane):
        for part in range(3):
            projected[plane, part] = dot(entering_one[...], fulls[0][plane, part], NN).astype(jnp.bfloat16)

    def attend(plane):
        live = members[...] >= 0
        for head in range(2):
            span = slice(head * HEAD_DIM, (head + 1) * HEAD_DIM)
            queries, keys_all, values_all = (projected[plane, part, :, span] for part in range(3))
            scores = jnp.where(live, dot(queries, keys_all, NT) * HEAD_DIM ** (-0.5), masked_score)
            exponent = jnp.exp(scores - jnp.max(scores, axis=-1, keepdims=True))
            probs = exponent * (1.0 / jnp.sum(exponent, axis=-1, keepdims=True))
            attended[plane, :, span] = dot(probs.astype(jnp.bfloat16), values_all, NN).astype(jnp.bfloat16)

    def branch(plane):
        def body(columns):
            residual[:, columns] += dot(attended[plane], fulls[1][plane, :, columns], NN)

        tiles(4, 256, body)

    def enter_two():
        norm_rows(residual, entering_two, norms[2:3, :], norms[3:4, :])
        latents[...] = residual[...]

    def widen(plane):
        def body(columns):
            u = dot(entering_two[...], fulls[2][plane, :, columns], NN)
            square = u * u
            bend = jnp.tanh(0.7978845608028654 * u * (1.0 + 0.044715 * square))
            activated[plane, :, columns] = (0.5 * u * (1.0 + bend)).astype(jnp.bfloat16)
            slope[plane, :, columns] = 0.5 * (1.0 + bend) + 0.5 * u * (1.0 - bend * bend) * (
                0.7978845608028654 * (1.0 + 3.0 * 0.044715 * square)
            )

        tiles(4, 256, body)

    def narrow(plane):
        def body(columns):
            latents[:, columns] += dot(activated[plane], fulls[3][plane, :, columns], NN)

        tiles(4, 256, body)

    def compute(w, k):
        plane = z if k is None else arrival(z, k)
        if w == 0:
            project(plane)
            attend(plane)
        elif w == 1:
            branch(plane)
        elif w == 2:
            widen(plane)
        else:
            narrow(plane)

    chunks = [(w, k) for w in range(4) for k in range(3)]
    lag = (1, 3, 5, 7)

    for w in range(4):
        own_load(w).start()
    for step in range(len(chunks) + lag[3]):
        for w in range(4):
            if step == max(0, 3 * w - 3):
                own_load(w).wait()
                keep_weight(w, None).start()
                for half in HALVES:
                    z_own(w, half).start()

                @pl.when(is_mid)
                def _():
                    for half in HALVES:
                        z_own_across(w, half).start()

        if 0 <= step - lag[0] < len(chunks):
            w, k = chunks[step - lag[0]]
            for half in HALVES:
                z_arrived(w, k, half).wait_recv()
                a_copy(w, k, half).start()

            @pl.when(is_mid)
            def _():
                for half in HALVES:
                    z_pass(w, k, half).start()

        if 0 <= step - lag[1] < len(chunks):
            w, k = chunks[step - lag[1]]
            for half in HALVES:
                a_copy(w, k, half).wait_recv()
                b_copy(w, k, half).start()
        if 0 <= step - lag[2] < len(chunks):
            w, k = chunks[step - lag[2]]
            for half in HALVES:
                b_copy(w, k, half).wait_recv()
                c_copy(w, k, half).start()
        if step == 0:
            enter()
            keep(0).start()
            keep(1).start()
            compute(0, None)
        if 0 <= step - lag[3] < len(chunks):
            w, k = chunks[step - lag[3]]
            for half in HALVES:
                c_copy(w, k, half).wait_recv()
            keep_weight(w, k).start()
            if k == 0 and w > 0:
                compute(w, None)
            compute(w, k)
            if k == 2:
                if w == 0:
                    keep(2).start()
                    keep(3).start()
                elif w == 1:
                    keep(4).start()
                    enter_two()
                    keep(5).start()
                elif w == 2:
                    keep(6).start()
                    keep(7).start()
    out = pltpu.make_async_copy(latents, latents_out, latents_sem)
    out.start()
    for w in range(4):
        for half in HALVES:
            z_own(w, half).wait_send()
            for k in range(3):
                a_copy(w, k, half).wait_send()
                b_copy(w, k, half).wait_send()
                c_copy(w, k, half).wait_send()

    @pl.when(is_mid)
    def _():
        for w in range(4):
            for half in HALVES:
                z_own_across(w, half).wait_send()
                for k in range(3):
                    z_pass(w, k, half).wait_send()

    for w in range(4):
        for k in (None, 0, 1, 2):
            keep_weight(w, k).wait()
    for n in range(8):
        keep(n).wait()
    out.wait()


def run_forward(shards, points, members, layer_norms):
    f32, bf16 = jnp.float32, jnp.bfloat16
    saved = [
        ((ROWS, D), f32),
        ((ROWS, D), bf16),
        ((PLANES, 3, ROWS, 256), bf16),
        ((PLANES, ROWS, 256), bf16),
        ((ROWS, D), f32),
        ((ROWS, D), bf16),
        ((PLANES, ROWS, D), bf16),
        ((PLANES, ROWS, D), f32),
    ]
    anywhere, vmem = pl.BlockSpec(memory_space=pl.ANY), pl.BlockSpec(memory_space=pltpu.VMEM)
    fulls = [((PLANES,) + s, bf16) for s in SHARDS]
    dma = pltpu.SemaphoreType.DMA
    result = pl.pallas_call(
        forward_kernel,
        out_shape=[jax.ShapeDtypeStruct(*a) for a in fulls + saved + [((ROWS, D), f32)]],
        in_specs=[anywhere] * 4 + [vmem] * 3,
        out_specs=[anywhere] * 13,
        scratch_shapes=[pltpu.VMEM(*a) for a in fulls + saved + [((ROWS, D), f32)]]
        + [dma((4,)), dma((4, 5, 2))]
        + [dma((4, 3, 2))] * 7
        + [dma((4, 4)), dma((8,)), dma],
        name="forward",
        compiler_params=pltpu.CompilerParams(
            collective_id=0, has_side_effects=True, vmem_limit_bytes=52 << 20
        ),
    )(*shards, points, members, layer_norms)
    return result[:4], result[4:12], result[12]


WIDTHS = (D, D, 256, 3 * 256)
BLOCK = D // OWNERS
HALF = BLOCK // 2
RING = 3
UNITS = [(w, i) for w in (0, 1, 3, 2) for i in range(PLANES)]


def backward_kernel(*refs):
    fulls, saved_in = refs[0:4], refs[4:12]
    cotangent_in, members, norms = refs[12:15]
    outs, norm_out, points_out = refs[15:19], refs[19], refs[20]
    saved, cotangent = refs[21:29], refs[29]
    inputs, entering_one, projected, attended, residual, entering_two, activated, slope = saved
    down_ring, up_ring, output_full, project_ring = refs[30:34]
    turned, upward_grad, residual_grad, branch_grad, projected_grad, normed_grad = refs[34:40]
    ring = refs[40]
    acc, one_in, two_in, z_in = refs[41:45], refs[45:49], refs[49:53], refs[53:57]
    norm_own, norm_in, norm_planes = refs[57:60]
    saved_sem, cotangent_sem, weight_sem = refs[60:63]
    c_send, c_recv, one_send, one_recv, two_send, two_recv, z_send, z_recv = refs[63:71]
    norm_send, norm_recv = refs[71:73]
    f32, bf16 = jnp.float32, jnp.bfloat16
    y, x, c, z = place()

    def load(n):
        return pltpu.make_async_copy(saved_in[n], saved[n], saved_sem.at[n])

    cotangent_load = pltpu.make_async_copy(cotangent_in, cotangent, cotangent_sem)
    cotangent_load.start()
    for n in (6, 5, 7, 4, 2, 3, 1, 0):
        load(n).start()

    def plane_of(i):
        return (z + 1 + i) % PLANES

    def weight_load(w, i):
        plane = plane_of(i)
        if w == 2:
            return pltpu.make_async_copy(fulls[1], output_full, weight_sem.at[2, 0])
        target = (down_ring, up_ring, None, project_ring.at[i % 2])[w]
        return pltpu.make_async_copy(fulls[(3, 2, 1, 0)[w]].at[plane], target, weight_sem.at[w, i])

    weight_load(0, 0).start()
    weight_load(1, 0).start()
    weight_load(2, 0).start()
    weight_load(3, 0).start()
    greet(y, x, c, z)
    sibling = device(y, x, 1 - c, z)
    over_x, over_y = device(y, 1 - x, c, z), device(1 - y, x, c, z)

    def remote(src, dst, send, recv, target):
        return pltpu.make_async_remote_copy(
            src_ref=src, dst_ref=dst, send_sem=send, recv_sem=recv, device_id=target, device_id_type=MESH
        )

    def pair_copy(t):
        w, i = UNITS[t]
        return remote(
            ring.at[t % RING, :, :, :, 0 : WIDTHS[w]], acc[w].at[i], c_send.at[t], c_recv.at[t], sibling
        )

    def half_rows(half):
        return pl.ds(half * HALF, HALF)

    def one_copy(t, half):
        w, i = UNITS[t]
        rows = half_rows(half)
        src = acc[w].at[i, 1 - y, :, rows] if half == 0 else acc[w].at[i, :, 1 - x, rows]
        return remote(
            src, one_in[w].at[i, half], one_send.at[t, half], one_recv.at[t, half], (over_y, over_x)[half]
        )

    def two_copy(t, half):
        w, i = UNITS[t]
        rows = half_rows(half)
        src = acc[w].at[i, y, 1 - x, rows] if half == 0 else acc[w].at[i, 1 - y, x, rows]
        return remote(
            src, two_in[w].at[i, half], two_send.at[t, half], two_recv.at[t, half], (over_x, over_y)[half]
        )

    def z_copy(t):
        w, i = UNITS[t]
        return remote(acc[w].at[i, y, x], z_in[w].at[i], z_send.at[t], z_recv.at[t], device(y, x, c, plane_of(i)))

    def add_rows(target, source):
        def body(r, carry):
            rows = pl.ds(pl.multiple_of(r * 16, 16), 16)
            target[rows] = (target[rows].astype(f32) + source[rows].astype(f32)).astype(bf16)
            return carry

        lax.fori_loop(0, HALF // 16, body, 0)

    def partial(w, i, parity, columns, n):
        plane = plane_of(i)
        if w == 3:
            right = projected_grad[plane, n]
        else:
            right = (activated, upward_grad, attended)[w][plane, :, columns]
        return dot(turned[w, parity], right, NN)

    def over_tiles(w, body):
        if w == 2:
            body(pl.ds(0, 256), 0)
            return

        def step(n, carry):
            body(pl.ds(pl.multiple_of(n * 256, 256), 256), n)
            return carry

        lax.fori_loop(0, WIDTHS[w] // 256, step, 0)

    def produce(t):
        w, i = UNITS[t]
        if t >= RING:
            pair_copy(t - RING).wait_send()

        def body(columns, n):
            product = partial(w, i, 1 - c, columns, n).astype(bf16)
            for k in range(4):
                ring[t % RING, k // 2, k % 2, :, columns] = product[k * BLOCK : (k + 1) * BLOCK]

        over_tiles(w, body)
        pair_copy(t).start()

    def join(t):
        w, i = UNITS[t]
        pair_copy(t).wait_recv()

        def body(columns, n):
            product = partial(w, i, c, columns, n)
            for k in range(4):
                came = acc[w][i, k // 2, k % 2, :, columns].astype(f32)
                acc[w][i, k // 2, k % 2, :, columns] = (product[k * BLOCK : (k + 1) * BLOCK] + came).astype(bf16)

        over_tiles(w, body)
        for half in HALVES:
            one_copy(t, half).start()

    def after_one(t):
        w, i = UNITS[t]
        for half in HALVES:
            one_copy(t, half).wait()
            rows = half_rows(half)
            for k in (0, 1):
                target = acc[w].at[i, y, k, rows] if half == 0 else acc[w].at[i, k, x, rows]
                add_rows(target, one_in[w].at[i, half, k])
            two_copy(t, half).start()

    def after_two(t):
        w, i = UNITS[t]
        for half in HALVES:
            two_copy(t, half).wait()
            add_rows(acc[w].at[i, y, x, half_rows(half)], two_in[w].at[i, half])
        if i < PLANES - 1:
            z_copy(t).start()

    def finish(w):
        for t, unit in enumerate(UNITS):
            if unit[0] == w and unit[1] < PLANES - 1:
                z_copy(t).wait()

        def body(n, carry):
            columns = pl.ds(pl.multiple_of(n * 128, 128), 128)
            total = acc[w].at[PLANES - 1, y, x][:, columns].astype(f32)
            for i in range(PLANES - 1):
                total = total + z_in[w].at[i][:, columns].astype(f32)
            if w in (0, 2):
                outs[w][columns, :] = total.T
            else:
                outs[w][:, columns] = total
            return carry

        lax.fori_loop(0, WIDTHS[w] // 128, body, 0)

    def turn(source, w):
        for owner in range(OWNERS):
            columns = slice(owner * BLOCK, (owner + 1) * BLOCK)
            place_at = slice((owner // 2) * BLOCK, (owner // 2 + 1) * BLOCK)
            turned[w, owner % 2, place_at, :] = source[:, columns].T

    def hidden_back(i):
        plane = plane_of(i)
        weight_load(0, i).wait()

        def grad(columns):
            product = dot(cotangent[...], down_ring[columns, :], NT)
            upward_grad[plane, :, columns] = (product * slope[plane, :, columns]).astype(bf16)

        tiles(4, 256, grad)
        if i < PLANES - 1:
            weight_load(0, i + 1).start()
        weight_load(1, i).wait()

        def normed(columns):
            product = dot(upward_grad[plane], up_ring[columns, :], NT)
            if i == 0:
                normed_grad[:, columns] = product
            else:
                normed_grad[:, columns] += product

        tiles(4, 256, normed)
        if i < PLANES - 1:
            weight_load(1, i + 1).start()

    def norm_back(source, gain, row, store):
        norm_own[0, row : row + 2, :] = jnp.zeros((2, D), f32)

        def strip(n, carry):
            rows = pl.ds(pl.multiple_of(n * 32, 32), 32)
            values = source[rows, :]
            center = values - jnp.mean(values, axis=-1, keepdims=True)
            scale = lax.rsqrt(jnp.mean(center * center, axis=-1, keepdims=True) + norm_epsilon)
            hat = center * scale
            grad = normed_grad[rows, :]
            norm_own[0, row : row + 1, :] += jnp.sum(grad * hat, axis=0, keepdims=True)
            norm_own[0, row + 1 : row + 2, :] += jnp.sum(grad, axis=0, keepdims=True)
            grad = grad * gain
            inner = jnp.mean(grad * hat, axis=-1, keepdims=True)
            store(rows, scale * (grad - jnp.mean(grad, axis=-1, keepdims=True) - hat * inner))
            return carry

        lax.fori_loop(0, ROWS // 32, strip, 0)

    def residual_back():
        def store(rows, part):
            total = part + cotangent[rows, :].astype(f32)
            residual_grad[rows, :] = total
            branch_grad[rows, :] = total.astype(bf16)

        norm_back(residual, norms[2:3, :], 2, store)

    def attend_back(i):
        plane = plane_of(i)
        live = members[...] >= 0
        attended_grad = dot(branch_grad[...], output_full[plane], NT).astype(bf16)
        scale = HEAD_DIM ** (-0.5)
        for head in range(2):
            span = slice(head * HEAD_DIM, (head + 1) * HEAD_DIM)
            queries, keys_all, values_all = (projected[plane, part, :, span] for part in range(3))
            scores = jnp.where(live, dot(queries, keys_all, NT) * scale, masked_score)
            exponent = jnp.exp(scores - jnp.max(scores, axis=-1, keepdims=True))
            probs = exponent * (1.0 / jnp.sum(exponent, axis=-1, keepdims=True))
            grad = attended_grad[:, span]
            projected_grad[plane, 2, :, span] = dot(probs.astype(bf16), grad, TN).astype(bf16)
            prob_grad = dot(grad, values_all, NT)
            inner = jnp.sum(probs * prob_grad, axis=-1, keepdims=True)
            score_grad = (probs * (prob_grad - inner)).astype(bf16)
            projected_grad[plane, 0, :, span] = (dot(score_grad, keys_all, NN) * scale).astype(bf16)
            projected_grad[plane, 1, :, span] = (dot(score_grad, queries, TN) * scale).astype(bf16)

    def project_back(i):
        plane = plane_of(i)
        weight_load(3, i).wait()
        if i < PLANES - 1:
            weight_load(3, i + 1).start()

        def normed(columns):
            total = dot(projected_grad[plane, 0], project_ring[i % 2, 0, columns, :], NT)
            for part in (1, 2):
                total += dot(projected_grad[plane, part], project_ring[i % 2, part, columns, :], NT)
            if i == 0:
                normed_grad[:, columns] = total
            else:
                normed_grad[:, columns] += total

        tiles(4, 256, normed)

    def input_back():
        def store(rows, part):
            residual_grad[rows, :] += part

        norm_back(inputs, norms[0:1, :], 0, store)

    def points_back():
        slot_of = lax.broadcasted_iota(jnp.int32, (ROWS, ROWS), 0) == members[...]
        chosen = slot_of.astype(f32).astype(bf16)

        def pick(columns):
            rest = residual_grad[:, columns]
            total = jnp.zeros((ROWS, 256), f32)
            for _ in range(3):
                low = rest.astype(bf16)
                total += dot(chosen, low, NN)
                rest = rest - low.astype(f32)
            points_out[:, columns] = total

        tiles(4, 256, pick)

    def norm_step(k):
        return remote(norm_own.at[k], norm_in.at[k], norm_send.at[k], norm_recv.at[k], (sibling, over_x, over_y)[k])

    def norm_plane(d):
        target = device(y, x, c, (z + d) % PLANES)
        return remote(norm_own.at[3], norm_planes.at[z], norm_send.at[2 + d], norm_recv.at[2 + d], target)

    def before(t):
        w, i = UNITS[t]
        if (w, i) == (0, 0):
            cotangent_load.wait()
            turn(cotangent, 0)
            load(6).wait()
        elif w == 1:
            if i == 0:
                load(5).wait()
                turn(entering_two, 1)
                load(7).wait()
            hidden_back(i)
        elif w == 3:
            if i == 0:
                load(4).wait()
                residual_back()
                load(2).wait()
                load(1).wait()
                turn(entering_one, 3)
                weight_load(2, 0).wait()
            attend_back(i)
            project_back(i)
        elif i == 0:
            load(3).wait()
            turn(branch_grad, 2)

    count = len(UNITS)
    lag = (2, 3, 4)
    before(0)
    produce(0)
    input_at = 1 + [t for t, unit in enumerate(UNITS) if unit == (3, 3)][0]
    last = {w: max(t for t, unit in enumerate(UNITS) if unit[0] == w) for w in range(4)}
    for step in range(count + lag[2]):
        if step + 1 < count:
            before(step + 1)
            produce(step + 1)
        if step < count:
            join(step)
        if 0 <= step - lag[0] < count:
            after_one(step - lag[0])
        if 0 <= step - lag[1] < count:
            after_two(step - lag[1])
        if step == input_at:
            load(0).wait()
            input_back()
            norm_step(0).start()
        if step == count:
            points_back()
        at = step - input_at - 1
        if 0 <= at < 3:
            norm_step(at).wait()
            norm_own[at + 1] = norm_own[at] + norm_in[at]
            if at < 2:
                norm_step(at + 1).start()
            else:
                norm_planes[z] = norm_own[3]
                for d in (1, 2, 3):
                    norm_plane(d).start()
        for w in range(4):
            if step - lag[2] == last[w]:
                finish(w)
    for d in (1, 2, 3):
        norm_plane(d).wait()
    norm_out[...] = (norm_planes[0] + norm_planes[1]) + (norm_planes[2] + norm_planes[3])
    for t in range(count - RING, count):
        pair_copy(t).wait_send()


def run_backward(fulls, saved, cotangent, members, layer_norms):
    f32, bf16 = jnp.float32, jnp.bfloat16
    rows_f32, rows_bf16 = pltpu.VMEM((ROWS, D), f32), pltpu.VMEM((ROWS, D), bf16)
    scratch = [pltpu.VMEM(a.shape, a.dtype) for a in saved] + [rows_bf16]
    scratch += [pltpu.VMEM((D, D), bf16)] * 2
    scratch += [pltpu.VMEM((PLANES, 256, D), bf16), pltpu.VMEM((2, 3, D, 256), bf16)]
    scratch += [pltpu.VMEM((4, 2, D // 2, ROWS), bf16), pltpu.VMEM((PLANES, ROWS, D), bf16)]
    scratch += [rows_f32, rows_bf16, pltpu.VMEM((PLANES, 3, ROWS, 256), bf16), rows_f32]
    scratch += [pltpu.VMEM((RING, 2, 2, BLOCK, D), bf16)]
    scratch += [pltpu.VMEM((4, 2, 2, BLOCK, n), bf16) for n in WIDTHS]
    scratch += [pltpu.VMEM((4, 2, 2, HALF, n), bf16) for n in WIDTHS]
    scratch += [pltpu.VMEM((4, 2, HALF, n), bf16) for n in WIDTHS]
    scratch += [pltpu.VMEM((3, BLOCK, n), bf16) for n in WIDTHS]
    scratch += [pltpu.VMEM((n, 4, D), f32) for n in (4, 3, 4)]
    dma = pltpu.SemaphoreType.DMA
    scratch += [dma((8,)), dma, dma((4, 4)), dma((16,)), dma((16,))]
    scratch += [dma((16, 2))] * 4 + [dma((16,))] * 2 + [dma((6,))] * 2
    anywhere, vmem = pl.BlockSpec(memory_space=pl.ANY), pl.BlockSpec(memory_space=pltpu.VMEM)
    blocks = [(WIDTHS[0], BLOCK), (BLOCK, WIDTHS[1]), (WIDTHS[2], BLOCK), (BLOCK, WIDTHS[3])]
    result = pl.pallas_call(
        backward_kernel,
        out_shape=[jax.ShapeDtypeStruct(s, f32) for s in blocks + [(4, D), (ROWS, D)]],
        in_specs=[anywhere] * 13 + [vmem] * 2,
        out_specs=[vmem] * 6,
        scratch_shapes=scratch,
        name="backward",
        compiler_params=pltpu.CompilerParams(
            collective_id=1, has_side_effects=True, vmem_limit_bytes=60 << 20
        ),
    )(*fulls, *saved, cotangent, members, layer_norms)
    return result[:4], result[4], result[5]


def on_device_cube(
    points,
    members,
    cotangent,
    project_weight,
    output_weight,
    upward_weight,
    downward_weight,
    layer_norms,
    project_master,
    project_first,
    project_second,
    output_master,
    output_first,
    output_second,
    upward_master,
    upward_first,
    upward_second,
    downward_master,
    downward_first,
    downward_second,
    norm_first,
    norm_second,
):
    bf16 = jnp.bfloat16
    fulls, saved, latents = run_forward(
        (jnp.transpose(project_weight, (1, 0, 2)), output_weight, upward_weight, downward_weight),
        points,
        members,
        layer_norms,
    )
    summed_blocks, norm_summed, point_gradient = run_backward(fulls, saved, cotangent, members, layer_norms)
    downward_summed, upward_summed, output_summed, project_block = summed_blocks
    project_summed = project_block.reshape(BLOCK, 3, 256)
    data_index = lax.axis_index("dp")
    norm_columns = norm_first.shape[1]
    norm_gradient = lax.dynamic_slice_in_dim(norm_summed, data_index * norm_columns, norm_columns, 1)
    norm_current = lax.dynamic_slice_in_dim(layer_norms, data_index * norm_columns, norm_columns, 1)
    results = [latents, point_gradient]
    for master, summed, first, second, rate in (
        (project_master, project_summed, project_first, project_second, D ** (-0.5)),
        (output_master, output_summed, output_first, output_second, max(1, D * 4 // LAT) ** (-0.5)),
        (upward_master, upward_summed, upward_first, upward_second, D ** (-0.5)),
        (downward_master, downward_summed, downward_first, downward_second, FF ** (-0.5)),
    ):
        updated, one_new, two_new = adamw_step(master, summed, first, second, rate)
        results += [summed, updated, one_new, two_new, updated.astype(bf16)]
    norm_new = adamw_step(norm_current, norm_gradient, norm_first, norm_second, 0.2)
    results += [norm_gradient, *norm_new]
    return tuple(results)


def solution(mesh):
    return jax.shard_map(
        on_device_cube if dict(mesh.shape) == {"dp": 8, "mp": 4} else on_device_any,
        mesh=mesh,
        in_specs=(
            P(("dp", "mp"), None),
            P(("dp", "mp"), None),
            P(("dp", "mp"), None),
            P(None, None, "mp"),
            P("mp", None),
            P(None, "mp"),
            P("mp", None),
            P(),
            P("dp", None, "mp"),
            P("dp", None, "mp"),
            P("dp", None, "mp"),
            P("mp", "dp"),
            P("mp", "dp"),
            P("mp", "dp"),
            P("dp", "mp"),
            P("dp", "mp"),
            P("dp", "mp"),
            P("mp", "dp"),
            P("mp", "dp"),
            P("mp", "dp"),
            P(None, "dp"),
            P(None, "dp"),
        ),
        out_specs=(
            P(("dp", "mp"), None),
            P(("dp", "mp"), None),
            P("dp", None, "mp"),
            P("dp", None, "mp"),
            P("dp", None, "mp"),
            P("dp", None, "mp"),
            P("dp", None, "mp"),
            P("mp", "dp"),
            P("mp", "dp"),
            P("mp", "dp"),
            P("mp", "dp"),
            P("mp", "dp"),
            P("dp", "mp"),
            P("dp", "mp"),
            P("dp", "mp"),
            P("dp", "mp"),
            P("dp", "mp"),
            P("mp", "dp"),
            P("mp", "dp"),
            P("mp", "dp"),
            P("mp", "dp"),
            P("mp", "dp"),
            P(None, "dp"),
            P(None, "dp"),
            P(None, "dp"),
            P(None, "dp"),
        ),
        check_vma=False,
    )
```

```python
import jax
import jax.numpy as jnp
from jax import lax
from jax.experimental import pallas as pl
from jax.experimental.pallas import tpu as pltpu
from jax.sharding import PartitionSpec as P

D = 1024
HEAD_DIM = 128
FF = 4096
LAT = 256
ADAM_STEP = 10


norm_epsilon = 1e-05
beta_one = 0.9
beta_two = 0.95
adam_epsilon = 1e-08
weight_decay = 0.1
masked_score = -1e30


def layer_norm(values, norm_gain, norm_shift):
    center = values - jnp.mean(values, axis=-1, keepdims=True)
    spread = jnp.mean(center * center, axis=-1, keepdims=True)
    return center * lax.rsqrt(spread + norm_epsilon) * norm_gain + norm_shift


def pick_rows(source_rows, row_index):
    return source_rows[row_index]


def adamw_step(weight, gradient, moment_one, moment_two, step_rate):
    one_new = beta_one * moment_one + (1.0 - beta_one) * gradient
    two_new = beta_two * moment_two + (1.0 - beta_two) * gradient * gradient
    corrected_one = one_new / (1.0 - beta_one**ADAM_STEP)
    corrected_two = two_new / (1.0 - beta_two**ADAM_STEP)
    updated = weight - step_rate * (
        corrected_one / (jnp.sqrt(corrected_two) + adam_epsilon) + weight_decay * weight
    )
    return (updated, one_new, two_new)


def masked_scores(queries, keys_all, key_mask, score_scale):
    raw_scores = (
        jnp.einsum("gqhe,gkhe->ghqk", queries, keys_all, preferred_element_type=jnp.float32)
        * score_scale
    )
    return jnp.where(key_mask, raw_scores, masked_score)


def on_device_any(
    points,
    members,
    cotangent,
    project_weight,
    output_weight,
    upward_weight,
    downward_weight,
    layer_norms,
    project_master,
    project_first,
    project_second,
    output_master,
    output_first,
    output_second,
    upward_master,
    upward_first,
    upward_second,
    downward_master,
    downward_first,
    downward_second,
    norm_first,
    norm_second,
):
    groups_here = members.shape[0]
    shard_rows = points.shape[0]
    model_width = points.shape[1]
    heads_here = project_weight.shape[2] // HEAD_DIM
    score_scale = HEAD_DIM ** (-0.5)
    grouped = points.reshape(groups_here, LAT, model_width)
    slot_index = jnp.maximum(members, 0)
    key_live = members >= 0
    picked = jax.vmap(pick_rows)(grouped, slot_index)
    inputs = jnp.where(key_live[:, :, None], picked.astype(jnp.float32), 0.0).reshape(
        shard_rows, model_width
    )
    normed, norm_back_one = jax.vjp(layer_norm, inputs, layer_norms[0], layer_norms[1])
    gathered, live_all = (
        lax.all_gather(normed.astype(jnp.bfloat16), "mp", axis=0, tiled=True),
        lax.all_gather(key_live.astype(jnp.bfloat16), "mp", axis=0, tiled=True),
    )
    total_rows = gathered.shape[0]
    total_groups = live_all.shape[0]
    key_mask = (live_all > 0)[:, None, None, :]
    projected = jnp.einsum(
        "rd,dcf->rcf", gathered, project_weight, preferred_element_type=jnp.float32
    ).astype(jnp.bfloat16)
    heads_view = projected.reshape(total_groups, LAT, 3, heads_here, HEAD_DIM)
    queries = heads_view[:, :, 0]
    keys_all = heads_view[:, :, 1]
    values_all = heads_view[:, :, 2]
    scores = masked_scores(queries, keys_all, key_mask, score_scale)
    row_top = jnp.max(scores, axis=-1, keepdims=True)
    exponent = jnp.exp(scores - row_top)
    row_total = jnp.sum(exponent, axis=-1, keepdims=True)
    attention_weights = exponent / row_total
    log_total = row_top + jnp.log(row_total)
    weights_low = attention_weights.astype(jnp.bfloat16)
    attended = jnp.einsum(
        "ghqk,gkhe->gqhe", weights_low, values_all, preferred_element_type=jnp.float32
    ).astype(jnp.bfloat16)
    attended = attended.reshape(total_rows, heads_here * HEAD_DIM)
    branch = lax.psum_scatter(
        jnp.dot(attended, output_weight, preferred_element_type=jnp.float32),
        "mp",
        scatter_dimension=0,
        tiled=True,
    )
    residual = inputs + branch
    normed_two, norm_back_two = jax.vjp(layer_norm, residual, layer_norms[2], layer_norms[3])
    gathered_two = lax.all_gather(normed_two.astype(jnp.bfloat16), "mp", axis=0, tiled=True)
    upward = jnp.dot(gathered_two, upward_weight, preferred_element_type=jnp.float32)
    activated_float, gelu_back = jax.vjp(jax.nn.gelu, upward)
    activated = activated_float.astype(jnp.bfloat16)
    latents = residual + lax.psum_scatter(
        jnp.dot(activated, downward_weight, preferred_element_type=jnp.float32).astype(
            jnp.bfloat16
        ),
        "mp",
        scatter_dimension=0,
        tiled=True,
    ).astype(jnp.float32)
    cotangent_all = lax.all_gather(cotangent, "mp", axis=0, tiled=True)
    downward_local = jnp.einsum(
        "rf,rd->fd", activated, cotangent_all, preferred_element_type=jnp.float32
    )
    activated_grad = jnp.einsum(
        "rd,fd->rf", cotangent_all, downward_weight, preferred_element_type=jnp.float32
    )
    upward_grad = gelu_back(activated_grad)[0].astype(jnp.bfloat16)
    upward_local = jnp.einsum(
        "rd,rf->df", gathered_two, upward_grad, preferred_element_type=jnp.float32
    )
    normed_two_grad = lax.psum_scatter(
        jnp.einsum("rf,df->rd", upward_grad, upward_weight, preferred_element_type=jnp.float32),
        "mp",
        scatter_dimension=0,
        tiled=True,
    )
    residual_part, gain_two_grad, shift_two_grad = norm_back_two(normed_two_grad)
    residual_grad = residual_part + cotangent.astype(jnp.float32)
    norm_two_local = jnp.stack([gain_two_grad, shift_two_grad])
    branch_grad = lax.all_gather(residual_grad.astype(jnp.bfloat16), "mp", axis=0, tiled=True)
    output_local = jnp.einsum(
        "rh,rd->hd", attended, branch_grad, preferred_element_type=jnp.float32
    )
    attended_grad = jnp.einsum(
        "rd,hd->rh", branch_grad, output_weight, preferred_element_type=jnp.float32
    ).astype(jnp.bfloat16)
    attended_grad = attended_grad.reshape(total_groups, LAT, heads_here, HEAD_DIM)
    scores_again = masked_scores(queries, keys_all, key_mask, score_scale)
    weights_again = jnp.exp(scores_again - log_total)
    weights_again_low = weights_again.astype(jnp.bfloat16)
    value_grad = jnp.einsum(
        "ghqk,gqhe->gkhe", weights_again_low, attended_grad, preferred_element_type=jnp.float32
    ).astype(jnp.bfloat16)
    weight_grad = jnp.einsum(
        "gqhe,gkhe->ghqk", attended_grad, values_all, preferred_element_type=jnp.float32
    )
    score_grad = (
        weights_again * (weight_grad - jnp.sum(weights_again * weight_grad, axis=-1, keepdims=True))
    ).astype(jnp.bfloat16)
    query_grad = (
        jnp.einsum("ghqk,gkhe->gqhe", score_grad, keys_all, preferred_element_type=jnp.float32)
        * score_scale
    ).astype(jnp.bfloat16)
    key_grad = (
        jnp.einsum("ghqk,gqhe->gkhe", score_grad, queries, preferred_element_type=jnp.float32)
        * score_scale
    ).astype(jnp.bfloat16)
    projected_grad = jnp.stack([query_grad, key_grad, value_grad], axis=2).reshape(
        total_rows, 3, heads_here * HEAD_DIM
    )
    project_local = jnp.einsum(
        "rd,rcf->dcf", gathered, projected_grad, preferred_element_type=jnp.float32
    )
    normed_grad = lax.psum_scatter(
        jnp.einsum(
            "rcf,dcf->rd", projected_grad, project_weight, preferred_element_type=jnp.float32
        ).astype(jnp.bfloat16),
        "mp",
        scatter_dimension=0,
        tiled=True,
    ).astype(jnp.float32)
    input_part, gain_one_grad, shift_one_grad = norm_back_one(normed_grad)
    input_grad = input_part + residual_grad
    norm_one_local = jnp.stack([gain_one_grad, shift_one_grad])
    matches = members[:, :, None] == jnp.arange(LAT, dtype=jnp.int32)[None, None, :]
    slot_of = jnp.argmax(matches, axis=1)
    point_used = jnp.any(matches, axis=1)
    grouped_grad = input_grad.reshape(groups_here, LAT, model_width)
    point_gradient = jnp.where(
        point_used[:, :, None], jax.vmap(pick_rows)(grouped_grad, slot_of), 0.0
    ).reshape(shard_rows, model_width)
    (
        project_summed,
        output_summed,
        upward_summed,
        downward_summed,
        norm_one_summed,
        norm_two_summed,
    ) = (
        lax.psum_scatter(project_local, "dp", scatter_dimension=0, tiled=True),
        lax.psum_scatter(output_local, "dp", scatter_dimension=1, tiled=True),
        lax.psum_scatter(upward_local, "dp", scatter_dimension=0, tiled=True),
        lax.psum_scatter(downward_local, "dp", scatter_dimension=1, tiled=True),
        lax.psum_scatter(norm_one_local, "dp", scatter_dimension=1, tiled=True),
        lax.psum_scatter(norm_two_local, "dp", scatter_dimension=1, tiled=True),
    )
    norm_gradient = lax.psum(jnp.concatenate([norm_one_summed, norm_two_summed], axis=0), "mp")
    data_index = lax.axis_index("dp")
    norm_columns = norm_first.shape[1]
    norm_current = lax.dynamic_slice_in_dim(layer_norms, data_index * norm_columns, norm_columns, 1)
    project_new = adamw_step(
        project_master, project_summed, project_first, project_second, D ** (-0.5)
    )
    output_new = adamw_step(
        output_master, output_summed, output_first, output_second, max(1, D * 4 // LAT) ** (-0.5)
    )
    upward_new = adamw_step(upward_master, upward_summed, upward_first, upward_second, D ** (-0.5))
    downward_new = adamw_step(
        downward_master, downward_summed, downward_first, downward_second, FF ** (-0.5)
    )
    norm_new = adamw_step(norm_current, norm_gradient, norm_first, norm_second, 0.2)
    return (
        latents,
        point_gradient,
        project_summed,
        project_new[0],
        project_new[1],
        project_new[2],
        project_new[0].astype(jnp.bfloat16),
        output_summed,
        output_new[0],
        output_new[1],
        output_new[2],
        output_new[0].astype(jnp.bfloat16),
        upward_summed,
        upward_new[0],
        upward_new[1],
        upward_new[2],
        upward_new[0].astype(jnp.bfloat16),
        downward_summed,
        downward_new[0],
        downward_new[1],
        downward_new[2],
        downward_new[0].astype(jnp.bfloat16),
        norm_gradient,
        norm_new[0],
        norm_new[1],
        norm_new[2],
    )


MESH = pl.DeviceIdType.MESH
PLANES = 4
OWNERS = 8
ROWS = LAT
HALVES = (0, 1)
SHARDS = ((3, D, 256), (256, D), (D, D), (D, D))


SHORT = (3,)


def place():
    dp = lax.axis_index("dp")
    return dp // 4, (dp // 2) % 2, dp % 2, lax.axis_index("mp")


def device(y, x, c, z):
    return (y * 4 + x * 2 + c, z)


def greet(y, x, c, z):
    barrier = pltpu.get_barrier_semaphore()
    partners = [device(1 - y, x, c, z), device(y, 1 - x, c, z), device(y, x, 1 - c, z)]
    partners += [device(y, x, c, (z + d) % PLANES) for d in (1, 2, 3)]
    for partner in partners:
        pl.semaphore_signal(barrier, inc=1, device_id=partner, device_id_type=MESH)
    pl.semaphore_wait(barrier, len(partners))


def arrival(z, k):
    return (z + 1 - 2 * (z % 2), 2 - z // 2, 3 - 3 * (z // 2))[k]


def dot(a, b, contract):
    return lax.dot_general(a, b, (contract, ((), ())), preferred_element_type=jnp.float32)


NN = ((1,), (0,))
NT = ((1,), (1,))
TN = ((0,), (0,))


def tiles(count, size, body):
    def step(n, carry):
        body(pl.ds(pl.multiple_of(n * size, size), size))
        return carry

    lax.fori_loop(0, count, step, 0)


def norm_rows(source, target, gain, shift, strip=64):
    def step(n, carry):
        rows = pl.ds(pl.multiple_of(n * strip, strip), strip)
        target[rows, :] = layer_norm(source[rows, :], gain, shift).astype(target.dtype)
        return carry

    lax.fori_loop(0, ROWS // strip, step, 0)


def forward_kernel(*refs):
    shards, (points, members, norms) = refs[0:4], refs[4:7]
    fulls_out, saved_out, latents_out = refs[7:11], refs[11:19], refs[19]
    fulls, saved, latents = refs[20:24], refs[24:32], refs[32]
    inputs, entering_one, projected, attended, residual, entering_two, activated, slope = saved
    own_sem, z_send, z_recv, a_send, a_recv, b_send, b_recv, c_send, c_recv = refs[33:42]
    weight_sem, saved_sem, latents_sem = refs[42:45]
    y, x, c, z = place()
    greet(y, x, c, z)
    is_mid = jnp.logical_or(z == 1, z == 2)
    sibling = device(y, x, 1 - c, z)
    over_x, over_y = device(y, 1 - x, c, z), device(1 - y, x, c, z)
    beside, across = device(y, x, c, arrival(z, 0)), device(y, x, c, 3 - z)

    def view(w, plane, rows):
        return fulls[w].at[plane, :, rows, :] if w == 0 else fulls[w].at[plane, rows, :]

    def block(w, half, first, count):
        height = SHARDS[w][-2]
        start = pl.multiple_of(half * (height // 2) + first * (height // 16), height // 16)
        return pl.ds(start, count * (height // 16))

    spot = (c * 4 + y * 2 + x, c * 4 + x * 2 + y)
    pair = (c * 4 + y * 2, c * 4 + x * 2)

    def remote(w, plane, rows, send, recv, target):
        return pltpu.make_async_remote_copy(
            src_ref=view(w, plane, rows),
            dst_ref=view(w, plane, rows),
            send_sem=send,
            recv_sem=recv,
            device_id=target,
            device_id_type=MESH,
        )

    def z_copy(w, plane, half, lane, k, target):
        rows = block(w, half, pair[half], 2) if w in SHORT else block(w, half, spot[half], 1)
        return remote(w, plane, rows, z_send.at[w, lane, half], z_recv.at[w, k, half], target)

    def z_own(w, half):
        return z_copy(w, z, half, 0, 0, beside)

    def z_own_across(w, half):
        return z_copy(w, z, half, 1, 1, across)

    def z_pass(w, k, half):
        lane, target, slot = ((2, across, 2), (3, beside, 1), (4, beside, 2))[k]
        return z_copy(w, arrival(z, k), half, lane, slot, target)

    def z_arrived(w, k, half):
        return z_copy(w, arrival(z, k), half, 0, k, beside)

    def a_copy(w, k, half):
        rows = block(w, half, spot[half], 1)
        return remote(
            w, arrival(z, k), rows, a_send.at[w, k, half], a_recv.at[w, k, half], (over_x, over_y)[half]
        )

    def b_copy(w, k, half):
        rows = block(w, half, pair[half], 2)
        return remote(
            w, arrival(z, k), rows, b_send.at[w, k, half], b_recv.at[w, k, half], (over_y, over_x)[half]
        )

    def c_copy(w, k, half):
        rows = block(w, half, c * 4, 4)
        return remote(w, arrival(z, k), rows, c_send.at[w, k, half], c_recv.at[w, k, half], sibling)

    def own_load(w):
        return pltpu.make_async_copy(shards[w], fulls[w].at[z], own_sem.at[w])

    def keep_weight(w, k):
        plane = z if k is None else arrival(z, k)
        slot = 3 if k is None else k
        return pltpu.make_async_copy(fulls[w].at[plane], fulls_out[w].at[plane], weight_sem.at[w, slot])

    def keep(n):
        return pltpu.make_async_copy(saved[n], saved_out[n], saved_sem.at[n])

    def enter():
        slot_of = lax.broadcasted_iota(jnp.int32, (ROWS, ROWS), 0) == members[...]
        chosen = slot_of.astype(jnp.float32).astype(jnp.bfloat16)

        def pick(columns):
            inputs[:, columns] = dot(chosen, points[:, columns], TN)

        tiles(4, 256, pick)
        norm_rows(inputs, entering_one, norms[0:1, :], norms[1:2, :])
        residual[...] = inputs[...]

    def project(plane):
        for part in range(3):
            projected[plane, part] = dot(entering_one[...], fulls[0][plane, part], NN).astype(jnp.bfloat16)

    def attend(plane):
        live = members[...] >= 0
        for head in range(2):
            span = slice(head * HEAD_DIM, (head + 1) * HEAD_DIM)
            queries, keys_all, values_all = (projected[plane, part, :, span] for part in range(3))
            scores = jnp.where(live, dot(queries, keys_all, NT) * HEAD_DIM ** (-0.5), masked_score)
            exponent = jnp.exp(scores - jnp.max(scores, axis=-1, keepdims=True))
            probs = exponent * (1.0 / jnp.sum(exponent, axis=-1, keepdims=True))
            attended[plane, :, span] = dot(probs.astype(jnp.bfloat16), values_all, NN).astype(jnp.bfloat16)

    def branch(plane):
        def body(columns):
            residual[:, columns] += dot(attended[plane], fulls[1][plane, :, columns], NN)

        tiles(4, 256, body)

    def enter_two():
        norm_rows(residual, entering_two, norms[2:3, :], norms[3:4, :])
        latents[...] = residual[...]

    def widen(plane):
        def body(columns):
            u = dot(entering_two[...], fulls[2][plane, :, columns], NN)
            square = u * u
            bend = jnp.tanh(0.7978845608028654 * u * (1.0 + 0.044715 * square))
            activated[plane, :, columns] = (0.5 * u * (1.0 + bend)).astype(jnp.bfloat16)
            slope[plane, :, columns] = 0.5 * (1.0 + bend) + 0.5 * u * (1.0 - bend * bend) * (
                0.7978845608028654 * (1.0 + 3.0 * 0.044715 * square)
            )

        tiles(4, 256, body)

    def narrow(plane):
        def body(columns):
            latents[:, columns] += dot(activated[plane], fulls[3][plane, :, columns], NN)

        tiles(4, 256, body)

    def compute(w, k):
        plane = z if k is None else arrival(z, k)
        if w == 0:
            project(plane)
            attend(plane)
        elif w == 1:
            branch(plane)
        elif w == 2:
            widen(plane)
        else:
            narrow(plane)

    def send_own(w):
        own_load(w).wait()
        for half in HALVES:
            z_own(w, half).start()

        @pl.when(is_mid)
        def _():
            for half in HALVES:
                z_own_across(w, half).start()

        keep_weight(w, None).start()

    def take(w, k):
        for half in HALVES:
            z_arrived(w, k, half).wait_recv()
            (b_copy if w in SHORT else a_copy)(w, k, half).start()

        @pl.when(is_mid)
        def _():
            for half in HALVES:
                z_pass(w, k, half).start()

    def finished(w, k):
        if w == 1:
            return
        compute(w, k)
        if k == 2:
            if w == 0:
                keep(2).start()
                keep(3).start()
                for at in (None, 0, 1, 2):
                    compute(1, at)
                keep(4).start()
                enter_two()
                keep(5).start()
                compute(2, None)
            elif w == 2:
                keep(6).start()
                keep(7).start()
                compute(3, None)

    order = (1, 0, 2, 3)
    chunks = [(w, k) for w in order for k in range(3)]
    for w in order:
        own_load(w).start()
    send_own(order[0])
    taken = 0
    for step in range(len(chunks) + 3):
        while taken < min(len(chunks), step + 1):
            if taken % 3 == 0 and taken // 3 + 1 < 4:
                send_own(order[taken // 3 + 1])
            take(*chunks[taken])
            taken += 1
        if 0 <= step - 1 < len(chunks):
            w, k = chunks[step - 1]
            if w not in SHORT:
                for half in HALVES:
                    a_copy(w, k, half).wait_recv()
                    b_copy(w, k, half).start()
        if 0 <= step - 2 < len(chunks):
            w, k = chunks[step - 2]
            for half in HALVES:
                b_copy(w, k, half).wait_recv()
                c_copy(w, k, half).start()
        if step == 1:
            enter()
            keep(0).start()
            keep(1).start()
            compute(0, None)
        if 0 <= step - 3 < len(chunks):
            w, k = chunks[step - 3]
            for half in HALVES:
                c_copy(w, k, half).wait_recv()
            keep_weight(w, k).start()
            finished(w, k)
    out = pltpu.make_async_copy(latents, latents_out, latents_sem)
    out.start()
    for w in range(4):
        for half in HALVES:
            z_own(w, half).wait_send()
            for k in range(3):
                if w not in SHORT:
                    a_copy(w, k, half).wait_send()
                b_copy(w, k, half).wait_send()
                c_copy(w, k, half).wait_send()

    @pl.when(is_mid)
    def _():
        for w in range(4):
            for half in HALVES:
                z_own_across(w, half).wait_send()
                for k in range(3):
                    z_pass(w, k, half).wait_send()

    for w in range(4):
        for k in (None, 0, 1, 2):
            keep_weight(w, k).wait()
    for n in range(8):
        keep(n).wait()
    out.wait()


def run_forward(shards, points, members, layer_norms):
    f32, bf16 = jnp.float32, jnp.bfloat16
    saved = [
        ((ROWS, D), f32),
        ((ROWS, D), bf16),
        ((PLANES, 3, ROWS, 256), bf16),
        ((PLANES, ROWS, 256), bf16),
        ((ROWS, D), f32),
        ((ROWS, D), bf16),
        ((PLANES, ROWS, D), bf16),
        ((PLANES, ROWS, D), f32),
    ]
    anywhere, vmem = pl.BlockSpec(memory_space=pl.ANY), pl.BlockSpec(memory_space=pltpu.VMEM)
    fulls = [((PLANES,) + s, bf16) for s in SHARDS]
    dma = pltpu.SemaphoreType.DMA
    result = pl.pallas_call(
        forward_kernel,
        out_shape=[jax.ShapeDtypeStruct(*a) for a in fulls + saved + [((ROWS, D), f32)]],
        in_specs=[anywhere] * 4 + [vmem] * 3,
        out_specs=[anywhere] * 13,
        scratch_shapes=[pltpu.VMEM(*a) for a in fulls + saved + [((ROWS, D), f32)]]
        + [dma((4,)), dma((4, 5, 2))]
        + [dma((4, 3, 2))] * 7
        + [dma((4, 4)), dma((8,)), dma],
        name="forward",
        compiler_params=pltpu.CompilerParams(
            collective_id=0, has_side_effects=True, vmem_limit_bytes=60 << 20
        ),
    )(*shards, points, members, layer_norms)
    return result[:4], result[4:12], result[12]


WIDTHS = (D, D, 256, 3 * 256)
BLOCK = D // OWNERS
HALF = BLOCK // 2
RING = 2
UNITS = [(w, i) for w in (0, 1, 3, 2) for i in range(PLANES)]
EARLY_Z = (0, 1)
OWN = PLANES - 1
LAG_ONE, LAG_TWO, LAG_Z, TAIL = 2, 4, 6, 7
OWN_AT = {0: 13, 1: 17}
FINISH_AT = {0: 15, 1: 20, 3: 19, 2: 22}


def backward_kernel(*refs):
    fulls, saved_in = refs[0:4], refs[4:12]
    cotangent_in, members, norms = refs[12:15]
    outs, norm_out, points_out = refs[15:23], refs[23], refs[24]
    saved, cotangent = refs[25:33], refs[33]
    inputs, entering_one, projected, attended, residual, entering_two, activated, slope = saved
    down_ring, up_ring, output_full, project_ring = refs[34:38]
    turned, upward_grad, residual_grad, branch_grad, projected_grad, normed_grad = refs[38:44]
    ring = refs[44]
    acc, one_in, two_in, z_in = refs[45:49], refs[49:53], refs[53:57], refs[57:61]
    norm_own, norm_in, norm_planes = refs[61:64]
    saved_sem, cotangent_sem, weight_sem, points_sem = refs[64:68]
    c_send, c_recv, one_send, one_recv, two_send, two_recv, z_send, z_recv = refs[68:76]
    norm_send, norm_recv = refs[76:78]
    f32, bf16 = jnp.float32, jnp.bfloat16
    y, x, c, z = place()

    def load(n):
        return pltpu.make_async_copy(saved_in[n], saved[n], saved_sem.at[n])

    cotangent_load = pltpu.make_async_copy(cotangent_in, cotangent, cotangent_sem)
    cotangent_load.start()
    for n in (6, 5, 7, 4, 2, 3, 1, 0):
        load(n).start()

    is_mid = jnp.logical_or(z == 1, z == 2)
    is_end = jnp.logical_not(is_mid)

    def plane_of(i):
        return z if i == OWN else arrival(z, 2 - i)

    def weight_load(w, i):
        plane = plane_of(i)
        if w == 2:
            return pltpu.make_async_copy(fulls[1], output_full, weight_sem.at[2, 0])
        target = (down_ring, up_ring, None, project_ring.at[i % 2])[w]
        return pltpu.make_async_copy(fulls[(3, 2, 1, 0)[w]].at[plane], target, weight_sem.at[w, i])

    weight_load(0, 0).start()
    weight_load(1, 0).start()
    weight_load(2, 0).start()
    weight_load(3, 0).start()
    greet(y, x, c, z)
    sibling = device(y, x, 1 - c, z)
    over_x, over_y = device(y, 1 - x, c, z), device(1 - y, x, c, z)
    beside, across = device(y, x, c, arrival(z, 0)), device(y, x, c, 3 - z)

    def remote(src, dst, send, recv, target):
        return pltpu.make_async_remote_copy(
            src_ref=src, dst_ref=dst, send_sem=send, recv_sem=recv, device_id=target, device_id_type=MESH
        )

    def pair_copy(t):
        w, i = UNITS[t]
        return remote(
            ring.at[t % RING, :, :, :, 0 : WIDTHS[w]], acc[w].at[i], c_send.at[t], c_recv.at[t], sibling
        )

    def half_rows(half):
        return pl.ds(half * HALF, HALF)

    def one_copy(t, half):
        w, i = UNITS[t]
        rows = half_rows(half)
        src = acc[w].at[i, 1 - y, :, rows] if half == 0 else acc[w].at[i, :, 1 - x, rows]
        return remote(
            src, one_in[w].at[i, half], one_send.at[t, half], one_recv.at[t, half], (over_y, over_x)[half]
        )

    def two_copy(t, half):
        w, i = UNITS[t]
        rows = half_rows(half)
        src = acc[w].at[i, y, 1 - x, rows] if half == 0 else acc[w].at[i, 1 - y, x, rows]
        slot = 0 if w in EARLY_Z else i
        return remote(
            src, two_in[w].at[slot, half], two_send.at[t, half], two_recv.at[t, half], (over_x, over_y)[half]
        )

    def z_piece(t, half):
        w, i = UNITS[t]
        if w in EARLY_Z:
            return acc[w].at[i, y, :, half_rows(half)] if half == 0 else acc[w].at[i, :, x, half_rows(half)]
        return acc[w].at[i, y, x, half_rows(half)]

    def z_copy(t, half, slot, target):
        w = UNITS[t][0]
        return remote(
            z_piece(t, half), z_in[w].at[slot, half], z_send.at[t, half], z_recv.at[w, slot, half], target
        )

    def z_add(t, slot):
        w = UNITS[t][0]
        for half in HALVES:
            z_copy(t, half, slot, beside).wait_recv()
            piece = z_piece(t, half)
            if w in EARLY_Z:
                for k in (0, 1):
                    add_rows(piece.at[k], z_in[w].at[slot, half, k])
            else:
                add_rows(piece, z_in[w].at[slot, half])

    def z_send_end(t):
        i = UNITS[t][1]

        @pl.when(is_end)
        def _():
            for half in HALVES:
                z_copy(t, half, 2 - i, beside).start()

    def z_send_mid(t):
        i = UNITS[t][1]

        @pl.when(is_mid)
        def _():
            z_add(t, (2, 1, 3)[i])
            for half in HALVES:
                z_copy(t, half, (3, 4, 0)[i], (across, across, beside)[i]).start()

    def add_rows(target, source):
        def body(r, carry):
            rows = pl.ds(pl.multiple_of(r * 16, 16), 16)
            target[rows] = (target[rows].astype(f32) + source[rows].astype(f32)).astype(bf16)
            return carry

        lax.fori_loop(0, HALF // 16, body, 0)

    def partial(w, i, parity, columns, n):
        plane = plane_of(i)
        if w == 3:
            right = projected_grad[plane, n]
        else:
            right = (activated, upward_grad, attended)[w][plane, :, columns]
        return dot(turned[w, parity], right, NN)

    def over_tiles(w, body):
        if w == 2:
            body(pl.ds(0, 256), 0)
            return

        def step(n, carry):
            body(pl.ds(pl.multiple_of(n * 256, 256), 256), n)
            return carry

        lax.fori_loop(0, WIDTHS[w] // 256, step, 0)

    def produce(t):
        w, i = UNITS[t]
        if t >= RING:
            pair_copy(t - RING).wait_send()

        def body(columns, n):
            product = partial(w, i, 1 - c, columns, n).astype(bf16)
            for k in range(4):
                ring[t % RING, k // 2, k % 2, :, columns] = product[k * BLOCK : (k + 1) * BLOCK]

        over_tiles(w, body)
        pair_copy(t).start()

    def join(t):
        w, i = UNITS[t]
        pair_copy(t).wait_recv()

        def body(columns, n):
            product = partial(w, i, c, columns, n)
            for k in range(4):
                came = acc[w][i, k // 2, k % 2, :, columns].astype(f32)
                acc[w][i, k // 2, k % 2, :, columns] = (product[k * BLOCK : (k + 1) * BLOCK] + came).astype(bf16)

        over_tiles(w, body)
        for half in HALVES:
            one_copy(t, half).start()

    def after_one(t):
        w, i = UNITS[t]
        for half in HALVES:
            one_copy(t, half).wait()
            rows = half_rows(half)
            for k in (0, 1):
                target = acc[w].at[i, y, k, rows] if half == 0 else acc[w].at[i, k, x, rows]
                add_rows(target, one_in[w].at[i, half, k])
            if w not in EARLY_Z:
                two_copy(t, half).start()
        if w in EARLY_Z and i < OWN:
            z_send_end(t)

    def after_two(t):
        w, i = UNITS[t]
        if w in EARLY_Z:
            return
        for half in HALVES:
            two_copy(t, half).wait()
            add_rows(acc[w].at[i, y, x, half_rows(half)], two_in[w].at[i, half])
        if i < OWN:
            z_send_end(t)

    def own_hop(w):
        t = UNITS.index((w, OWN))
        z_add(t, 0)

        @pl.when(is_mid)
        def _():
            z_add(t, 4)

        for half in HALVES:
            two_copy(t, half).start()

    def finish(w):
        t = UNITS.index((w, OWN))
        mine = acc[w].at[OWN, y, x]
        if w in EARLY_Z:
            for half in HALVES:
                two_copy(t, half).wait()
        else:
            for half in HALVES:
                z_copy(t, half, 0, beside).wait_recv()

            @pl.when(is_mid)
            def _():
                for half in HALVES:
                    z_copy(t, half, 4, across).wait_recv()

        def body(n, carry):
            columns = pl.ds(pl.multiple_of(n * 128, 128), 128)
            first = mine[:, columns].astype(f32)
            if w in EARLY_Z:
                second = [two_in[w][0, half, :, columns] for half in HALVES]
            else:
                second = [z_in[w][0, half, :, columns] for half in HALVES]
                third = [z_in[w][4, half, :, columns] for half in HALVES]
                first += jnp.where(is_mid, jnp.concatenate(third, axis=0).astype(f32), 0.0)
            second = jnp.concatenate(second, axis=0).astype(f32)
            for n_out, value in ((w, first), (4 + w, second)):
                if w in (0, 2):
                    outs[n_out][columns, :] = value.T.astype(outs[n_out].dtype)
                elif w == 1:
                    outs[n_out][:, columns] = value.astype(outs[n_out].dtype)
                else:
                    part_columns = pl.ds(pl.multiple_of((n % 2) * 128, 128), 128)
                    outs[n_out][n // 2, :, part_columns] = value.astype(outs[n_out].dtype)
            return carry

        lax.fori_loop(0, WIDTHS[w] // 128, body, 0)

    def turn(source, w):
        for owner in range(OWNERS):
            columns = slice(owner * BLOCK, (owner + 1) * BLOCK)
            place_at = slice((owner // 2) * BLOCK, (owner // 2 + 1) * BLOCK)
            turned[w, owner % 2, place_at, :] = source[:, columns].T

    def hidden_back(i):
        plane = plane_of(i)
        weight_load(0, i).wait()

        def grad(columns):
            product = dot(cotangent[...], down_ring[columns, :], NT)
            upward_grad[plane, :, columns] = (product * slope[plane, :, columns]).astype(bf16)

        tiles(4, 256, grad)
        if i < PLANES - 1:
            weight_load(0, i + 1).start()
        weight_load(1, i).wait()

        def normed(columns):
            product = dot(upward_grad[plane], up_ring[columns, :], NT)
            if i == 0:
                normed_grad[:, columns] = product
            else:
                normed_grad[:, columns] += product

        tiles(4, 256, normed)
        if i < PLANES - 1:
            weight_load(1, i + 1).start()

    def norm_back(source, gain, row, store):
        norm_own[0, row : row + 2, :] = jnp.zeros((2, D), f32)

        def strip(n, carry):
            rows = pl.ds(pl.multiple_of(n * 32, 32), 32)
            values = source[rows, :]
            center = values - jnp.mean(values, axis=-1, keepdims=True)
            scale = lax.rsqrt(jnp.mean(center * center, axis=-1, keepdims=True) + norm_epsilon)
            hat = center * scale
            grad = normed_grad[rows, :]
            norm_own[0, row : row + 1, :] += jnp.sum(grad * hat, axis=0, keepdims=True)
            norm_own[0, row + 1 : row + 2, :] += jnp.sum(grad, axis=0, keepdims=True)
            grad = grad * gain
            inner = jnp.mean(grad * hat, axis=-1, keepdims=True)
            store(rows, scale * (grad - jnp.mean(grad, axis=-1, keepdims=True) - hat * inner))
            return carry

        lax.fori_loop(0, ROWS // 32, strip, 0)

    def residual_back():
        def store(rows, part):
            total = part + cotangent[rows, :].astype(f32)
            residual_grad[rows, :] = total
            branch_grad[rows, :] = total.astype(bf16)

        norm_back(residual, norms[2:3, :], 2, store)

    def attend_back(i):
        plane = plane_of(i)
        live = members[...] >= 0
        attended_grad = dot(branch_grad[...], output_full[plane], NT).astype(bf16)
        scale = HEAD_DIM ** (-0.5)
        for head in range(2):
            span = slice(head * HEAD_DIM, (head + 1) * HEAD_DIM)
            queries, keys_all, values_all = (projected[plane, part, :, span] for part in range(3))
            scores = jnp.where(live, dot(queries, keys_all, NT) * scale, masked_score)
            exponent = jnp.exp(scores - jnp.max(scores, axis=-1, keepdims=True))
            probs = exponent * (1.0 / jnp.sum(exponent, axis=-1, keepdims=True))
            grad = attended_grad[:, span]
            projected_grad[plane, 2, :, span] = dot(probs.astype(bf16), grad, TN).astype(bf16)
            prob_grad = dot(grad, values_all, NT)
            inner = jnp.sum(probs * prob_grad, axis=-1, keepdims=True)
            score_grad = (probs * (prob_grad - inner)).astype(bf16)
            projected_grad[plane, 0, :, span] = (dot(score_grad, keys_all, NN) * scale).astype(bf16)
            projected_grad[plane, 1, :, span] = (dot(score_grad, queries, TN) * scale).astype(bf16)

    def project_back(i):
        plane = plane_of(i)
        weight_load(3, i).wait()
        if i < PLANES - 1:
            weight_load(3, i + 1).start()

        def normed(columns):
            total = dot(projected_grad[plane, 0], project_ring[i % 2, 0, columns, :], NT)
            for part in (1, 2):
                total += dot(projected_grad[plane, part], project_ring[i % 2, part, columns, :], NT)
            if i == 0:
                normed_grad[:, columns] = total
            else:
                normed_grad[:, columns] += total

        tiles(4, 256, normed)

    def input_back():
        def store(rows, part):
            residual_grad[rows, :] += part

        norm_back(inputs, norms[0:1, :], 0, store)

    points_copy = pltpu.make_async_copy(inputs, points_out, points_sem)

    def points_back():
        slot_of = lax.broadcasted_iota(jnp.int32, (ROWS, ROWS), 0) == members[...]
        chosen = slot_of.astype(f32).astype(bf16)

        def pick(columns):
            rest = residual_grad[:, columns]
            total = jnp.zeros((ROWS, 256), f32)
            for _ in range(3):
                low = rest.astype(bf16)
                total += dot(chosen, low, NN)
                rest = rest - low.astype(f32)
            inputs[:, columns] = total

        tiles(4, 256, pick)
        points_copy.start()

    def norm_step(k):
        return remote(norm_own.at[k], norm_in.at[k], norm_send.at[k], norm_recv.at[k], (sibling, over_x, over_y)[k])

    def norm_plane(d):
        target = device(y, x, c, (z + d) % PLANES)
        return remote(norm_own.at[3], norm_planes.at[z], norm_send.at[2 + d], norm_recv.at[2 + d], target)

    def before(t):
        w, i = UNITS[t]
        if (w, i) == (0, 0):
            cotangent_load.wait()
            turn(cotangent, 0)
            load(6).wait()
        elif w == 1:
            if i == 0:
                load(5).wait()
                turn(entering_two, 1)
                load(7).wait()
            hidden_back(i)
        elif w == 3:
            if i == 0:
                load(4).wait()
                residual_back()
                load(2).wait()
                load(1).wait()
                turn(entering_one, 3)
                weight_load(2, 0).wait()
            attend_back(i)
            project_back(i)
        elif i == 0:
            load(3).wait()
            turn(branch_grad, 2)

    count = len(UNITS)
    before(0)
    produce(0)
    input_at = 1 + UNITS.index((3, OWN))
    for step in range(count + TAIL):
        if step + 1 < count:
            before(step + 1)
            produce(step + 1)
        if step < count:
            join(step)
        if 0 <= step - LAG_ONE < count:
            after_one(step - LAG_ONE)
        if 0 <= step - LAG_TWO < count:
            after_two(step - LAG_TWO)
        if 0 <= step - LAG_Z < count and UNITS[step - LAG_Z][1] < OWN:
            z_send_mid(step - LAG_Z)
        if step == input_at:
            load(0).wait()
            input_back()
            norm_step(0).start()
        if step == count:
            points_back()
        at = step - input_at - 1
        if 0 <= at < 3:
            norm_step(at).wait()
            norm_own[at + 1] = norm_own[at] + norm_in[at]
            if at < 2:
                norm_step(at + 1).start()
            else:
                norm_planes[z] = norm_own[3]
                for d in (1, 2, 3):
                    norm_plane(d).start()
        for w in range(4):
            if w in EARLY_Z and step == OWN_AT[w]:
                own_hop(w)
            if step == FINISH_AT[w]:
                finish(w)
    for d in (1, 2, 3):
        norm_plane(d).wait()
    norm_out[...] = (norm_planes[0] + norm_planes[1]) + (norm_planes[2] + norm_planes[3])
    for t in range(count - RING, count):
        pair_copy(t).wait_send()
    for t in range(count):
        if UNITS[t][1] < OWN:
            for half in HALVES:
                z_copy(t, half, 0, beside).wait_send()
    points_copy.wait()


def run_backward(fulls, saved, cotangent, members, layer_norms):
    f32, bf16 = jnp.float32, jnp.bfloat16
    rows_f32, rows_bf16 = pltpu.VMEM((ROWS, D), f32), pltpu.VMEM((ROWS, D), bf16)
    scratch = [pltpu.VMEM(a.shape, a.dtype) for a in saved] + [rows_bf16]
    scratch += [pltpu.VMEM((D, D), bf16)] * 2
    scratch += [pltpu.VMEM((PLANES, 256, D), bf16), pltpu.VMEM((2, 3, D, 256), bf16)]
    scratch += [pltpu.VMEM((4, 2, D // 2, ROWS), bf16), pltpu.VMEM((PLANES, ROWS, D), bf16)]
    scratch += [rows_f32, rows_bf16, pltpu.VMEM((PLANES, 3, ROWS, 256), bf16), rows_f32]
    scratch += [pltpu.VMEM((RING, 2, 2, BLOCK, D), bf16)]
    scratch += [pltpu.VMEM((4, 2, 2, BLOCK, n), bf16) for n in WIDTHS]
    scratch += [pltpu.VMEM((4, 2, 2, HALF, n), bf16) for n in WIDTHS]
    scratch += [pltpu.VMEM((1 if w in EARLY_Z else 4, 2, HALF, WIDTHS[w]), bf16) for w in range(4)]
    scratch += [pltpu.VMEM((5, 2) + ((2,) if w in EARLY_Z else ()) + (HALF, WIDTHS[w]), bf16) for w in range(4)]
    scratch += [pltpu.VMEM((n, 4, D), f32) for n in (4, 3, 4)]
    dma = pltpu.SemaphoreType.DMA
    scratch += [dma((8,)), dma, dma((4, 4)), dma, dma((16,)), dma((16,))]
    scratch += [dma((16, 2))] * 5 + [dma((4, 5, 2))] + [dma((6,))] * 2
    anywhere, vmem = pl.BlockSpec(memory_space=pl.ANY), pl.BlockSpec(memory_space=pltpu.VMEM)
    blocks = [(WIDTHS[0], BLOCK), (BLOCK, WIDTHS[1]), (WIDTHS[2], BLOCK), (3, BLOCK, 256)]
    result = pl.pallas_call(
        backward_kernel,
        out_shape=[jax.ShapeDtypeStruct(blocks[w], bf16 if w in EARLY_Z else f32) for w in range(4)]
        + [jax.ShapeDtypeStruct(s, bf16) for s in blocks]
        + [jax.ShapeDtypeStruct((4, D), f32), jax.ShapeDtypeStruct((ROWS, D), f32)],
        in_specs=[anywhere] * 13 + [vmem] * 2,
        out_specs=[vmem] * 9 + [anywhere],
        scratch_shapes=scratch,
        name="backward",
        compiler_params=pltpu.CompilerParams(
            collective_id=1, has_side_effects=True, vmem_limit_bytes=60 << 20
        ),
    )(*fulls, *saved, cotangent, members, layer_norms)
    return result[:4], result[4:8], result[8], result[9]


def on_device_cube(
    points,
    members,
    cotangent,
    project_weight,
    output_weight,
    upward_weight,
    downward_weight,
    layer_norms,
    project_master,
    project_first,
    project_second,
    output_master,
    output_first,
    output_second,
    upward_master,
    upward_first,
    upward_second,
    downward_master,
    downward_first,
    downward_second,
    norm_first,
    norm_second,
):
    bf16 = jnp.bfloat16
    fulls, saved, latents = run_forward(
        (jnp.transpose(project_weight, (1, 0, 2)), output_weight, upward_weight, downward_weight),
        points,
        members,
        layer_norms,
    )
    firsts, seconds, norm_summed, point_gradient = run_backward(fulls, saved, cotangent, members, layer_norms)
    data_index = lax.axis_index("dp")
    norm_columns = norm_first.shape[1]
    norm_gradient = lax.dynamic_slice_in_dim(norm_summed, data_index * norm_columns, norm_columns, 1)
    norm_current = lax.dynamic_slice_in_dim(layer_norms, data_index * norm_columns, norm_columns, 1)
    results = [latents, point_gradient]
    swap = lambda array: jnp.transpose(array, (1, 0, 2))
    for w, states, rate in (
        (3, [swap(a) for a in (project_master, project_first, project_second)], D ** (-0.5)),
        (2, [output_master, output_first, output_second], max(1, D * 4 // LAT) ** (-0.5)),
        (1, [upward_master, upward_first, upward_second], D ** (-0.5)),
        (0, [downward_master, downward_first, downward_second], FF ** (-0.5)),
    ):
        master, first, second = states
        summed = firsts[w].astype(jnp.float32) + seconds[w].astype(jnp.float32)
        updated, one_new, two_new = adamw_step(master, summed, first, second, rate)
        new = [summed, updated, one_new, two_new, updated.astype(bf16)]
        results += [swap(a) for a in new] if w == 3 else new
    norm_new = adamw_step(norm_current, norm_gradient, norm_first, norm_second, 0.2)
    results += [norm_gradient, *norm_new]
    return tuple(results)


def solution(mesh):
    return jax.shard_map(
        on_device_cube if dict(mesh.shape) == {"dp": 8, "mp": 4} else on_device_any,
        mesh=mesh,
        in_specs=(
            P(("dp", "mp"), None),
            P(("dp", "mp"), None),
            P(("dp", "mp"), None),
            P(None, None, "mp"),
            P("mp", None),
            P(None, "mp"),
            P("mp", None),
            P(),
            P("dp", None, "mp"),
            P("dp", None, "mp"),
            P("dp", None, "mp"),
            P("mp", "dp"),
            P("mp", "dp"),
            P("mp", "dp"),
            P("dp", "mp"),
            P("dp", "mp"),
            P("dp", "mp"),
            P("mp", "dp"),
            P("mp", "dp"),
            P("mp", "dp"),
            P(None, "dp"),
            P(None, "dp"),
        ),
        out_specs=(
            P(("dp", "mp"), None),
            P(("dp", "mp"), None),
            P("dp", None, "mp"),
            P("dp", None, "mp"),
            P("dp", None, "mp"),
            P("dp", None, "mp"),
            P("dp", None, "mp"),
            P("mp", "dp"),
            P("mp", "dp"),
            P("mp", "dp"),
            P("mp", "dp"),
            P("mp", "dp"),
            P("dp", "mp"),
            P("dp", "mp"),
            P("dp", "mp"),
            P("dp", "mp"),
            P("dp", "mp"),
            P("mp", "dp"),
            P("mp", "dp"),
            P("mp", "dp"),
            P("mp", "dp"),
            P("mp", "dp"),
            P(None, "dp"),
            P(None, "dp"),
            P(None, "dp"),
            P(None, "dp"),
        ),
        check_vma=False,
    )
```

```python
import jax
import jax.numpy as jnp
from jax import lax
from jax.experimental import pallas as pl
from jax.experimental.pallas import tpu as pltpu
from jax.sharding import PartitionSpec as P

D = 1024
HEAD_DIM = 128
FF = 4096
LAT = 256
ADAM_STEP = 10


norm_epsilon = 1e-05
beta_one = 0.9
beta_two = 0.95
adam_epsilon = 1e-08
weight_decay = 0.1
masked_score = -1e30


def layer_norm(values, norm_gain, norm_shift):
    center = values - jnp.mean(values, axis=-1, keepdims=True)
    spread = jnp.mean(center * center, axis=-1, keepdims=True)
    return center * lax.rsqrt(spread + norm_epsilon) * norm_gain + norm_shift


def pick_rows(source_rows, row_index):
    return source_rows[row_index]


def adamw_step(weight, gradient, moment_one, moment_two, step_rate):
    one_new = beta_one * moment_one + (1.0 - beta_one) * gradient
    two_new = beta_two * moment_two + (1.0 - beta_two) * gradient * gradient
    corrected_one = one_new / (1.0 - beta_one**ADAM_STEP)
    corrected_two = two_new / (1.0 - beta_two**ADAM_STEP)
    updated = weight - step_rate * (
        corrected_one / (jnp.sqrt(corrected_two) + adam_epsilon) + weight_decay * weight
    )
    return (updated, one_new, two_new)


def masked_scores(queries, keys_all, key_mask, score_scale):
    raw_scores = (
        jnp.einsum("gqhe,gkhe->ghqk", queries, keys_all, preferred_element_type=jnp.float32)
        * score_scale
    )
    return jnp.where(key_mask, raw_scores, masked_score)


def on_device_any(
    points,
    members,
    cotangent,
    project_weight,
    output_weight,
    upward_weight,
    downward_weight,
    layer_norms,
    project_master,
    project_first,
    project_second,
    output_master,
    output_first,
    output_second,
    upward_master,
    upward_first,
    upward_second,
    downward_master,
    downward_first,
    downward_second,
    norm_first,
    norm_second,
):
    groups_here = members.shape[0]
    shard_rows = points.shape[0]
    model_width = points.shape[1]
    heads_here = project_weight.shape[2] // HEAD_DIM
    score_scale = HEAD_DIM ** (-0.5)
    grouped = points.reshape(groups_here, LAT, model_width)
    slot_index = jnp.maximum(members, 0)
    key_live = members >= 0
    picked = jax.vmap(pick_rows)(grouped, slot_index)
    inputs = jnp.where(key_live[:, :, None], picked.astype(jnp.float32), 0.0).reshape(
        shard_rows, model_width
    )
    normed, norm_back_one = jax.vjp(layer_norm, inputs, layer_norms[0], layer_norms[1])
    gathered, live_all = (
        lax.all_gather(normed.astype(jnp.bfloat16), "mp", axis=0, tiled=True),
        lax.all_gather(key_live.astype(jnp.bfloat16), "mp", axis=0, tiled=True),
    )
    total_rows = gathered.shape[0]
    total_groups = live_all.shape[0]
    key_mask = (live_all > 0)[:, None, None, :]
    projected = jnp.einsum(
        "rd,dcf->rcf", gathered, project_weight, preferred_element_type=jnp.float32
    ).astype(jnp.bfloat16)
    heads_view = projected.reshape(total_groups, LAT, 3, heads_here, HEAD_DIM)
    queries = heads_view[:, :, 0]
    keys_all = heads_view[:, :, 1]
    values_all = heads_view[:, :, 2]
    scores = masked_scores(queries, keys_all, key_mask, score_scale)
    row_top = jnp.max(scores, axis=-1, keepdims=True)
    exponent = jnp.exp(scores - row_top)
    row_total = jnp.sum(exponent, axis=-1, keepdims=True)
    attention_weights = exponent / row_total
    log_total = row_top + jnp.log(row_total)
    weights_low = attention_weights.astype(jnp.bfloat16)
    attended = jnp.einsum(
        "ghqk,gkhe->gqhe", weights_low, values_all, preferred_element_type=jnp.float32
    ).astype(jnp.bfloat16)
    attended = attended.reshape(total_rows, heads_here * HEAD_DIM)
    branch = lax.psum_scatter(
        jnp.dot(attended, output_weight, preferred_element_type=jnp.float32),
        "mp",
        scatter_dimension=0,
        tiled=True,
    )
    residual = inputs + branch
    normed_two, norm_back_two = jax.vjp(layer_norm, residual, layer_norms[2], layer_norms[3])
    gathered_two = lax.all_gather(normed_two.astype(jnp.bfloat16), "mp", axis=0, tiled=True)
    upward = jnp.dot(gathered_two, upward_weight, preferred_element_type=jnp.float32)
    activated_float, gelu_back = jax.vjp(jax.nn.gelu, upward)
    activated = activated_float.astype(jnp.bfloat16)
    latents = residual + lax.psum_scatter(
        jnp.dot(activated, downward_weight, preferred_element_type=jnp.float32).astype(
            jnp.bfloat16
        ),
        "mp",
        scatter_dimension=0,
        tiled=True,
    ).astype(jnp.float32)
    cotangent_all = lax.all_gather(cotangent, "mp", axis=0, tiled=True)
    downward_local = jnp.einsum(
        "rf,rd->fd", activated, cotangent_all, preferred_element_type=jnp.float32
    )
    activated_grad = jnp.einsum(
        "rd,fd->rf", cotangent_all, downward_weight, preferred_element_type=jnp.float32
    )
    upward_grad = gelu_back(activated_grad)[0].astype(jnp.bfloat16)
    upward_local = jnp.einsum(
        "rd,rf->df", gathered_two, upward_grad, preferred_element_type=jnp.float32
    )
    normed_two_grad = lax.psum_scatter(
        jnp.einsum("rf,df->rd", upward_grad, upward_weight, preferred_element_type=jnp.float32),
        "mp",
        scatter_dimension=0,
        tiled=True,
    )
    residual_part, gain_two_grad, shift_two_grad = norm_back_two(normed_two_grad)
    residual_grad = residual_part + cotangent.astype(jnp.float32)
    norm_two_local = jnp.stack([gain_two_grad, shift_two_grad])
    branch_grad = lax.all_gather(residual_grad.astype(jnp.bfloat16), "mp", axis=0, tiled=True)
    output_local = jnp.einsum(
        "rh,rd->hd", attended, branch_grad, preferred_element_type=jnp.float32
    )
    attended_grad = jnp.einsum(
        "rd,hd->rh", branch_grad, output_weight, preferred_element_type=jnp.float32
    ).astype(jnp.bfloat16)
    attended_grad = attended_grad.reshape(total_groups, LAT, heads_here, HEAD_DIM)
    scores_again = masked_scores(queries, keys_all, key_mask, score_scale)
    weights_again = jnp.exp(scores_again - log_total)
    weights_again_low = weights_again.astype(jnp.bfloat16)
    value_grad = jnp.einsum(
        "ghqk,gqhe->gkhe", weights_again_low, attended_grad, preferred_element_type=jnp.float32
    ).astype(jnp.bfloat16)
    weight_grad = jnp.einsum(
        "gqhe,gkhe->ghqk", attended_grad, values_all, preferred_element_type=jnp.float32
    )
    score_grad = (
        weights_again * (weight_grad - jnp.sum(weights_again * weight_grad, axis=-1, keepdims=True))
    ).astype(jnp.bfloat16)
    query_grad = (
        jnp.einsum("ghqk,gkhe->gqhe", score_grad, keys_all, preferred_element_type=jnp.float32)
        * score_scale
    ).astype(jnp.bfloat16)
    key_grad = (
        jnp.einsum("ghqk,gqhe->gkhe", score_grad, queries, preferred_element_type=jnp.float32)
        * score_scale
    ).astype(jnp.bfloat16)
    projected_grad = jnp.stack([query_grad, key_grad, value_grad], axis=2).reshape(
        total_rows, 3, heads_here * HEAD_DIM
    )
    project_local = jnp.einsum(
        "rd,rcf->dcf", gathered, projected_grad, preferred_element_type=jnp.float32
    )
    normed_grad = lax.psum_scatter(
        jnp.einsum(
            "rcf,dcf->rd", projected_grad, project_weight, preferred_element_type=jnp.float32
        ).astype(jnp.bfloat16),
        "mp",
        scatter_dimension=0,
        tiled=True,
    ).astype(jnp.float32)
    input_part, gain_one_grad, shift_one_grad = norm_back_one(normed_grad)
    input_grad = input_part + residual_grad
    norm_one_local = jnp.stack([gain_one_grad, shift_one_grad])
    matches = members[:, :, None] == jnp.arange(LAT, dtype=jnp.int32)[None, None, :]
    slot_of = jnp.argmax(matches, axis=1)
    point_used = jnp.any(matches, axis=1)
    grouped_grad = input_grad.reshape(groups_here, LAT, model_width)
    point_gradient = jnp.where(
        point_used[:, :, None], jax.vmap(pick_rows)(grouped_grad, slot_of), 0.0
    ).reshape(shard_rows, model_width)
    (
        project_summed,
        output_summed,
        upward_summed,
        downward_summed,
        norm_one_summed,
        norm_two_summed,
    ) = (
        lax.psum_scatter(project_local, "dp", scatter_dimension=0, tiled=True),
        lax.psum_scatter(output_local, "dp", scatter_dimension=1, tiled=True),
        lax.psum_scatter(upward_local, "dp", scatter_dimension=0, tiled=True),
        lax.psum_scatter(downward_local, "dp", scatter_dimension=1, tiled=True),
        lax.psum_scatter(norm_one_local, "dp", scatter_dimension=1, tiled=True),
        lax.psum_scatter(norm_two_local, "dp", scatter_dimension=1, tiled=True),
    )
    norm_gradient = lax.psum(jnp.concatenate([norm_one_summed, norm_two_summed], axis=0), "mp")
    data_index = lax.axis_index("dp")
    norm_columns = norm_first.shape[1]
    norm_current = lax.dynamic_slice_in_dim(layer_norms, data_index * norm_columns, norm_columns, 1)
    project_new = adamw_step(
        project_master, project_summed, project_first, project_second, D ** (-0.5)
    )
    output_new = adamw_step(
        output_master, output_summed, output_first, output_second, max(1, D * 4 // LAT) ** (-0.5)
    )
    upward_new = adamw_step(upward_master, upward_summed, upward_first, upward_second, D ** (-0.5))
    downward_new = adamw_step(
        downward_master, downward_summed, downward_first, downward_second, FF ** (-0.5)
    )
    norm_new = adamw_step(norm_current, norm_gradient, norm_first, norm_second, 0.2)
    return (
        latents,
        point_gradient,
        project_summed,
        project_new[0],
        project_new[1],
        project_new[2],
        project_new[0].astype(jnp.bfloat16),
        output_summed,
        output_new[0],
        output_new[1],
        output_new[2],
        output_new[0].astype(jnp.bfloat16),
        upward_summed,
        upward_new[0],
        upward_new[1],
        upward_new[2],
        upward_new[0].astype(jnp.bfloat16),
        downward_summed,
        downward_new[0],
        downward_new[1],
        downward_new[2],
        downward_new[0].astype(jnp.bfloat16),
        norm_gradient,
        norm_new[0],
        norm_new[1],
        norm_new[2],
    )


MESH = pl.DeviceIdType.MESH
PLANES = 4
OWNERS = 8
ROWS = LAT
HALVES = (0, 1)
SHARDS = ((3, D, 256), (256, D), (D, D), (D, D))
GATHER_ORDER = (1, 0, 2, 3)
SHORT = (3,)
CHUNKS = [(w, k) for w in GATHER_ORDER for k in range(3)]
SLOTS = 3
LOADS = [(0, None), (0, 0), (0, 1), (0, 2)]
LOADS += [(2, None), (2, 0), (2, 1), (2, 2)]
LOADS += [(3, None), (3, 0), (3, 1), (3, 2)]
LOADS += [(2, 2), (2, 1), (2, 0), (2, None)]
LOADS += [(0, 2), (0, 1), (0, 0), (0, None)]

WIDTHS = (D, D, 256, 3 * 256)
BLOCK = D // OWNERS
HALF = BLOCK // 2
RING = 2
OWN = PLANES - 1
UNITS = [(w, i) for w in (0, 1, 3, 2) for i in range(PLANES)]
EARLY_Z = (0, 1)
TURNED_AT = (0, 1, 1, 0)
LAG_ONE, LAG_TWO, LAG_Z, TAIL = 2, 4, 6, 7
OWN_AT = {0: 13, 1: 17}
FINISH_AT = {0: 15, 1: 20, 3: 19, 2: 22}
JOIN_FROM = 13

NN = ((1,), (0,))
NT = ((1,), (1,))
TN = ((0,), (0,))


def place():
    dp = lax.axis_index("dp")
    return dp // 4, (dp // 2) % 2, dp % 2, lax.axis_index("mp")


def device(y, x, c, z):
    return (y * 4 + x * 2 + c, z)


def greet(y, x, c, z):
    barrier = pltpu.get_barrier_semaphore()
    partners = [device(1 - y, x, c, z), device(y, 1 - x, c, z), device(y, x, 1 - c, z)]
    partners += [device(y, x, c, (z + d) % PLANES) for d in (1, 2, 3)]
    for partner in partners:
        pl.semaphore_signal(barrier, inc=1, device_id=partner, device_id_type=MESH)
    pl.semaphore_wait(barrier, len(partners))


def arrival(z, k):
    return (z + 1 - 2 * (z % 2), 2 - z // 2, 3 - 3 * (z // 2))[k]


def dot(a, b, contract):
    return lax.dot_general(a, b, (contract, ((), ())), preferred_element_type=jnp.float32)


def tiles(count, size, body):
    def step(n, carry):
        body(pl.ds(pl.multiple_of(n * size, size), size))
        return carry

    lax.fori_loop(0, count, step, 0)


def norm_rows(source, target, gain, shift, strip=64):
    def step(n, carry):
        rows = pl.ds(pl.multiple_of(n * strip, strip), strip)
        target[rows, :] = layer_norm(source[rows, :], gain, shift).astype(target.dtype)
        return carry

    lax.fori_loop(0, ROWS // strip, step, 0)


def step_kernel(*refs):
    f32, bf16 = jnp.float32, jnp.bfloat16
    shards, (points, cotangent, members, norms) = refs[0:4], refs[4:8]
    outs, norm_out, latents_out, points_out, fulls = refs[8:16], refs[16], refs[17], refs[18], refs[19:23]
    inputs, entering_one, projected, attended, residual, entering_two, activated, slope, latents = refs[23:32]
    turned, upward_grad, branch_grad, projected_grad, normed_grad = refs[32:37]
    slots, output_full, ring = refs[37:40]
    acc, one_in, two_in, z_in = refs[40:44], refs[44:48], refs[48:52], refs[52:56]
    norm_own, norm_in, norm_planes = refs[56:59]
    load_sem, output_sem, out_sem = refs[59:62]
    gz_send, gz_recv, ga_send, ga_recv, gb_send, gb_recv, gc_send, gc_recv = refs[62:70]
    c_send, c_recv, one_send, one_recv, two_send, two_recv, z_send, z_recv = refs[70:78]
    norm_send, norm_recv = refs[78:80]
    residual_grad = residual
    y, x, c, z = place()
    is_mid = jnp.logical_or(z == 1, z == 2)
    is_end = jnp.logical_not(is_mid)
    sibling = device(y, x, 1 - c, z)
    over_x, over_y = device(y, 1 - x, c, z), device(1 - y, x, c, z)
    beside, across = device(y, x, c, arrival(z, 0)), device(y, x, c, 3 - z)

    def plane_at(k):
        return z if k is None else arrival(z, k)

    def plane_of(i):
        return z if i == OWN else arrival(z, 2 - i)

    def remote(src, dst, send, recv, target):
        return pltpu.make_async_remote_copy(
            src_ref=src, dst_ref=dst, send_sem=send, recv_sem=recv, device_id=target, device_id_type=MESH
        )

    def rows_of(ref, w, rows):
        return ref.at[:, rows, :] if w == 0 else ref.at[rows, :]

    def view(w, plane, rows):
        return rows_of(fulls[w].at[plane], w, rows)

    def block(w, half, first, count):
        height = SHARDS[w][-2]
        start = pl.multiple_of(half * (height // 2) + first * (height // 16), height // 16)
        return pl.ds(start, count * (height // 16))

    spot = (c * 4 + y * 2 + x, c * 4 + x * 2 + y)
    pair = (c * 4 + y * 2, c * 4 + x * 2)

    def gz_rows(w, half):
        return block(w, half, pair[half], 2) if w in SHORT else block(w, half, spot[half], 1)

    def gz_own(w, half, lane, slot, target):
        rows = gz_rows(w, half)
        send, recv = gz_send.at[w, lane, half], gz_recv.at[w, slot, half]
        return remote(rows_of(shards[w], w, rows), view(w, z, rows), send, recv, target)

    def gz_beside(w, half):
        return gz_own(w, half, 0, 0, beside)

    def gz_across(w, half):
        return gz_own(w, half, 1, 1, across)

    def gz_foreign(w, k, half, lane, slot, target):
        here = view(w, arrival(z, k), gz_rows(w, half))
        return remote(here, here, gz_send.at[w, lane, half], gz_recv.at[w, slot, half], target)

    def gz_pass(w, k, half):
        lane, target, slot = ((2, across, 2), (3, beside, 1), (4, beside, 2))[k]
        return gz_foreign(w, k, half, lane, slot, target)

    def gz_arrived(w, k, half):
        return gz_foreign(w, k, half, 0, k, beside)

    def ga_copy(w, k, half):
        here = view(w, arrival(z, k), block(w, half, spot[half], 1))
        return remote(here, here, ga_send.at[w, k, half], ga_recv.at[w, k, half], (over_x, over_y)[half])

    def gb_copy(w, k, half):
        here = view(w, arrival(z, k), block(w, half, pair[half], 2))
        return remote(here, here, gb_send.at[w, k, half], gb_recv.at[w, k, half], (over_y, over_x)[half])

    def gc_copy(w, k, half):
        here = view(w, arrival(z, k), block(w, half, c * 4, 4))
        return remote(here, here, gc_send.at[w, k, half], gc_recv.at[w, k, half], sibling)

    def send_own(w):
        for half in HALVES:
            gz_beside(w, half).start()

        @pl.when(is_mid)
        def _():
            for half in HALVES:
                gz_across(w, half).start()

    def take(w, k):
        for half in HALVES:
            gz_arrived(w, k, half).wait_recv()
            (gb_copy if w in SHORT else ga_copy)(w, k, half).start()

        @pl.when(is_mid)
        def _():
            for half in HALVES:
                gz_pass(w, k, half).start()

    def loads(n):
        w, k = LOADS[n]
        source = shards[w] if k is None else fulls[w].at[arrival(z, k)]
        if w != 0:
            return [pltpu.make_async_copy(source, slots.at[n % SLOTS], load_sem.at[n, 0])]
        return [
            pltpu.make_async_copy(
                source.at[part], slots.at[n % SLOTS, :, part * 256 : (part + 1) * 256], load_sem.at[n, part]
            )
            for part in range(3)
        ]

    def start_load(n):
        for copy in loads(n):
            copy.start()

    def wait_load(n):
        for copy in loads(n):
            copy.wait()

    def output_load(k):
        source = shards[1] if k is None else fulls[1].at[arrival(z, k)]
        return pltpu.make_async_copy(source, output_full.at[plane_at(k)], output_sem.at[3 if k is None else k])

    def enter():
        slot_of = lax.broadcasted_iota(jnp.int32, (ROWS, ROWS), 0) == members[...]
        chosen = slot_of.astype(f32).astype(bf16)

        def pick(columns):
            inputs[:, columns] = dot(chosen, points[:, columns], TN)

        tiles(4, 256, pick)
        norm_rows(inputs, entering_one, norms[0:1, :], norms[1:2, :])
        residual[...] = inputs[...]

    def softmax_parts(plane, span):
        queries, keys_all = projected[plane, 0, :, span], projected[plane, 1, :, span]
        scores = jnp.where(members[...] >= 0, dot(queries, keys_all, NT) * HEAD_DIM ** (-0.5), masked_score)
        exponent = jnp.exp(scores - jnp.max(scores, axis=-1, keepdims=True))
        return queries, keys_all, exponent * (1.0 / jnp.sum(exponent, axis=-1, keepdims=True))

    def project_attend(n):
        wait_load(n)
        plane, slot = plane_at(LOADS[n][1]), n % SLOTS
        for part in range(3):
            right = slots[slot, :, part * 256 : (part + 1) * 256]
            projected[plane, part] = dot(entering_one[...], right, NN).astype(bf16)
        for head in range(2):
            span = slice(head * HEAD_DIM, (head + 1) * HEAD_DIM)
            probs = softmax_parts(plane, span)[2]
            attended[plane, :, span] = dot(probs.astype(bf16), projected[plane, 2, :, span], NN).astype(bf16)

    def branch(k):
        plane = plane_at(k)
        output_load(k).wait()

        def body(columns):
            residual[:, columns] += dot(attended[plane], output_full[plane, :, columns], NN)

        tiles(4, 256, body)

    def enter_two():
        norm_rows(residual, entering_two, norms[2:3, :], norms[3:4, :])
        latents[...] = residual[...]

    def widen(n):
        wait_load(n)
        plane, slot = plane_at(LOADS[n][1]), n % SLOTS

        def body(columns):
            u = dot(entering_two[...], slots[slot, :, columns], NN)
            square = u * u
            bend = jnp.tanh(0.7978845608028654 * u * (1.0 + 0.044715 * square))
            activated[plane, :, columns] = (0.5 * u * (1.0 + bend)).astype(bf16)
            slope[plane, :, columns] = 0.5 * (1.0 + bend) + 0.5 * u * (1.0 - bend * bend) * (
                0.7978845608028654 * (1.0 + 3.0 * 0.044715 * square)
            )

        tiles(4, 256, body)

    def narrow(n):
        wait_load(n)
        plane, slot = plane_at(LOADS[n][1]), n % SLOTS

        def body(columns):
            latents[:, columns] += dot(activated[plane], slots[slot, :, columns], NN)
            product = dot(cotangent[...], slots[slot, columns, :], NT)
            upward_grad[plane, :, columns] = (product * slope[plane, :, columns]).astype(bf16)

        tiles(4, 256, body)

    def pair_copy(t):
        w, i = UNITS[t]
        return remote(
            ring.at[t % RING, :, :, :, 0 : WIDTHS[w]], acc[w].at[i], c_send.at[t], c_recv.at[t], sibling
        )

    def half_rows(half):
        return pl.ds(half * HALF, HALF)

    def one_copy(t, half):
        w, i = UNITS[t]
        rows = half_rows(half)
        src = acc[w].at[i, 1 - y, :, rows] if half == 0 else acc[w].at[i, :, 1 - x, rows]
        return remote(
            src, one_in[w].at[i, half], one_send.at[t, half], one_recv.at[t, half], (over_y, over_x)[half]
        )

    def two_copy(t, half):
        w, i = UNITS[t]
        rows = half_rows(half)
        src = acc[w].at[i, y, 1 - x, rows] if half == 0 else acc[w].at[i, 1 - y, x, rows]
        slot = 0 if w in EARLY_Z else i
        return remote(
            src, two_in[w].at[slot, half], two_send.at[t, half], two_recv.at[t, half], (over_x, over_y)[half]
        )

    def z_piece(t, half):
        w, i = UNITS[t]
        if w in EARLY_Z:
            return acc[w].at[i, y, :, half_rows(half)] if half == 0 else acc[w].at[i, :, x, half_rows(half)]
        return acc[w].at[i, y, x, half_rows(half)]

    def z_copy(t, half, slot, target):
        w = UNITS[t][0]
        return remote(
            z_piece(t, half), z_in[w].at[slot, half], z_send.at[t, half], z_recv.at[w, slot, half], target
        )

    def z_add(t, slot):
        w = UNITS[t][0]
        for half in HALVES:
            z_copy(t, half, slot, beside).wait_recv()
            piece = z_piece(t, half)
            if w in EARLY_Z:
                for k in (0, 1):
                    add_rows(piece.at[k], z_in[w].at[slot, half, k])
            else:
                add_rows(piece, z_in[w].at[slot, half])

    def z_send_end(t):
        i = UNITS[t][1]

        @pl.when(is_end)
        def _():
            for half in HALVES:
                z_copy(t, half, 2 - i, beside).start()

    def z_send_mid(t):
        i = UNITS[t][1]

        @pl.when(is_mid)
        def _():
            z_add(t, (2, 1, 3)[i])
            for half in HALVES:
                z_copy(t, half, (3, 4, 0)[i], (across, across, beside)[i]).start()

    def add_rows(target, source):
        def body(r, carry):
            rows = pl.ds(pl.multiple_of(r * 16, 16), 16)
            target[rows] = (target[rows].astype(f32) + source[rows].astype(f32)).astype(bf16)
            return carry

        lax.fori_loop(0, HALF // 16, body, 0)

    def partial(w, i, parity, columns, n):
        plane = plane_of(i)
        if w == 3:
            right = projected_grad[plane, n]
        else:
            right = (activated, upward_grad, attended)[w][plane, :, columns]
        return dot(turned[TURNED_AT[w], parity], right, NN)

    def over_tiles(w, body):
        if w == 2:
            body(pl.ds(0, 256), 0)
            return

        def step(n, carry):
            body(pl.ds(pl.multiple_of(n * 256, 256), 256), n)
            return carry

        lax.fori_loop(0, WIDTHS[w] // 256, step, 0)

    def produce(t):
        w, i = UNITS[t]
        if t >= RING:
            pair_copy(t - RING).wait_send()

        def body(columns, n):
            product = partial(w, i, 1 - c, columns, n).astype(bf16)
            for k in range(4):
                ring[t % RING, k // 2, k % 2, :, columns] = product[k * BLOCK : (k + 1) * BLOCK]

        over_tiles(w, body)
        pair_copy(t).start()

    def join(t):
        w, i = UNITS[t]
        pair_copy(t).wait_recv()

        def body(columns, n):
            product = partial(w, i, c, columns, n)
            for k in range(4):
                came = acc[w][i, k // 2, k % 2, :, columns].astype(f32)
                acc[w][i, k // 2, k % 2, :, columns] = (product[k * BLOCK : (k + 1) * BLOCK] + came).astype(bf16)

        over_tiles(w, body)
        for half in HALVES:
            one_copy(t, half).start()

    def after_one(t):
        w, i = UNITS[t]
        for half in HALVES:
            one_copy(t, half).wait()
            rows = half_rows(half)
            for k in (0, 1):
                target = acc[w].at[i, y, k, rows] if half == 0 else acc[w].at[i, k, x, rows]
                add_rows(target, one_in[w].at[i, half, k])
            if w not in EARLY_Z:
                two_copy(t, half).start()
        if w in EARLY_Z and i < OWN:
            z_send_end(t)

    def after_two(t):
        w, i = UNITS[t]
        if w in EARLY_Z:
            return
        for half in HALVES:
            two_copy(t, half).wait()
            add_rows(acc[w].at[i, y, x, half_rows(half)], two_in[w].at[i, half])
        if i < OWN:
            z_send_end(t)

    def own_hop(w):
        t = UNITS.index((w, OWN))
        z_add(t, 0)

        @pl.when(is_mid)
        def _():
            z_add(t, 4)

        for half in HALVES:
            two_copy(t, half).start()

    def finish(w):
        t = UNITS.index((w, OWN))
        mine = acc[w].at[OWN, y, x]
        if w in EARLY_Z:
            for half in HALVES:
                two_copy(t, half).wait()
        else:
            for half in HALVES:
                z_copy(t, half, 0, beside).wait_recv()

            @pl.when(is_mid)
            def _():
                for half in HALVES:
                    z_copy(t, half, 4, across).wait_recv()

        def body(n, carry):
            columns = pl.ds(pl.multiple_of(n * 128, 128), 128)
            first = mine[:, columns].astype(f32)
            if w in EARLY_Z:
                second = [two_in[w][0, half, :, columns] for half in HALVES]
            else:
                second = [z_in[w][0, half, :, columns] for half in HALVES]
                third = [z_in[w][4, half, :, columns] for half in HALVES]
                first += jnp.where(is_mid, jnp.concatenate(third, axis=0).astype(f32), 0.0)
            second = jnp.concatenate(second, axis=0).astype(f32)
            for n_out, value in ((w, first), (4 + w, second)):
                if w in (0, 2):
                    outs[n_out][columns, :] = value.T.astype(outs[n_out].dtype)
                elif w == 1:
                    outs[n_out][:, columns] = value.astype(outs[n_out].dtype)
                else:
                    part_columns = pl.ds(pl.multiple_of((n % 2) * 128, 128), 128)
                    outs[n_out][n // 2, :, part_columns] = value.astype(outs[n_out].dtype)
            return carry

        lax.fori_loop(0, WIDTHS[w] // 128, body, 0)

    def turn(source, w):
        for owner in range(OWNERS):
            columns = slice(owner * BLOCK, (owner + 1) * BLOCK)
            place_at = slice((owner // 2) * BLOCK, (owner // 2 + 1) * BLOCK)
            turned[TURNED_AT[w], owner % 2, place_at, :] = source[:, columns].T

    def hidden_back(i):
        n = 12 + i
        wait_load(n)
        plane, slot = plane_of(i), n % SLOTS

        def normed(columns):
            product = dot(upward_grad[plane], slots[slot, columns, :], NT)
            if i == 0:
                normed_grad[:, columns] = product
            else:
                normed_grad[:, columns] += product

        tiles(4, 256, normed)
        start_load(n + SLOTS)

    def norm_back(source, gain, row, store):
        norm_own[0, row : row + 2, :] = jnp.zeros((2, D), f32)

        def strip(n, carry):
            rows = pl.ds(pl.multiple_of(n * 32, 32), 32)
            values = source[rows, :]
            center = values - jnp.mean(values, axis=-1, keepdims=True)
            scale = lax.rsqrt(jnp.mean(center * center, axis=-1, keepdims=True) + norm_epsilon)
            hat = center * scale
            grad = normed_grad[rows, :]
            norm_own[0, row : row + 1, :] += jnp.sum(grad * hat, axis=0, keepdims=True)
            norm_own[0, row + 1 : row + 2, :] += jnp.sum(grad, axis=0, keepdims=True)
            grad = grad * gain
            inner = jnp.mean(grad * hat, axis=-1, keepdims=True)
            store(rows, scale * (grad - jnp.mean(grad, axis=-1, keepdims=True) - hat * inner))
            return carry

        lax.fori_loop(0, ROWS // 32, strip, 0)

    def residual_back():
        def store(rows, part):
            total = part + cotangent[rows, :].astype(f32)
            residual_grad[rows, :] = total
            branch_grad[rows, :] = total.astype(bf16)

        norm_back(residual, norms[2:3, :], 2, store)

    def attend_back(i):
        plane = plane_of(i)
        attended_grad = dot(branch_grad[...], output_full[plane], NT).astype(bf16)
        scale = HEAD_DIM ** (-0.5)
        for head in range(2):
            span = slice(head * HEAD_DIM, (head + 1) * HEAD_DIM)
            queries, keys_all, probs = softmax_parts(plane, span)
            grad = attended_grad[:, span]
            projected_grad[plane, 2, :, span] = dot(probs.astype(bf16), grad, TN).astype(bf16)
            prob_grad = dot(grad, projected[plane, 2, :, span], NT)
            inner = jnp.sum(probs * prob_grad, axis=-1, keepdims=True)
            score_grad = (probs * (prob_grad - inner)).astype(bf16)
            projected_grad[plane, 0, :, span] = (dot(score_grad, keys_all, NN) * scale).astype(bf16)
            projected_grad[plane, 1, :, span] = (dot(score_grad, queries, TN) * scale).astype(bf16)

    def project_back(i):
        n = 16 + i
        wait_load(n)
        plane, slot = plane_of(i), n % SLOTS

        def normed(columns):
            total = dot(projected_grad[plane, 0], slots[slot, columns, 0:256], NT)
            for part in (1, 2):
                total += dot(projected_grad[plane, part], slots[slot, columns, part * 256 : (part + 1) * 256], NT)
            if i == 0:
                normed_grad[:, columns] = total
            else:
                normed_grad[:, columns] += total

        tiles(4, 256, normed)
        if n + SLOTS < len(LOADS):
            start_load(n + SLOTS)

    def input_back():
        def store(rows, part):
            residual_grad[rows, :] += part

        norm_back(inputs, norms[0:1, :], 0, store)

    points_copy = pltpu.make_async_copy(inputs, points_out, out_sem.at[1])

    def points_back():
        slot_of = lax.broadcasted_iota(jnp.int32, (ROWS, ROWS), 0) == members[...]
        chosen = slot_of.astype(f32).astype(bf16)

        def pick(columns):
            rest = residual_grad[:, columns]
            total = jnp.zeros((ROWS, 256), f32)
            for _ in range(3):
                low = rest.astype(bf16)
                total += dot(chosen, low, NN)
                rest = rest - low.astype(f32)
            inputs[:, columns] = total

        tiles(4, 256, pick)
        points_copy.start()

    def norm_step(k):
        return remote(norm_own.at[k], norm_in.at[k], norm_send.at[k], norm_recv.at[k], (sibling, over_x, over_y)[k])

    def norm_plane(d):
        target = device(y, x, c, (z + d) % PLANES)
        return remote(norm_own.at[3], norm_planes.at[z], norm_send.at[2 + d], norm_recv.at[2 + d], target)

    def before(t):
        w, i = UNITS[t]
        if w == 0 and i == 0:
            turn(cotangent, 0)
        elif w == 1:
            if i == 0:
                turn(entering_two, 1)
            hidden_back(i)
        elif w == 3:
            if i == 0:
                residual_back()
                turn(entering_one, 3)
            attend_back(i)
            project_back(i)
        elif w == 2 and i == 0:
            turn(branch_grad, 2)

    count = len(UNITS)
    input_at = 1 + UNITS.index((3, OWN))

    def reduce_step(step):
        if 0 <= step + 1 < count:
            before(step + 1)
            produce(step + 1)
        if 0 <= step < count:
            join(step)
        if 0 <= step - LAG_ONE < count:
            after_one(step - LAG_ONE)
        if 0 <= step - LAG_TWO < count:
            after_two(step - LAG_TWO)
        if 0 <= step - LAG_Z < count and UNITS[step - LAG_Z][1] < OWN:
            z_send_mid(step - LAG_Z)
        if step == input_at:
            input_back()
            norm_step(0).start()
        if step == count:
            points_back()
        at = step - input_at - 1
        if 0 <= at < 3:
            norm_step(at).wait()
            norm_own[at + 1] = norm_own[at] + norm_in[at]
            if at < 2:
                norm_step(at + 1).start()
            else:
                norm_planes[z] = norm_own[3]
                for d in (1, 2, 3):
                    norm_plane(d).start()
        for w in range(4):
            if w in EARLY_Z and step == OWN_AT[w]:
                own_hop(w)
            if step == FINISH_AT[w]:
                finish(w)

    latents_copy = pltpu.make_async_copy(latents, latents_out, out_sem.at[0])
    start_load(0)
    output_load(None).start()
    greet(y, x, c, z)
    send_own(GATHER_ORDER[0])
    starts = {6: (1,), 7: (2,), 8: (3, 4), 9: (5,), 10: (6,), 11: (7, 8), 12: (9,), 13: (10,), 14: (11, 12), 15: (13,)}
    uses = {7: (1,), 8: (2,), 9: (3, 4), 10: (5,), 11: (6,), 12: (7, 8), 13: (9,), 14: (10,), 15: (11,)}
    for step in range(JOIN_FROM + count + TAIL):
        if step < len(CHUNKS):
            if step % 3 == 0 and step // 3 + 1 < 4:
                send_own(GATHER_ORDER[step // 3 + 1])
            take(*CHUNKS[step])
        if 0 <= step - 1 < len(CHUNKS):
            w, k = CHUNKS[step - 1]
            if w not in SHORT:
                for half in HALVES:
                    ga_copy(w, k, half).wait_recv()
                    gb_copy(w, k, half).start()
        if 0 <= step - 2 < len(CHUNKS):
            w, k = CHUNKS[step - 2]
            for half in HALVES:
                gb_copy(w, k, half).wait_recv()
                gc_copy(w, k, half).start()
        if 0 <= step - 3 < len(CHUNKS):
            w, k = CHUNKS[step - 3]
            for half in HALVES:
                gc_copy(w, k, half).wait_recv()
            if w == 1:
                output_load(k).start()
        for n in starts.get(step, ()):
            start_load(n)
        if step == 1:
            enter()
            project_attend(0)
        for n in uses.get(step, ()):
            w, k = LOADS[n]
            if w == 0:
                project_attend(n)
                if k == 2:
                    for at in (None, 0, 1, 2):
                        branch(at)
                    enter_two()
            elif w == 2:
                widen(n)
            else:
                narrow(n)
        if step == 15:
            latents_copy.start()
            start_load(14)
        reduce_step(step - JOIN_FROM)
    for d in (1, 2, 3):
        norm_plane(d).wait()
    norm_out[...] = (norm_planes[0] + norm_planes[1]) + (norm_planes[2] + norm_planes[3])
    for w, k in CHUNKS:
        for half in HALVES:
            if w not in SHORT:
                ga_copy(w, k, half).wait_send()
            gb_copy(w, k, half).wait_send()
            gc_copy(w, k, half).wait_send()
    for w in range(4):
        for half in HALVES:
            gz_beside(w, half).wait_send()

    @pl.when(is_mid)
    def _():
        for w in range(4):
            for half in HALVES:
                gz_across(w, half).wait_send()
                for k in range(3):
                    gz_pass(w, k, half).wait_send()

    for t in range(count - RING, count):
        pair_copy(t).wait_send()
    for t in range(count):
        if UNITS[t][1] < OWN:
            for half in HALVES:
                z_copy(t, half, 0, beside).wait_send()
    points_copy.wait()
    latents_copy.wait()


def run_step(shards, points, cotangent, members, layer_norms):
    f32, bf16 = jnp.float32, jnp.bfloat16
    blocks = [(WIDTHS[0], BLOCK), (BLOCK, WIDTHS[1]), (WIDTHS[2], BLOCK), (3, BLOCK, 256)]
    out_shape = [jax.ShapeDtypeStruct(blocks[w], bf16 if w in EARLY_Z else f32) for w in range(4)]
    out_shape += [jax.ShapeDtypeStruct(s, bf16) for s in blocks]
    out_shape += [jax.ShapeDtypeStruct(s, f32) for s in ((4, D), (ROWS, D), (ROWS, D))]
    out_shape += [jax.ShapeDtypeStruct((PLANES,) + s, bf16) for s in SHARDS]
    rows_f32, rows_bf16 = pltpu.VMEM((ROWS, D), f32), pltpu.VMEM((ROWS, D), bf16)
    parts = pltpu.VMEM((PLANES, 3, ROWS, 256), bf16)
    hidden = pltpu.VMEM((PLANES, ROWS, D), bf16)
    scratch = [rows_f32, rows_bf16, parts, pltpu.VMEM((PLANES, ROWS, 256), bf16), rows_f32, rows_bf16, hidden]
    scratch += [pltpu.VMEM((PLANES, ROWS, D), f32), rows_f32]
    scratch += [pltpu.VMEM((2, 2, D // 2, ROWS), bf16), hidden, rows_bf16, parts, rows_f32]
    scratch += [pltpu.VMEM((SLOTS, D, D), bf16), pltpu.VMEM((PLANES, 256, D), bf16)]
    scratch += [pltpu.VMEM((RING, 2, 2, BLOCK, D), bf16)]
    scratch += [pltpu.VMEM((4, 2, 2, BLOCK, n), bf16) for n in WIDTHS]
    scratch += [pltpu.VMEM((4, 2, 2, HALF, n), bf16) for n in WIDTHS]
    scratch += [pltpu.VMEM((1 if w in EARLY_Z else 4, 2, HALF, WIDTHS[w]), bf16) for w in range(4)]
    scratch += [pltpu.VMEM((5, 2) + ((2,) if w in EARLY_Z else ()) + (HALF, WIDTHS[w]), bf16) for w in range(4)]
    scratch += [pltpu.VMEM((n, 4, D), f32) for n in (4, 3, 4)]
    dma = pltpu.SemaphoreType.DMA
    scratch += [dma((len(LOADS), 3)), dma((4,)), dma((2,)), dma((4, 5, 2))]
    scratch += [dma((4, 3, 2))] * 7
    scratch += [dma((16,))] * 2 + [dma((16, 2))] * 5 + [dma((4, 5, 2))] + [dma((6,))] * 2
    anywhere, vmem = pl.BlockSpec(memory_space=pl.ANY), pl.BlockSpec(memory_space=pltpu.VMEM)
    result = pl.pallas_call(
        step_kernel,
        out_shape=out_shape,
        in_specs=[anywhere] * 4 + [vmem] * 4,
        out_specs=[vmem] * 9 + [anywhere] * 6,
        scratch_shapes=scratch,
        name="step",
        compiler_params=pltpu.CompilerParams(
            collective_id=0, has_side_effects=True, vmem_limit_bytes=60 << 20
        ),
    )(*shards, points, cotangent, members, layer_norms)
    return result[:4], result[4:8], result[8], result[9], result[10]


def on_device_cube(
    points,
    members,
    cotangent,
    project_weight,
    output_weight,
    upward_weight,
    downward_weight,
    layer_norms,
    project_master,
    project_first,
    project_second,
    output_master,
    output_first,
    output_second,
    upward_master,
    upward_first,
    upward_second,
    downward_master,
    downward_first,
    downward_second,
    norm_first,
    norm_second,
):
    bf16 = jnp.bfloat16
    firsts, seconds, norm_summed, latents, point_gradient = run_step(
        (jnp.transpose(project_weight, (1, 0, 2)), output_weight, upward_weight, downward_weight),
        points,
        cotangent,
        members,
        layer_norms,
    )
    data_index = lax.axis_index("dp")
    norm_columns = norm_first.shape[1]
    norm_gradient = lax.dynamic_slice_in_dim(norm_summed, data_index * norm_columns, norm_columns, 1)
    norm_current = lax.dynamic_slice_in_dim(layer_norms, data_index * norm_columns, norm_columns, 1)
    results = [latents, point_gradient]
    swap = lambda array: jnp.transpose(array, (1, 0, 2))
    for w, states, rate in (
        (3, [swap(a) for a in (project_master, project_first, project_second)], D ** (-0.5)),
        (2, [output_master, output_first, output_second], max(1, D * 4 // LAT) ** (-0.5)),
        (1, [upward_master, upward_first, upward_second], D ** (-0.5)),
        (0, [downward_master, downward_first, downward_second], FF ** (-0.5)),
    ):
        master, first, second = states
        summed = firsts[w].astype(jnp.float32) + seconds[w].astype(jnp.float32)
        updated, one_new, two_new = adamw_step(master, summed, first, second, rate)
        new = [summed, updated, one_new, two_new, updated.astype(bf16)]
        results += [swap(a) for a in new] if w == 3 else new
    norm_new = adamw_step(norm_current, norm_gradient, norm_first, norm_second, 0.2)
    results += [norm_gradient, *norm_new]
    return tuple(results)


def solution(mesh):
    return jax.shard_map(
        on_device_cube if dict(mesh.shape) == {"dp": 8, "mp": 4} else on_device_any,
        mesh=mesh,
        in_specs=(
            P(("dp", "mp"), None),
            P(("dp", "mp"), None),
            P(("dp", "mp"), None),
            P(None, None, "mp"),
            P("mp", None),
            P(None, "mp"),
            P("mp", None),
            P(),
            P("dp", None, "mp"),
            P("dp", None, "mp"),
            P("dp", None, "mp"),
            P("mp", "dp"),
            P("mp", "dp"),
            P("mp", "dp"),
            P("dp", "mp"),
            P("dp", "mp"),
            P("dp", "mp"),
            P("mp", "dp"),
            P("mp", "dp"),
            P("mp", "dp"),
            P(None, "dp"),
            P(None, "dp"),
        ),
        out_specs=(
            P(("dp", "mp"), None),
            P(("dp", "mp"), None),
            P("dp", None, "mp"),
            P("dp", None, "mp"),
            P("dp", None, "mp"),
            P("dp", None, "mp"),
            P("dp", None, "mp"),
            P("mp", "dp"),
            P("mp", "dp"),
            P("mp", "dp"),
            P("mp", "dp"),
            P("mp", "dp"),
            P("dp", "mp"),
            P("dp", "mp"),
            P("dp", "mp"),
            P("dp", "mp"),
            P("dp", "mp"),
            P("mp", "dp"),
            P("mp", "dp"),
            P("mp", "dp"),
            P("mp", "dp"),
            P("mp", "dp"),
            P(None, "dp"),
            P(None, "dp"),
            P(None, "dp"),
            P(None, "dp"),
        ),
        check_vma=False,
    )
```

```python
import jax
import jax.numpy as jnp
from jax import lax
from jax.experimental import pallas as pl
from jax.experimental.pallas import tpu as pltpu
from jax.sharding import PartitionSpec as P

D = 1024
HEAD_DIM = 128
FF = 4096
LAT = 256
ADAM_STEP = 10


norm_epsilon = 1e-05
beta_one = 0.9
beta_two = 0.95
adam_epsilon = 1e-08
weight_decay = 0.1
masked_score = -1e30


def layer_norm(values, norm_gain, norm_shift):
    center = values - jnp.mean(values, axis=-1, keepdims=True)
    spread = jnp.mean(center * center, axis=-1, keepdims=True)
    return center * lax.rsqrt(spread + norm_epsilon) * norm_gain + norm_shift


def pick_rows(source_rows, row_index):
    return source_rows[row_index]


def adamw_step(weight, gradient, moment_one, moment_two, step_rate):
    one_new = beta_one * moment_one + (1.0 - beta_one) * gradient
    two_new = beta_two * moment_two + (1.0 - beta_two) * gradient * gradient
    corrected_one = one_new / (1.0 - beta_one**ADAM_STEP)
    corrected_two = two_new / (1.0 - beta_two**ADAM_STEP)
    updated = weight - step_rate * (
        corrected_one / (jnp.sqrt(corrected_two) + adam_epsilon) + weight_decay * weight
    )
    return (updated, one_new, two_new)


def masked_scores(queries, keys_all, key_mask, score_scale):
    raw_scores = (
        jnp.einsum("gqhe,gkhe->ghqk", queries, keys_all, preferred_element_type=jnp.float32)
        * score_scale
    )
    return jnp.where(key_mask, raw_scores, masked_score)


def on_device_any(
    points,
    members,
    cotangent,
    project_weight,
    output_weight,
    upward_weight,
    downward_weight,
    layer_norms,
    project_master,
    project_first,
    project_second,
    output_master,
    output_first,
    output_second,
    upward_master,
    upward_first,
    upward_second,
    downward_master,
    downward_first,
    downward_second,
    norm_first,
    norm_second,
):
    groups_here = members.shape[0]
    shard_rows = points.shape[0]
    model_width = points.shape[1]
    heads_here = project_weight.shape[2] // HEAD_DIM
    score_scale = HEAD_DIM ** (-0.5)
    grouped = points.reshape(groups_here, LAT, model_width)
    slot_index = jnp.maximum(members, 0)
    key_live = members >= 0
    picked = jax.vmap(pick_rows)(grouped, slot_index)
    inputs = jnp.where(key_live[:, :, None], picked.astype(jnp.float32), 0.0).reshape(
        shard_rows, model_width
    )
    normed, norm_back_one = jax.vjp(layer_norm, inputs, layer_norms[0], layer_norms[1])
    gathered, live_all = (
        lax.all_gather(normed.astype(jnp.bfloat16), "mp", axis=0, tiled=True),
        lax.all_gather(key_live.astype(jnp.bfloat16), "mp", axis=0, tiled=True),
    )
    total_rows = gathered.shape[0]
    total_groups = live_all.shape[0]
    key_mask = (live_all > 0)[:, None, None, :]
    projected = jnp.einsum(
        "rd,dcf->rcf", gathered, project_weight, preferred_element_type=jnp.float32
    ).astype(jnp.bfloat16)
    heads_view = projected.reshape(total_groups, LAT, 3, heads_here, HEAD_DIM)
    queries = heads_view[:, :, 0]
    keys_all = heads_view[:, :, 1]
    values_all = heads_view[:, :, 2]
    scores = masked_scores(queries, keys_all, key_mask, score_scale)
    row_top = jnp.max(scores, axis=-1, keepdims=True)
    exponent = jnp.exp(scores - row_top)
    row_total = jnp.sum(exponent, axis=-1, keepdims=True)
    attention_weights = exponent / row_total
    log_total = row_top + jnp.log(row_total)
    weights_low = attention_weights.astype(jnp.bfloat16)
    attended = jnp.einsum(
        "ghqk,gkhe->gqhe", weights_low, values_all, preferred_element_type=jnp.float32
    ).astype(jnp.bfloat16)
    attended = attended.reshape(total_rows, heads_here * HEAD_DIM)
    branch = lax.psum_scatter(
        jnp.dot(attended, output_weight, preferred_element_type=jnp.float32),
        "mp",
        scatter_dimension=0,
        tiled=True,
    )
    residual = inputs + branch
    normed_two, norm_back_two = jax.vjp(layer_norm, residual, layer_norms[2], layer_norms[3])
    gathered_two = lax.all_gather(normed_two.astype(jnp.bfloat16), "mp", axis=0, tiled=True)
    upward = jnp.dot(gathered_two, upward_weight, preferred_element_type=jnp.float32)
    activated_float, gelu_back = jax.vjp(jax.nn.gelu, upward)
    activated = activated_float.astype(jnp.bfloat16)
    latents = residual + lax.psum_scatter(
        jnp.dot(activated, downward_weight, preferred_element_type=jnp.float32).astype(
            jnp.bfloat16
        ),
        "mp",
        scatter_dimension=0,
        tiled=True,
    ).astype(jnp.float32)
    cotangent_all = lax.all_gather(cotangent, "mp", axis=0, tiled=True)
    downward_local = jnp.einsum(
        "rf,rd->fd", activated, cotangent_all, preferred_element_type=jnp.float32
    )
    activated_grad = jnp.einsum(
        "rd,fd->rf", cotangent_all, downward_weight, preferred_element_type=jnp.float32
    )
    upward_grad = gelu_back(activated_grad)[0].astype(jnp.bfloat16)
    upward_local = jnp.einsum(
        "rd,rf->df", gathered_two, upward_grad, preferred_element_type=jnp.float32
    )
    normed_two_grad = lax.psum_scatter(
        jnp.einsum("rf,df->rd", upward_grad, upward_weight, preferred_element_type=jnp.float32),
        "mp",
        scatter_dimension=0,
        tiled=True,
    )
    residual_part, gain_two_grad, shift_two_grad = norm_back_two(normed_two_grad)
    residual_grad = residual_part + cotangent.astype(jnp.float32)
    norm_two_local = jnp.stack([gain_two_grad, shift_two_grad])
    branch_grad = lax.all_gather(residual_grad.astype(jnp.bfloat16), "mp", axis=0, tiled=True)
    output_local = jnp.einsum(
        "rh,rd->hd", attended, branch_grad, preferred_element_type=jnp.float32
    )
    attended_grad = jnp.einsum(
        "rd,hd->rh", branch_grad, output_weight, preferred_element_type=jnp.float32
    ).astype(jnp.bfloat16)
    attended_grad = attended_grad.reshape(total_groups, LAT, heads_here, HEAD_DIM)
    scores_again = masked_scores(queries, keys_all, key_mask, score_scale)
    weights_again = jnp.exp(scores_again - log_total)
    weights_again_low = weights_again.astype(jnp.bfloat16)
    value_grad = jnp.einsum(
        "ghqk,gqhe->gkhe", weights_again_low, attended_grad, preferred_element_type=jnp.float32
    ).astype(jnp.bfloat16)
    weight_grad = jnp.einsum(
        "gqhe,gkhe->ghqk", attended_grad, values_all, preferred_element_type=jnp.float32
    )
    score_grad = (
        weights_again * (weight_grad - jnp.sum(weights_again * weight_grad, axis=-1, keepdims=True))
    ).astype(jnp.bfloat16)
    query_grad = (
        jnp.einsum("ghqk,gkhe->gqhe", score_grad, keys_all, preferred_element_type=jnp.float32)
        * score_scale
    ).astype(jnp.bfloat16)
    key_grad = (
        jnp.einsum("ghqk,gqhe->gkhe", score_grad, queries, preferred_element_type=jnp.float32)
        * score_scale
    ).astype(jnp.bfloat16)
    projected_grad = jnp.stack([query_grad, key_grad, value_grad], axis=2).reshape(
        total_rows, 3, heads_here * HEAD_DIM
    )
    project_local = jnp.einsum(
        "rd,rcf->dcf", gathered, projected_grad, preferred_element_type=jnp.float32
    )
    normed_grad = lax.psum_scatter(
        jnp.einsum(
            "rcf,dcf->rd", projected_grad, project_weight, preferred_element_type=jnp.float32
        ).astype(jnp.bfloat16),
        "mp",
        scatter_dimension=0,
        tiled=True,
    ).astype(jnp.float32)
    input_part, gain_one_grad, shift_one_grad = norm_back_one(normed_grad)
    input_grad = input_part + residual_grad
    norm_one_local = jnp.stack([gain_one_grad, shift_one_grad])
    matches = members[:, :, None] == jnp.arange(LAT, dtype=jnp.int32)[None, None, :]
    slot_of = jnp.argmax(matches, axis=1)
    point_used = jnp.any(matches, axis=1)
    grouped_grad = input_grad.reshape(groups_here, LAT, model_width)
    point_gradient = jnp.where(
        point_used[:, :, None], jax.vmap(pick_rows)(grouped_grad, slot_of), 0.0
    ).reshape(shard_rows, model_width)
    (
        project_summed,
        output_summed,
        upward_summed,
        downward_summed,
        norm_one_summed,
        norm_two_summed,
    ) = (
        lax.psum_scatter(project_local, "dp", scatter_dimension=0, tiled=True),
        lax.psum_scatter(output_local, "dp", scatter_dimension=1, tiled=True),
        lax.psum_scatter(upward_local, "dp", scatter_dimension=0, tiled=True),
        lax.psum_scatter(downward_local, "dp", scatter_dimension=1, tiled=True),
        lax.psum_scatter(norm_one_local, "dp", scatter_dimension=1, tiled=True),
        lax.psum_scatter(norm_two_local, "dp", scatter_dimension=1, tiled=True),
    )
    norm_gradient = lax.psum(jnp.concatenate([norm_one_summed, norm_two_summed], axis=0), "mp")
    data_index = lax.axis_index("dp")
    norm_columns = norm_first.shape[1]
    norm_current = lax.dynamic_slice_in_dim(layer_norms, data_index * norm_columns, norm_columns, 1)
    project_new = adamw_step(
        project_master, project_summed, project_first, project_second, D ** (-0.5)
    )
    output_new = adamw_step(
        output_master, output_summed, output_first, output_second, max(1, D * 4 // LAT) ** (-0.5)
    )
    upward_new = adamw_step(upward_master, upward_summed, upward_first, upward_second, D ** (-0.5))
    downward_new = adamw_step(
        downward_master, downward_summed, downward_first, downward_second, FF ** (-0.5)
    )
    norm_new = adamw_step(norm_current, norm_gradient, norm_first, norm_second, 0.2)
    return (
        latents,
        point_gradient,
        project_summed,
        project_new[0],
        project_new[1],
        project_new[2],
        project_new[0].astype(jnp.bfloat16),
        output_summed,
        output_new[0],
        output_new[1],
        output_new[2],
        output_new[0].astype(jnp.bfloat16),
        upward_summed,
        upward_new[0],
        upward_new[1],
        upward_new[2],
        upward_new[0].astype(jnp.bfloat16),
        downward_summed,
        downward_new[0],
        downward_new[1],
        downward_new[2],
        downward_new[0].astype(jnp.bfloat16),
        norm_gradient,
        norm_new[0],
        norm_new[1],
        norm_new[2],
    )


MESH = pl.DeviceIdType.MESH
PLANES = 4
OWNERS = 8
ROWS = LAT
HALVES = (0, 1)
SHARDS = ((3, D, 256), (256, D), (D, D), (D, D))
SHORT = ()
CHUNKS = [(w, k) for w in (0, 1) for k in range(3)] + [(2, 0), (3, 0)]
SLOTS = 4
LOADS = (
    (0, None), (0, 0), (0, 1), (0, 2), (2, None), (2, 0), (3, None), (3, 0), (0, 2), (0, 1), (0, 0), (0, None),
)

WIDTHS = (D, D, 256, 3 * 256)
BLOCK = D // OWNERS
HALF = BLOCK // 2
RING = 2
OWN = PLANES - 1
UNITS = (
    (0, 0), (0, 3), (1, 0), (1, 3), (3, 0), (3, 1), (3, 2), (3, 3), (2, 0), (2, 1), (2, 2), (2, 3),
)
TURNED_AT = (0, 1, 1, 0)
(
    SEND_OWN, TAKE, CORNER, CROSS, WHOLE, LOAD, READY, ENTER, PROJECT, BRANCH, SEND_COTANGENT, CAME, WIDEN,
    NARROW_BACK, WIDEN_BACK, NARROW, LATENTS, RESIDUAL, ATTEND, INWARD, TURN, PRODUCE, JOIN, ONE, TWO, ALONG,
    FINISH, INPUTS, NORM, NORMS_OUT, POINTS,
) = range(31)
SCHEDULE = (
    (SEND_OWN, 1), (SEND_OWN, 0), (TAKE, 1, 0, 0), (CORNER, 1, 0, 0), (TAKE, 0, 0, 0), (TAKE, 1, 0, 1),
    (TAKE, 0, 1, 0), (TAKE, 0, 0, 1), (TAKE, 0, 1, 1), (CORNER, 1, 0, 1), (CROSS, 1, 0, 0), (TAKE, 1, 1, 1),
    (CORNER, 0, 0, 1), (TAKE, 1, 1, 0), (TAKE, 1, 2, 1), (TAKE, 1, 2, 0), (LOAD, 0), (CORNER, 0, 1, 0),
    (TAKE, 0, 2, 0), (TAKE, 0, 2, 1), (SEND_OWN, 2), (CORNER, 0, 1, 1), (SEND_OWN, 3), (ENTER,), (CORNER, 0, 0, 0),
    (SEND_COTANGENT,), (CORNER, 0, 2, 1), (CORNER, 1, 2, 1), (PROJECT, 0), (CORNER, 1, 2, 0), (CROSS, 0, 1, 1),
    (CROSS, 0, 1, 0), (CROSS, 0, 0, 0), (CORNER, 0, 2, 0), (CROSS, 0, 0, 1), (CORNER, 1, 1, 1), (LOAD, 4),
    (CROSS, 1, 0, 1), (WHOLE, 0, 0), (LOAD, 1), (CROSS, 0, 2, 1), (CORNER, 1, 1, 0), (TAKE, 2, 0, 0), (WHOLE, 0, 1),
    (LOAD, 2), (TAKE, 2, 0, 1), (PROJECT, 1), (CROSS, 0, 2, 0), (CROSS, 1, 2, 1), (TAKE, 3, 0, 0), (CROSS, 1, 2, 0),
    (CROSS, 1, 1, 0), (WHOLE, 0, 2), (LOAD, 3), (PROJECT, 2), (WHOLE, 1, 2), (READY, 4), (CROSS, 1, 1, 1),
    (TAKE, 3, 0, 1), (CORNER, 2, 0, 1), (WHOLE, 1, 1), (WHOLE, 1, 0), (CORNER, 2, 0, 0), (PROJECT, 3), (BRANCH,),
    (CAME, 0), (LOAD, 6), (TURN, 0), (CORNER, 3, 0, 0), (READY, 6), (CROSS, 2, 0, 1), (CORNER, 3, 0, 1),
    (WIDEN, 0, 0), (CROSS, 2, 0, 0), (WHOLE, 2, 0), (NARROW_BACK, 0, 0), (LOAD, 5), (READY, 5), (CROSS, 3, 0, 1),
    (CROSS, 3, 0, 0), (WIDEN, 1, 0), (WHOLE, 3, 0), (LOAD, 7), (CAME, 1), (WIDEN, 1, 1), (PRODUCE, 0), (WIDEN, 0, 1),
    (PRODUCE, 1), (JOIN, 0), (READY, 7), (NARROW_BACK, 0, 1), (NARROW_BACK, 1, 1), (JOIN, 1), (NARROW_BACK, 1, 0),
    (WIDEN_BACK, 1), (TURN, 1), (ONE, 0, 1), (PRODUCE, 2), (ONE, 0, 0), (PRODUCE, 3), (JOIN, 2), (TURN, 3),
    (WIDEN_BACK, 0), (JOIN, 3), (NARROW, 1), (RESIDUAL,), (ATTEND, 4), (PRODUCE, 4), (ONE, 2, 1), (ONE, 2, 0),
    (ATTEND, 5), (JOIN, 4), (LOAD, 8), (PRODUCE, 5), (ATTEND, 6), (TWO, 2, 1), (JOIN, 5), (ONE, 1, 1), (ONE, 4, 0),
    (LOAD, 9), (ONE, 4, 1), (PRODUCE, 6), (TURN, 2), (ATTEND, 7), (JOIN, 6), (TWO, 2, 0), (PRODUCE, 7), (TWO, 4, 0),
    (TWO, 0, 0), (PRODUCE, 8), (PRODUCE, 9), (ONE, 3, 0), (JOIN, 9), (ONE, 5, 1), (JOIN, 8), (ONE, 5, 0), (NARROW, 0),
    (TWO, 4, 1), (ONE, 9, 1), (ONE, 9, 0), (PRODUCE, 10), (TWO, 0, 1), (ALONG, 4, 0), (ONE, 3, 1), (LOAD, 10),
    (ONE, 6, 0), (PRODUCE, 11), (ALONG, 4, 1), (INWARD, 8), (TWO, 5, 1), (JOIN, 7), (LOAD, 11), (TWO, 1, 1),
    (JOIN, 10), (TWO, 9, 1), (TWO, 5, 0), (ONE, 8, 1), (TWO, 9, 0), (ONE, 6, 1), (INWARD, 9), (INWARD, 10),
    (INWARD, 11), (JOIN, 11), (INPUTS,), (TWO, 6, 0), (ALONG, 5, 1), (ALONG, 9, 1), (ONE, 8, 0), (NORM, 0),
    (ALONG, 6, 0), (ONE, 10, 0), (ONE, 1, 0), (ONE, 10, 1), (TWO, 8, 1), (TWO, 8, 0), (NORM, 1), (ONE, 7, 0),
    (ONE, 11, 1), (ALONG, 8, 1), (TWO, 10, 0), (LATENTS,), (TWO, 6, 1), (ALONG, 6, 1), (ALONG, 8, 0), (ONE, 7, 1),
    (TWO, 10, 1), (ALONG, 5, 0), (ALONG, 10, 1), (TWO, 1, 0), (NORM, 2), (ONE, 11, 0), (TWO, 11, 1), (TWO, 3, 1),
    (TWO, 3, 0), (FINISH, 1), (ALONG, 9, 0), (ALONG, 10, 0), (FINISH, 0), (POINTS,), (TWO, 7, 1), (TWO, 7, 0),
    (TWO, 11, 0), (FINISH, 3), (NORMS_OUT,), (FINISH, 2),
)
NN = ((1,), (0,))
NT = ((1,), (1,))
TN = ((0,), (0,))


def place():
    dp = lax.axis_index("dp")
    return dp // 4, (dp // 2) % 2, dp % 2, lax.axis_index("mp")


def device(y, x, c, z):
    return (y * 4 + x * 2 + c, z)


def greet(y, x, c, z):
    barrier = pltpu.get_barrier_semaphore()
    partners = [device(1 - y, x, c, z), device(y, 1 - x, c, z), device(y, x, 1 - c, z)]
    partners += [device(y, x, c, (z + d) % PLANES) for d in (1, 2, 3)]
    for partner in partners:
        pl.semaphore_signal(barrier, inc=1, device_id=partner, device_id_type=MESH)
    pl.semaphore_wait(barrier, len(partners))


def arrival(z, k):
    return (z + 1 - 2 * (z % 2), 2 - z // 2, 3 - 3 * (z // 2))[k]


def dot(a, b, contract):
    return lax.dot_general(a, b, (contract, ((), ())), preferred_element_type=jnp.float32)


def tiles(count, size, body):
    def step(n, carry):
        body(pl.ds(pl.multiple_of(n * size, size), size))
        return carry

    lax.fori_loop(0, count, step, 0)


def norm_rows(source, target, gain, shift, strip=64):
    def step(n, carry):
        rows = pl.ds(pl.multiple_of(n * strip, strip), strip)
        target[rows, :] = layer_norm(source[rows, :], gain, shift).astype(target.dtype)
        return carry

    lax.fori_loop(0, ROWS // strip, step, 0)


def step_kernel(*refs):
    f32, bf16 = jnp.float32, jnp.bfloat16
    shards, cotangent_in, (points, members, norms) = refs[0:4], refs[4], refs[5:8]
    outs, norm_out, latents_out, points_out, fulls = refs[8:16], refs[16], refs[17], refs[18], refs[19:23]
    inputs, entering_one, projected, attended, residual, latents = refs[23:29]
    entering_two, cotangent, activated, slope, upward_grad = refs[29:34]
    turned, branch_grad, projected_grad, normed_grad, sent, came = refs[34:40]
    slots, output_full, ring = refs[40:43]
    acc, one_in, two_in, z_in = refs[43:47], refs[47:51], refs[51:55], refs[55:59]
    norm_own, norm_in, norm_planes = refs[59:62]
    load_sem, output_sem, out_sem, swap_send, swap_recv = refs[62:67]
    gz_send, gz_recv, ga_send, ga_recv, gb_send, gb_recv, gc_send, gc_recv = refs[67:75]
    c_send, c_recv, one_send, one_recv, two_send, two_recv, z_send, z_recv = refs[75:83]
    norm_send, norm_recv = refs[83:85]
    residual_grad = residual
    y, x, c, z = place()
    is_mid = jnp.logical_or(z == 1, z == 2)
    is_end = jnp.logical_not(is_mid)
    sibling = device(y, x, 1 - c, z)
    over_x, over_y = device(y, 1 - x, c, z), device(1 - y, x, c, z)
    beside, across = device(y, x, c, arrival(z, 0)), device(y, x, c, 3 - z)
    opposite = device(y, x, c, (z + 2) % PLANES)

    def plane_at(k):
        return z if k is None else arrival(z, k)

    def plane_of(i):
        return z if i == OWN else arrival(z, 2 - i)

    def remote(src, dst, send, recv, target):
        return pltpu.make_async_remote_copy(
            src_ref=src, dst_ref=dst, send_sem=send, recv_sem=recv, device_id=target, device_id_type=MESH
        )

    def rows_of(ref, w, rows):
        return ref.at[:, rows, :] if w == 0 else ref.at[rows, :]

    def view(w, plane, rows):
        return fulls[w].at[rows, :] if w >= 2 else rows_of(fulls[w].at[plane], w, rows)

    def block(w, half, first, count):
        height = SHARDS[w][-2]
        start = pl.multiple_of(half * (height // 2) + first * (height // 16), height // 16)
        return pl.ds(start, count * (height // 16))

    spot = (c * 4 + y * 2 + x, c * 4 + x * 2 + y)
    pair = (c * 4 + y * 2, c * 4 + x * 2)

    def gz_rows(w, half):
        return block(w, half, pair[half], 2) if w in SHORT else block(w, half, spot[half], 1)

    def gz_own(w, half, lane, slot, target):
        rows = gz_rows(w, half)
        send, recv = gz_send.at[w, lane, half], gz_recv.at[w, slot, half]
        return remote(rows_of(shards[w], w, rows), view(w, z, rows), send, recv, target)

    def gz_first(w, half):
        return gz_own(w, half, 0, 0, opposite if w >= 2 else beside)

    def gz_across(w, half):
        return gz_own(w, half, 1, 1, across)

    def gz_foreign(w, k, half, lane, slot, target):
        here = view(w, arrival(z, k), gz_rows(w, half))
        return remote(here, here, gz_send.at[w, lane, half], gz_recv.at[w, slot, half], target)

    def gz_pass(w, k, half):
        lane, target, slot = ((2, across, 2), (3, beside, 1), (4, beside, 2))[k]
        return gz_foreign(w, k, half, lane, slot, target)

    def gz_arrived(w, k, half):
        return gz_foreign(w, k, half, 0, k, beside)

    def ga_copy(w, k, half):
        here = view(w, arrival(z, k), block(w, half, spot[half], 1))
        return remote(here, here, ga_send.at[w, k, half], ga_recv.at[w, k, half], (over_x, over_y)[half])

    def gb_copy(w, k, half):
        here = view(w, arrival(z, k), block(w, half, pair[half], 2))
        return remote(here, here, gb_send.at[w, k, half], gb_recv.at[w, k, half], (over_y, over_x)[half])

    def gc_copy(w, k, half):
        here = view(w, arrival(z, k), block(w, half, c * 4, 4))
        return remote(here, here, gc_send.at[w, k, half], gc_recv.at[w, k, half], sibling)

    def send_own(w):
        for half in HALVES:
            gz_first(w, half).start()
        if w < 2:

            @pl.when(is_mid)
            def _():
                for half in HALVES:
                    gz_across(w, half).start()

    def take(w, k, half):
        gz_arrived(w, k, half).wait_recv()
        (gb_copy if w in SHORT else ga_copy)(w, k, half).start()
        if w < 2:

            @pl.when(is_mid)
            def _():
                gz_pass(w, k, half).start()

    def corner(w, k, half):
        ga_copy(w, k, half).wait_recv()
        gb_copy(w, k, half).start()

    def cross(w, k, half):
        gb_copy(w, k, half).wait_recv()
        gc_copy(w, k, half).start()

    def whole(w, k):
        for half in HALVES:
            gc_copy(w, k, half).wait_recv()
        if w == 1:
            output_load(k).start()

    def loads(n):
        w, k = LOADS[n]
        if w >= 2:
            source = shards[w] if k is None else fulls[w]
            return [pltpu.make_async_copy(source, slots.at[n % SLOTS], load_sem.at[n, 0])]
        source = shards[w] if k is None else fulls[w].at[arrival(z, k)]
        return [
            pltpu.make_async_copy(
                source.at[part], slots.at[n % SLOTS, :, part * 256 : (part + 1) * 256], load_sem.at[n, part]
            )
            for part in range(3)
        ]

    def start_load(n):
        for copy in loads(n):
            copy.start()

    def wait_load(n):
        for copy in loads(n):
            copy.wait()

    def output_load(k):
        source = shards[1] if k is None else fulls[1].at[arrival(z, k)]
        return pltpu.make_async_copy(source, output_full.at[plane_at(k)], output_sem.at[3 if k is None else k])

    mine, theirs = pl.ds(0, ROWS), pl.ds(ROWS, ROWS)

    def swap(n):
        src, dst = (
            (cotangent.at[mine], cotangent.at[theirs]),
            (entering_two.at[mine], entering_two.at[theirs]),
            (sent.at[0], came.at[0]),
            (sent.at[1], came.at[1]),
        )[n]
        return remote(src, dst, swap_send.at[n], swap_recv.at[n], beside)

    cotangent_load = pltpu.make_async_copy(cotangent_in, cotangent.at[mine], out_sem.at[2])

    def send_cotangent():
        cotangent_load.wait()
        swap(0).start()

    def swap_came(n):
        swap(n).wait_recv()

    def enter():
        slot_of = lax.broadcasted_iota(jnp.int32, (ROWS, ROWS), 0) == members[...]
        chosen = slot_of.astype(f32).astype(bf16)

        def pick(columns):
            inputs[:, columns] = dot(chosen, points[:, columns], TN)

        tiles(4, 256, pick)
        norm_rows(inputs, entering_one, norms[0:1, :], norms[1:2, :])
        residual[...] = inputs[...]

    def softmax_parts(plane, span):
        queries, keys_all = projected[plane, 0, :, span], projected[plane, 1, :, span]
        scores = jnp.where(members[...] >= 0, dot(queries, keys_all, NT) * HEAD_DIM ** (-0.5), masked_score)
        exponent = jnp.exp(scores - jnp.max(scores, axis=-1, keepdims=True))
        return queries, keys_all, exponent * (1.0 / jnp.sum(exponent, axis=-1, keepdims=True))

    def project_attend(n):
        wait_load(n)
        plane, slot = plane_at(LOADS[n][1]), n % SLOTS
        for part in range(3):
            right = slots[slot, :, part * 256 : (part + 1) * 256]
            projected[plane, part] = dot(entering_one[...], right, NN).astype(bf16)
        for head in range(2):
            span = slice(head * HEAD_DIM, (head + 1) * HEAD_DIM)
            probs = softmax_parts(plane, span)[2]
            attended[plane, :, span] = dot(probs.astype(bf16), projected[plane, 2, :, span], NN).astype(bf16)

    def branches():
        for k in (None, 0, 1, 2):
            plane = plane_at(k)
            output_load(k).wait()

            def body(columns):
                residual[:, columns] += dot(attended[plane], output_full[plane, :, columns], NN)

            tiles(4, 256, body)
        norm_rows(residual, entering_two, norms[2:3, :], norms[3:4, :])
        swap(1).start()
        latents[...] = residual[...]

    def rows_at(b):
        return theirs if b else mine

    def widen(j, b):
        rows = rows_at(b)

        def body(columns):
            u = dot(entering_two[rows, :], slots[j, :, columns], NN)
            square = u * u
            bend = jnp.tanh(0.7978845608028654 * u * (1.0 + 0.044715 * square))
            activated[j, rows, columns] = (0.5 * u * (1.0 + bend)).astype(bf16)
            slope[j, rows, columns] = 0.5 * (1.0 + bend) + 0.5 * u * (1.0 - bend * bend) * (
                0.7978845608028654 * (1.0 + 3.0 * 0.044715 * square)
            )

        tiles(4, 256, body)

    def narrow_back(j, b):
        rows = rows_at(b)

        def body(columns):
            product = dot(cotangent[rows, :], slots[2 + j, columns, :], NT)
            upward_grad[j, rows, columns] = (product * slope[j, rows, columns]).astype(bf16)

        tiles(4, 256, body)

    def widen_back(b):
        rows = rows_at(b)

        def body(columns):
            total = dot(upward_grad[0, rows, :], slots[0, columns, :], NT)
            total += dot(upward_grad[1, rows, :], slots[1, columns, :], NT)
            if b:
                sent[1, :, columns] = total.astype(bf16)
            else:
                normed_grad[:, columns] = total

        tiles(4, 256, body)
        if b:
            swap(3).start()

    def narrow(b):
        rows = rows_at(b)

        def body(columns):
            total = dot(activated[0, rows, :], slots[2, :, columns], NN)
            total += dot(activated[1, rows, :], slots[3, :, columns], NN)
            if b:
                sent[0, :, columns] = total.astype(bf16)
            else:
                latents[:, columns] += total

        tiles(4, 256, body)
        if b:
            swap(2).start()

    latents_copy = pltpu.make_async_copy(latents, latents_out, out_sem.at[0])

    def add_came(n, target):
        swap_came(2 + n)

        def strip(r, carry):
            rows = pl.ds(pl.multiple_of(r * 32, 32), 32)
            target[rows, :] += came[n, rows, :].astype(f32)
            return carry

        lax.fori_loop(0, ROWS // 32, strip, 0)

    def latents_done():
        add_came(0, latents)
        latents_copy.start()

    def here(t):
        w, i = UNITS[t]
        return acc[w].at[i if w >= 2 else i // OWN]

    def pair_copy(t):
        w = UNITS[t][0]
        return remote(ring.at[t % RING, :, :, :, 0 : WIDTHS[w]], here(t), c_send.at[t], c_recv.at[t], sibling)

    def half_rows(half):
        return pl.ds(half * HALF, HALF)

    def one_in_at(t, half):
        w, i = UNITS[t]
        return one_in[w].at[i if w >= 2 else i // OWN, half]

    def two_in_at(t, half):
        w, i = UNITS[t]
        return two_in[w].at[i if w >= 2 else i // OWN, half]

    def one_copy(t, half):
        rows = half_rows(half)
        src = here(t).at[1 - y, :, rows] if half == 0 else here(t).at[:, 1 - x, rows]
        send, recv = one_send.at[t, half], one_recv.at[t, half]
        return remote(src, one_in_at(t, half), send, recv, (over_y, over_x)[half])

    def two_copy(t, half):
        rows = half_rows(half)
        src = here(t).at[y, 1 - x, rows] if half == 0 else here(t).at[1 - y, x, rows]
        send, recv = two_send.at[t, half], two_recv.at[t, half]
        return remote(src, two_in_at(t, half), send, recv, (over_x, over_y)[half])

    def z_copy(t, half, slot, target):
        w = UNITS[t][0]
        send, recv = z_send.at[t, half], z_recv.at[w, slot, half]
        return remote(here(t).at[y, x, half_rows(half)], z_in[w].at[slot, half], send, recv, target)

    def z_first(t, half):
        w, i = UNITS[t]
        if w < 2:
            z_copy(t, half, 0, opposite).start()
            return

        @pl.when(is_end)
        def _():
            z_copy(t, half, 2 - i, beside).start()

    def z_pass(t, half):
        w, i = UNITS[t]

        @pl.when(is_mid)
        def _():
            slot = (2, 1, 3)[i]
            z_copy(t, half, slot, beside).wait_recv()
            add_rows(here(t).at[y, x, half_rows(half)], z_in[w].at[slot, half])
            z_copy(t, half, (3, 4, 0)[i], (across, across, beside)[i]).start()

    def add_rows(target, source):
        def body(r, carry):
            rows = pl.ds(pl.multiple_of(r * 16, 16), 16)
            target[rows] = (target[rows].astype(f32) + source[rows].astype(f32)).astype(bf16)
            return carry

        lax.fori_loop(0, HALF // 16, body, 0)

    def partial(w, i, parity, columns, n):
        if w < 2:
            right = (activated, upward_grad)[w][1 - i // OWN, :, columns]
            return dot(turned[w, parity], right, NN)
        plane = plane_of(i)
        right = projected_grad[plane, n] if w == 3 else attended[plane, :, columns]
        return dot(turned[TURNED_AT[w], parity, :, 0:ROWS], right, NN)

    def over_tiles(w, body):
        if w == 2:
            body(pl.ds(0, 256), 0)
            return

        def step(n, carry):
            body(pl.ds(pl.multiple_of(n * 256, 256), 256), n)
            return carry

        lax.fori_loop(0, WIDTHS[w] // 256, step, 0)

    def produce(t):
        w, i = UNITS[t]
        if t >= RING:
            pair_copy(t - RING).wait_send()

        def body(columns, n):
            product = partial(w, i, 1 - c, columns, n).astype(bf16)
            for k in range(4):
                ring[t % RING, k // 2, k % 2, :, columns] = product[k * BLOCK : (k + 1) * BLOCK]

        over_tiles(w, body)
        pair_copy(t).start()

    def join(t):
        w, i = UNITS[t]
        at = i if w >= 2 else i // OWN
        pair_copy(t).wait_recv()

        def body(columns, n):
            product = partial(w, i, c, columns, n)
            for k in range(4):
                other = acc[w][at, k // 2, k % 2, :, columns].astype(f32)
                acc[w][at, k // 2, k % 2, :, columns] = (product[k * BLOCK : (k + 1) * BLOCK] + other).astype(bf16)

        over_tiles(w, body)
        for half in HALVES:
            one_copy(t, half).start()

    def after_one(t, half):
        one_copy(t, half).wait()
        rows = half_rows(half)
        for k in (0, 1):
            target = here(t).at[y, k, rows] if half == 0 else here(t).at[k, x, rows]
            add_rows(target, one_in_at(t, half).at[k])
        two_copy(t, half).start()

    def after_two(t, half):
        two_copy(t, half).wait()
        add_rows(here(t).at[y, x, half_rows(half)], two_in_at(t, half))
        if UNITS[t][1] < OWN:
            z_first(t, half)

    def finish(w):
        t = UNITS.index((w, OWN))
        for half in HALVES:
            z_copy(t, half, 0, beside).wait_recv()
        if w >= 2:

            @pl.when(is_mid)
            def _():
                for half in HALVES:
                    z_copy(t, half, 4, across).wait_recv()

        def body(n, carry):
            columns = pl.ds(pl.multiple_of(n * 128, 128), 128)
            first = here(t).at[y, x][:, columns].astype(f32)
            second = [z_in[w][0, half, :, columns] for half in HALVES]
            if w >= 2:
                third = [z_in[w][4, half, :, columns] for half in HALVES]
                first += jnp.where(is_mid, jnp.concatenate(third, axis=0).astype(f32), 0.0)
            second = jnp.concatenate(second, axis=0).astype(f32)
            for n_out, value in ((w, first), (4 + w, second)):
                if w in (0, 2):
                    outs[n_out][columns, :] = value.T.astype(outs[n_out].dtype)
                elif w == 1:
                    outs[n_out][:, columns] = value.astype(outs[n_out].dtype)
                else:
                    part_columns = pl.ds(pl.multiple_of((n % 2) * 128, 128), 128)
                    outs[n_out][n // 2, :, part_columns] = value.astype(outs[n_out].dtype)
            return carry

        lax.fori_loop(0, WIDTHS[w] // 128, body, 0)

    def turn(w):
        source = (cotangent, entering_two, branch_grad, entering_one)[w]
        for owner in range(OWNERS):
            columns = slice(owner * BLOCK, (owner + 1) * BLOCK)
            place_at = slice((owner // 2) * BLOCK, (owner // 2 + 1) * BLOCK)
            flat = source[:, columns].T
            if w < 2:
                turned[w, owner % 2, place_at, :] = flat
            else:
                turned[TURNED_AT[w], owner % 2, place_at, 0:ROWS] = flat

    def norm_back(source, gain, row, store):
        norm_own[0, row : row + 2, :] = jnp.zeros((2, D), f32)

        def strip(n, carry):
            rows = pl.ds(pl.multiple_of(n * 32, 32), 32)
            values = source[rows, :]
            center = values - jnp.mean(values, axis=-1, keepdims=True)
            scale = lax.rsqrt(jnp.mean(center * center, axis=-1, keepdims=True) + norm_epsilon)
            hat = center * scale
            grad = normed_grad[rows, :]
            norm_own[0, row : row + 1, :] += jnp.sum(grad * hat, axis=0, keepdims=True)
            norm_own[0, row + 1 : row + 2, :] += jnp.sum(grad, axis=0, keepdims=True)
            grad = grad * gain
            inner = jnp.mean(grad * hat, axis=-1, keepdims=True)
            store(rows, scale * (grad - jnp.mean(grad, axis=-1, keepdims=True) - hat * inner))
            return carry

        lax.fori_loop(0, ROWS // 32, strip, 0)

    def residual_back():
        add_came(1, normed_grad)

        def store(rows, part):
            total = part + cotangent[rows, :].astype(f32)
            residual_grad[rows, :] = total
            branch_grad[rows, :] = total.astype(bf16)

        norm_back(residual, norms[2:3, :], 2, store)

    def attend_back(t):
        plane = plane_of(UNITS[t][1])
        attended_grad = dot(branch_grad[...], output_full[plane], NT).astype(bf16)
        scale = HEAD_DIM ** (-0.5)
        for head in range(2):
            span = slice(head * HEAD_DIM, (head + 1) * HEAD_DIM)
            queries, keys_all, probs = softmax_parts(plane, span)
            grad = attended_grad[:, span]
            projected_grad[plane, 2, :, span] = dot(probs.astype(bf16), grad, TN).astype(bf16)
            prob_grad = dot(grad, projected[plane, 2, :, span], NT)
            inner = jnp.sum(probs * prob_grad, axis=-1, keepdims=True)
            score_grad = (probs * (prob_grad - inner)).astype(bf16)
            projected_grad[plane, 0, :, span] = (dot(score_grad, keys_all, NN) * scale).astype(bf16)
            projected_grad[plane, 1, :, span] = (dot(score_grad, queries, TN) * scale).astype(bf16)

    def project_back(n):
        wait_load(n)
        plane, slot = plane_at(LOADS[n][1]), n % SLOTS
        first = n == 8

        def normed(columns):
            total = dot(projected_grad[plane, 0], slots[slot, columns, 0:256], NT)
            for part in (1, 2):
                total += dot(projected_grad[plane, part], slots[slot, columns, part * 256 : (part + 1) * 256], NT)
            if first:
                normed_grad[:, columns] = total
            else:
                normed_grad[:, columns] += total

        tiles(4, 256, normed)

    def norm_step(k):
        return remote(norm_own.at[k], norm_in.at[k], norm_send.at[k], norm_recv.at[k], (sibling, over_x, over_y)[k])

    def norm_plane(d):
        target = device(y, x, c, (z + d) % PLANES)
        return remote(norm_own.at[3], norm_planes.at[z], norm_send.at[2 + d], norm_recv.at[2 + d], target)

    def inputs_back():
        def store(rows, part):
            residual_grad[rows, :] += part

        norm_back(inputs, norms[0:1, :], 0, store)
        norm_step(0).start()

    def norm_hop(k):
        norm_step(k).wait()
        norm_own[k + 1] = norm_own[k] + norm_in[k]
        if k < 2:
            norm_step(k + 1).start()
        else:
            norm_planes[z] = norm_own[3]
            for d in (1, 2, 3):
                norm_plane(d).start()

    def norms_out():
        for d in (1, 2, 3):
            norm_plane(d).wait()
        norm_out[...] = (norm_planes[0] + norm_planes[1]) + (norm_planes[2] + norm_planes[3])

    points_copy = pltpu.make_async_copy(inputs, points_out, out_sem.at[1])

    def points_back():
        slot_of = lax.broadcasted_iota(jnp.int32, (ROWS, ROWS), 0) == members[...]
        chosen = slot_of.astype(f32).astype(bf16)

        def pick(columns):
            rest = residual_grad[:, columns]
            total = jnp.zeros((ROWS, 256), f32)
            for _ in range(3):
                low = rest.astype(bf16)
                total += dot(chosen, low, NN)
                rest = rest - low.astype(f32)
            inputs[:, columns] = total

        tiles(4, 256, pick)
        points_copy.start()

    steps = (
        send_own, take, corner, cross, whole, start_load, wait_load, enter, project_attend, branches, send_cotangent,
        swap_came, widen, narrow_back, widen_back, narrow, latents_done, residual_back, attend_back, project_back,
        turn, produce, join, after_one, after_two, z_pass, finish, inputs_back, norm_hop, norms_out, points_back,
    )
    cotangent_load.start()
    output_load(None).start()
    greet(y, x, c, z)
    for step, *at in SCHEDULE:
        steps[step](*at)
    for w, k in CHUNKS:
        for half in HALVES:
            if w not in SHORT:
                ga_copy(w, k, half).wait_send()
            gb_copy(w, k, half).wait_send()
            gc_copy(w, k, half).wait_send()
    for w in range(4):
        for half in HALVES:
            gz_first(w, half).wait_send()

    @pl.when(is_mid)
    def _():
        for w in (0, 1):
            for half in HALVES:
                gz_across(w, half).wait_send()
                for k in range(3):
                    gz_pass(w, k, half).wait_send()

    for n in range(4):
        swap(n).wait_send()
    for t in range(len(UNITS) - RING, len(UNITS)):
        pair_copy(t).wait_send()
    for t, unit in enumerate(UNITS):
        if unit[1] < OWN:
            for half in HALVES:
                z_copy(t, half, 0, beside).wait_send()
    points_copy.wait()
    latents_copy.wait()


def run_step(shards, points, cotangent, members, layer_norms):
    f32, bf16 = jnp.float32, jnp.bfloat16
    vmem_of = pltpu.VMEM
    blocks = [(WIDTHS[0], BLOCK), (BLOCK, WIDTHS[1]), (WIDTHS[2], BLOCK), (3, BLOCK, 256)]
    out_shape = [jax.ShapeDtypeStruct(blocks[w], bf16 if w < 2 else f32) for w in range(4)]
    out_shape += [jax.ShapeDtypeStruct(s, bf16) for s in blocks]
    out_shape += [jax.ShapeDtypeStruct(s, f32) for s in ((4, D), (ROWS, D), (ROWS, D))]
    out_shape += [jax.ShapeDtypeStruct(((PLANES,) if w < 2 else ()) + SHARDS[w], bf16) for w in range(4)]
    rows_f32, rows_bf16 = vmem_of((ROWS, D), f32), vmem_of((ROWS, D), bf16)
    both_bf16, hidden = vmem_of((2 * ROWS, D), bf16), vmem_of((2, 2 * ROWS, D), bf16)
    parts = vmem_of((PLANES, 3, ROWS, 256), bf16)
    scratch = [rows_f32, rows_bf16, parts, vmem_of((PLANES, ROWS, 256), bf16), rows_f32, rows_f32]
    scratch += [both_bf16, both_bf16, hidden, vmem_of((2, 2 * ROWS, D), f32), hidden]
    scratch += [vmem_of((2, 2, D // 2, 2 * ROWS), bf16), rows_bf16, parts, rows_f32]
    scratch += [vmem_of((2, ROWS, D), bf16)] * 2
    scratch += [vmem_of((SLOTS, D, D), bf16), vmem_of((PLANES, 256, D), bf16), vmem_of((RING, 2, 2, BLOCK, D), bf16)]
    counts = (2, 2, 4, 4)
    scratch += [vmem_of((counts[w], 2, 2, BLOCK, WIDTHS[w]), bf16) for w in range(4)]
    scratch += [vmem_of((counts[w], 2, 2, HALF, WIDTHS[w]), bf16) for w in range(4)]
    scratch += [vmem_of((counts[w], 2, HALF, WIDTHS[w]), bf16) for w in range(4)]
    scratch += [vmem_of((1 if w < 2 else 5, 2, HALF, WIDTHS[w]), bf16) for w in range(4)]
    scratch += [vmem_of((n, 4, D), f32) for n in (4, 3, 4)]
    dma = pltpu.SemaphoreType.DMA
    units = len(UNITS)
    scratch += [dma((len(LOADS), 3)), dma((4,)), dma((3,)), dma((4,)), dma((4,)), dma((4, 5, 2))]
    scratch += [dma((4, 3, 2))] * 7
    scratch += [dma((units,))] * 2 + [dma((units, 2))] * 5 + [dma((4, 5, 2))] + [dma((6,))] * 2
    anywhere, vmem = pl.BlockSpec(memory_space=pl.ANY), pl.BlockSpec(memory_space=pltpu.VMEM)
    result = pl.pallas_call(
        step_kernel,
        out_shape=out_shape,
        in_specs=[anywhere] * 5 + [vmem] * 3,
        out_specs=[vmem] * 9 + [anywhere] * 6,
        scratch_shapes=scratch,
        name="step",
        compiler_params=pltpu.CompilerParams(
            collective_id=0, has_side_effects=True, vmem_limit_bytes=60 << 20
        ),
    )(*shards, cotangent, points, members, layer_norms)
    return result[:4], result[4:8], result[8], result[9], result[10]


def on_device_cube(
    points,
    members,
    cotangent,
    project_weight,
    output_weight,
    upward_weight,
    downward_weight,
    layer_norms,
    project_master,
    project_first,
    project_second,
    output_master,
    output_first,
    output_second,
    upward_master,
    upward_first,
    upward_second,
    downward_master,
    downward_first,
    downward_second,
    norm_first,
    norm_second,
):
    bf16 = jnp.bfloat16
    firsts, seconds, norm_summed, latents, point_gradient = run_step(
        (jnp.transpose(project_weight, (1, 0, 2)), output_weight, upward_weight, downward_weight),
        points,
        cotangent,
        members,
        layer_norms,
    )
    data_index = lax.axis_index("dp")
    norm_columns = norm_first.shape[1]
    norm_gradient = lax.dynamic_slice_in_dim(norm_summed, data_index * norm_columns, norm_columns, 1)
    norm_current = lax.dynamic_slice_in_dim(layer_norms, data_index * norm_columns, norm_columns, 1)
    results = [latents, point_gradient]
    swap = lambda array: jnp.transpose(array, (1, 0, 2))
    for w, states, rate in (
        (3, [swap(a) for a in (project_master, project_first, project_second)], D ** (-0.5)),
        (2, [output_master, output_first, output_second], max(1, D * 4 // LAT) ** (-0.5)),
        (1, [upward_master, upward_first, upward_second], D ** (-0.5)),
        (0, [downward_master, downward_first, downward_second], FF ** (-0.5)),
    ):
        master, first, second = states
        summed = firsts[w].astype(jnp.float32) + seconds[w].astype(jnp.float32)
        updated, one_new, two_new = adamw_step(master, summed, first, second, rate)
        new = [summed, updated, one_new, two_new, updated.astype(bf16)]
        results += [swap(a) for a in new] if w == 3 else new
    norm_new = adamw_step(norm_current, norm_gradient, norm_first, norm_second, 0.2)
    results += [norm_gradient, *norm_new]
    return tuple(results)


def solution(mesh):
    return jax.shard_map(
        on_device_cube if dict(mesh.shape) == {"dp": 8, "mp": 4} else on_device_any,
        mesh=mesh,
        in_specs=(
            P(("dp", "mp"), None),
            P(("dp", "mp"), None),
            P(("dp", "mp"), None),
            P(None, None, "mp"),
            P("mp", None),
            P(None, "mp"),
            P("mp", None),
            P(),
            P("dp", None, "mp"),
            P("dp", None, "mp"),
            P("dp", None, "mp"),
            P("mp", "dp"),
            P("mp", "dp"),
            P("mp", "dp"),
            P("dp", "mp"),
            P("dp", "mp"),
            P("dp", "mp"),
            P("mp", "dp"),
            P("mp", "dp"),
            P("mp", "dp"),
            P(None, "dp"),
            P(None, "dp"),
        ),
        out_specs=(
            P(("dp", "mp"), None),
            P(("dp", "mp"), None),
            P("dp", None, "mp"),
            P("dp", None, "mp"),
            P("dp", None, "mp"),
            P("dp", None, "mp"),
            P("dp", None, "mp"),
            P("mp", "dp"),
            P("mp", "dp"),
            P("mp", "dp"),
            P("mp", "dp"),
            P("mp", "dp"),
            P("dp", "mp"),
            P("dp", "mp"),
            P("dp", "mp"),
            P("dp", "mp"),
            P("dp", "mp"),
            P("mp", "dp"),
            P("mp", "dp"),
            P("mp", "dp"),
            P("mp", "dp"),
            P("mp", "dp"),
            P(None, "dp"),
            P(None, "dp"),
            P(None, "dp"),
            P(None, "dp"),
        ),
        check_vma=False,
    )
```

```python
import jax
import jax.numpy as jnp
from jax import lax
from jax.experimental import pallas as pl
from jax.experimental.pallas import tpu as pltpu
from jax.sharding import PartitionSpec as P

D = 1024
HEAD_DIM = 128
FF = 4096
LAT = 256
ADAM_STEP = 10


norm_epsilon = 1e-05
beta_one = 0.9
beta_two = 0.95
adam_epsilon = 1e-08
weight_decay = 0.1
masked_score = -1e30


def layer_norm(values, norm_gain, norm_shift):
    center = values - jnp.mean(values, axis=-1, keepdims=True)
    spread = jnp.mean(center * center, axis=-1, keepdims=True)
    return center * lax.rsqrt(spread + norm_epsilon) * norm_gain + norm_shift


def pick_rows(source_rows, row_index):
    return source_rows[row_index]


def adamw_step(weight, gradient, moment_one, moment_two, step_rate):
    one_new = beta_one * moment_one + (1.0 - beta_one) * gradient
    two_new = beta_two * moment_two + (1.0 - beta_two) * gradient * gradient
    corrected_one = one_new / (1.0 - beta_one**ADAM_STEP)
    corrected_two = two_new / (1.0 - beta_two**ADAM_STEP)
    updated = weight - step_rate * (
        corrected_one / (jnp.sqrt(corrected_two) + adam_epsilon) + weight_decay * weight
    )
    return (updated, one_new, two_new)


def masked_scores(queries, keys_all, key_mask, score_scale):
    raw_scores = (
        jnp.einsum("gqhe,gkhe->ghqk", queries, keys_all, preferred_element_type=jnp.float32)
        * score_scale
    )
    return jnp.where(key_mask, raw_scores, masked_score)


def on_device_any(
    points,
    members,
    cotangent,
    project_weight,
    output_weight,
    upward_weight,
    downward_weight,
    layer_norms,
    project_master,
    project_first,
    project_second,
    output_master,
    output_first,
    output_second,
    upward_master,
    upward_first,
    upward_second,
    downward_master,
    downward_first,
    downward_second,
    norm_first,
    norm_second,
):
    groups_here = members.shape[0]
    shard_rows = points.shape[0]
    model_width = points.shape[1]
    heads_here = project_weight.shape[2] // HEAD_DIM
    score_scale = HEAD_DIM ** (-0.5)
    grouped = points.reshape(groups_here, LAT, model_width)
    slot_index = jnp.maximum(members, 0)
    key_live = members >= 0
    picked = jax.vmap(pick_rows)(grouped, slot_index)
    inputs = jnp.where(key_live[:, :, None], picked.astype(jnp.float32), 0.0).reshape(
        shard_rows, model_width
    )
    normed, norm_back_one = jax.vjp(layer_norm, inputs, layer_norms[0], layer_norms[1])
    gathered, live_all = (
        lax.all_gather(normed.astype(jnp.bfloat16), "mp", axis=0, tiled=True),
        lax.all_gather(key_live.astype(jnp.bfloat16), "mp", axis=0, tiled=True),
    )
    total_rows = gathered.shape[0]
    total_groups = live_all.shape[0]
    key_mask = (live_all > 0)[:, None, None, :]
    projected = jnp.einsum(
        "rd,dcf->rcf", gathered, project_weight, preferred_element_type=jnp.float32
    ).astype(jnp.bfloat16)
    heads_view = projected.reshape(total_groups, LAT, 3, heads_here, HEAD_DIM)
    queries = heads_view[:, :, 0]
    keys_all = heads_view[:, :, 1]
    values_all = heads_view[:, :, 2]
    scores = masked_scores(queries, keys_all, key_mask, score_scale)
    row_top = jnp.max(scores, axis=-1, keepdims=True)
    exponent = jnp.exp(scores - row_top)
    row_total = jnp.sum(exponent, axis=-1, keepdims=True)
    attention_weights = exponent / row_total
    log_total = row_top + jnp.log(row_total)
    weights_low = attention_weights.astype(jnp.bfloat16)
    attended = jnp.einsum(
        "ghqk,gkhe->gqhe", weights_low, values_all, preferred_element_type=jnp.float32
    ).astype(jnp.bfloat16)
    attended = attended.reshape(total_rows, heads_here * HEAD_DIM)
    branch = lax.psum_scatter(
        jnp.dot(attended, output_weight, preferred_element_type=jnp.float32),
        "mp",
        scatter_dimension=0,
        tiled=True,
    )
    residual = inputs + branch
    normed_two, norm_back_two = jax.vjp(layer_norm, residual, layer_norms[2], layer_norms[3])
    gathered_two = lax.all_gather(normed_two.astype(jnp.bfloat16), "mp", axis=0, tiled=True)
    upward = jnp.dot(gathered_two, upward_weight, preferred_element_type=jnp.float32)
    activated_float, gelu_back = jax.vjp(jax.nn.gelu, upward)
    activated = activated_float.astype(jnp.bfloat16)
    latents = residual + lax.psum_scatter(
        jnp.dot(activated, downward_weight, preferred_element_type=jnp.float32).astype(
            jnp.bfloat16
        ),
        "mp",
        scatter_dimension=0,
        tiled=True,
    ).astype(jnp.float32)
    cotangent_all = lax.all_gather(cotangent, "mp", axis=0, tiled=True)
    downward_local = jnp.einsum(
        "rf,rd->fd", activated, cotangent_all, preferred_element_type=jnp.float32
    )
    activated_grad = jnp.einsum(
        "rd,fd->rf", cotangent_all, downward_weight, preferred_element_type=jnp.float32
    )
    upward_grad = gelu_back(activated_grad)[0].astype(jnp.bfloat16)
    upward_local = jnp.einsum(
        "rd,rf->df", gathered_two, upward_grad, preferred_element_type=jnp.float32
    )
    normed_two_grad = lax.psum_scatter(
        jnp.einsum("rf,df->rd", upward_grad, upward_weight, preferred_element_type=jnp.float32),
        "mp",
        scatter_dimension=0,
        tiled=True,
    )
    residual_part, gain_two_grad, shift_two_grad = norm_back_two(normed_two_grad)
    residual_grad = residual_part + cotangent.astype(jnp.float32)
    norm_two_local = jnp.stack([gain_two_grad, shift_two_grad])
    branch_grad = lax.all_gather(residual_grad.astype(jnp.bfloat16), "mp", axis=0, tiled=True)
    output_local = jnp.einsum(
        "rh,rd->hd", attended, branch_grad, preferred_element_type=jnp.float32
    )
    attended_grad = jnp.einsum(
        "rd,hd->rh", branch_grad, output_weight, preferred_element_type=jnp.float32
    ).astype(jnp.bfloat16)
    attended_grad = attended_grad.reshape(total_groups, LAT, heads_here, HEAD_DIM)
    scores_again = masked_scores(queries, keys_all, key_mask, score_scale)
    weights_again = jnp.exp(scores_again - log_total)
    weights_again_low = weights_again.astype(jnp.bfloat16)
    value_grad = jnp.einsum(
        "ghqk,gqhe->gkhe", weights_again_low, attended_grad, preferred_element_type=jnp.float32
    ).astype(jnp.bfloat16)
    weight_grad = jnp.einsum(
        "gqhe,gkhe->ghqk", attended_grad, values_all, preferred_element_type=jnp.float32
    )
    score_grad = (
        weights_again * (weight_grad - jnp.sum(weights_again * weight_grad, axis=-1, keepdims=True))
    ).astype(jnp.bfloat16)
    query_grad = (
        jnp.einsum("ghqk,gkhe->gqhe", score_grad, keys_all, preferred_element_type=jnp.float32)
        * score_scale
    ).astype(jnp.bfloat16)
    key_grad = (
        jnp.einsum("ghqk,gqhe->gkhe", score_grad, queries, preferred_element_type=jnp.float32)
        * score_scale
    ).astype(jnp.bfloat16)
    projected_grad = jnp.stack([query_grad, key_grad, value_grad], axis=2).reshape(
        total_rows, 3, heads_here * HEAD_DIM
    )
    project_local = jnp.einsum(
        "rd,rcf->dcf", gathered, projected_grad, preferred_element_type=jnp.float32
    )
    normed_grad = lax.psum_scatter(
        jnp.einsum(
            "rcf,dcf->rd", projected_grad, project_weight, preferred_element_type=jnp.float32
        ).astype(jnp.bfloat16),
        "mp",
        scatter_dimension=0,
        tiled=True,
    ).astype(jnp.float32)
    input_part, gain_one_grad, shift_one_grad = norm_back_one(normed_grad)
    input_grad = input_part + residual_grad
    norm_one_local = jnp.stack([gain_one_grad, shift_one_grad])
    matches = members[:, :, None] == jnp.arange(LAT, dtype=jnp.int32)[None, None, :]
    slot_of = jnp.argmax(matches, axis=1)
    point_used = jnp.any(matches, axis=1)
    grouped_grad = input_grad.reshape(groups_here, LAT, model_width)
    point_gradient = jnp.where(
        point_used[:, :, None], jax.vmap(pick_rows)(grouped_grad, slot_of), 0.0
    ).reshape(shard_rows, model_width)
    (
        project_summed,
        output_summed,
        upward_summed,
        downward_summed,
        norm_one_summed,
        norm_two_summed,
    ) = (
        lax.psum_scatter(project_local, "dp", scatter_dimension=0, tiled=True),
        lax.psum_scatter(output_local, "dp", scatter_dimension=1, tiled=True),
        lax.psum_scatter(upward_local, "dp", scatter_dimension=0, tiled=True),
        lax.psum_scatter(downward_local, "dp", scatter_dimension=1, tiled=True),
        lax.psum_scatter(norm_one_local, "dp", scatter_dimension=1, tiled=True),
        lax.psum_scatter(norm_two_local, "dp", scatter_dimension=1, tiled=True),
    )
    norm_gradient = lax.psum(jnp.concatenate([norm_one_summed, norm_two_summed], axis=0), "mp")
    data_index = lax.axis_index("dp")
    norm_columns = norm_first.shape[1]
    norm_current = lax.dynamic_slice_in_dim(layer_norms, data_index * norm_columns, norm_columns, 1)
    project_new = adamw_step(
        project_master, project_summed, project_first, project_second, D ** (-0.5)
    )
    output_new = adamw_step(
        output_master, output_summed, output_first, output_second, max(1, D * 4 // LAT) ** (-0.5)
    )
    upward_new = adamw_step(upward_master, upward_summed, upward_first, upward_second, D ** (-0.5))
    downward_new = adamw_step(
        downward_master, downward_summed, downward_first, downward_second, FF ** (-0.5)
    )
    norm_new = adamw_step(norm_current, norm_gradient, norm_first, norm_second, 0.2)
    return (
        latents,
        point_gradient,
        project_summed,
        project_new[0],
        project_new[1],
        project_new[2],
        project_new[0].astype(jnp.bfloat16),
        output_summed,
        output_new[0],
        output_new[1],
        output_new[2],
        output_new[0].astype(jnp.bfloat16),
        upward_summed,
        upward_new[0],
        upward_new[1],
        upward_new[2],
        upward_new[0].astype(jnp.bfloat16),
        downward_summed,
        downward_new[0],
        downward_new[1],
        downward_new[2],
        downward_new[0].astype(jnp.bfloat16),
        norm_gradient,
        norm_new[0],
        norm_new[1],
        norm_new[2],
    )


MESH = pl.DeviceIdType.MESH
PLANES = 4
OWNERS = 8
ROWS = LAT
HALVES = (0, 1)
SHARDS = ((3, D, 256), (256, D), (D, D), (D, D))
SHORT = ()
CHUNKS = [(w, k) for w in (0, 1) for k in range(3)] + [(2, 0), (3, 0)]
SLOTS = 4
LOADS = (
    (0, None), (0, 0), (0, 1), (0, 2), (2, None), (2, 0), (3, None), (3, 0), (0, 2), (0, 1), (0, 0), (0, None),
)

WIDTHS = (D, D, 256, 3 * 256)
BLOCK = D // OWNERS
HALF = BLOCK // 2
RING = 2
OWN = PLANES - 1
UNITS = (
    (0, 3), (0, 0), (1, 3), (1, 0), (3, 0), (3, 1), (3, 2), (3, 3), (2, 0), (2, 1), (2, 2), (2, 3),
)
TURNED_AT = (0, 1, 1, 0)
(
    SEND_OWN, TAKE, CORNER, CROSS, WHOLE, LOAD, READY, ENTER, PROJECT, BRANCH, SEND_COTANGENT, CAME, WIDEN,
    NARROW_BACK, WIDEN_BACK, NARROW, LATENTS, RESIDUAL, ATTEND, INWARD, TURN, PRODUCE, JOIN, ONE, TWO, ALONG,
    FINISH, INPUTS, NORM, NORMS_OUT, POINTS,
) = range(31)
SCHEDULE = (
    (SEND_OWN, 0), (TAKE, 0, 0, 0), (SEND_OWN, 1), (TAKE, 0, 0, 1), (TAKE, 0, 1, 0), (CORNER, 0, 0, 0),
    (TAKE, 0, 2, 0), (CORNER, 0, 0, 1), (TAKE, 0, 1, 1), (CORNER, 0, 1, 0), (TAKE, 1, 0, 0), (TAKE, 1, 0, 1),
    (TAKE, 0, 2, 1), (SEND_OWN, 2), (ENTER,), (CORNER, 0, 1, 1), (TAKE, 1, 1, 0), (CROSS, 0, 0, 1), (TAKE, 1, 2, 1),
    (TAKE, 1, 2, 0), (CROSS, 0, 0, 0), (CORNER, 1, 0, 1), (CORNER, 0, 2, 0), (TAKE, 1, 1, 1), (SEND_OWN, 3),
    (LOAD, 0), (CORNER, 0, 2, 1), (CROSS, 0, 1, 1), (WHOLE, 0, 0), (CORNER, 1, 2, 1), (CROSS, 0, 1, 0), (LOAD, 1),
    (CORNER, 1, 2, 0), (PROJECT, 0), (CROSS, 1, 0, 1), (SEND_COTANGENT,), (WHOLE, 0, 1), (LOAD, 4), (LOAD, 2),
    (PROJECT, 1), (CORNER, 1, 0, 0), (CORNER, 1, 1, 1), (CORNER, 1, 1, 0), (CROSS, 0, 2, 0), (TAKE, 2, 0, 1),
    (TAKE, 2, 0, 0), (CROSS, 0, 2, 1), (PROJECT, 2), (WHOLE, 0, 2), (LOAD, 3), (CROSS, 1, 1, 1), (LOAD, 6),
    (TAKE, 3, 0, 1), (TAKE, 3, 0, 0), (CROSS, 1, 0, 0), (CROSS, 1, 2, 0), (CROSS, 1, 1, 0), (CROSS, 1, 2, 1),
    (PROJECT, 3), (WHOLE, 1, 0), (READY, 4), (CORNER, 2, 0, 0), (CORNER, 2, 0, 1), (WHOLE, 1, 2), (WHOLE, 1, 1),
    (BRANCH,), (CORNER, 3, 0, 0), (CAME, 0), (CORNER, 3, 0, 1), (CROSS, 2, 0, 1), (READY, 6), (CROSS, 2, 0, 0),
    (TURN, 0), (WIDEN, 0, 0), (WHOLE, 2, 0), (LOAD, 5), (NARROW_BACK, 0, 0), (CROSS, 3, 0, 1), (READY, 5),
    (CROSS, 3, 0, 0), (WIDEN, 1, 0), (CAME, 1), (WIDEN, 0, 1), (PRODUCE, 0), (WHOLE, 3, 0), (WIDEN, 1, 1),
    (PRODUCE, 1), (JOIN, 0), (LOAD, 7), (TURN, 1), (JOIN, 1), (READY, 7), (NARROW_BACK, 0, 1), (NARROW_BACK, 1, 1),
    (WIDEN_BACK, 1), (PRODUCE, 2), (NARROW_BACK, 1, 0), (ONE, 0, 0), (ONE, 0, 1), (PRODUCE, 3), (JOIN, 2), (TURN, 3),
    (NARROW, 1), (JOIN, 3), (ONE, 1, 0), (WIDEN_BACK, 0), (ONE, 1, 1), (RESIDUAL,), (ATTEND, 4), (PRODUCE, 4),
    (ATTEND, 5), (ONE, 3, 0), (ONE, 3, 1), (JOIN, 4), (PRODUCE, 5), (ATTEND, 6), (LOAD, 9), (JOIN, 5), (PRODUCE, 6),
    (LOAD, 8), (TWO, 0, 0), (TWO, 3, 0), (ATTEND, 7), (PRODUCE, 7), (NARROW, 0), (TWO, 3, 1), (JOIN, 6), (ONE, 4, 1),
    (TWO, 1, 1), (LOAD, 10), (LOAD, 11), (TURN, 2), (PRODUCE, 8), (INWARD, 8), (ONE, 5, 1), (ONE, 4, 0), (INWARD, 9),
    (PRODUCE, 9), (JOIN, 8), (ONE, 2, 0), (JOIN, 9), (INWARD, 10), (TWO, 4, 1), (PRODUCE, 10), (PRODUCE, 11),
    (ONE, 6, 1), (INWARD, 11), (TWO, 4, 0), (ONE, 8, 1), (ONE, 5, 0), (TWO, 5, 1), (TWO, 1, 0), (ONE, 8, 0),
    (ALONG, 4, 1), (JOIN, 7), (JOIN, 10), (ONE, 9, 1), (INPUTS,), (TWO, 0, 1), (NORM, 0), (ONE, 9, 0), (TWO, 2, 0),
    (ONE, 6, 0), (ALONG, 4, 0), (TWO, 6, 1), (POINTS,), (JOIN, 11), (ALONG, 5, 1), (TWO, 8, 0), (TWO, 8, 1),
    (ALONG, 6, 1), (TWO, 5, 0), (ONE, 7, 1), (NORM, 1), (ONE, 10, 1), (ONE, 10, 0), (ONE, 7, 0), (ALONG, 8, 0),
    (ONE, 2, 1), (TWO, 9, 1), (ALONG, 8, 1), (TWO, 9, 0), (TWO, 6, 0), (ALONG, 6, 0), (ONE, 11, 0), (ALONG, 5, 0),
    (LATENTS,), (ONE, 11, 1), (TWO, 10, 1), (ALONG, 10, 1), (TWO, 7, 1), (ALONG, 9, 0), (TWO, 10, 0), (ALONG, 10, 0),
    (NORM, 2), (ALONG, 9, 1), (TWO, 2, 1), (FINISH, 1), (TWO, 7, 0), (TWO, 11, 0), (FINISH, 3), (FINISH, 0),
    (TWO, 11, 1), (FINISH, 2), (NORMS_OUT,),
)
NN = ((1,), (0,))
NT = ((1,), (1,))
TN = ((0,), (0,))


def place():
    dp = lax.axis_index("dp")
    return dp // 4, (dp // 2) % 2, dp % 2, lax.axis_index("mp")


def device(y, x, c, z):
    return (y * 4 + x * 2 + c, z)


def greet(y, x, c, z):
    barrier = pltpu.get_barrier_semaphore()
    partners = [device(1 - y, x, c, z), device(y, 1 - x, c, z), device(y, x, 1 - c, z)]
    partners += [device(y, x, c, (z + d) % PLANES) for d in (1, 2, 3)]
    for partner in partners:
        pl.semaphore_signal(barrier, inc=1, device_id=partner, device_id_type=MESH)
    pl.semaphore_wait(barrier, len(partners))


def arrival(z, k):
    return (z + 1 - 2 * (z % 2), 2 - z // 2, 3 - 3 * (z // 2))[k]


def dot(a, b, contract):
    return lax.dot_general(a, b, (contract, ((), ())), preferred_element_type=jnp.float32)


def tiles(count, size, body):
    def step(n, carry):
        body(pl.ds(pl.multiple_of(n * size, size), size))
        return carry

    lax.fori_loop(0, count, step, 0)


def norm_rows(source, target, gain, shift, strip=64):
    def step(n, carry):
        rows = pl.ds(pl.multiple_of(n * strip, strip), strip)
        target[rows, :] = layer_norm(source[rows, :], gain, shift).astype(target.dtype)
        return carry

    lax.fori_loop(0, ROWS // strip, step, 0)


def step_kernel(*refs):
    f32, bf16 = jnp.float32, jnp.bfloat16
    shards, cotangent_in, (points, members, norms) = refs[0:4], refs[4], refs[5:8]
    outs, norm_out, latents_out, points_out, fulls = refs[8:16], refs[16], refs[17], refs[18], refs[19:23]
    inputs, entering_one, projected, attended, residual, latents = refs[23:29]
    entering_two, cotangent, activated, slope, upward_grad = refs[29:34]
    turned, branch_grad, projected_grad, normed_grad, sent, came = refs[34:40]
    slots, output_full, ring = refs[40:43]
    acc, one_in, two_in, z_in = refs[43:47], refs[47:51], refs[51:55], refs[55:59]
    norm_own, norm_in, norm_planes = refs[59:62]
    load_sem, output_sem, out_sem, swap_send, swap_recv = refs[62:67]
    gz_send, gz_recv, ga_send, ga_recv, gb_send, gb_recv, gc_send, gc_recv = refs[67:75]
    c_send, c_recv, one_send, one_recv, two_send, two_recv, z_send, z_recv = refs[75:83]
    norm_send, norm_recv = refs[83:85]
    residual_grad = residual
    y, x, c, z = place()
    is_mid = jnp.logical_or(z == 1, z == 2)
    is_end = jnp.logical_not(is_mid)
    sibling = device(y, x, 1 - c, z)
    over_x, over_y = device(y, 1 - x, c, z), device(1 - y, x, c, z)
    beside, across = device(y, x, c, arrival(z, 0)), device(y, x, c, 3 - z)
    opposite = device(y, x, c, (z + 2) % PLANES)

    def plane_at(k):
        return z if k is None else arrival(z, k)

    def plane_of(i):
        return z if i == OWN else arrival(z, 2 - i)

    def remote(src, dst, send, recv, target):
        return pltpu.make_async_remote_copy(
            src_ref=src, dst_ref=dst, send_sem=send, recv_sem=recv, device_id=target, device_id_type=MESH
        )

    def rows_of(ref, w, rows):
        return ref.at[:, rows, :] if w == 0 else ref.at[rows, :]

    def view(w, plane, rows):
        return fulls[w].at[rows, :] if w >= 2 else rows_of(fulls[w].at[plane], w, rows)

    def block(w, half, first, count):
        height = SHARDS[w][-2]
        start = pl.multiple_of(half * (height // 2) + first * (height // 16), height // 16)
        return pl.ds(start, count * (height // 16))

    spot = (c * 4 + y * 2 + x, c * 4 + x * 2 + y)
    pair = (c * 4 + y * 2, c * 4 + x * 2)

    def gz_rows(w, half):
        return block(w, half, pair[half], 2) if w in SHORT else block(w, half, spot[half], 1)

    def gz_own(w, half, lane, slot, target):
        rows = gz_rows(w, half)
        send, recv = gz_send.at[w, lane, half], gz_recv.at[w, slot, half]
        return remote(rows_of(shards[w], w, rows), view(w, z, rows), send, recv, target)

    def gz_first(w, half):
        return gz_own(w, half, 0, 0, opposite if w >= 2 else beside)

    def gz_across(w, half):
        return gz_own(w, half, 1, 1, across)

    def gz_foreign(w, k, half, lane, slot, target):
        here = view(w, arrival(z, k), gz_rows(w, half))
        return remote(here, here, gz_send.at[w, lane, half], gz_recv.at[w, slot, half], target)

    def gz_pass(w, k, half):
        lane, target, slot = ((2, across, 2), (3, beside, 1), (4, beside, 2))[k]
        return gz_foreign(w, k, half, lane, slot, target)

    def gz_arrived(w, k, half):
        return gz_foreign(w, k, half, 0, k, beside)

    def ga_copy(w, k, half):
        here = view(w, arrival(z, k), block(w, half, spot[half], 1))
        return remote(here, here, ga_send.at[w, k, half], ga_recv.at[w, k, half], (over_x, over_y)[half])

    def gb_copy(w, k, half):
        here = view(w, arrival(z, k), block(w, half, pair[half], 2))
        return remote(here, here, gb_send.at[w, k, half], gb_recv.at[w, k, half], (over_y, over_x)[half])

    def gc_copy(w, k, half):
        here = view(w, arrival(z, k), block(w, half, c * 4, 4))
        return remote(here, here, gc_send.at[w, k, half], gc_recv.at[w, k, half], sibling)

    def send_own(w):
        for half in HALVES:
            gz_first(w, half).start()
        if w < 2:

            @pl.when(is_mid)
            def _():
                for half in HALVES:
                    gz_across(w, half).start()

    def take(w, k, half):
        gz_arrived(w, k, half).wait_recv()
        (gb_copy if w in SHORT else ga_copy)(w, k, half).start()
        if w < 2:

            @pl.when(is_mid)
            def _():
                gz_pass(w, k, half).start()

    def corner(w, k, half):
        ga_copy(w, k, half).wait_recv()
        gb_copy(w, k, half).start()

    def cross(w, k, half):
        gb_copy(w, k, half).wait_recv()
        gc_copy(w, k, half).start()

    def whole(w, k):
        for half in HALVES:
            gc_copy(w, k, half).wait_recv()
        if w == 1:
            output_load(k).start()

    def loads(n):
        w, k = LOADS[n]
        if w >= 2:
            source = shards[w] if k is None else fulls[w]
            return [pltpu.make_async_copy(source, slots.at[n % SLOTS], load_sem.at[n, 0])]
        source = shards[w] if k is None else fulls[w].at[arrival(z, k)]
        return [
            pltpu.make_async_copy(
                source.at[part], slots.at[n % SLOTS, :, part * 256 : (part + 1) * 256], load_sem.at[n, part]
            )
            for part in range(3)
        ]

    def start_load(n):
        for copy in loads(n):
            copy.start()

    def wait_load(n):
        for copy in loads(n):
            copy.wait()

    def output_load(k):
        source = shards[1] if k is None else fulls[1].at[arrival(z, k)]
        return pltpu.make_async_copy(source, output_full.at[plane_at(k)], output_sem.at[3 if k is None else k])

    mine, theirs = pl.ds(0, ROWS), pl.ds(ROWS, ROWS)

    def swap(n):
        src, dst = (
            (cotangent.at[mine], cotangent.at[theirs]),
            (entering_two.at[mine], entering_two.at[theirs]),
            (sent.at[0], came.at[0]),
            (sent.at[1], came.at[1]),
        )[n]
        return remote(src, dst, swap_send.at[n], swap_recv.at[n], beside)

    cotangent_load = pltpu.make_async_copy(cotangent_in, cotangent.at[mine], out_sem.at[2])

    def send_cotangent():
        cotangent_load.wait()
        swap(0).start()

    def swap_came(n):
        swap(n).wait_recv()

    def enter():
        slot_of = lax.broadcasted_iota(jnp.int32, (ROWS, ROWS), 0) == members[...]
        chosen = slot_of.astype(f32).astype(bf16)

        def pick(columns):
            inputs[:, columns] = dot(chosen, points[:, columns], TN)

        tiles(4, 256, pick)
        norm_rows(inputs, entering_one, norms[0:1, :], norms[1:2, :])
        residual[...] = inputs[...]

    def softmax_parts(plane, span):
        queries, keys_all = projected[plane, 0, :, span], projected[plane, 1, :, span]
        scores = jnp.where(members[...] >= 0, dot(queries, keys_all, NT) * HEAD_DIM ** (-0.5), masked_score)
        exponent = jnp.exp(scores - jnp.max(scores, axis=-1, keepdims=True))
        return queries, keys_all, exponent * (1.0 / jnp.sum(exponent, axis=-1, keepdims=True))

    def project_attend(n):
        wait_load(n)
        plane, slot = plane_at(LOADS[n][1]), n % SLOTS
        for part in range(3):
            right = slots[slot, :, part * 256 : (part + 1) * 256]
            projected[plane, part] = dot(entering_one[...], right, NN).astype(bf16)
        for head in range(2):
            span = slice(head * HEAD_DIM, (head + 1) * HEAD_DIM)
            probs = softmax_parts(plane, span)[2]
            attended[plane, :, span] = dot(probs.astype(bf16), projected[plane, 2, :, span], NN).astype(bf16)

    def branches():
        for k in (None, 0, 1, 2):
            plane = plane_at(k)
            output_load(k).wait()

            def body(columns):
                residual[:, columns] += dot(attended[plane], output_full[plane, :, columns], NN)

            tiles(4, 256, body)
        norm_rows(residual, entering_two, norms[2:3, :], norms[3:4, :])
        swap(1).start()
        latents[...] = residual[...]

    def rows_at(b):
        return theirs if b else mine

    def widen(j, b):
        rows = rows_at(b)

        def body(columns):
            u = dot(entering_two[rows, :], slots[j, :, columns], NN)
            square = u * u
            bend = jnp.tanh(0.7978845608028654 * u * (1.0 + 0.044715 * square))
            activated[j, rows, columns] = (0.5 * u * (1.0 + bend)).astype(bf16)
            slope[j, rows, columns] = 0.5 * (1.0 + bend) + 0.5 * u * (1.0 - bend * bend) * (
                0.7978845608028654 * (1.0 + 3.0 * 0.044715 * square)
            )

        tiles(4, 256, body)

    def narrow_back(j, b):
        rows = rows_at(b)

        def body(columns):
            product = dot(cotangent[rows, :], slots[2 + j, columns, :], NT)
            upward_grad[j, rows, columns] = (product * slope[j, rows, columns]).astype(bf16)

        tiles(4, 256, body)

    def widen_back(b):
        rows = rows_at(b)

        def body(columns):
            total = dot(upward_grad[0, rows, :], slots[0, columns, :], NT)
            total += dot(upward_grad[1, rows, :], slots[1, columns, :], NT)
            if b:
                sent[1, :, columns] = total.astype(bf16)
            else:
                normed_grad[:, columns] = total

        tiles(4, 256, body)
        if b:
            swap(3).start()

    def narrow(b):
        rows = rows_at(b)

        def body(columns):
            total = dot(activated[0, rows, :], slots[2, :, columns], NN)
            total += dot(activated[1, rows, :], slots[3, :, columns], NN)
            if b:
                sent[0, :, columns] = total.astype(bf16)
            else:
                latents[:, columns] += total

        tiles(4, 256, body)
        if b:
            swap(2).start()

    latents_copy = pltpu.make_async_copy(latents, latents_out, out_sem.at[0])

    def add_came(n, target):
        swap_came(2 + n)

        def strip(r, carry):
            rows = pl.ds(pl.multiple_of(r * 32, 32), 32)
            target[rows, :] += came[n, rows, :].astype(f32)
            return carry

        lax.fori_loop(0, ROWS // 32, strip, 0)

    def latents_done():
        add_came(0, latents)
        latents_copy.start()

    def here(t):
        w, i = UNITS[t]
        return acc[w].at[i if w >= 2 else i // OWN]

    def pair_copy(t):
        w = UNITS[t][0]
        return remote(ring.at[t % RING, :, :, :, 0 : WIDTHS[w]], here(t), c_send.at[t], c_recv.at[t], sibling)

    def half_rows(half):
        return pl.ds(half * HALF, HALF)

    def one_in_at(t, half):
        w, i = UNITS[t]
        return one_in[w].at[i if w >= 2 else i // OWN, half]

    def two_in_at(t, half):
        w, i = UNITS[t]
        return two_in[w].at[i if w >= 2 else i // OWN, half]

    def one_copy(t, half):
        rows = half_rows(half)
        src = here(t).at[1 - y, :, rows] if half == 0 else here(t).at[:, 1 - x, rows]
        send, recv = one_send.at[t, half], one_recv.at[t, half]
        return remote(src, one_in_at(t, half), send, recv, (over_y, over_x)[half])

    def two_copy(t, half):
        rows = half_rows(half)
        src = here(t).at[y, 1 - x, rows] if half == 0 else here(t).at[1 - y, x, rows]
        send, recv = two_send.at[t, half], two_recv.at[t, half]
        return remote(src, two_in_at(t, half), send, recv, (over_x, over_y)[half])

    def z_copy(t, half, slot, target):
        w = UNITS[t][0]
        send, recv = z_send.at[t, half], z_recv.at[w, slot, half]
        return remote(here(t).at[y, x, half_rows(half)], z_in[w].at[slot, half], send, recv, target)

    def z_first(t, half):
        w, i = UNITS[t]
        if w < 2:
            z_copy(t, half, 0, opposite).start()
            return

        @pl.when(is_end)
        def _():
            z_copy(t, half, 2 - i, beside).start()

    def z_pass(t, half):
        w, i = UNITS[t]

        @pl.when(is_mid)
        def _():
            slot = (2, 1, 3)[i]
            z_copy(t, half, slot, beside).wait_recv()
            add_rows(here(t).at[y, x, half_rows(half)], z_in[w].at[slot, half])
            z_copy(t, half, (3, 4, 0)[i], (across, across, beside)[i]).start()

    def add_rows(target, source):
        def body(r, carry):
            rows = pl.ds(pl.multiple_of(r * 16, 16), 16)
            target[rows] = (target[rows].astype(f32) + source[rows].astype(f32)).astype(bf16)
            return carry

        lax.fori_loop(0, HALF // 16, body, 0)

    def partial(w, i, parity, columns, n):
        if w < 2:
            right = (activated, upward_grad)[w][1 - i // OWN, :, columns]
            return dot(turned[w, parity], right, NN)
        plane = plane_of(i)
        right = projected_grad[plane, n] if w == 3 else attended[plane, :, columns]
        return dot(turned[TURNED_AT[w], parity, :, 0:ROWS], right, NN)

    def over_tiles(w, body):
        if w == 2:
            body(pl.ds(0, 256), 0)
            return

        def step(n, carry):
            body(pl.ds(pl.multiple_of(n * 256, 256), 256), n)
            return carry

        lax.fori_loop(0, WIDTHS[w] // 256, step, 0)

    def produce(t):
        w, i = UNITS[t]
        if t >= RING:
            pair_copy(t - RING).wait_send()

        def body(columns, n):
            product = partial(w, i, 1 - c, columns, n).astype(bf16)
            for k in range(4):
                ring[t % RING, k // 2, k % 2, :, columns] = product[k * BLOCK : (k + 1) * BLOCK]

        over_tiles(w, body)
        pair_copy(t).start()

    def join(t):
        w, i = UNITS[t]
        at = i if w >= 2 else i // OWN
        pair_copy(t).wait_recv()

        def body(columns, n):
            product = partial(w, i, c, columns, n)
            for k in range(4):
                other = acc[w][at, k // 2, k % 2, :, columns].astype(f32)
                acc[w][at, k // 2, k % 2, :, columns] = (product[k * BLOCK : (k + 1) * BLOCK] + other).astype(bf16)

        over_tiles(w, body)
        for half in HALVES:
            one_copy(t, half).start()

    def after_one(t, half):
        one_copy(t, half).wait()
        rows = half_rows(half)
        for k in (0, 1):
            target = here(t).at[y, k, rows] if half == 0 else here(t).at[k, x, rows]
            add_rows(target, one_in_at(t, half).at[k])
        two_copy(t, half).start()

    def after_two(t, half):
        two_copy(t, half).wait()
        add_rows(here(t).at[y, x, half_rows(half)], two_in_at(t, half))
        if UNITS[t][1] < OWN:
            z_first(t, half)

    def finish(w):
        t = UNITS.index((w, OWN))
        for half in HALVES:
            z_copy(t, half, 0, beside).wait_recv()
        if w >= 2:

            @pl.when(is_mid)
            def _():
                for half in HALVES:
                    z_copy(t, half, 4, across).wait_recv()

        def body(n, carry):
            columns = pl.ds(pl.multiple_of(n * 128, 128), 128)
            first = here(t).at[y, x][:, columns].astype(f32)
            second = [z_in[w][0, half, :, columns] for half in HALVES]
            if w >= 2:
                third = [z_in[w][4, half, :, columns] for half in HALVES]
                first += jnp.where(is_mid, jnp.concatenate(third, axis=0).astype(f32), 0.0)
            second = jnp.concatenate(second, axis=0).astype(f32)
            for n_out, value in ((w, first), (4 + w, second)):
                if w in (0, 2):
                    outs[n_out][columns, :] = value.T.astype(outs[n_out].dtype)
                elif w == 1:
                    outs[n_out][:, columns] = value.astype(outs[n_out].dtype)
                else:
                    part_columns = pl.ds(pl.multiple_of((n % 2) * 128, 128), 128)
                    outs[n_out][n // 2, :, part_columns] = value.astype(outs[n_out].dtype)
            return carry

        lax.fori_loop(0, WIDTHS[w] // 128, body, 0)

    def turn(w):
        source = (cotangent, entering_two, branch_grad, entering_one)[w]
        for owner in range(OWNERS):
            columns = slice(owner * BLOCK, (owner + 1) * BLOCK)
            place_at = slice((owner // 2) * BLOCK, (owner // 2 + 1) * BLOCK)
            flat = source[:, columns].T
            if w < 2:
                turned[w, owner % 2, place_at, :] = flat
            else:
                turned[TURNED_AT[w], owner % 2, place_at, 0:ROWS] = flat

    def norm_back(source, gain, row, store):
        norm_own[0, row : row + 2, :] = jnp.zeros((2, D), f32)

        def strip(n, carry):
            rows = pl.ds(pl.multiple_of(n * 32, 32), 32)
            values = source[rows, :]
            center = values - jnp.mean(values, axis=-1, keepdims=True)
            scale = lax.rsqrt(jnp.mean(center * center, axis=-1, keepdims=True) + norm_epsilon)
            hat = center * scale
            grad = normed_grad[rows, :]
            norm_own[0, row : row + 1, :] += jnp.sum(grad * hat, axis=0, keepdims=True)
            norm_own[0, row + 1 : row + 2, :] += jnp.sum(grad, axis=0, keepdims=True)
            grad = grad * gain
            inner = jnp.mean(grad * hat, axis=-1, keepdims=True)
            store(rows, scale * (grad - jnp.mean(grad, axis=-1, keepdims=True) - hat * inner))
            return carry

        lax.fori_loop(0, ROWS // 32, strip, 0)

    def residual_back():
        add_came(1, normed_grad)

        def store(rows, part):
            total = part + cotangent[rows, :].astype(f32)
            residual_grad[rows, :] = total
            branch_grad[rows, :] = total.astype(bf16)

        norm_back(residual, norms[2:3, :], 2, store)

    def attend_back(t):
        plane = plane_of(UNITS[t][1])
        attended_grad = dot(branch_grad[...], output_full[plane], NT).astype(bf16)
        scale = HEAD_DIM ** (-0.5)
        for head in range(2):
            span = slice(head * HEAD_DIM, (head + 1) * HEAD_DIM)
            queries, keys_all, probs = softmax_parts(plane, span)
            grad = attended_grad[:, span]
            projected_grad[plane, 2, :, span] = dot(probs.astype(bf16), grad, TN).astype(bf16)
            prob_grad = dot(grad, projected[plane, 2, :, span], NT)
            inner = jnp.sum(probs * prob_grad, axis=-1, keepdims=True)
            score_grad = (probs * (prob_grad - inner)).astype(bf16)
            projected_grad[plane, 0, :, span] = (dot(score_grad, keys_all, NN) * scale).astype(bf16)
            projected_grad[plane, 1, :, span] = (dot(score_grad, queries, TN) * scale).astype(bf16)

    def project_back(n):
        wait_load(n)
        plane, slot = plane_at(LOADS[n][1]), n % SLOTS
        first = n == 8

        def normed(columns):
            total = dot(projected_grad[plane, 0], slots[slot, columns, 0:256], NT)
            for part in (1, 2):
                total += dot(projected_grad[plane, part], slots[slot, columns, part * 256 : (part + 1) * 256], NT)
            if first:
                normed_grad[:, columns] = total
            else:
                normed_grad[:, columns] += total

        tiles(4, 256, normed)

    def norm_step(k):
        return remote(norm_own.at[k], norm_in.at[k], norm_send.at[k], norm_recv.at[k], (sibling, over_x, over_y)[k])

    def norm_plane(d):
        target = device(y, x, c, (z + d) % PLANES)
        return remote(norm_own.at[3], norm_planes.at[z], norm_send.at[2 + d], norm_recv.at[2 + d], target)

    def inputs_back():
        def store(rows, part):
            residual_grad[rows, :] += part

        norm_back(inputs, norms[0:1, :], 0, store)
        norm_step(0).start()

    def norm_hop(k):
        norm_step(k).wait()
        norm_own[k + 1] = norm_own[k] + norm_in[k]
        if k < 2:
            norm_step(k + 1).start()
        else:
            norm_planes[z] = norm_own[3]
            for d in (1, 2, 3):
                norm_plane(d).start()

    def norms_out():
        for d in (1, 2, 3):
            norm_plane(d).wait()
        norm_out[...] = (norm_planes[0] + norm_planes[1]) + (norm_planes[2] + norm_planes[3])

    points_copy = pltpu.make_async_copy(inputs, points_out, out_sem.at[1])

    def points_back():
        slot_of = lax.broadcasted_iota(jnp.int32, (ROWS, ROWS), 0) == members[...]
        chosen = slot_of.astype(f32).astype(bf16)

        def pick(columns):
            rest = residual_grad[:, columns]
            total = jnp.zeros((ROWS, 256), f32)
            for _ in range(3):
                low = rest.astype(bf16)
                total += dot(chosen, low, NN)
                rest = rest - low.astype(f32)
            inputs[:, columns] = total

        tiles(4, 256, pick)
        points_copy.start()

    steps = (
        send_own, take, corner, cross, whole, start_load, wait_load, enter, project_attend, branches, send_cotangent,
        swap_came, widen, narrow_back, widen_back, narrow, latents_done, residual_back, attend_back, project_back,
        turn, produce, join, after_one, after_two, z_pass, finish, inputs_back, norm_hop, norms_out, points_back,
    )
    cotangent_load.start()
    output_load(None).start()
    greet(y, x, c, z)
    for step, *at in SCHEDULE:
        steps[step](*at)
    for w, k in CHUNKS:
        for half in HALVES:
            if w not in SHORT:
                ga_copy(w, k, half).wait_send()
            gb_copy(w, k, half).wait_send()
            gc_copy(w, k, half).wait_send()
    for w in range(4):
        for half in HALVES:
            gz_first(w, half).wait_send()

    @pl.when(is_mid)
    def _():
        for w in (0, 1):
            for half in HALVES:
                gz_across(w, half).wait_send()
                for k in range(3):
                    gz_pass(w, k, half).wait_send()

    for n in range(4):
        swap(n).wait_send()
    for t in range(len(UNITS) - RING, len(UNITS)):
        pair_copy(t).wait_send()
    for t, unit in enumerate(UNITS):
        if unit[1] < OWN:
            for half in HALVES:
                z_copy(t, half, 0, beside).wait_send()
    points_copy.wait()
    latents_copy.wait()


def run_step(shards, points, cotangent, members, layer_norms):
    f32, bf16 = jnp.float32, jnp.bfloat16
    vmem_of = pltpu.VMEM
    blocks = [(WIDTHS[0], BLOCK), (BLOCK, WIDTHS[1]), (WIDTHS[2], BLOCK), (3, BLOCK, 256)]
    out_shape = [jax.ShapeDtypeStruct(blocks[w], bf16 if w < 2 else f32) for w in range(4)]
    out_shape += [jax.ShapeDtypeStruct(s, bf16) for s in blocks]
    out_shape += [jax.ShapeDtypeStruct(s, f32) for s in ((4, D), (ROWS, D), (ROWS, D))]
    out_shape += [jax.ShapeDtypeStruct(((PLANES,) if w < 2 else ()) + SHARDS[w], bf16) for w in range(4)]
    rows_f32, rows_bf16 = vmem_of((ROWS, D), f32), vmem_of((ROWS, D), bf16)
    both_bf16, hidden = vmem_of((2 * ROWS, D), bf16), vmem_of((2, 2 * ROWS, D), bf16)
    parts = vmem_of((PLANES, 3, ROWS, 256), bf16)
    scratch = [rows_f32, rows_bf16, parts, vmem_of((PLANES, ROWS, 256), bf16), rows_f32, rows_f32]
    scratch += [both_bf16, both_bf16, hidden, vmem_of((2, 2 * ROWS, D), f32), hidden]
    scratch += [vmem_of((2, 2, D // 2, 2 * ROWS), bf16), rows_bf16, parts, rows_f32]
    scratch += [vmem_of((2, ROWS, D), bf16)] * 2
    scratch += [vmem_of((SLOTS, D, D), bf16), vmem_of((PLANES, 256, D), bf16), vmem_of((RING, 2, 2, BLOCK, D), bf16)]
    counts = (2, 2, 4, 4)
    scratch += [vmem_of((counts[w], 2, 2, BLOCK, WIDTHS[w]), bf16) for w in range(4)]
    scratch += [vmem_of((counts[w], 2, 2, HALF, WIDTHS[w]), bf16) for w in range(4)]
    scratch += [vmem_of((counts[w], 2, HALF, WIDTHS[w]), bf16) for w in range(4)]
    scratch += [vmem_of((1 if w < 2 else 5, 2, HALF, WIDTHS[w]), bf16) for w in range(4)]
    scratch += [vmem_of((n, 4, D), f32) for n in (4, 3, 4)]
    dma = pltpu.SemaphoreType.DMA
    units = len(UNITS)
    scratch += [dma((len(LOADS), 3)), dma((4,)), dma((3,)), dma((4,)), dma((4,)), dma((4, 5, 2))]
    scratch += [dma((4, 3, 2))] * 7
    scratch += [dma((units,))] * 2 + [dma((units, 2))] * 5 + [dma((4, 5, 2))] + [dma((6,))] * 2
    anywhere, vmem = pl.BlockSpec(memory_space=pl.ANY), pl.BlockSpec(memory_space=pltpu.VMEM)
    result = pl.pallas_call(
        step_kernel,
        out_shape=out_shape,
        in_specs=[anywhere] * 5 + [vmem] * 3,
        out_specs=[vmem] * 9 + [anywhere] * 6,
        scratch_shapes=scratch,
        name="step",
        compiler_params=pltpu.CompilerParams(
            collective_id=0, has_side_effects=True, vmem_limit_bytes=60 << 20
        ),
    )(*shards, cotangent, points, members, layer_norms)
    return result[:4], result[4:8], result[8], result[9], result[10]


UPDATES = ((3, D ** (-0.5)), (2, max(1, D * 4 // LAT) ** (-0.5)), (1, D ** (-0.5)), (0, FF ** (-0.5)))


def update_kernel(*refs):
    given, passed, (norm_sum, norms, norm_first, norm_second) = refs[0:20], refs[20:22], refs[22:26]
    passed_out, new_out, norm_out = refs[26:28], refs[28:48], refs[48:52]
    here, rows_here, new, in_sem, out_sem = refs[52:72], refs[72:74], refs[74:94], refs[94], refs[95]
    loads = [pltpu.make_async_copy(a, b, in_sem.at[n]) for n, (a, b) in enumerate(zip(given, here))]
    loads += [pltpu.make_async_copy(a, b, in_sem.at[20 + n]) for n, (a, b) in enumerate(zip(passed, rows_here))]
    stores = [pltpu.make_async_copy(a, b, out_sem.at[n]) for n, (a, b) in enumerate(zip(new, new_out))]
    stores += [pltpu.make_async_copy(a, b, out_sem.at[20 + n]) for n, (a, b) in enumerate(zip(rows_here, passed_out))]
    for copy in loads:
        copy.start()
    columns = pl.ds(pl.multiple_of(lax.axis_index("dp") * BLOCK, BLOCK), BLOCK)
    gradient = norm_sum[:, columns]
    norm_out[0][...] = gradient
    results = adamw_step(norms[:, columns], gradient, norm_first[...], norm_second[...], 0.2)
    for n in range(3):
        norm_out[1 + n][...] = results[n]
    for n, (_, rate) in enumerate(UPDATES):
        for copy in loads[5 * n : 5 * n + 5]:
            copy.wait()
        first, second, master, one, two = here[5 * n : 5 * n + 5]
        targets = new[5 * n : 5 * n + 5]
        width = first.shape[-1]
        strip = 16 * D // width
        strip = min(strip, first.shape[-2])

        def update(at, rate=rate, first=first, second=second, master=master, one=one, two=two, targets=targets):
            total = first[at].astype(jnp.float32) + second[at].astype(jnp.float32)
            updated, one_new, two_new = adamw_step(master[at], total, one[at], two[at], rate)
            for target, value in zip(targets, (total, updated, one_new, two_new, updated)):
                target[at] = value.astype(target.dtype)

        def step(r, carry, strip=strip, update=update, parts=first.shape[:-2]):
            rows = pl.ds(pl.multiple_of(r * strip, strip), strip)
            if parts:
                for part in range(parts[0]):
                    update((part, rows, slice(None)))
            else:
                update((rows, slice(None)))
            return carry

        lax.fori_loop(0, first.shape[-2] // strip, step, 0)
        for copy in stores[5 * n : 5 * n + 5]:
            copy.start()
    for n in (20, 21):
        loads[n].wait()
        stores[n].start()
    for copy in stores:
        copy.wait()


def run_update(given, passed, norm_sum, norms, norm_first, norm_second):
    f32, bf16 = jnp.float32, jnp.bfloat16
    vmem_of, dma = pltpu.VMEM, pltpu.SemaphoreType.DMA
    new = [(a.shape, bf16 if n == 4 else f32) for a in given[2::5] for n in range(5)]
    norm_new = [(norm_first.shape, f32)] * 4
    rows_new = [(a.shape, a.dtype) for a in passed]
    anywhere, vmem = pl.BlockSpec(memory_space=pl.ANY), pl.BlockSpec(memory_space=pltpu.VMEM)
    scratch = [vmem_of(a.shape, a.dtype) for a in (*given, *passed)] + [vmem_of(*a) for a in new]
    return pl.pallas_call(
        update_kernel,
        out_shape=[jax.ShapeDtypeStruct(*a) for a in rows_new + new + norm_new],
        in_specs=[anywhere] * 22 + [vmem] * 4,
        out_specs=[anywhere] * 22 + [vmem] * 4,
        scratch_shapes=scratch + [dma((22,)), dma((22,))],
        name="update",
        compiler_params=pltpu.CompilerParams(vmem_limit_bytes=60 << 20),
    )(*given, *passed, norm_sum, norms, norm_first, norm_second)


def on_device_cube(
    points,
    members,
    cotangent,
    project_weight,
    output_weight,
    upward_weight,
    downward_weight,
    layer_norms,
    project_master,
    project_first,
    project_second,
    output_master,
    output_first,
    output_second,
    upward_master,
    upward_first,
    upward_second,
    downward_master,
    downward_first,
    downward_second,
    norm_first,
    norm_second,
):
    firsts, seconds, norm_summed, latents, point_gradient = run_step(
        (jnp.transpose(project_weight, (1, 0, 2)), output_weight, upward_weight, downward_weight),
        points,
        cotangent,
        members,
        layer_norms,
    )
    swap = lambda array: jnp.transpose(array, (1, 0, 2))
    states = {
        3: [swap(a) for a in (project_master, project_first, project_second)],
        2: [output_master, output_first, output_second],
        1: [upward_master, upward_first, upward_second],
        0: [downward_master, downward_first, downward_second],
    }
    given = [array for w, _ in UPDATES for array in (firsts[w], seconds[w], *states[w])]
    results = run_update(given, (latents, point_gradient), norm_summed, layer_norms, norm_first, norm_second)
    return (*results[:2], *[swap(a) for a in results[2:7]], *results[7:])


def solution(mesh):
    return jax.shard_map(
        on_device_cube if dict(mesh.shape) == {"dp": 8, "mp": 4} else on_device_any,
        mesh=mesh,
        in_specs=(
            P(("dp", "mp"), None),
            P(("dp", "mp"), None),
            P(("dp", "mp"), None),
            P(None, None, "mp"),
            P("mp", None),
            P(None, "mp"),
            P("mp", None),
            P(),
            P("dp", None, "mp"),
            P("dp", None, "mp"),
            P("dp", None, "mp"),
            P("mp", "dp"),
            P("mp", "dp"),
            P("mp", "dp"),
            P("dp", "mp"),
            P("dp", "mp"),
            P("dp", "mp"),
            P("mp", "dp"),
            P("mp", "dp"),
            P("mp", "dp"),
            P(None, "dp"),
            P(None, "dp"),
        ),
        out_specs=(
            P(("dp", "mp"), None),
            P(("dp", "mp"), None),
            P("dp", None, "mp"),
            P("dp", None, "mp"),
            P("dp", None, "mp"),
            P("dp", None, "mp"),
            P("dp", None, "mp"),
            P("mp", "dp"),
            P("mp", "dp"),
            P("mp", "dp"),
            P("mp", "dp"),
            P("mp", "dp"),
            P("dp", "mp"),
            P("dp", "mp"),
            P("dp", "mp"),
            P("dp", "mp"),
            P("dp", "mp"),
            P("mp", "dp"),
            P("mp", "dp"),
            P("mp", "dp"),
            P("mp", "dp"),
            P("mp", "dp"),
            P(None, "dp"),
            P(None, "dp"),
            P(None, "dp"),
            P(None, "dp"),
        ),
        check_vma=False,
    )
```

```python
import jax
import jax.numpy as jnp
from jax import lax
from jax.experimental import pallas as pl
from jax.experimental.pallas import tpu as pltpu
from jax.sharding import PartitionSpec as P

D = 1024
HEAD_DIM = 128
FF = 4096
LAT = 256
ADAM_STEP = 10


norm_epsilon = 1e-05
beta_one = 0.9
beta_two = 0.95
adam_epsilon = 1e-08
weight_decay = 0.1
masked_score = -1e30


def layer_norm(values, norm_gain, norm_shift):
    center = values - jnp.mean(values, axis=-1, keepdims=True)
    spread = jnp.mean(center * center, axis=-1, keepdims=True)
    return center * lax.rsqrt(spread + norm_epsilon) * norm_gain + norm_shift


def pick_rows(source_rows, row_index):
    return source_rows[row_index]


def adamw_step(weight, gradient, moment_one, moment_two, step_rate):
    one_new = beta_one * moment_one + (1.0 - beta_one) * gradient
    two_new = beta_two * moment_two + (1.0 - beta_two) * gradient * gradient
    corrected_one = one_new / (1.0 - beta_one**ADAM_STEP)
    corrected_two = two_new / (1.0 - beta_two**ADAM_STEP)
    updated = weight - step_rate * (
        corrected_one / (jnp.sqrt(corrected_two) + adam_epsilon) + weight_decay * weight
    )
    return (updated, one_new, two_new)


def masked_scores(queries, keys_all, key_mask, score_scale):
    raw_scores = (
        jnp.einsum("gqhe,gkhe->ghqk", queries, keys_all, preferred_element_type=jnp.float32)
        * score_scale
    )
    return jnp.where(key_mask, raw_scores, masked_score)


def on_device_any(
    points,
    members,
    cotangent,
    project_weight,
    output_weight,
    upward_weight,
    downward_weight,
    layer_norms,
    project_master,
    project_first,
    project_second,
    output_master,
    output_first,
    output_second,
    upward_master,
    upward_first,
    upward_second,
    downward_master,
    downward_first,
    downward_second,
    norm_first,
    norm_second,
):
    groups_here = members.shape[0]
    shard_rows = points.shape[0]
    model_width = points.shape[1]
    heads_here = project_weight.shape[2] // HEAD_DIM
    score_scale = HEAD_DIM ** (-0.5)
    grouped = points.reshape(groups_here, LAT, model_width)
    slot_index = jnp.maximum(members, 0)
    key_live = members >= 0
    picked = jax.vmap(pick_rows)(grouped, slot_index)
    inputs = jnp.where(key_live[:, :, None], picked.astype(jnp.float32), 0.0).reshape(
        shard_rows, model_width
    )
    normed, norm_back_one = jax.vjp(layer_norm, inputs, layer_norms[0], layer_norms[1])
    gathered, live_all = (
        lax.all_gather(normed.astype(jnp.bfloat16), "mp", axis=0, tiled=True),
        lax.all_gather(key_live.astype(jnp.bfloat16), "mp", axis=0, tiled=True),
    )
    total_rows = gathered.shape[0]
    total_groups = live_all.shape[0]
    key_mask = (live_all > 0)[:, None, None, :]
    projected = jnp.einsum(
        "rd,dcf->rcf", gathered, project_weight, preferred_element_type=jnp.float32
    ).astype(jnp.bfloat16)
    heads_view = projected.reshape(total_groups, LAT, 3, heads_here, HEAD_DIM)
    queries = heads_view[:, :, 0]
    keys_all = heads_view[:, :, 1]
    values_all = heads_view[:, :, 2]
    scores = masked_scores(queries, keys_all, key_mask, score_scale)
    row_top = jnp.max(scores, axis=-1, keepdims=True)
    exponent = jnp.exp(scores - row_top)
    row_total = jnp.sum(exponent, axis=-1, keepdims=True)
    attention_weights = exponent / row_total
    log_total = row_top + jnp.log(row_total)
    weights_low = attention_weights.astype(jnp.bfloat16)
    attended = jnp.einsum(
        "ghqk,gkhe->gqhe", weights_low, values_all, preferred_element_type=jnp.float32
    ).astype(jnp.bfloat16)
    attended = attended.reshape(total_rows, heads_here * HEAD_DIM)
    branch = lax.psum_scatter(
        jnp.dot(attended, output_weight, preferred_element_type=jnp.float32),
        "mp",
        scatter_dimension=0,
        tiled=True,
    )
    residual = inputs + branch
    normed_two, norm_back_two = jax.vjp(layer_norm, residual, layer_norms[2], layer_norms[3])
    gathered_two = lax.all_gather(normed_two.astype(jnp.bfloat16), "mp", axis=0, tiled=True)
    upward = jnp.dot(gathered_two, upward_weight, preferred_element_type=jnp.float32)
    activated_float, gelu_back = jax.vjp(jax.nn.gelu, upward)
    activated = activated_float.astype(jnp.bfloat16)
    latents = residual + lax.psum_scatter(
        jnp.dot(activated, downward_weight, preferred_element_type=jnp.float32).astype(
            jnp.bfloat16
        ),
        "mp",
        scatter_dimension=0,
        tiled=True,
    ).astype(jnp.float32)
    cotangent_all = lax.all_gather(cotangent, "mp", axis=0, tiled=True)
    downward_local = jnp.einsum(
        "rf,rd->fd", activated, cotangent_all, preferred_element_type=jnp.float32
    )
    activated_grad = jnp.einsum(
        "rd,fd->rf", cotangent_all, downward_weight, preferred_element_type=jnp.float32
    )
    upward_grad = gelu_back(activated_grad)[0].astype(jnp.bfloat16)
    upward_local = jnp.einsum(
        "rd,rf->df", gathered_two, upward_grad, preferred_element_type=jnp.float32
    )
    normed_two_grad = lax.psum_scatter(
        jnp.einsum("rf,df->rd", upward_grad, upward_weight, preferred_element_type=jnp.float32),
        "mp",
        scatter_dimension=0,
        tiled=True,
    )
    residual_part, gain_two_grad, shift_two_grad = norm_back_two(normed_two_grad)
    residual_grad = residual_part + cotangent.astype(jnp.float32)
    norm_two_local = jnp.stack([gain_two_grad, shift_two_grad])
    branch_grad = lax.all_gather(residual_grad.astype(jnp.bfloat16), "mp", axis=0, tiled=True)
    output_local = jnp.einsum(
        "rh,rd->hd", attended, branch_grad, preferred_element_type=jnp.float32
    )
    attended_grad = jnp.einsum(
        "rd,hd->rh", branch_grad, output_weight, preferred_element_type=jnp.float32
    ).astype(jnp.bfloat16)
    attended_grad = attended_grad.reshape(total_groups, LAT, heads_here, HEAD_DIM)
    scores_again = masked_scores(queries, keys_all, key_mask, score_scale)
    weights_again = jnp.exp(scores_again - log_total)
    weights_again_low = weights_again.astype(jnp.bfloat16)
    value_grad = jnp.einsum(
        "ghqk,gqhe->gkhe", weights_again_low, attended_grad, preferred_element_type=jnp.float32
    ).astype(jnp.bfloat16)
    weight_grad = jnp.einsum(
        "gqhe,gkhe->ghqk", attended_grad, values_all, preferred_element_type=jnp.float32
    )
    score_grad = (
        weights_again * (weight_grad - jnp.sum(weights_again * weight_grad, axis=-1, keepdims=True))
    ).astype(jnp.bfloat16)
    query_grad = (
        jnp.einsum("ghqk,gkhe->gqhe", score_grad, keys_all, preferred_element_type=jnp.float32)
        * score_scale
    ).astype(jnp.bfloat16)
    key_grad = (
        jnp.einsum("ghqk,gqhe->gkhe", score_grad, queries, preferred_element_type=jnp.float32)
        * score_scale
    ).astype(jnp.bfloat16)
    projected_grad = jnp.stack([query_grad, key_grad, value_grad], axis=2).reshape(
        total_rows, 3, heads_here * HEAD_DIM
    )
    project_local = jnp.einsum(
        "rd,rcf->dcf", gathered, projected_grad, preferred_element_type=jnp.float32
    )
    normed_grad = lax.psum_scatter(
        jnp.einsum(
            "rcf,dcf->rd", projected_grad, project_weight, preferred_element_type=jnp.float32
        ).astype(jnp.bfloat16),
        "mp",
        scatter_dimension=0,
        tiled=True,
    ).astype(jnp.float32)
    input_part, gain_one_grad, shift_one_grad = norm_back_one(normed_grad)
    input_grad = input_part + residual_grad
    norm_one_local = jnp.stack([gain_one_grad, shift_one_grad])
    matches = members[:, :, None] == jnp.arange(LAT, dtype=jnp.int32)[None, None, :]
    slot_of = jnp.argmax(matches, axis=1)
    point_used = jnp.any(matches, axis=1)
    grouped_grad = input_grad.reshape(groups_here, LAT, model_width)
    point_gradient = jnp.where(
        point_used[:, :, None], jax.vmap(pick_rows)(grouped_grad, slot_of), 0.0
    ).reshape(shard_rows, model_width)
    (
        project_summed,
        output_summed,
        upward_summed,
        downward_summed,
        norm_one_summed,
        norm_two_summed,
    ) = (
        lax.psum_scatter(project_local, "dp", scatter_dimension=0, tiled=True),
        lax.psum_scatter(output_local, "dp", scatter_dimension=1, tiled=True),
        lax.psum_scatter(upward_local, "dp", scatter_dimension=0, tiled=True),
        lax.psum_scatter(downward_local, "dp", scatter_dimension=1, tiled=True),
        lax.psum_scatter(norm_one_local, "dp", scatter_dimension=1, tiled=True),
        lax.psum_scatter(norm_two_local, "dp", scatter_dimension=1, tiled=True),
    )
    norm_gradient = lax.psum(jnp.concatenate([norm_one_summed, norm_two_summed], axis=0), "mp")
    data_index = lax.axis_index("dp")
    norm_columns = norm_first.shape[1]
    norm_current = lax.dynamic_slice_in_dim(layer_norms, data_index * norm_columns, norm_columns, 1)
    project_new = adamw_step(
        project_master, project_summed, project_first, project_second, D ** (-0.5)
    )
    output_new = adamw_step(
        output_master, output_summed, output_first, output_second, max(1, D * 4 // LAT) ** (-0.5)
    )
    upward_new = adamw_step(upward_master, upward_summed, upward_first, upward_second, D ** (-0.5))
    downward_new = adamw_step(
        downward_master, downward_summed, downward_first, downward_second, FF ** (-0.5)
    )
    norm_new = adamw_step(norm_current, norm_gradient, norm_first, norm_second, 0.2)
    return (
        latents,
        point_gradient,
        project_summed,
        project_new[0],
        project_new[1],
        project_new[2],
        project_new[0].astype(jnp.bfloat16),
        output_summed,
        output_new[0],
        output_new[1],
        output_new[2],
        output_new[0].astype(jnp.bfloat16),
        upward_summed,
        upward_new[0],
        upward_new[1],
        upward_new[2],
        upward_new[0].astype(jnp.bfloat16),
        downward_summed,
        downward_new[0],
        downward_new[1],
        downward_new[2],
        downward_new[0].astype(jnp.bfloat16),
        norm_gradient,
        norm_new[0],
        norm_new[1],
        norm_new[2],
    )


MESH = pl.DeviceIdType.MESH
PLANES = 4
OWNERS = 8
ROWS = LAT
HALVES = (0, 1)
SHARDS = ((3, D, 256), (256, D), (D, D), (D, D))
SHORT = ()
CHUNKS = [(w, k) for w in (0, 1) for k in range(3)] + [(2, 0), (3, 0)]
SLOTS = 4
LOADS = (
    (0, None), (0, 0), (0, 1), (0, 2), (2, None), (2, 0), (3, None), (3, 0), (0, 2), (0, 1), (0, 0), (0, None),
)

WIDTHS = (D, D, 256, 3 * 256)
BLOCK = D // OWNERS
HALF = BLOCK // 2
RING = 2
OWN = PLANES - 1
UNITS = (
    (0, 0), (0, 3), (1, 0), (1, 3), (3, 0), (3, 1), (3, 2), (3, 3), (2, 0), (2, 1), (2, 2), (2, 3),
)
EARLY = (3,)
TURNED_AT = (0, 1, 1, 0)
(
    SEND_OWN, TAKE, CORNER, CROSS, WHOLE, LOAD, READY, ENTER, PROJECT, BRANCH, SEND_COTANGENT, CAME, WIDEN,
    NARROW_BACK, WIDEN_BACK, NARROW, LATENTS, RESIDUAL, ATTEND, INWARD, TURN, PRODUCE, JOIN, ONE, TWO, ALONG,
    LAST, FINISH, INPUTS, NORM, NORMS_OUT, POINTS,
) = range(32)
SCHEDULE = (
    (SEND_OWN, 0), (LOAD, 0), (SEND_OWN, 1), (ENTER,), (TAKE, 0, 0, 0), (TAKE, 0, 1, 0), (TAKE, 0, 0, 1),
    (TAKE, 0, 1, 1), (TAKE, 1, 0, 1), (TAKE, 1, 0, 0), (TAKE, 0, 2, 0), (SEND_OWN, 2), (CORNER, 0, 0, 1),
    (CORNER, 0, 1, 0), (CORNER, 0, 2, 0), (CORNER, 1, 0, 1), (CORNER, 0, 1, 1), (TAKE, 1, 1, 0), (TAKE, 0, 2, 1),
    (CROSS, 0, 0, 1), (CORNER, 0, 0, 0), (TAKE, 1, 1, 1), (TAKE, 1, 2, 1), (PROJECT, 0), (CORNER, 1, 0, 0),
    (CROSS, 0, 1, 0), (TAKE, 1, 2, 0), (SEND_OWN, 3), (CORNER, 0, 2, 1), (CROSS, 0, 1, 1), (CORNER, 1, 2, 0),
    (CORNER, 1, 1, 0), (CROSS, 1, 0, 1), (CROSS, 0, 2, 0), (LOAD, 4), (SEND_COTANGENT,), (CROSS, 0, 0, 0),
    (CORNER, 1, 1, 1), (CORNER, 1, 2, 1), (WHOLE, 0, 0), (LOAD, 1), (CROSS, 0, 2, 1), (CROSS, 1, 0, 0),
    (TAKE, 2, 0, 1), (TAKE, 2, 0, 0), (WHOLE, 0, 1), (TAKE, 3, 0, 0), (READY, 4), (CROSS, 1, 2, 0), (WHOLE, 0, 2),
    (LOAD, 2), (LOAD, 3), (PROJECT, 1), (TAKE, 3, 0, 1), (CROSS, 1, 1, 1), (CROSS, 1, 1, 0), (CROSS, 1, 2, 1),
    (PROJECT, 2), (LOAD, 6), (WHOLE, 1, 0), (WHOLE, 1, 2), (CORNER, 2, 0, 1), (WHOLE, 1, 1), (CORNER, 2, 0, 0),
    (PROJECT, 3), (BRANCH,), (WIDEN, 0, 0), (CORNER, 3, 0, 0), (CAME, 0), (CORNER, 3, 0, 1), (READY, 6),
    (CROSS, 2, 0, 0), (CROSS, 2, 0, 1), (NARROW_BACK, 0, 0), (WHOLE, 2, 0), (LOAD, 5), (TURN, 0), (CROSS, 3, 0, 0),
    (CROSS, 3, 0, 1), (READY, 5), (WIDEN, 1, 0), (CAME, 1), (WIDEN, 1, 1), (PRODUCE, 0), (WIDEN, 0, 1), (WHOLE, 3, 0),
    (LOAD, 7), (PRODUCE, 1), (JOIN, 0), (READY, 7), (NARROW_BACK, 1, 1), (NARROW_BACK, 0, 1), (WIDEN_BACK, 1),
    (JOIN, 1), (NARROW_BACK, 1, 0), (TURN, 1), (PRODUCE, 2), (ONE, 0, 0), (PRODUCE, 3), (ONE, 0, 1), (NARROW, 1),
    (JOIN, 2), (TURN, 3), (JOIN, 3), (WIDEN_BACK, 0), (RESIDUAL,), (TWO, 0, 1), (ATTEND, 4), (ONE, 2, 1), (ONE, 2, 0),
    (PRODUCE, 4), (ATTEND, 5), (TWO, 0, 0), (JOIN, 4), (PRODUCE, 5), (ATTEND, 7), (TWO, 2, 1), (JOIN, 5), (TWO, 2, 0),
    (ATTEND, 6), (PRODUCE, 6), (PRODUCE, 7), (ONE, 3, 1), (LOAD, 8), (LOAD, 9), (ONE, 4, 0), (TURN, 2), (JOIN, 6),
    (PRODUCE, 8), (INWARD, 8), (PRODUCE, 9), (JOIN, 8), (ONE, 4, 1), (NARROW, 0), (JOIN, 9), (LOAD, 10), (ONE, 5, 0),
    (PRODUCE, 10), (ONE, 1, 0), (ONE, 5, 1), (INWARD, 9), (LOAD, 11), (ALONG, 4, 0), (ONE, 1, 1), (TWO, 3, 1),
    (ONE, 8, 1), (PRODUCE, 11), (INWARD, 10), (INWARD, 11), (JOIN, 11), (ONE, 6, 0), (ALONG, 4, 1), (JOIN, 10),
    (INPUTS,), (ONE, 8, 0), (ALONG, 6, 0), (TWO, 1, 0), (ALONG, 5, 0), (ONE, 9, 0), (JOIN, 7), (ONE, 10, 0),
    (TWO, 8, 0), (NORM, 0), (ONE, 9, 1), (TWO, 8, 1), (TWO, 1, 1), (ONE, 10, 1), (ONE, 3, 0), (ALONG, 5, 1),
    (ONE, 6, 1), (ONE, 11, 1), (ALONG, 6, 1), (TWO, 9, 0), (POINTS,), (ONE, 7, 1), (NORM, 1), (TWO, 9, 1),
    (FINISH, 0), (TWO, 10, 0), (ALONG, 8, 1), (ONE, 7, 0), (ONE, 11, 0), (TWO, 10, 1), (LAST, 3, 0), (ALONG, 8, 0),
    (LATENTS,), (NORM, 2), (TWO, 3, 0), (FINISH, 1), (TWO, 11, 1), (LAST, 3, 1), (ALONG, 10, 1), (ALONG, 9, 0),
    (ALONG, 10, 0), (ALONG, 9, 1), (NORMS_OUT,), (TWO, 11, 0), (FINISH, 2), (FINISH, 3),
)
NN = ((1,), (0,))
NT = ((1,), (1,))
TN = ((0,), (0,))


def place():
    dp = lax.axis_index("dp")
    return dp // 4, (dp // 2) % 2, dp % 2, lax.axis_index("mp")


def device(y, x, c, z):
    return (y * 4 + x * 2 + c, z)


def greet(y, x, c, z):
    barrier = pltpu.get_barrier_semaphore()
    partners = [device(1 - y, x, c, z), device(y, 1 - x, c, z), device(y, x, 1 - c, z)]
    partners += [device(y, x, c, (z + d) % PLANES) for d in (1, 2, 3)]
    for partner in partners:
        pl.semaphore_signal(barrier, inc=1, device_id=partner, device_id_type=MESH)
    pl.semaphore_wait(barrier, len(partners))


def arrival(z, k):
    return (z + 1 - 2 * (z % 2), 2 - z // 2, 3 - 3 * (z // 2))[k]


def dot(a, b, contract):
    return lax.dot_general(a, b, (contract, ((), ())), preferred_element_type=jnp.float32)


def tiles(count, size, body):
    def step(n, carry):
        body(pl.ds(pl.multiple_of(n * size, size), size))
        return carry

    lax.fori_loop(0, count, step, 0)


def norm_rows(source, target, gain, shift, strip=64):
    def step(n, carry):
        rows = pl.ds(pl.multiple_of(n * strip, strip), strip)
        target[rows, :] = layer_norm(source[rows, :], gain, shift).astype(target.dtype)
        return carry

    lax.fori_loop(0, ROWS // strip, step, 0)


def step_kernel(*refs):
    f32, bf16 = jnp.float32, jnp.bfloat16
    shards, cotangent_in, (points, members, norms) = refs[0:4], refs[4], refs[5:8]
    outs, norm_out, latents_out, points_out, fulls = refs[8:16], refs[16], refs[17], refs[18], refs[19:23]
    inputs, entering_one, projected, attended, residual, latents = refs[23:29]
    entering_two, cotangent, activated, slope, upward_grad = refs[29:34]
    turned, branch_grad, projected_grad, normed_grad, sent, came = refs[34:40]
    slots, output_full, ring = refs[40:43]
    acc, one_in, two_in, z_in = refs[43:47], refs[47:51], refs[51:55], refs[55:59]
    norm_own, norm_in, norm_planes = refs[59:62]
    load_sem, output_sem, out_sem, swap_send, swap_recv = refs[62:67]
    gz_send, gz_recv, ga_send, ga_recv, gb_send, gb_recv, gc_send, gc_recv = refs[67:75]
    c_send, c_recv, one_send, one_recv, two_send, two_recv, z_send, z_recv = refs[75:83]
    norm_send, norm_recv = refs[83:85]
    residual_grad = residual
    y, x, c, z = place()
    is_mid = jnp.logical_or(z == 1, z == 2)
    is_end = jnp.logical_not(is_mid)
    sibling = device(y, x, 1 - c, z)
    over_x, over_y = device(y, 1 - x, c, z), device(1 - y, x, c, z)
    beside, across = device(y, x, c, arrival(z, 0)), device(y, x, c, 3 - z)
    opposite = device(y, x, c, (z + 2) % PLANES)

    def plane_at(k):
        return z if k is None else arrival(z, k)

    def plane_of(i):
        return z if i == OWN else arrival(z, 2 - i)

    def remote(src, dst, send, recv, target):
        return pltpu.make_async_remote_copy(
            src_ref=src, dst_ref=dst, send_sem=send, recv_sem=recv, device_id=target, device_id_type=MESH
        )

    def rows_of(ref, w, rows):
        return ref.at[:, rows, :] if w == 0 else ref.at[rows, :]

    def view(w, plane, rows):
        return fulls[w].at[rows, :] if w >= 2 else rows_of(fulls[w].at[plane], w, rows)

    def block(w, half, first, count):
        height = SHARDS[w][-2]
        start = pl.multiple_of(half * (height // 2) + first * (height // 16), height // 16)
        return pl.ds(start, count * (height // 16))

    spot = (c * 4 + y * 2 + x, c * 4 + x * 2 + y)
    pair = (c * 4 + y * 2, c * 4 + x * 2)

    def gz_rows(w, half):
        return block(w, half, pair[half], 2) if w in SHORT else block(w, half, spot[half], 1)

    def gz_own(w, half, lane, slot, target):
        rows = gz_rows(w, half)
        send, recv = gz_send.at[w, lane, half], gz_recv.at[w, slot, half]
        return remote(rows_of(shards[w], w, rows), view(w, z, rows), send, recv, target)

    def gz_first(w, half):
        return gz_own(w, half, 0, 0, opposite if w >= 2 else beside)

    def gz_across(w, half):
        return gz_own(w, half, 1, 1, across)

    def gz_foreign(w, k, half, lane, slot, target):
        here = view(w, arrival(z, k), gz_rows(w, half))
        return remote(here, here, gz_send.at[w, lane, half], gz_recv.at[w, slot, half], target)

    def gz_pass(w, k, half):
        lane, target, slot = ((2, across, 2), (3, beside, 1), (4, beside, 2))[k]
        return gz_foreign(w, k, half, lane, slot, target)

    def gz_arrived(w, k, half):
        return gz_foreign(w, k, half, 0, k, beside)

    def ga_copy(w, k, half):
        here = view(w, arrival(z, k), block(w, half, spot[half], 1))
        return remote(here, here, ga_send.at[w, k, half], ga_recv.at[w, k, half], (over_x, over_y)[half])

    def gb_copy(w, k, half):
        here = view(w, arrival(z, k), block(w, half, pair[half], 2))
        return remote(here, here, gb_send.at[w, k, half], gb_recv.at[w, k, half], (over_y, over_x)[half])

    def gc_copy(w, k, half):
        here = view(w, arrival(z, k), block(w, half, c * 4, 4))
        return remote(here, here, gc_send.at[w, k, half], gc_recv.at[w, k, half], sibling)

    def send_own(w):
        for half in HALVES:
            gz_first(w, half).start()
        if w < 2:

            @pl.when(is_mid)
            def _():
                for half in HALVES:
                    gz_across(w, half).start()

    def take(w, k, half):
        gz_arrived(w, k, half).wait_recv()
        (gb_copy if w in SHORT else ga_copy)(w, k, half).start()
        if w < 2:

            @pl.when(is_mid)
            def _():
                gz_pass(w, k, half).start()

    def corner(w, k, half):
        ga_copy(w, k, half).wait_recv()
        gb_copy(w, k, half).start()

    def cross(w, k, half):
        gb_copy(w, k, half).wait_recv()
        gc_copy(w, k, half).start()

    def whole(w, k):
        for half in HALVES:
            gc_copy(w, k, half).wait_recv()
        if w == 1:
            output_load(k).start()

    def loads(n):
        w, k = LOADS[n]
        if w >= 2:
            source = shards[w] if k is None else fulls[w]
            return [pltpu.make_async_copy(source, slots.at[n % SLOTS], load_sem.at[n, 0])]
        source = shards[w] if k is None else fulls[w].at[arrival(z, k)]
        return [
            pltpu.make_async_copy(
                source.at[part], slots.at[n % SLOTS, :, part * 256 : (part + 1) * 256], load_sem.at[n, part]
            )
            for part in range(3)
        ]

    def start_load(n):
        for copy in loads(n):
            copy.start()

    def wait_load(n):
        for copy in loads(n):
            copy.wait()

    def output_load(k):
        source = shards[1] if k is None else fulls[1].at[arrival(z, k)]
        return pltpu.make_async_copy(source, output_full.at[plane_at(k)], output_sem.at[3 if k is None else k])

    mine, theirs = pl.ds(0, ROWS), pl.ds(ROWS, ROWS)

    def swap(n):
        src, dst = (
            (cotangent.at[mine], cotangent.at[theirs]),
            (entering_two.at[mine], entering_two.at[theirs]),
            (sent.at[0], came.at[0]),
            (sent.at[1], came.at[1]),
        )[n]
        return remote(src, dst, swap_send.at[n], swap_recv.at[n], beside)

    cotangent_load = pltpu.make_async_copy(cotangent_in, cotangent.at[mine], out_sem.at[2])

    def send_cotangent():
        cotangent_load.wait()
        swap(0).start()

    def swap_came(n):
        swap(n).wait_recv()

    def enter():
        slot_of = lax.broadcasted_iota(jnp.int32, (ROWS, ROWS), 0) == members[...]
        chosen = slot_of.astype(f32).astype(bf16)

        def pick(columns):
            inputs[:, columns] = dot(chosen, points[:, columns], TN)

        tiles(4, 256, pick)
        norm_rows(inputs, entering_one, norms[0:1, :], norms[1:2, :])
        residual[...] = inputs[...]

    def softmax_parts(plane, span):
        queries, keys_all = projected[plane, 0, :, span], projected[plane, 1, :, span]
        scores = jnp.where(members[...] >= 0, dot(queries, keys_all, NT) * HEAD_DIM ** (-0.5), masked_score)
        exponent = jnp.exp(scores - jnp.max(scores, axis=-1, keepdims=True))
        return queries, keys_all, exponent * (1.0 / jnp.sum(exponent, axis=-1, keepdims=True))

    def project_attend(n):
        wait_load(n)
        plane, slot = plane_at(LOADS[n][1]), n % SLOTS
        for part in range(3):
            right = slots[slot, :, part * 256 : (part + 1) * 256]
            projected[plane, part] = dot(entering_one[...], right, NN).astype(bf16)
        for head in range(2):
            span = slice(head * HEAD_DIM, (head + 1) * HEAD_DIM)
            probs = softmax_parts(plane, span)[2]
            attended[plane, :, span] = dot(probs.astype(bf16), projected[plane, 2, :, span], NN).astype(bf16)

    def branches():
        for k in (None, 0, 1, 2):
            plane = plane_at(k)
            output_load(k).wait()

            def body(columns):
                residual[:, columns] += dot(attended[plane], output_full[plane, :, columns], NN)

            tiles(4, 256, body)
        norm_rows(residual, entering_two, norms[2:3, :], norms[3:4, :])
        swap(1).start()
        latents[...] = residual[...]

    def rows_at(b):
        return theirs if b else mine

    def widen(j, b):
        rows = rows_at(b)

        def body(columns):
            u = dot(entering_two[rows, :], slots[j, :, columns], NN)
            square = u * u
            bend = jnp.tanh(0.7978845608028654 * u * (1.0 + 0.044715 * square))
            activated[j, rows, columns] = (0.5 * u * (1.0 + bend)).astype(bf16)
            slope[j, rows, columns] = 0.5 * (1.0 + bend) + 0.5 * u * (1.0 - bend * bend) * (
                0.7978845608028654 * (1.0 + 3.0 * 0.044715 * square)
            )

        tiles(4, 256, body)

    def narrow_back(j, b):
        rows = rows_at(b)

        def body(columns):
            product = dot(cotangent[rows, :], slots[2 + j, columns, :], NT)
            upward_grad[j, rows, columns] = (product * slope[j, rows, columns]).astype(bf16)

        tiles(4, 256, body)

    def widen_back(b):
        rows = rows_at(b)

        def body(columns):
            total = dot(upward_grad[0, rows, :], slots[0, columns, :], NT)
            total += dot(upward_grad[1, rows, :], slots[1, columns, :], NT)
            if b:
                sent[1, :, columns] = total.astype(bf16)
            else:
                normed_grad[:, columns] = total

        tiles(4, 256, body)
        if b:
            swap(3).start()

    def narrow(b):
        rows = rows_at(b)

        def body(columns):
            total = dot(activated[0, rows, :], slots[2, :, columns], NN)
            total += dot(activated[1, rows, :], slots[3, :, columns], NN)
            if b:
                sent[0, :, columns] = total.astype(bf16)
            else:
                latents[:, columns] += total

        tiles(4, 256, body)
        if b:
            swap(2).start()

    latents_copy = pltpu.make_async_copy(latents, latents_out, out_sem.at[0])

    def add_came(n, target):
        swap_came(2 + n)

        def strip(r, carry):
            rows = pl.ds(pl.multiple_of(r * 32, 32), 32)
            target[rows, :] += came[n, rows, :].astype(f32)
            return carry

        lax.fori_loop(0, ROWS // 32, strip, 0)

    def latents_done():
        add_came(0, latents)
        latents_copy.start()

    def here(t):
        w, i = UNITS[t]
        return acc[w].at[i if w >= 2 else i // OWN]

    def pair_copy(t):
        w = UNITS[t][0]
        return remote(ring.at[t % RING, :, :, :, 0 : WIDTHS[w]], here(t), c_send.at[t], c_recv.at[t], sibling)

    def half_rows(half):
        return pl.ds(half * HALF, HALF)

    def one_in_at(t, half):
        w, i = UNITS[t]
        return one_in[w].at[i if w >= 2 else i // OWN, half]

    def two_in_at(t, half):
        w, i = UNITS[t]
        return two_in[w].at[0 if w in EARLY else i if w >= 2 else i // OWN, half]

    def one_copy(t, half):
        rows = half_rows(half)
        src = here(t).at[1 - y, :, rows] if half == 0 else here(t).at[:, 1 - x, rows]
        send, recv = one_send.at[t, half], one_recv.at[t, half]
        return remote(src, one_in_at(t, half), send, recv, (over_y, over_x)[half])

    def two_copy(t, half):
        rows = half_rows(half)
        src = here(t).at[y, 1 - x, rows] if half == 0 else here(t).at[1 - y, x, rows]
        send, recv = two_send.at[t, half], two_recv.at[t, half]
        return remote(src, two_in_at(t, half), send, recv, (over_x, over_y)[half])

    def z_piece(t, half):
        rows = half_rows(half)
        if UNITS[t][0] in EARLY:
            return here(t).at[y, :, rows] if half == 0 else here(t).at[:, x, rows]
        return here(t).at[y, x, rows]

    def z_copy(t, half, slot, target):
        w = UNITS[t][0]
        send, recv = z_send.at[t, half], z_recv.at[w, slot, half]
        return remote(z_piece(t, half), z_in[w].at[slot, half], send, recv, target)

    def z_add(t, half, slot):
        w = UNITS[t][0]
        z_copy(t, half, slot, beside).wait_recv()
        piece = z_piece(t, half)
        if w in EARLY:
            for k in (0, 1):
                add_rows(piece.at[k], z_in[w].at[slot, half, k])
        else:
            add_rows(piece, z_in[w].at[slot, half])

    def z_first(t, half):
        w, i = UNITS[t]
        if w < 2:
            z_copy(t, half, 0, opposite).start()
            return

        @pl.when(is_end)
        def _():
            z_copy(t, half, 2 - i, beside).start()

    def z_pass(t, half):
        i = UNITS[t][1]

        @pl.when(is_mid)
        def _():
            z_add(t, half, (2, 1, 3)[i])
            z_copy(t, half, (3, 4, 0)[i], (across, across, beside)[i]).start()

    def add_rows(target, source):
        def body(r, carry):
            rows = pl.ds(pl.multiple_of(r * 16, 16), 16)
            target[rows] = (target[rows].astype(f32) + source[rows].astype(f32)).astype(bf16)
            return carry

        lax.fori_loop(0, HALF // 16, body, 0)

    def partial(w, i, parity, columns, n):
        if w < 2:
            right = (activated, upward_grad)[w][1 - i // OWN, :, columns]
            return dot(turned[w, parity], right, NN)
        plane = plane_of(i)
        right = projected_grad[plane, n] if w == 3 else attended[plane, :, columns]
        return dot(turned[TURNED_AT[w], parity, :, 0:ROWS], right, NN)

    def over_tiles(w, body):
        if w == 2:
            body(pl.ds(0, 256), 0)
            return

        def step(n, carry):
            body(pl.ds(pl.multiple_of(n * 256, 256), 256), n)
            return carry

        lax.fori_loop(0, WIDTHS[w] // 256, step, 0)

    def produce(t):
        w, i = UNITS[t]
        if t >= RING:
            pair_copy(t - RING).wait_send()

        def body(columns, n):
            product = partial(w, i, 1 - c, columns, n).astype(bf16)
            for k in range(4):
                ring[t % RING, k // 2, k % 2, :, columns] = product[k * BLOCK : (k + 1) * BLOCK]

        over_tiles(w, body)
        pair_copy(t).start()

    def join(t):
        w, i = UNITS[t]
        at = i if w >= 2 else i // OWN
        pair_copy(t).wait_recv()

        def body(columns, n):
            product = partial(w, i, c, columns, n)
            for k in range(4):
                other = acc[w][at, k // 2, k % 2, :, columns].astype(f32)
                acc[w][at, k // 2, k % 2, :, columns] = (product[k * BLOCK : (k + 1) * BLOCK] + other).astype(bf16)

        over_tiles(w, body)
        for half in HALVES:
            one_copy(t, half).start()

    def after_one(t, half):
        one_copy(t, half).wait()
        rows = half_rows(half)
        for k in (0, 1):
            target = here(t).at[y, k, rows] if half == 0 else here(t).at[k, x, rows]
            add_rows(target, one_in_at(t, half).at[k])
        if UNITS[t][0] not in EARLY:
            two_copy(t, half).start()
        elif UNITS[t][1] < OWN:
            z_first(t, half)

    def after_two(t, half):
        two_copy(t, half).wait()
        add_rows(here(t).at[y, x, half_rows(half)], two_in_at(t, half))
        if UNITS[t][1] < OWN:
            z_first(t, half)

    def own_hop(w, half):
        t = UNITS.index((w, OWN))
        z_add(t, half, 0)
        if w >= 2:

            @pl.when(is_mid)
            def _():
                z_add(t, half, 4)

        two_copy(t, half).start()

    def finish(w):
        t = UNITS.index((w, OWN))
        for half in HALVES:
            if w in EARLY:
                two_copy(t, half).wait()
            else:
                z_copy(t, half, 0, beside).wait_recv()
        if w >= 2 and w not in EARLY:

            @pl.when(is_mid)
            def _():
                for half in HALVES:
                    z_copy(t, half, 4, across).wait_recv()

        def body(n, carry):
            columns = pl.ds(pl.multiple_of(n * 128, 128), 128)
            first = here(t).at[y, x][:, columns].astype(f32)
            if w in EARLY:
                second = [two_in[w][0, half, :, columns] for half in HALVES]
            else:
                second = [z_in[w][0, half, :, columns] for half in HALVES]
            if w >= 2 and w not in EARLY:
                third = [z_in[w][4, half, :, columns] for half in HALVES]
                first += jnp.where(is_mid, jnp.concatenate(third, axis=0).astype(f32), 0.0)
            second = jnp.concatenate(second, axis=0).astype(f32)
            for n_out, value in ((w, first), (4 + w, second)):
                if w in (0, 2):
                    outs[n_out][columns, :] = value.T.astype(outs[n_out].dtype)
                elif w == 1:
                    outs[n_out][:, columns] = value.astype(outs[n_out].dtype)
                else:
                    part_columns = pl.ds(pl.multiple_of((n % 2) * 128, 128), 128)
                    outs[n_out][n // 2, :, part_columns] = value.astype(outs[n_out].dtype)
            return carry

        lax.fori_loop(0, WIDTHS[w] // 128, body, 0)

    def turn(w):
        source = (cotangent, entering_two, branch_grad, entering_one)[w]
        for owner in range(OWNERS):
            columns = slice(owner * BLOCK, (owner + 1) * BLOCK)
            place_at = slice((owner // 2) * BLOCK, (owner // 2 + 1) * BLOCK)
            flat = source[:, columns].T
            if w < 2:
                turned[w, owner % 2, place_at, :] = flat
            else:
                turned[TURNED_AT[w], owner % 2, place_at, 0:ROWS] = flat

    def norm_back(source, gain, row, store):
        norm_own[0, row : row + 2, :] = jnp.zeros((2, D), f32)

        def strip(n, carry):
            rows = pl.ds(pl.multiple_of(n * 32, 32), 32)
            values = source[rows, :]
            center = values - jnp.mean(values, axis=-1, keepdims=True)
            scale = lax.rsqrt(jnp.mean(center * center, axis=-1, keepdims=True) + norm_epsilon)
            hat = center * scale
            grad = normed_grad[rows, :]
            norm_own[0, row : row + 1, :] += jnp.sum(grad * hat, axis=0, keepdims=True)
            norm_own[0, row + 1 : row + 2, :] += jnp.sum(grad, axis=0, keepdims=True)
            grad = grad * gain
            inner = jnp.mean(grad * hat, axis=-1, keepdims=True)
            store(rows, scale * (grad - jnp.mean(grad, axis=-1, keepdims=True) - hat * inner))
            return carry

        lax.fori_loop(0, ROWS // 32, strip, 0)

    def residual_back():
        add_came(1, normed_grad)

        def store(rows, part):
            total = part + cotangent[rows, :].astype(f32)
            residual_grad[rows, :] = total
            branch_grad[rows, :] = total.astype(bf16)

        norm_back(residual, norms[2:3, :], 2, store)

    def attend_back(t):
        plane = plane_of(UNITS[t][1])
        attended_grad = dot(branch_grad[...], output_full[plane], NT).astype(bf16)
        scale = HEAD_DIM ** (-0.5)
        for head in range(2):
            span = slice(head * HEAD_DIM, (head + 1) * HEAD_DIM)
            queries, keys_all, probs = softmax_parts(plane, span)
            grad = attended_grad[:, span]
            projected_grad[plane, 2, :, span] = dot(probs.astype(bf16), grad, TN).astype(bf16)
            prob_grad = dot(grad, projected[plane, 2, :, span], NT)
            inner = jnp.sum(probs * prob_grad, axis=-1, keepdims=True)
            score_grad = (probs * (prob_grad - inner)).astype(bf16)
            projected_grad[plane, 0, :, span] = (dot(score_grad, keys_all, NN) * scale).astype(bf16)
            projected_grad[plane, 1, :, span] = (dot(score_grad, queries, TN) * scale).astype(bf16)

    def project_back(n):
        wait_load(n)
        plane, slot = plane_at(LOADS[n][1]), n % SLOTS
        first = n == 8

        def normed(columns):
            total = dot(projected_grad[plane, 0], slots[slot, columns, 0:256], NT)
            for part in (1, 2):
                total += dot(projected_grad[plane, part], slots[slot, columns, part * 256 : (part + 1) * 256], NT)
            if first:
                normed_grad[:, columns] = total
            else:
                normed_grad[:, columns] += total

        tiles(4, 256, normed)

    def norm_step(k):
        return remote(norm_own.at[k], norm_in.at[k], norm_send.at[k], norm_recv.at[k], (sibling, over_x, over_y)[k])

    def norm_plane(d):
        target = device(y, x, c, (z + d) % PLANES)
        return remote(norm_own.at[3], norm_planes.at[z], norm_send.at[2 + d], norm_recv.at[2 + d], target)

    def inputs_back():
        def store(rows, part):
            residual_grad[rows, :] += part

        norm_back(inputs, norms[0:1, :], 0, store)
        norm_step(0).start()

    def norm_hop(k):
        norm_step(k).wait()
        norm_own[k + 1] = norm_own[k] + norm_in[k]
        if k < 2:
            norm_step(k + 1).start()
        else:
            norm_planes[z] = norm_own[3]
            for d in (1, 2, 3):
                norm_plane(d).start()

    def norms_out():
        for d in (1, 2, 3):
            norm_plane(d).wait()
        norm_out[...] = (norm_planes[0] + norm_planes[1]) + (norm_planes[2] + norm_planes[3])

    points_copy = pltpu.make_async_copy(inputs, points_out, out_sem.at[1])

    def points_back():
        slot_of = lax.broadcasted_iota(jnp.int32, (ROWS, ROWS), 0) == members[...]
        chosen = slot_of.astype(f32).astype(bf16)

        def pick(columns):
            rest = residual_grad[:, columns]
            total = jnp.zeros((ROWS, 256), f32)
            for _ in range(3):
                low = rest.astype(bf16)
                total += dot(chosen, low, NN)
                rest = rest - low.astype(f32)
            inputs[:, columns] = total

        tiles(4, 256, pick)
        points_copy.start()

    steps = (
        send_own, take, corner, cross, whole, start_load, wait_load, enter, project_attend, branches, send_cotangent,
        swap_came, widen, narrow_back, widen_back, narrow, latents_done, residual_back, attend_back, project_back,
        turn, produce, join, after_one, after_two, z_pass, own_hop, finish, inputs_back, norm_hop, norms_out, points_back,
    )
    cotangent_load.start()
    output_load(None).start()
    greet(y, x, c, z)
    for step, *at in SCHEDULE:
        steps[step](*at)
    for w, k in CHUNKS:
        for half in HALVES:
            if w not in SHORT:
                ga_copy(w, k, half).wait_send()
            gb_copy(w, k, half).wait_send()
            gc_copy(w, k, half).wait_send()
    for w in range(4):
        for half in HALVES:
            gz_first(w, half).wait_send()

    @pl.when(is_mid)
    def _():
        for w in (0, 1):
            for half in HALVES:
                gz_across(w, half).wait_send()
                for k in range(3):
                    gz_pass(w, k, half).wait_send()

    for n in range(4):
        swap(n).wait_send()
    for t in range(len(UNITS) - RING, len(UNITS)):
        pair_copy(t).wait_send()
    for t, unit in enumerate(UNITS):
        if unit[1] < OWN:
            for half in HALVES:
                z_copy(t, half, 0, beside).wait_send()
    points_copy.wait()
    latents_copy.wait()


def run_step(shards, points, cotangent, members, layer_norms):
    f32, bf16 = jnp.float32, jnp.bfloat16
    vmem_of = pltpu.VMEM
    blocks = [(WIDTHS[0], BLOCK), (BLOCK, WIDTHS[1]), (WIDTHS[2], BLOCK), (3, BLOCK, 256)]
    out_shape = [jax.ShapeDtypeStruct(blocks[w], bf16 if w < 2 else f32) for w in range(4)]
    out_shape += [jax.ShapeDtypeStruct(s, bf16) for s in blocks]
    out_shape += [jax.ShapeDtypeStruct(s, f32) for s in ((4, D), (ROWS, D), (ROWS, D))]
    out_shape += [jax.ShapeDtypeStruct(((PLANES,) if w < 2 else ()) + SHARDS[w], bf16) for w in range(4)]
    rows_f32, rows_bf16 = vmem_of((ROWS, D), f32), vmem_of((ROWS, D), bf16)
    both_bf16, hidden = vmem_of((2 * ROWS, D), bf16), vmem_of((2, 2 * ROWS, D), bf16)
    parts = vmem_of((PLANES, 3, ROWS, 256), bf16)
    scratch = [rows_f32, rows_bf16, parts, vmem_of((PLANES, ROWS, 256), bf16), rows_f32, rows_f32]
    scratch += [both_bf16, both_bf16, hidden, vmem_of((2, 2 * ROWS, D), f32), hidden]
    scratch += [vmem_of((2, 2, D // 2, 2 * ROWS), bf16), rows_bf16, parts, rows_f32]
    scratch += [vmem_of((2, ROWS, D), bf16)] * 2
    scratch += [vmem_of((SLOTS, D, D), bf16), vmem_of((PLANES, 256, D), bf16), vmem_of((RING, 2, 2, BLOCK, D), bf16)]
    counts = (2, 2, 4, 4)
    scratch += [vmem_of((counts[w], 2, 2, BLOCK, WIDTHS[w]), bf16) for w in range(4)]
    scratch += [vmem_of((counts[w], 2, 2, HALF, WIDTHS[w]), bf16) for w in range(4)]
    scratch += [vmem_of((1 if w in EARLY else counts[w], 2, HALF, WIDTHS[w]), bf16) for w in range(4)]
    scratch += [vmem_of((1 if w < 2 else 5, 2) + ((2,) if w in EARLY else ()) + (HALF, WIDTHS[w]), bf16) for w in range(4)]
    scratch += [vmem_of((n, 4, D), f32) for n in (4, 3, 4)]
    dma = pltpu.SemaphoreType.DMA
    units = len(UNITS)
    scratch += [dma((len(LOADS), 3)), dma((4,)), dma((3,)), dma((4,)), dma((4,)), dma((4, 5, 2))]
    scratch += [dma((4, 3, 2))] * 7
    scratch += [dma((units,))] * 2 + [dma((units, 2))] * 5 + [dma((4, 5, 2))] + [dma((6,))] * 2
    anywhere, vmem = pl.BlockSpec(memory_space=pl.ANY), pl.BlockSpec(memory_space=pltpu.VMEM)
    result = pl.pallas_call(
        step_kernel,
        out_shape=out_shape,
        in_specs=[anywhere] * 5 + [vmem] * 3,
        out_specs=[vmem] * 9 + [anywhere] * 6,
        scratch_shapes=scratch,
        name="step",
        compiler_params=pltpu.CompilerParams(
            collective_id=0, has_side_effects=True, vmem_limit_bytes=60 << 20
        ),
    )(*shards, cotangent, points, members, layer_norms)
    return result[:4], result[4:8], result[8], result[9], result[10]


UPDATES = ((3, D ** (-0.5)), (2, max(1, D * 4 // LAT) ** (-0.5)), (1, D ** (-0.5)), (0, FF ** (-0.5)))


def update_kernel(*refs):
    given, passed, (norm_sum, norms, norm_first, norm_second) = refs[0:20], refs[20:22], refs[22:26]
    passed_out, new_out, norm_out = refs[26:28], refs[28:48], refs[48:52]
    here, rows_here, new, in_sem, out_sem = refs[52:72], refs[72:74], refs[74:94], refs[94], refs[95]
    loads = [pltpu.make_async_copy(a, b, in_sem.at[n]) for n, (a, b) in enumerate(zip(given, here))]
    loads += [pltpu.make_async_copy(a, b, in_sem.at[20 + n]) for n, (a, b) in enumerate(zip(passed, rows_here))]
    stores = [pltpu.make_async_copy(a, b, out_sem.at[n]) for n, (a, b) in enumerate(zip(new, new_out))]
    stores += [pltpu.make_async_copy(a, b, out_sem.at[20 + n]) for n, (a, b) in enumerate(zip(rows_here, passed_out))]
    for copy in loads:
        copy.start()
    columns = pl.ds(pl.multiple_of(lax.axis_index("dp") * BLOCK, BLOCK), BLOCK)
    gradient = norm_sum[:, columns]
    norm_out[0][...] = gradient
    results = adamw_step(norms[:, columns], gradient, norm_first[...], norm_second[...], 0.2)
    for n in range(3):
        norm_out[1 + n][...] = results[n]
    for n, (_, rate) in enumerate(UPDATES):
        for copy in loads[5 * n : 5 * n + 5]:
            copy.wait()
        first, second, master, one, two = here[5 * n : 5 * n + 5]
        targets = new[5 * n : 5 * n + 5]
        width = first.shape[-1]
        strip = 16 * D // width
        strip = min(strip, first.shape[-2])

        def update(at, rate=rate, first=first, second=second, master=master, one=one, two=two, targets=targets):
            total = first[at].astype(jnp.float32) + second[at].astype(jnp.float32)
            updated, one_new, two_new = adamw_step(master[at], total, one[at], two[at], rate)
            for target, value in zip(targets, (total, updated, one_new, two_new, updated)):
                target[at] = value.astype(target.dtype)

        def step(r, carry, strip=strip, update=update, parts=first.shape[:-2]):
            rows = pl.ds(pl.multiple_of(r * strip, strip), strip)
            if parts:
                for part in range(parts[0]):
                    update((part, rows, slice(None)))
            else:
                update((rows, slice(None)))
            return carry

        lax.fori_loop(0, first.shape[-2] // strip, step, 0)
        for copy in stores[5 * n : 5 * n + 5]:
            copy.start()
    for n in (20, 21):
        loads[n].wait()
        stores[n].start()
    for copy in stores:
        copy.wait()


def run_update(given, passed, norm_sum, norms, norm_first, norm_second):
    f32, bf16 = jnp.float32, jnp.bfloat16
    vmem_of, dma = pltpu.VMEM, pltpu.SemaphoreType.DMA
    new = [(a.shape, bf16 if n == 4 else f32) for a in given[2::5] for n in range(5)]
    norm_new = [(norm_first.shape, f32)] * 4
    rows_new = [(a.shape, a.dtype) for a in passed]
    anywhere, vmem = pl.BlockSpec(memory_space=pl.ANY), pl.BlockSpec(memory_space=pltpu.VMEM)
    scratch = [vmem_of(a.shape, a.dtype) for a in (*given, *passed)] + [vmem_of(*a) for a in new]
    return pl.pallas_call(
        update_kernel,
        out_shape=[jax.ShapeDtypeStruct(*a) for a in rows_new + new + norm_new],
        in_specs=[anywhere] * 22 + [vmem] * 4,
        out_specs=[anywhere] * 22 + [vmem] * 4,
        scratch_shapes=scratch + [dma((22,)), dma((22,))],
        name="update",
        compiler_params=pltpu.CompilerParams(vmem_limit_bytes=60 << 20),
    )(*given, *passed, norm_sum, norms, norm_first, norm_second)


def on_device_cube(
    points,
    members,
    cotangent,
    project_weight,
    output_weight,
    upward_weight,
    downward_weight,
    layer_norms,
    project_master,
    project_first,
    project_second,
    output_master,
    output_first,
    output_second,
    upward_master,
    upward_first,
    upward_second,
    downward_master,
    downward_first,
    downward_second,
    norm_first,
    norm_second,
):
    firsts, seconds, norm_summed, latents, point_gradient = run_step(
        (jnp.transpose(project_weight, (1, 0, 2)), output_weight, upward_weight, downward_weight),
        points,
        cotangent,
        members,
        layer_norms,
    )
    swap = lambda array: jnp.transpose(array, (1, 0, 2))
    states = {
        3: [swap(a) for a in (project_master, project_first, project_second)],
        2: [output_master, output_first, output_second],
        1: [upward_master, upward_first, upward_second],
        0: [downward_master, downward_first, downward_second],
    }
    given = [array for w, _ in UPDATES for array in (firsts[w], seconds[w], *states[w])]
    results = run_update(given, (latents, point_gradient), norm_summed, layer_norms, norm_first, norm_second)
    return (*results[:2], *[swap(a) for a in results[2:7]], *results[7:])


def solution(mesh):
    return jax.shard_map(
        on_device_cube if dict(mesh.shape) == {"dp": 8, "mp": 4} else on_device_any,
        mesh=mesh,
        in_specs=(
            P(("dp", "mp"), None),
            P(("dp", "mp"), None),
            P(("dp", "mp"), None),
            P(None, None, "mp"),
            P("mp", None),
            P(None, "mp"),
            P("mp", None),
            P(),
            P("dp", None, "mp"),
            P("dp", None, "mp"),
            P("dp", None, "mp"),
            P("mp", "dp"),
            P("mp", "dp"),
            P("mp", "dp"),
            P("dp", "mp"),
            P("dp", "mp"),
            P("dp", "mp"),
            P("mp", "dp"),
            P("mp", "dp"),
            P("mp", "dp"),
            P(None, "dp"),
            P(None, "dp"),
        ),
        out_specs=(
            P(("dp", "mp"), None),
            P(("dp", "mp"), None),
            P("dp", None, "mp"),
            P("dp", None, "mp"),
            P("dp", None, "mp"),
            P("dp", None, "mp"),
            P("dp", None, "mp"),
            P("mp", "dp"),
            P("mp", "dp"),
            P("mp", "dp"),
            P("mp", "dp"),
            P("mp", "dp"),
            P("dp", "mp"),
            P("dp", "mp"),
            P("dp", "mp"),
            P("dp", "mp"),
            P("dp", "mp"),
            P("mp", "dp"),
            P("mp", "dp"),
            P("mp", "dp"),
            P("mp", "dp"),
            P("mp", "dp"),
            P(None, "dp"),
            P(None, "dp"),
            P(None, "dp"),
            P(None, "dp"),
        ),
        check_vma=False,
    )
```

```python
import jax
import jax.numpy as jnp
from jax import lax
from jax.experimental import pallas as pl
from jax.experimental.pallas import tpu as pltpu
from jax.sharding import PartitionSpec as P

D = 1024
HEAD_DIM = 128
FF = 4096
LAT = 256
ADAM_STEP = 10


norm_epsilon = 1e-05
beta_one = 0.9
beta_two = 0.95
adam_epsilon = 1e-08
weight_decay = 0.1
masked_score = -1e30


def layer_norm(values, norm_gain, norm_shift):
    center = values - jnp.mean(values, axis=-1, keepdims=True)
    spread = jnp.mean(center * center, axis=-1, keepdims=True)
    return center * lax.rsqrt(spread + norm_epsilon) * norm_gain + norm_shift


def pick_rows(source_rows, row_index):
    return source_rows[row_index]


def adamw_step(weight, gradient, moment_one, moment_two, step_rate):
    one_new = beta_one * moment_one + (1.0 - beta_one) * gradient
    two_new = beta_two * moment_two + (1.0 - beta_two) * gradient * gradient
    corrected_one = one_new / (1.0 - beta_one**ADAM_STEP)
    corrected_two = two_new / (1.0 - beta_two**ADAM_STEP)
    updated = weight - step_rate * (
        corrected_one / (jnp.sqrt(corrected_two) + adam_epsilon) + weight_decay * weight
    )
    return (updated, one_new, two_new)


def masked_scores(queries, keys_all, key_mask, score_scale):
    raw_scores = (
        jnp.einsum("gqhe,gkhe->ghqk", queries, keys_all, preferred_element_type=jnp.float32)
        * score_scale
    )
    return jnp.where(key_mask, raw_scores, masked_score)


def on_device_any(
    points,
    members,
    cotangent,
    project_weight,
    output_weight,
    upward_weight,
    downward_weight,
    layer_norms,
    project_master,
    project_first,
    project_second,
    output_master,
    output_first,
    output_second,
    upward_master,
    upward_first,
    upward_second,
    downward_master,
    downward_first,
    downward_second,
    norm_first,
    norm_second,
):
    groups_here = members.shape[0]
    shard_rows = points.shape[0]
    model_width = points.shape[1]
    heads_here = project_weight.shape[2] // HEAD_DIM
    score_scale = HEAD_DIM ** (-0.5)
    grouped = points.reshape(groups_here, LAT, model_width)
    slot_index = jnp.maximum(members, 0)
    key_live = members >= 0
    picked = jax.vmap(pick_rows)(grouped, slot_index)
    inputs = jnp.where(key_live[:, :, None], picked.astype(jnp.float32), 0.0).reshape(
        shard_rows, model_width
    )
    normed, norm_back_one = jax.vjp(layer_norm, inputs, layer_norms[0], layer_norms[1])
    gathered, live_all = (
        lax.all_gather(normed.astype(jnp.bfloat16), "mp", axis=0, tiled=True),
        lax.all_gather(key_live.astype(jnp.bfloat16), "mp", axis=0, tiled=True),
    )
    total_rows = gathered.shape[0]
    total_groups = live_all.shape[0]
    key_mask = (live_all > 0)[:, None, None, :]
    projected = jnp.einsum(
        "rd,dcf->rcf", gathered, project_weight, preferred_element_type=jnp.float32
    ).astype(jnp.bfloat16)
    heads_view = projected.reshape(total_groups, LAT, 3, heads_here, HEAD_DIM)
    queries = heads_view[:, :, 0]
    keys_all = heads_view[:, :, 1]
    values_all = heads_view[:, :, 2]
    scores = masked_scores(queries, keys_all, key_mask, score_scale)
    row_top = jnp.max(scores, axis=-1, keepdims=True)
    exponent = jnp.exp(scores - row_top)
    row_total = jnp.sum(exponent, axis=-1, keepdims=True)
    attention_weights = exponent / row_total
    log_total = row_top + jnp.log(row_total)
    weights_low = attention_weights.astype(jnp.bfloat16)
    attended = jnp.einsum(
        "ghqk,gkhe->gqhe", weights_low, values_all, preferred_element_type=jnp.float32
    ).astype(jnp.bfloat16)
    attended = attended.reshape(total_rows, heads_here * HEAD_DIM)
    branch = lax.psum_scatter(
        jnp.dot(attended, output_weight, preferred_element_type=jnp.float32),
        "mp",
        scatter_dimension=0,
        tiled=True,
    )
    residual = inputs + branch
    normed_two, norm_back_two = jax.vjp(layer_norm, residual, layer_norms[2], layer_norms[3])
    gathered_two = lax.all_gather(normed_two.astype(jnp.bfloat16), "mp", axis=0, tiled=True)
    upward = jnp.dot(gathered_two, upward_weight, preferred_element_type=jnp.float32)
    activated_float, gelu_back = jax.vjp(jax.nn.gelu, upward)
    activated = activated_float.astype(jnp.bfloat16)
    latents = residual + lax.psum_scatter(
        jnp.dot(activated, downward_weight, preferred_element_type=jnp.float32).astype(
            jnp.bfloat16
        ),
        "mp",
        scatter_dimension=0,
        tiled=True,
    ).astype(jnp.float32)
    cotangent_all = lax.all_gather(cotangent, "mp", axis=0, tiled=True)
    downward_local = jnp.einsum(
        "rf,rd->fd", activated, cotangent_all, preferred_element_type=jnp.float32
    )
    activated_grad = jnp.einsum(
        "rd,fd->rf", cotangent_all, downward_weight, preferred_element_type=jnp.float32
    )
    upward_grad = gelu_back(activated_grad)[0].astype(jnp.bfloat16)
    upward_local = jnp.einsum(
        "rd,rf->df", gathered_two, upward_grad, preferred_element_type=jnp.float32
    )
    normed_two_grad = lax.psum_scatter(
        jnp.einsum("rf,df->rd", upward_grad, upward_weight, preferred_element_type=jnp.float32),
        "mp",
        scatter_dimension=0,
        tiled=True,
    )
    residual_part, gain_two_grad, shift_two_grad = norm_back_two(normed_two_grad)
    residual_grad = residual_part + cotangent.astype(jnp.float32)
    norm_two_local = jnp.stack([gain_two_grad, shift_two_grad])
    branch_grad = lax.all_gather(residual_grad.astype(jnp.bfloat16), "mp", axis=0, tiled=True)
    output_local = jnp.einsum(
        "rh,rd->hd", attended, branch_grad, preferred_element_type=jnp.float32
    )
    attended_grad = jnp.einsum(
        "rd,hd->rh", branch_grad, output_weight, preferred_element_type=jnp.float32
    ).astype(jnp.bfloat16)
    attended_grad = attended_grad.reshape(total_groups, LAT, heads_here, HEAD_DIM)
    scores_again = masked_scores(queries, keys_all, key_mask, score_scale)
    weights_again = jnp.exp(scores_again - log_total)
    weights_again_low = weights_again.astype(jnp.bfloat16)
    value_grad = jnp.einsum(
        "ghqk,gqhe->gkhe", weights_again_low, attended_grad, preferred_element_type=jnp.float32
    ).astype(jnp.bfloat16)
    weight_grad = jnp.einsum(
        "gqhe,gkhe->ghqk", attended_grad, values_all, preferred_element_type=jnp.float32
    )
    score_grad = (
        weights_again * (weight_grad - jnp.sum(weights_again * weight_grad, axis=-1, keepdims=True))
    ).astype(jnp.bfloat16)
    query_grad = (
        jnp.einsum("ghqk,gkhe->gqhe", score_grad, keys_all, preferred_element_type=jnp.float32)
        * score_scale
    ).astype(jnp.bfloat16)
    key_grad = (
        jnp.einsum("ghqk,gqhe->gkhe", score_grad, queries, preferred_element_type=jnp.float32)
        * score_scale
    ).astype(jnp.bfloat16)
    projected_grad = jnp.stack([query_grad, key_grad, value_grad], axis=2).reshape(
        total_rows, 3, heads_here * HEAD_DIM
    )
    project_local = jnp.einsum(
        "rd,rcf->dcf", gathered, projected_grad, preferred_element_type=jnp.float32
    )
    normed_grad = lax.psum_scatter(
        jnp.einsum(
            "rcf,dcf->rd", projected_grad, project_weight, preferred_element_type=jnp.float32
        ).astype(jnp.bfloat16),
        "mp",
        scatter_dimension=0,
        tiled=True,
    ).astype(jnp.float32)
    input_part, gain_one_grad, shift_one_grad = norm_back_one(normed_grad)
    input_grad = input_part + residual_grad
    norm_one_local = jnp.stack([gain_one_grad, shift_one_grad])
    matches = members[:, :, None] == jnp.arange(LAT, dtype=jnp.int32)[None, None, :]
    slot_of = jnp.argmax(matches, axis=1)
    point_used = jnp.any(matches, axis=1)
    grouped_grad = input_grad.reshape(groups_here, LAT, model_width)
    point_gradient = jnp.where(
        point_used[:, :, None], jax.vmap(pick_rows)(grouped_grad, slot_of), 0.0
    ).reshape(shard_rows, model_width)
    (
        project_summed,
        output_summed,
        upward_summed,
        downward_summed,
        norm_one_summed,
        norm_two_summed,
    ) = (
        lax.psum_scatter(project_local, "dp", scatter_dimension=0, tiled=True),
        lax.psum_scatter(output_local, "dp", scatter_dimension=1, tiled=True),
        lax.psum_scatter(upward_local, "dp", scatter_dimension=0, tiled=True),
        lax.psum_scatter(downward_local, "dp", scatter_dimension=1, tiled=True),
        lax.psum_scatter(norm_one_local, "dp", scatter_dimension=1, tiled=True),
        lax.psum_scatter(norm_two_local, "dp", scatter_dimension=1, tiled=True),
    )
    norm_gradient = lax.psum(jnp.concatenate([norm_one_summed, norm_two_summed], axis=0), "mp")
    data_index = lax.axis_index("dp")
    norm_columns = norm_first.shape[1]
    norm_current = lax.dynamic_slice_in_dim(layer_norms, data_index * norm_columns, norm_columns, 1)
    project_new = adamw_step(
        project_master, project_summed, project_first, project_second, D ** (-0.5)
    )
    output_new = adamw_step(
        output_master, output_summed, output_first, output_second, max(1, D * 4 // LAT) ** (-0.5)
    )
    upward_new = adamw_step(upward_master, upward_summed, upward_first, upward_second, D ** (-0.5))
    downward_new = adamw_step(
        downward_master, downward_summed, downward_first, downward_second, FF ** (-0.5)
    )
    norm_new = adamw_step(norm_current, norm_gradient, norm_first, norm_second, 0.2)
    return (
        latents,
        point_gradient,
        project_summed,
        project_new[0],
        project_new[1],
        project_new[2],
        project_new[0].astype(jnp.bfloat16),
        output_summed,
        output_new[0],
        output_new[1],
        output_new[2],
        output_new[0].astype(jnp.bfloat16),
        upward_summed,
        upward_new[0],
        upward_new[1],
        upward_new[2],
        upward_new[0].astype(jnp.bfloat16),
        downward_summed,
        downward_new[0],
        downward_new[1],
        downward_new[2],
        downward_new[0].astype(jnp.bfloat16),
        norm_gradient,
        norm_new[0],
        norm_new[1],
        norm_new[2],
    )


MESH = pl.DeviceIdType.MESH
PLANES = 4
OWNERS = 8
ROWS = LAT
HALVES = (0, 1)
SHARDS = ((3, D, 256), (256, D), (D, D), (D, D))
SHORT = ()
CHUNKS = [(w, k) for w in (0, 1) for k in range(3)] + [(2, 0), (3, 0)]
SLOTS = 4
LOADS = (
    (0, None), (0, 0), (0, 1), (0, 2), (2, None), (2, 0), (3, None), (3, 0), (0, 2), (0, 1), (0, 0), (0, None),
)

WIDTHS = (D, D, 256, 3 * 256)
BLOCK = D // OWNERS
HALF = BLOCK // 2
RING = 2
OWN = PLANES - 1
UNITS = (
    (0, 0), (0, 3), (1, 0), (1, 3), (3, 0), (3, 1), (3, 2), (3, 3), (2, 0), (2, 1), (2, 2), (2, 3),
)
EARLY = (3,)
TURNED_AT = (0, 1, 1, 0)
(
    SEND_OWN, TAKE, CORNER, CROSS, WHOLE, LOAD, READY, ENTER, PROJECT, BRANCH, SEND_COTANGENT, CAME, WIDEN,
    NARROW_BACK, WIDEN_BACK, NARROW, LATENTS, RESIDUAL, ATTEND, INWARD, TURN, PRODUCE, JOIN, ONE, TWO, ALONG,
    LAST, FINISH, INPUTS, NORM, NORMS_OUT, POINTS,
) = range(32)
SCHEDULE = (
    (SEND_OWN, 0), (SEND_OWN, 1), (TAKE, 0, 1, 0), (TAKE, 0, 0, 0), (TAKE, 0, 0, 1), (TAKE, 0, 1, 1), (TAKE, 1, 0, 1),
    (TAKE, 0, 2, 0), (TAKE, 1, 0, 0), (CORNER, 0, 0, 1), (CORNER, 0, 1, 0), (SEND_OWN, 2), (CORNER, 0, 1, 1),
    (CORNER, 0, 2, 0), (TAKE, 0, 2, 1), (CORNER, 0, 0, 0), (TAKE, 1, 1, 1), (LOAD, 0), (TAKE, 1, 1, 0),
    (TAKE, 1, 2, 1), (TAKE, 1, 2, 0), (SEND_OWN, 3), (CORNER, 1, 0, 1), (CORNER, 1, 0, 0), (ENTER,),
    (CORNER, 0, 2, 1), (SEND_COTANGENT,), (CROSS, 0, 0, 1), (CROSS, 0, 1, 1), (CROSS, 0, 1, 0), (PROJECT, 0),
    (CORNER, 1, 2, 0), (CROSS, 0, 0, 0), (CORNER, 1, 1, 1), (LOAD, 4), (CORNER, 1, 1, 0), (CROSS, 1, 0, 1),
    (CORNER, 1, 2, 1), (CROSS, 0, 2, 0), (TAKE, 2, 0, 0), (WHOLE, 0, 0), (LOAD, 1), (TAKE, 2, 0, 1), (WHOLE, 0, 1),
    (CROSS, 0, 2, 1), (CROSS, 1, 2, 0), (TAKE, 3, 0, 0), (LOAD, 2), (WHOLE, 0, 2), (CROSS, 1, 1, 1), (CROSS, 1, 0, 0),
    (PROJECT, 1), (LOAD, 3), (CROSS, 1, 1, 0), (READY, 4), (TAKE, 3, 0, 1), (PROJECT, 2), (LOAD, 6), (CROSS, 1, 2, 1),
    (CORNER, 2, 0, 1), (CORNER, 2, 0, 0), (WHOLE, 1, 0), (PROJECT, 3), (WHOLE, 1, 1), (WHOLE, 1, 2), (BRANCH,),
    (CORNER, 3, 0, 1), (CORNER, 3, 0, 0), (WIDEN, 0, 0), (CAME, 0), (READY, 6), (CROSS, 2, 0, 1), (CROSS, 2, 0, 0),
    (NARROW_BACK, 0, 0), (TURN, 0), (WHOLE, 2, 0), (LOAD, 5), (CROSS, 3, 0, 1), (READY, 5), (WIDEN, 1, 0),
    (CROSS, 3, 0, 0), (CAME, 1), (WIDEN, 1, 1), (PRODUCE, 0), (WHOLE, 3, 0), (WIDEN, 0, 1), (LOAD, 7), (PRODUCE, 1),
    (JOIN, 0), (READY, 7), (NARROW_BACK, 0, 1), (NARROW_BACK, 1, 1), (WIDEN_BACK, 1), (JOIN, 1), (TURN, 1),
    (NARROW_BACK, 1, 0), (ONE, 0, 1), (PRODUCE, 2), (ONE, 0, 0), (PRODUCE, 3), (NARROW, 1), (JOIN, 2), (JOIN, 3),
    (TURN, 3), (WIDEN_BACK, 0), (TWO, 0, 1), (RESIDUAL,), (TWO, 0, 0), (ATTEND, 4), (PRODUCE, 4), (ONE, 2, 0),
    (ONE, 2, 1), (ATTEND, 5), (PRODUCE, 5), (JOIN, 4), (ATTEND, 7), (TWO, 2, 1), (JOIN, 5), (TWO, 2, 0), (ATTEND, 6),
    (TURN, 2), (ONE, 1, 0), (PRODUCE, 6), (ONE, 4, 0), (ONE, 3, 1), (PRODUCE, 7), (PRODUCE, 8), (JOIN, 6),
    (ONE, 4, 1), (JOIN, 8), (LOAD, 8), (LOAD, 9), (ONE, 1, 1), (PRODUCE, 9), (PRODUCE, 10), (ONE, 5, 0), (TWO, 1, 0),
    (ALONG, 4, 0), (PRODUCE, 11), (NARROW, 0), (JOIN, 9), (INWARD, 8), (JOIN, 11), (LOAD, 10), (LOAD, 11),
    (ONE, 5, 1), (ALONG, 4, 1), (INWARD, 9), (ONE, 8, 0), (INWARD, 10), (JOIN, 10), (ONE, 8, 1), (INWARD, 11),
    (JOIN, 7), (ALONG, 5, 0), (ONE, 9, 0), (ONE, 6, 0), (ALONG, 6, 0), (ONE, 9, 1), (TWO, 8, 0), (INPUTS,),
    (TWO, 8, 1), (ALONG, 5, 1), (ONE, 10, 1), (NORM, 0), (ONE, 6, 1), (TWO, 1, 1), (ONE, 10, 0), (ONE, 3, 0),
    (ALONG, 6, 1), (NORM, 1), (TWO, 9, 0), (ONE, 7, 1), (FINISH, 0), (ONE, 11, 1), (ONE, 7, 0), (TWO, 3, 1),
    (ALONG, 8, 0), (TWO, 9, 1), (ONE, 11, 0), (ALONG, 8, 1), (TWO, 10, 1), (LAST, 3, 0), (TWO, 3, 0), (TWO, 10, 0),
    (TWO, 11, 1), (LATENTS,), (NORM, 2), (LAST, 3, 1), (ALONG, 10, 0), (ALONG, 10, 1), (ALONG, 9, 0), (TWO, 11, 0),
    (ALONG, 9, 1), (FINISH, 1), (POINTS,), (FINISH, 2), (NORMS_OUT,), (FINISH, 3),
)
NN = ((1,), (0,))
NT = ((1,), (1,))
TN = ((0,), (0,))


def place():
    dp = lax.axis_index("dp")
    return dp // 4, (dp // 2) % 2, dp % 2, lax.axis_index("mp")


def device(y, x, c, z):
    return (y * 4 + x * 2 + c, z)


def greet(y, x, c, z):
    barrier = pltpu.get_barrier_semaphore()
    partners = [device(1 - y, x, c, z), device(y, 1 - x, c, z), device(y, x, 1 - c, z)]
    partners += [device(y, x, c, (z + d) % PLANES) for d in (1, 2, 3)]
    for partner in partners:
        pl.semaphore_signal(barrier, inc=1, device_id=partner, device_id_type=MESH)
    pl.semaphore_wait(barrier, len(partners))


def arrival(z, k):
    return (z + 1 - 2 * (z % 2), 2 - z // 2, 3 - 3 * (z // 2))[k]


def dot(a, b, contract):
    return lax.dot_general(a, b, (contract, ((), ())), preferred_element_type=jnp.float32)


def tiles(count, size, body):
    def step(n, carry):
        body(pl.ds(pl.multiple_of(n * size, size), size))
        return carry

    lax.fori_loop(0, count, step, 0)


def norm_rows(source, target, gain, shift, strip=64):
    def step(n, carry):
        rows = pl.ds(pl.multiple_of(n * strip, strip), strip)
        target[rows, :] = layer_norm(source[rows, :], gain, shift).astype(target.dtype)
        return carry

    lax.fori_loop(0, ROWS // strip, step, 0)


def step_kernel(*refs):
    f32, bf16 = jnp.float32, jnp.bfloat16
    shards, cotangent_in, (points, members, norms) = refs[0:4], refs[4], refs[5:8]
    outs, norm_out, latents_out, points_out, fulls = refs[8:16], refs[16], refs[17], refs[18], refs[19:23]
    inputs, entering_one, projected, attended, residual, latents = refs[23:29]
    entering_two, cotangent, activated, slope, upward_grad = refs[29:34]
    turned, branch_grad, projected_grad, normed_grad, sent, came = refs[34:40]
    slots, output_full, ring = refs[40:43]
    acc, one_in, two_in, z_in = refs[43:47], refs[47:51], refs[51:55], refs[55:59]
    norm_own, norm_in, norm_planes = refs[59:62]
    load_sem, output_sem, out_sem, swap_send, swap_recv = refs[62:67]
    gz_send, gz_recv, ga_send, ga_recv, gb_send, gb_recv, gc_send, gc_recv = refs[67:75]
    c_send, c_recv, one_send, one_recv, two_send, two_recv, z_send, z_recv = refs[75:83]
    norm_send, norm_recv = refs[83:85]
    residual_grad = residual
    y, x, c, z = place()
    is_mid = jnp.logical_or(z == 1, z == 2)
    is_end = jnp.logical_not(is_mid)
    sibling = device(y, x, 1 - c, z)
    over_x, over_y = device(y, 1 - x, c, z), device(1 - y, x, c, z)
    beside, across = device(y, x, c, arrival(z, 0)), device(y, x, c, 3 - z)
    opposite = device(y, x, c, (z + 2) % PLANES)

    def plane_at(k):
        return z if k is None else arrival(z, k)

    def plane_of(i):
        return z if i == OWN else arrival(z, 2 - i)

    def remote(src, dst, send, recv, target):
        return pltpu.make_async_remote_copy(
            src_ref=src, dst_ref=dst, send_sem=send, recv_sem=recv, device_id=target, device_id_type=MESH
        )

    def rows_of(ref, w, rows):
        return ref.at[:, rows, :] if w == 0 else ref.at[rows, :]

    def view(w, plane, rows):
        return fulls[w].at[rows, :] if w >= 2 else rows_of(fulls[w].at[plane], w, rows)

    def block(w, half, first, count):
        height = SHARDS[w][-2]
        start = pl.multiple_of(half * (height // 2) + first * (height // 16), height // 16)
        return pl.ds(start, count * (height // 16))

    spot = (c * 4 + y * 2 + x, c * 4 + x * 2 + y)
    pair = (c * 4 + y * 2, c * 4 + x * 2)

    def gz_rows(w, half):
        return block(w, half, pair[half], 2) if w in SHORT else block(w, half, spot[half], 1)

    def gz_own(w, half, lane, slot, target):
        rows = gz_rows(w, half)
        send, recv = gz_send.at[w, lane, half], gz_recv.at[w, slot, half]
        return remote(rows_of(shards[w], w, rows), view(w, z, rows), send, recv, target)

    def gz_first(w, half):
        return gz_own(w, half, 0, 0, opposite if w >= 2 else beside)

    def gz_across(w, half):
        return gz_own(w, half, 1, 1, across)

    def gz_foreign(w, k, half, lane, slot, target):
        here = view(w, arrival(z, k), gz_rows(w, half))
        return remote(here, here, gz_send.at[w, lane, half], gz_recv.at[w, slot, half], target)

    def gz_pass(w, k, half):
        lane, target, slot = ((2, across, 2), (3, beside, 1), (4, beside, 2))[k]
        return gz_foreign(w, k, half, lane, slot, target)

    def gz_arrived(w, k, half):
        return gz_foreign(w, k, half, 0, k, beside)

    def ga_copy(w, k, half):
        here = view(w, arrival(z, k), block(w, half, spot[half], 1))
        return remote(here, here, ga_send.at[w, k, half], ga_recv.at[w, k, half], (over_x, over_y)[half])

    def gb_copy(w, k, half):
        here = view(w, arrival(z, k), block(w, half, pair[half], 2))
        return remote(here, here, gb_send.at[w, k, half], gb_recv.at[w, k, half], (over_y, over_x)[half])

    def gc_copy(w, k, half):
        here = view(w, arrival(z, k), block(w, half, c * 4, 4))
        return remote(here, here, gc_send.at[w, k, half], gc_recv.at[w, k, half], sibling)

    def send_own(w):
        for half in HALVES:
            gz_first(w, half).start()
        if w < 2:

            @pl.when(is_mid)
            def _():
                for half in HALVES:
                    gz_across(w, half).start()

    def take(w, k, half):
        gz_arrived(w, k, half).wait_recv()
        (gb_copy if w in SHORT else ga_copy)(w, k, half).start()
        if w < 2:

            @pl.when(is_mid)
            def _():
                gz_pass(w, k, half).start()

    def corner(w, k, half):
        ga_copy(w, k, half).wait_recv()
        gb_copy(w, k, half).start()

    def cross(w, k, half):
        gb_copy(w, k, half).wait_recv()
        gc_copy(w, k, half).start()

    def whole(w, k):
        for half in HALVES:
            gc_copy(w, k, half).wait_recv()
        if w == 1:
            output_load(k).start()

    def loads(n):
        w, k = LOADS[n]
        if w >= 2:
            source = shards[w] if k is None else fulls[w]
            return [pltpu.make_async_copy(source, slots.at[n % SLOTS], load_sem.at[n, 0])]
        source = shards[w] if k is None else fulls[w].at[arrival(z, k)]
        return [
            pltpu.make_async_copy(
                source.at[part], slots.at[n % SLOTS, :, part * 256 : (part + 1) * 256], load_sem.at[n, part]
            )
            for part in range(3)
        ]

    def start_load(n):
        for copy in loads(n):
            copy.start()

    def wait_load(n):
        for copy in loads(n):
            copy.wait()

    def output_load(k):
        source = shards[1] if k is None else fulls[1].at[arrival(z, k)]
        return pltpu.make_async_copy(source, output_full.at[plane_at(k)], output_sem.at[3 if k is None else k])

    mine, theirs = pl.ds(0, ROWS), pl.ds(ROWS, ROWS)

    def swap(n):
        src, dst = (
            (cotangent.at[mine], cotangent.at[theirs]),
            (entering_two.at[mine], entering_two.at[theirs]),
            (sent.at[0], came.at[0]),
            (sent.at[1], came.at[1]),
        )[n]
        return remote(src, dst, swap_send.at[n], swap_recv.at[n], beside)

    cotangent_load = pltpu.make_async_copy(cotangent_in, cotangent.at[mine], out_sem.at[2])

    def send_cotangent():
        cotangent_load.wait()
        swap(0).start()

    def swap_came(n):
        swap(n).wait_recv()

    def enter():
        slot_of = lax.broadcasted_iota(jnp.int32, (ROWS, ROWS), 0) == members[...]
        chosen = slot_of.astype(f32).astype(bf16)

        def pick(columns):
            inputs[:, columns] = dot(chosen, points[:, columns], TN)

        tiles(4, 256, pick)
        norm_rows(inputs, entering_one, norms[0:1, :], norms[1:2, :])
        residual[...] = inputs[...]

    def softmax_parts(plane, span):
        queries, keys_all = projected[plane, 0, :, span], projected[plane, 1, :, span]
        scores = jnp.where(members[...] >= 0, dot(queries, keys_all, NT) * HEAD_DIM ** (-0.5), masked_score)
        exponent = jnp.exp(scores - jnp.max(scores, axis=-1, keepdims=True))
        return queries, keys_all, exponent * (1.0 / jnp.sum(exponent, axis=-1, keepdims=True))

    def project_attend(n):
        wait_load(n)
        plane, slot = plane_at(LOADS[n][1]), n % SLOTS
        for part in range(3):
            right = slots[slot, :, part * 256 : (part + 1) * 256]
            projected[plane, part] = dot(entering_one[...], right, NN).astype(bf16)
        for head in range(2):
            span = slice(head * HEAD_DIM, (head + 1) * HEAD_DIM)
            probs = softmax_parts(plane, span)[2]
            attended[plane, :, span] = dot(probs.astype(bf16), projected[plane, 2, :, span], NN).astype(bf16)

    def branches():
        for k in (None, 0, 1, 2):
            plane = plane_at(k)
            output_load(k).wait()

            def body(columns):
                residual[:, columns] += dot(attended[plane], output_full[plane, :, columns], NN)

            tiles(4, 256, body)
        norm_rows(residual, entering_two, norms[2:3, :], norms[3:4, :])
        swap(1).start()
        latents[...] = residual[...]

    def rows_at(b):
        return theirs if b else mine

    def widen(j, b):
        rows = rows_at(b)

        def body(columns):
            u = dot(entering_two[rows, :], slots[j, :, columns], NN)
            square = u * u
            bend = jnp.tanh(0.7978845608028654 * u * (1.0 + 0.044715 * square))
            activated[j, rows, columns] = (0.5 * u * (1.0 + bend)).astype(bf16)
            slope[j, rows, columns] = 0.5 * (1.0 + bend) + 0.5 * u * (1.0 - bend * bend) * (
                0.7978845608028654 * (1.0 + 3.0 * 0.044715 * square)
            )

        tiles(4, 256, body)

    def narrow_back(j, b):
        rows = rows_at(b)

        def body(columns):
            product = dot(cotangent[rows, :], slots[2 + j, columns, :], NT)
            upward_grad[j, rows, columns] = (product * slope[j, rows, columns]).astype(bf16)

        tiles(4, 256, body)

    def widen_back(b):
        rows = rows_at(b)

        def body(columns):
            total = dot(upward_grad[0, rows, :], slots[0, columns, :], NT)
            total += dot(upward_grad[1, rows, :], slots[1, columns, :], NT)
            if b:
                sent[1, :, columns] = total.astype(bf16)
            else:
                normed_grad[:, columns] = total

        tiles(4, 256, body)
        if b:
            swap(3).start()

    def narrow(b):
        rows = rows_at(b)

        def body(columns):
            total = dot(activated[0, rows, :], slots[2, :, columns], NN)
            total += dot(activated[1, rows, :], slots[3, :, columns], NN)
            if b:
                sent[0, :, columns] = total.astype(bf16)
            else:
                latents[:, columns] += total

        tiles(4, 256, body)
        if b:
            swap(2).start()

    latents_copy = pltpu.make_async_copy(latents, latents_out, out_sem.at[0])

    def add_came(n, target):
        swap_came(2 + n)

        def strip(r, carry):
            rows = pl.ds(pl.multiple_of(r * 32, 32), 32)
            target[rows, :] += came[n, rows, :].astype(f32)
            return carry

        lax.fori_loop(0, ROWS // 32, strip, 0)

    def latents_done():
        add_came(0, latents)
        latents_copy.start()

    def here(t):
        w, i = UNITS[t]
        return acc[w].at[i if w >= 2 else i // OWN]

    def pair_copy(t):
        w = UNITS[t][0]
        return remote(ring.at[t % RING, :, :, :, 0 : WIDTHS[w]], here(t), c_send.at[t], c_recv.at[t], sibling)

    def half_rows(half):
        return pl.ds(half * HALF, HALF)

    def one_in_at(t, half):
        w, i = UNITS[t]
        return one_in[w].at[i if w >= 2 else i // OWN, half]

    def two_in_at(t, half):
        w, i = UNITS[t]
        return two_in[w].at[0 if w in EARLY else i if w >= 2 else i // OWN, half]

    def one_copy(t, half):
        rows = half_rows(half)
        src = here(t).at[1 - y, :, rows] if half == 0 else here(t).at[:, 1 - x, rows]
        send, recv = one_send.at[t, half], one_recv.at[t, half]
        return remote(src, one_in_at(t, half), send, recv, (over_y, over_x)[half])

    def two_copy(t, half):
        rows = half_rows(half)
        src = here(t).at[y, 1 - x, rows] if half == 0 else here(t).at[1 - y, x, rows]
        send, recv = two_send.at[t, half], two_recv.at[t, half]
        return remote(src, two_in_at(t, half), send, recv, (over_x, over_y)[half])

    def z_piece(t, half):
        rows = half_rows(half)
        if UNITS[t][0] in EARLY:
            return here(t).at[y, :, rows] if half == 0 else here(t).at[:, x, rows]
        return here(t).at[y, x, rows]

    def z_copy(t, half, slot, target):
        w = UNITS[t][0]
        send, recv = z_send.at[t, half], z_recv.at[w, slot, half]
        return remote(z_piece(t, half), z_in[w].at[slot, half], send, recv, target)

    def z_add(t, half, slot):
        w = UNITS[t][0]
        z_copy(t, half, slot, beside).wait_recv()
        piece = z_piece(t, half)
        if w in EARLY:
            for k in (0, 1):
                add_rows(piece.at[k], z_in[w].at[slot, half, k])
        else:
            add_rows(piece, z_in[w].at[slot, half])

    def z_first(t, half):
        w, i = UNITS[t]
        if w < 2:
            z_copy(t, half, 0, opposite).start()
            return

        @pl.when(is_end)
        def _():
            z_copy(t, half, 2 - i, beside).start()

    def z_pass(t, half):
        i = UNITS[t][1]

        @pl.when(is_mid)
        def _():
            z_add(t, half, (2, 1, 3)[i])
            z_copy(t, half, (3, 4, 0)[i], (across, across, beside)[i]).start()

    def add_rows(target, source):
        def body(r, carry):
            rows = pl.ds(pl.multiple_of(r * 16, 16), 16)
            target[rows] = (target[rows].astype(f32) + source[rows].astype(f32)).astype(bf16)
            return carry

        lax.fori_loop(0, HALF // 16, body, 0)

    def partial(w, i, parity, columns, n):
        if w < 2:
            right = (activated, upward_grad)[w][1 - i // OWN, :, columns]
            return dot(turned[w, parity], right, NN)
        plane = plane_of(i)
        right = projected_grad[plane, n] if w == 3 else attended[plane, :, columns]
        return dot(turned[TURNED_AT[w], parity, :, 0:ROWS], right, NN)

    def over_tiles(w, body):
        if w == 2:
            body(pl.ds(0, 256), 0)
            return

        def step(n, carry):
            body(pl.ds(pl.multiple_of(n * 256, 256), 256), n)
            return carry

        lax.fori_loop(0, WIDTHS[w] // 256, step, 0)

    def produce(t):
        w, i = UNITS[t]
        if t >= RING:
            pair_copy(t - RING).wait_send()

        def body(columns, n):
            product = partial(w, i, 1 - c, columns, n).astype(bf16)
            for k in range(4):
                ring[t % RING, k // 2, k % 2, :, columns] = product[k * BLOCK : (k + 1) * BLOCK]

        over_tiles(w, body)
        pair_copy(t).start()

    def join(t):
        w, i = UNITS[t]
        at = i if w >= 2 else i // OWN
        pair_copy(t).wait_recv()

        def body(columns, n):
            product = partial(w, i, c, columns, n)
            for k in range(4):
                other = acc[w][at, k // 2, k % 2, :, columns].astype(f32)
                acc[w][at, k // 2, k % 2, :, columns] = (product[k * BLOCK : (k + 1) * BLOCK] + other).astype(bf16)

        over_tiles(w, body)
        for half in HALVES:
            one_copy(t, half).start()

    def after_one(t, half):
        one_copy(t, half).wait()
        rows = half_rows(half)
        for k in (0, 1):
            target = here(t).at[y, k, rows] if half == 0 else here(t).at[k, x, rows]
            add_rows(target, one_in_at(t, half).at[k])
        if UNITS[t][0] not in EARLY:
            two_copy(t, half).start()
        elif UNITS[t][1] < OWN:
            z_first(t, half)

    def after_two(t, half):
        two_copy(t, half).wait()
        add_rows(here(t).at[y, x, half_rows(half)], two_in_at(t, half))
        if UNITS[t][1] < OWN:
            z_first(t, half)

    def own_hop(w, half):
        t = UNITS.index((w, OWN))
        z_add(t, half, 0)
        if w >= 2:

            @pl.when(is_mid)
            def _():
                z_add(t, half, 4)

        two_copy(t, half).start()

    def finish(w):
        t = UNITS.index((w, OWN))
        for half in HALVES:
            if w in EARLY:
                two_copy(t, half).wait()
            else:
                z_copy(t, half, 0, beside).wait_recv()
        if w >= 2 and w not in EARLY:

            @pl.when(is_mid)
            def _():
                for half in HALVES:
                    z_copy(t, half, 4, across).wait_recv()

        def body(n, carry):
            columns = pl.ds(pl.multiple_of(n * 128, 128), 128)
            first = here(t).at[y, x][:, columns].astype(f32)
            if w in EARLY:
                second = [two_in[w][0, half, :, columns] for half in HALVES]
            else:
                second = [z_in[w][0, half, :, columns] for half in HALVES]
            if w >= 2 and w not in EARLY:
                third = [z_in[w][4, half, :, columns] for half in HALVES]
                first += jnp.where(is_mid, jnp.concatenate(third, axis=0).astype(f32), 0.0)
            second = jnp.concatenate(second, axis=0).astype(f32)
            for n_out, value in ((w, first), (4 + w, second)):
                if w in (0, 2):
                    outs[n_out][columns, :] = value.T.astype(outs[n_out].dtype)
                elif w == 1:
                    outs[n_out][:, columns] = value.astype(outs[n_out].dtype)
                else:
                    part_columns = pl.ds(pl.multiple_of((n % 2) * 128, 128), 128)
                    outs[n_out][n // 2, :, part_columns] = value.astype(outs[n_out].dtype)
            return carry

        lax.fori_loop(0, WIDTHS[w] // 128, body, 0)

    def turn(w):
        source = (cotangent, entering_two, branch_grad, entering_one)[w]
        for owner in range(OWNERS):
            columns = slice(owner * BLOCK, (owner + 1) * BLOCK)
            place_at = slice((owner // 2) * BLOCK, (owner // 2 + 1) * BLOCK)
            flat = source[:, columns].T
            if w < 2:
                turned[w, owner % 2, place_at, :] = flat
            else:
                turned[TURNED_AT[w], owner % 2, place_at, 0:ROWS] = flat

    def norm_back(source, gain, row, store):
        norm_own[0, row : row + 2, :] = jnp.zeros((2, D), f32)

        def strip(n, carry):
            rows = pl.ds(pl.multiple_of(n * 32, 32), 32)
            values = source[rows, :]
            center = values - jnp.mean(values, axis=-1, keepdims=True)
            scale = lax.rsqrt(jnp.mean(center * center, axis=-1, keepdims=True) + norm_epsilon)
            hat = center * scale
            grad = normed_grad[rows, :]
            norm_own[0, row : row + 1, :] += jnp.sum(grad * hat, axis=0, keepdims=True)
            norm_own[0, row + 1 : row + 2, :] += jnp.sum(grad, axis=0, keepdims=True)
            grad = grad * gain
            inner = jnp.mean(grad * hat, axis=-1, keepdims=True)
            store(rows, scale * (grad - jnp.mean(grad, axis=-1, keepdims=True) - hat * inner))
            return carry

        lax.fori_loop(0, ROWS // 32, strip, 0)

    def residual_back():
        add_came(1, normed_grad)

        def store(rows, part):
            total = part + cotangent[rows, :].astype(f32)
            residual_grad[rows, :] = total
            branch_grad[rows, :] = total.astype(bf16)

        norm_back(residual, norms[2:3, :], 2, store)

    def attend_back(t):
        plane = plane_of(UNITS[t][1])
        attended_grad = dot(branch_grad[...], output_full[plane], NT).astype(bf16)
        scale = HEAD_DIM ** (-0.5)
        for head in range(2):
            span = slice(head * HEAD_DIM, (head + 1) * HEAD_DIM)
            queries, keys_all, probs = softmax_parts(plane, span)
            grad = attended_grad[:, span]
            projected_grad[plane, 2, :, span] = dot(probs.astype(bf16), grad, TN).astype(bf16)
            prob_grad = dot(grad, projected[plane, 2, :, span], NT)
            inner = jnp.sum(probs * prob_grad, axis=-1, keepdims=True)
            score_grad = (probs * (prob_grad - inner)).astype(bf16)
            projected_grad[plane, 0, :, span] = (dot(score_grad, keys_all, NN) * scale).astype(bf16)
            projected_grad[plane, 1, :, span] = (dot(score_grad, queries, TN) * scale).astype(bf16)

    def project_back(n):
        wait_load(n)
        plane, slot = plane_at(LOADS[n][1]), n % SLOTS
        first = n == 8

        def normed(columns):
            total = dot(projected_grad[plane, 0], slots[slot, columns, 0:256], NT)
            for part in (1, 2):
                total += dot(projected_grad[plane, part], slots[slot, columns, part * 256 : (part + 1) * 256], NT)
            if first:
                normed_grad[:, columns] = total
            else:
                normed_grad[:, columns] += total

        tiles(4, 256, normed)

    def norm_step(k):
        return remote(norm_own.at[k], norm_in.at[k], norm_send.at[k], norm_recv.at[k], (sibling, over_x, over_y)[k])

    def norm_plane(d):
        target = device(y, x, c, (z + d) % PLANES)
        return remote(norm_own.at[3], norm_planes.at[z], norm_send.at[2 + d], norm_recv.at[2 + d], target)

    def inputs_back():
        def store(rows, part):
            residual_grad[rows, :] += part

        norm_back(inputs, norms[0:1, :], 0, store)
        norm_step(0).start()

    def norm_hop(k):
        norm_step(k).wait()
        norm_own[k + 1] = norm_own[k] + norm_in[k]
        if k < 2:
            norm_step(k + 1).start()
        else:
            norm_planes[z] = norm_own[3]
            for d in (1, 2, 3):
                norm_plane(d).start()

    def norms_out():
        for d in (1, 2, 3):
            norm_plane(d).wait()
        norm_out[...] = (norm_planes[0] + norm_planes[1]) + (norm_planes[2] + norm_planes[3])

    points_copy = pltpu.make_async_copy(inputs, points_out, out_sem.at[1])

    def points_back():
        slot_of = lax.broadcasted_iota(jnp.int32, (ROWS, ROWS), 0) == members[...]
        chosen = slot_of.astype(f32).astype(bf16)

        def pick(columns):
            rest = residual_grad[:, columns]
            total = jnp.zeros((ROWS, 256), f32)
            for _ in range(3):
                low = rest.astype(bf16)
                total += dot(chosen, low, NN)
                rest = rest - low.astype(f32)
            inputs[:, columns] = total

        tiles(4, 256, pick)
        points_copy.start()

    steps = (
        send_own, take, corner, cross, whole, start_load, wait_load, enter, project_attend, branches, send_cotangent,
        swap_came, widen, narrow_back, widen_back, narrow, latents_done, residual_back, attend_back, project_back,
        turn, produce, join, after_one, after_two, z_pass, own_hop, finish, inputs_back, norm_hop, norms_out, points_back,
    )
    cotangent_load.start()
    output_load(None).start()
    greet(y, x, c, z)
    for step, *at in SCHEDULE:
        steps[step](*at)
    for w, k in CHUNKS:
        for half in HALVES:
            if w not in SHORT:
                ga_copy(w, k, half).wait_send()
            gb_copy(w, k, half).wait_send()
            gc_copy(w, k, half).wait_send()
    for w in range(4):
        for half in HALVES:
            gz_first(w, half).wait_send()

    @pl.when(is_mid)
    def _():
        for w in (0, 1):
            for half in HALVES:
                gz_across(w, half).wait_send()
                for k in range(3):
                    gz_pass(w, k, half).wait_send()

    for n in range(4):
        swap(n).wait_send()
    for t in range(len(UNITS) - RING, len(UNITS)):
        pair_copy(t).wait_send()
    for t, unit in enumerate(UNITS):
        if unit[1] < OWN:
            for half in HALVES:
                z_copy(t, half, 0, beside).wait_send()
    points_copy.wait()
    latents_copy.wait()


def run_step(shards, points, cotangent, members, layer_norms):
    f32, bf16 = jnp.float32, jnp.bfloat16
    vmem_of = pltpu.VMEM
    blocks = [(WIDTHS[0], BLOCK), (BLOCK, WIDTHS[1]), (WIDTHS[2], BLOCK), (3, BLOCK, 256)]
    out_shape = [jax.ShapeDtypeStruct(blocks[w], bf16 if w < 2 else f32) for w in range(4)]
    out_shape += [jax.ShapeDtypeStruct(s, bf16) for s in blocks]
    out_shape += [jax.ShapeDtypeStruct(s, f32) for s in ((4, D), (ROWS, D), (ROWS, D))]
    out_shape += [jax.ShapeDtypeStruct(((PLANES,) if w < 2 else ()) + SHARDS[w], bf16) for w in range(4)]
    rows_f32, rows_bf16 = vmem_of((ROWS, D), f32), vmem_of((ROWS, D), bf16)
    both_bf16, hidden = vmem_of((2 * ROWS, D), bf16), vmem_of((2, 2 * ROWS, D), bf16)
    parts = vmem_of((PLANES, 3, ROWS, 256), bf16)
    scratch = [rows_f32, rows_bf16, parts, vmem_of((PLANES, ROWS, 256), bf16), rows_f32, rows_f32]
    scratch += [both_bf16, both_bf16, hidden, vmem_of((2, 2 * ROWS, D), f32), hidden]
    scratch += [vmem_of((2, 2, D // 2, 2 * ROWS), bf16), rows_bf16, parts, rows_f32]
    scratch += [vmem_of((2, ROWS, D), bf16)] * 2
    scratch += [vmem_of((SLOTS, D, D), bf16), vmem_of((PLANES, 256, D), bf16), vmem_of((RING, 2, 2, BLOCK, D), bf16)]
    counts = (2, 2, 4, 4)
    scratch += [vmem_of((counts[w], 2, 2, BLOCK, WIDTHS[w]), bf16) for w in range(4)]
    scratch += [vmem_of((counts[w], 2, 2, HALF, WIDTHS[w]), bf16) for w in range(4)]
    scratch += [vmem_of((1 if w in EARLY else counts[w], 2, HALF, WIDTHS[w]), bf16) for w in range(4)]
    scratch += [vmem_of((1 if w < 2 else 5, 2) + ((2,) if w in EARLY else ()) + (HALF, WIDTHS[w]), bf16) for w in range(4)]
    scratch += [vmem_of((n, 4, D), f32) for n in (4, 3, 4)]
    dma = pltpu.SemaphoreType.DMA
    units = len(UNITS)
    scratch += [dma((len(LOADS), 3)), dma((4,)), dma((3,)), dma((4,)), dma((4,)), dma((4, 5, 2))]
    scratch += [dma((4, 3, 2))] * 7
    scratch += [dma((units,))] * 2 + [dma((units, 2))] * 5 + [dma((4, 5, 2))] + [dma((6,))] * 2
    anywhere, vmem = pl.BlockSpec(memory_space=pl.ANY), pl.BlockSpec(memory_space=pltpu.VMEM)
    result = pl.pallas_call(
        step_kernel,
        out_shape=out_shape,
        in_specs=[anywhere] * 5 + [vmem] * 3,
        out_specs=[vmem] * 9 + [anywhere] * 6,
        scratch_shapes=scratch,
        name="step",
        compiler_params=pltpu.CompilerParams(
            collective_id=0, has_side_effects=True, vmem_limit_bytes=60 << 20
        ),
    )(*shards, cotangent, points, members, layer_norms)
    return result[:4], result[4:8], result[8], result[9], result[10]


UPDATES = ((3, D ** (-0.5)), (2, max(1, D * 4 // LAT) ** (-0.5)), (1, D ** (-0.5)), (0, FF ** (-0.5)))
ORDER = (2, 3, 0, 1)


def update_kernel(*refs):
    given, passed, (norm_sum, norms, norm_first, norm_second) = refs[0:20], refs[20:22], refs[22:26]
    passed_out, new_out, norm_out = refs[26:28], refs[28:48], refs[48:52]
    here, rows_here, new, in_sem, out_sem = refs[52:72], refs[72:74], refs[74:94], refs[94], refs[95]
    loads = [pltpu.make_async_copy(a, b, in_sem.at[n]) for n, (a, b) in enumerate(zip(given, here))]
    loads += [pltpu.make_async_copy(a, b, in_sem.at[20 + n]) for n, (a, b) in enumerate(zip(passed, rows_here))]
    stores = [pltpu.make_async_copy(a, b, out_sem.at[n]) for n, (a, b) in enumerate(zip(new, new_out))]
    stores += [pltpu.make_async_copy(a, b, out_sem.at[20 + n]) for n, (a, b) in enumerate(zip(rows_here, passed_out))]
    for n in (20, 21):
        loads[n].start()
    for n in ORDER:
        for copy in loads[5 * n : 5 * n + 5]:
            copy.start()
    for n in (20, 21):
        loads[n].wait()
        stores[n].start()
    columns = pl.ds(pl.multiple_of(lax.axis_index("dp") * BLOCK, BLOCK), BLOCK)
    gradient = norm_sum[:, columns]
    norm_out[0][...] = gradient
    results = adamw_step(norms[:, columns], gradient, norm_first[...], norm_second[...], 0.2)
    for n in range(3):
        norm_out[1 + n][...] = results[n]
    for n in ORDER:
        rate = UPDATES[n][1]
        for copy in loads[5 * n : 5 * n + 5]:
            copy.wait()
        first, second, master, one, two = here[5 * n : 5 * n + 5]
        targets = new[5 * n : 5 * n + 5]
        width = first.shape[-1]
        strip = 16 * D // width
        strip = min(strip, first.shape[-2])

        def update(at, rate=rate, first=first, second=second, master=master, one=one, two=two, targets=targets):
            total = first[at].astype(jnp.float32) + second[at].astype(jnp.float32)
            updated, one_new, two_new = adamw_step(master[at], total, one[at], two[at], rate)
            for target, value in zip(targets, (total, updated, one_new, two_new, updated)):
                target[at] = value.astype(target.dtype)

        def step(r, carry, strip=strip, update=update, parts=first.shape[:-2]):
            rows = pl.ds(pl.multiple_of(r * strip, strip), strip)
            if parts:
                for part in range(parts[0]):
                    update((part, rows, slice(None)))
            else:
                update((rows, slice(None)))
            return carry

        lax.fori_loop(0, first.shape[-2] // strip, step, 0)
        for copy in stores[5 * n : 5 * n + 5]:
            copy.start()
    for copy in stores:
        copy.wait()


def run_update(given, passed, norm_sum, norms, norm_first, norm_second):
    f32, bf16 = jnp.float32, jnp.bfloat16
    vmem_of, dma = pltpu.VMEM, pltpu.SemaphoreType.DMA
    new = [(a.shape, bf16 if n == 4 else f32) for a in given[2::5] for n in range(5)]
    norm_new = [(norm_first.shape, f32)] * 4
    rows_new = [(a.shape, a.dtype) for a in passed]
    anywhere, vmem = pl.BlockSpec(memory_space=pl.ANY), pl.BlockSpec(memory_space=pltpu.VMEM)
    scratch = [vmem_of(a.shape, a.dtype) for a in (*given, *passed)] + [vmem_of(*a) for a in new]
    return pl.pallas_call(
        update_kernel,
        out_shape=[jax.ShapeDtypeStruct(*a) for a in rows_new + new + norm_new],
        in_specs=[anywhere] * 22 + [vmem] * 4,
        out_specs=[anywhere] * 22 + [vmem] * 4,
        scratch_shapes=scratch + [dma((22,)), dma((22,))],
        name="update",
        compiler_params=pltpu.CompilerParams(vmem_limit_bytes=60 << 20),
    )(*given, *passed, norm_sum, norms, norm_first, norm_second)


def on_device_cube(
    points,
    members,
    cotangent,
    project_weight,
    output_weight,
    upward_weight,
    downward_weight,
    layer_norms,
    project_master,
    project_first,
    project_second,
    output_master,
    output_first,
    output_second,
    upward_master,
    upward_first,
    upward_second,
    downward_master,
    downward_first,
    downward_second,
    norm_first,
    norm_second,
):
    firsts, seconds, norm_summed, latents, point_gradient = run_step(
        (jnp.transpose(project_weight, (1, 0, 2)), output_weight, upward_weight, downward_weight),
        points,
        cotangent,
        members,
        layer_norms,
    )
    swap = lambda array: jnp.transpose(array, (1, 0, 2))
    states = {
        3: [swap(a) for a in (project_master, project_first, project_second)],
        2: [output_master, output_first, output_second],
        1: [upward_master, upward_first, upward_second],
        0: [downward_master, downward_first, downward_second],
    }
    given = [array for w, _ in UPDATES for array in (firsts[w], seconds[w], *states[w])]
    results = run_update(given, (latents, point_gradient), norm_summed, layer_norms, norm_first, norm_second)
    return (*results[:2], *[swap(a) for a in results[2:7]], *results[7:])


def solution(mesh):
    return jax.shard_map(
        on_device_cube if dict(mesh.shape) == {"dp": 8, "mp": 4} else on_device_any,
        mesh=mesh,
        in_specs=(
            P(("dp", "mp"), None),
            P(("dp", "mp"), None),
            P(("dp", "mp"), None),
            P(None, None, "mp"),
            P("mp", None),
            P(None, "mp"),
            P("mp", None),
            P(),
            P("dp", None, "mp"),
            P("dp", None, "mp"),
            P("dp", None, "mp"),
            P("mp", "dp"),
            P("mp", "dp"),
            P("mp", "dp"),
            P("dp", "mp"),
            P("dp", "mp"),
            P("dp", "mp"),
            P("mp", "dp"),
            P("mp", "dp"),
            P("mp", "dp"),
            P(None, "dp"),
            P(None, "dp"),
        ),
        out_specs=(
            P(("dp", "mp"), None),
            P(("dp", "mp"), None),
            P("dp", None, "mp"),
            P("dp", None, "mp"),
            P("dp", None, "mp"),
            P("dp", None, "mp"),
            P("dp", None, "mp"),
            P("mp", "dp"),
            P("mp", "dp"),
            P("mp", "dp"),
            P("mp", "dp"),
            P("mp", "dp"),
            P("dp", "mp"),
            P("dp", "mp"),
            P("dp", "mp"),
            P("dp", "mp"),
            P("dp", "mp"),
            P("mp", "dp"),
            P("mp", "dp"),
            P("mp", "dp"),
            P("mp", "dp"),
            P("mp", "dp"),
            P(None, "dp"),
            P(None, "dp"),
            P(None, "dp"),
            P(None, "dp"),
        ),
        check_vma=False,
    )
```

```python
import jax
import jax.numpy as jnp
from jax import lax
from jax.experimental import pallas as pl
from jax.experimental.pallas import tpu as pltpu
from jax.sharding import PartitionSpec as P

D = 1024
HEAD_DIM = 128
FF = 4096
LAT = 256
ADAM_STEP = 10


norm_epsilon = 1e-05
beta_one = 0.9
beta_two = 0.95
adam_epsilon = 1e-08
weight_decay = 0.1
masked_score = -1e30


def layer_norm(values, norm_gain, norm_shift):
    center = values - jnp.mean(values, axis=-1, keepdims=True)
    spread = jnp.mean(center * center, axis=-1, keepdims=True)
    return center * lax.rsqrt(spread + norm_epsilon) * norm_gain + norm_shift


def pick_rows(source_rows, row_index):
    return source_rows[row_index]


def adamw_step(weight, gradient, moment_one, moment_two, step_rate):
    one_new = beta_one * moment_one + (1.0 - beta_one) * gradient
    two_new = beta_two * moment_two + (1.0 - beta_two) * gradient * gradient
    corrected_one = one_new / (1.0 - beta_one**ADAM_STEP)
    corrected_two = two_new / (1.0 - beta_two**ADAM_STEP)
    updated = weight - step_rate * (
        corrected_one / (jnp.sqrt(corrected_two) + adam_epsilon) + weight_decay * weight
    )
    return (updated, one_new, two_new)


def masked_scores(queries, keys_all, key_mask, score_scale):
    raw_scores = (
        jnp.einsum("gqhe,gkhe->ghqk", queries, keys_all, preferred_element_type=jnp.float32)
        * score_scale
    )
    return jnp.where(key_mask, raw_scores, masked_score)


def on_device_any(
    points,
    members,
    cotangent,
    project_weight,
    output_weight,
    upward_weight,
    downward_weight,
    layer_norms,
    project_master,
    project_first,
    project_second,
    output_master,
    output_first,
    output_second,
    upward_master,
    upward_first,
    upward_second,
    downward_master,
    downward_first,
    downward_second,
    norm_first,
    norm_second,
):
    groups_here = members.shape[0]
    shard_rows = points.shape[0]
    model_width = points.shape[1]
    heads_here = project_weight.shape[2] // HEAD_DIM
    score_scale = HEAD_DIM ** (-0.5)
    grouped = points.reshape(groups_here, LAT, model_width)
    slot_index = jnp.maximum(members, 0)
    key_live = members >= 0
    picked = jax.vmap(pick_rows)(grouped, slot_index)
    inputs = jnp.where(key_live[:, :, None], picked.astype(jnp.float32), 0.0).reshape(
        shard_rows, model_width
    )
    normed, norm_back_one = jax.vjp(layer_norm, inputs, layer_norms[0], layer_norms[1])
    gathered, live_all = (
        lax.all_gather(normed.astype(jnp.bfloat16), "mp", axis=0, tiled=True),
        lax.all_gather(key_live.astype(jnp.bfloat16), "mp", axis=0, tiled=True),
    )
    total_rows = gathered.shape[0]
    total_groups = live_all.shape[0]
    key_mask = (live_all > 0)[:, None, None, :]
    projected = jnp.einsum(
        "rd,dcf->rcf", gathered, project_weight, preferred_element_type=jnp.float32
    ).astype(jnp.bfloat16)
    heads_view = projected.reshape(total_groups, LAT, 3, heads_here, HEAD_DIM)
    queries = heads_view[:, :, 0]
    keys_all = heads_view[:, :, 1]
    values_all = heads_view[:, :, 2]
    scores = masked_scores(queries, keys_all, key_mask, score_scale)
    row_top = jnp.max(scores, axis=-1, keepdims=True)
    exponent = jnp.exp(scores - row_top)
    row_total = jnp.sum(exponent, axis=-1, keepdims=True)
    attention_weights = exponent / row_total
    log_total = row_top + jnp.log(row_total)
    weights_low = attention_weights.astype(jnp.bfloat16)
    attended = jnp.einsum(
        "ghqk,gkhe->gqhe", weights_low, values_all, preferred_element_type=jnp.float32
    ).astype(jnp.bfloat16)
    attended = attended.reshape(total_rows, heads_here * HEAD_DIM)
    branch = lax.psum_scatter(
        jnp.dot(attended, output_weight, preferred_element_type=jnp.float32),
        "mp",
        scatter_dimension=0,
        tiled=True,
    )
    residual = inputs + branch
    normed_two, norm_back_two = jax.vjp(layer_norm, residual, layer_norms[2], layer_norms[3])
    gathered_two = lax.all_gather(normed_two.astype(jnp.bfloat16), "mp", axis=0, tiled=True)
    upward = jnp.dot(gathered_two, upward_weight, preferred_element_type=jnp.float32)
    activated_float, gelu_back = jax.vjp(jax.nn.gelu, upward)
    activated = activated_float.astype(jnp.bfloat16)
    latents = residual + lax.psum_scatter(
        jnp.dot(activated, downward_weight, preferred_element_type=jnp.float32).astype(
            jnp.bfloat16
        ),
        "mp",
        scatter_dimension=0,
        tiled=True,
    ).astype(jnp.float32)
    cotangent_all = lax.all_gather(cotangent, "mp", axis=0, tiled=True)
    downward_local = jnp.einsum(
        "rf,rd->fd", activated, cotangent_all, preferred_element_type=jnp.float32
    )
    activated_grad = jnp.einsum(
        "rd,fd->rf", cotangent_all, downward_weight, preferred_element_type=jnp.float32
    )
    upward_grad = gelu_back(activated_grad)[0].astype(jnp.bfloat16)
    upward_local = jnp.einsum(
        "rd,rf->df", gathered_two, upward_grad, preferred_element_type=jnp.float32
    )
    normed_two_grad = lax.psum_scatter(
        jnp.einsum("rf,df->rd", upward_grad, upward_weight, preferred_element_type=jnp.float32),
        "mp",
        scatter_dimension=0,
        tiled=True,
    )
    residual_part, gain_two_grad, shift_two_grad = norm_back_two(normed_two_grad)
    residual_grad = residual_part + cotangent.astype(jnp.float32)
    norm_two_local = jnp.stack([gain_two_grad, shift_two_grad])
    branch_grad = lax.all_gather(residual_grad.astype(jnp.bfloat16), "mp", axis=0, tiled=True)
    output_local = jnp.einsum(
        "rh,rd->hd", attended, branch_grad, preferred_element_type=jnp.float32
    )
    attended_grad = jnp.einsum(
        "rd,hd->rh", branch_grad, output_weight, preferred_element_type=jnp.float32
    ).astype(jnp.bfloat16)
    attended_grad = attended_grad.reshape(total_groups, LAT, heads_here, HEAD_DIM)
    scores_again = masked_scores(queries, keys_all, key_mask, score_scale)
    weights_again = jnp.exp(scores_again - log_total)
    weights_again_low = weights_again.astype(jnp.bfloat16)
    value_grad = jnp.einsum(
        "ghqk,gqhe->gkhe", weights_again_low, attended_grad, preferred_element_type=jnp.float32
    ).astype(jnp.bfloat16)
    weight_grad = jnp.einsum(
        "gqhe,gkhe->ghqk", attended_grad, values_all, preferred_element_type=jnp.float32
    )
    score_grad = (
        weights_again * (weight_grad - jnp.sum(weights_again * weight_grad, axis=-1, keepdims=True))
    ).astype(jnp.bfloat16)
    query_grad = (
        jnp.einsum("ghqk,gkhe->gqhe", score_grad, keys_all, preferred_element_type=jnp.float32)
        * score_scale
    ).astype(jnp.bfloat16)
    key_grad = (
        jnp.einsum("ghqk,gqhe->gkhe", score_grad, queries, preferred_element_type=jnp.float32)
        * score_scale
    ).astype(jnp.bfloat16)
    projected_grad = jnp.stack([query_grad, key_grad, value_grad], axis=2).reshape(
        total_rows, 3, heads_here * HEAD_DIM
    )
    project_local = jnp.einsum(
        "rd,rcf->dcf", gathered, projected_grad, preferred_element_type=jnp.float32
    )
    normed_grad = lax.psum_scatter(
        jnp.einsum(
            "rcf,dcf->rd", projected_grad, project_weight, preferred_element_type=jnp.float32
        ).astype(jnp.bfloat16),
        "mp",
        scatter_dimension=0,
        tiled=True,
    ).astype(jnp.float32)
    input_part, gain_one_grad, shift_one_grad = norm_back_one(normed_grad)
    input_grad = input_part + residual_grad
    norm_one_local = jnp.stack([gain_one_grad, shift_one_grad])
    matches = members[:, :, None] == jnp.arange(LAT, dtype=jnp.int32)[None, None, :]
    slot_of = jnp.argmax(matches, axis=1)
    point_used = jnp.any(matches, axis=1)
    grouped_grad = input_grad.reshape(groups_here, LAT, model_width)
    point_gradient = jnp.where(
        point_used[:, :, None], jax.vmap(pick_rows)(grouped_grad, slot_of), 0.0
    ).reshape(shard_rows, model_width)
    (
        project_summed,
        output_summed,
        upward_summed,
        downward_summed,
        norm_one_summed,
        norm_two_summed,
    ) = (
        lax.psum_scatter(project_local, "dp", scatter_dimension=0, tiled=True),
        lax.psum_scatter(output_local, "dp", scatter_dimension=1, tiled=True),
        lax.psum_scatter(upward_local, "dp", scatter_dimension=0, tiled=True),
        lax.psum_scatter(downward_local, "dp", scatter_dimension=1, tiled=True),
        lax.psum_scatter(norm_one_local, "dp", scatter_dimension=1, tiled=True),
        lax.psum_scatter(norm_two_local, "dp", scatter_dimension=1, tiled=True),
    )
    norm_gradient = lax.psum(jnp.concatenate([norm_one_summed, norm_two_summed], axis=0), "mp")
    data_index = lax.axis_index("dp")
    norm_columns = norm_first.shape[1]
    norm_current = lax.dynamic_slice_in_dim(layer_norms, data_index * norm_columns, norm_columns, 1)
    project_new = adamw_step(
        project_master, project_summed, project_first, project_second, D ** (-0.5)
    )
    output_new = adamw_step(
        output_master, output_summed, output_first, output_second, max(1, D * 4 // LAT) ** (-0.5)
    )
    upward_new = adamw_step(upward_master, upward_summed, upward_first, upward_second, D ** (-0.5))
    downward_new = adamw_step(
        downward_master, downward_summed, downward_first, downward_second, FF ** (-0.5)
    )
    norm_new = adamw_step(norm_current, norm_gradient, norm_first, norm_second, 0.2)
    return (
        latents,
        point_gradient,
        project_summed,
        project_new[0],
        project_new[1],
        project_new[2],
        project_new[0].astype(jnp.bfloat16),
        output_summed,
        output_new[0],
        output_new[1],
        output_new[2],
        output_new[0].astype(jnp.bfloat16),
        upward_summed,
        upward_new[0],
        upward_new[1],
        upward_new[2],
        upward_new[0].astype(jnp.bfloat16),
        downward_summed,
        downward_new[0],
        downward_new[1],
        downward_new[2],
        downward_new[0].astype(jnp.bfloat16),
        norm_gradient,
        norm_new[0],
        norm_new[1],
        norm_new[2],
    )


MESH = pl.DeviceIdType.MESH
PLANES = 4
OWNERS = 8
ROWS = LAT
HALVES = (0, 1)
SHARDS = ((3, D, 256), (256, D), (D, D), (D, D))
SHORT = ()
CHUNKS = [(w, k) for w in (0, 1) for k in range(3)] + [(2, 0), (3, 0)]
SLOTS = 4
LOADS = (
    (0, None), (0, 0), (0, 1), (0, 2), (2, None), (2, 0), (3, None), (3, 0), (0, 2), (0, 1), (0, 0), (0, None),
)

WIDTHS = (D, D, 256, 3 * 256)
BLOCK = D // OWNERS
HALF = BLOCK // 2
RING = 2
OWN = PLANES - 1
UNITS = (
    (0, 0), (0, 3), (1, 0), (1, 3), (3, 0), (3, 1), (3, 2), (3, 3), (2, 0), (2, 1), (2, 2), (2, 3),
)
EARLY = (3,)
TURNED_AT = (0, 1, 1, 0)
(
    SEND_OWN, TAKE, CORNER, CROSS, WHOLE, LOAD, READY, ENTER, PROJECT, BRANCH, SEND_COTANGENT, CAME, WIDEN,
    NARROW_BACK, WIDEN_BACK, NARROW, LATENTS, RESIDUAL, ATTEND, INWARD, TURN, PRODUCE, JOIN, ONE, TWO, ALONG,
    LAST, FINISH, INPUTS, NORM, NORMS_OUT, POINTS,
) = range(32)
SCHEDULE = (
    (SEND_OWN, 0), (SEND_OWN, 1), (TAKE, 0, 1, 0), (TAKE, 0, 0, 0), (TAKE, 0, 0, 1), (TAKE, 0, 1, 1), (TAKE, 1, 0, 1),
    (TAKE, 0, 2, 0), (TAKE, 1, 0, 0), (CORNER, 0, 0, 1), (CORNER, 0, 1, 0), (SEND_OWN, 2), (CORNER, 0, 1, 1),
    (CORNER, 0, 2, 0), (TAKE, 0, 2, 1), (CORNER, 0, 0, 0), (TAKE, 1, 1, 1), (LOAD, 0), (TAKE, 1, 1, 0),
    (TAKE, 1, 2, 1), (TAKE, 1, 2, 0), (SEND_OWN, 3), (CORNER, 1, 0, 1), (CORNER, 1, 0, 0), (ENTER,),
    (CORNER, 0, 2, 1), (SEND_COTANGENT,), (CROSS, 0, 0, 1), (CROSS, 0, 1, 1), (CROSS, 0, 1, 0), (PROJECT, 0),
    (CORNER, 1, 2, 0), (CROSS, 0, 0, 0), (CORNER, 1, 1, 1), (LOAD, 4), (CORNER, 1, 1, 0), (CROSS, 1, 0, 1),
    (CORNER, 1, 2, 1), (CROSS, 0, 2, 0), (TAKE, 2, 0, 0), (WHOLE, 0, 0), (LOAD, 1), (TAKE, 2, 0, 1), (WHOLE, 0, 1),
    (CROSS, 0, 2, 1), (CROSS, 1, 2, 0), (TAKE, 3, 0, 0), (LOAD, 2), (WHOLE, 0, 2), (CROSS, 1, 1, 1), (CROSS, 1, 0, 0),
    (PROJECT, 1), (LOAD, 3), (CROSS, 1, 1, 0), (READY, 4), (TAKE, 3, 0, 1), (PROJECT, 2), (LOAD, 6), (CROSS, 1, 2, 1),
    (CORNER, 2, 0, 1), (CORNER, 2, 0, 0), (WHOLE, 1, 0), (PROJECT, 3), (WHOLE, 1, 1), (WHOLE, 1, 2), (BRANCH,),
    (CORNER, 3, 0, 1), (CORNER, 3, 0, 0), (WIDEN, 0, 0), (CAME, 0), (READY, 6), (CROSS, 2, 0, 1), (CROSS, 2, 0, 0),
    (NARROW_BACK, 0, 0), (TURN, 0), (WHOLE, 2, 0), (LOAD, 5), (CROSS, 3, 0, 1), (READY, 5), (WIDEN, 1, 0),
    (CROSS, 3, 0, 0), (CAME, 1), (WIDEN, 1, 1), (PRODUCE, 0), (WHOLE, 3, 0), (WIDEN, 0, 1), (LOAD, 7), (PRODUCE, 1),
    (JOIN, 0), (READY, 7), (NARROW_BACK, 0, 1), (NARROW_BACK, 1, 1), (WIDEN_BACK, 1), (JOIN, 1), (TURN, 1),
    (NARROW_BACK, 1, 0), (ONE, 0, 1), (PRODUCE, 2), (ONE, 0, 0), (PRODUCE, 3), (NARROW, 1), (JOIN, 2), (JOIN, 3),
    (TURN, 3), (WIDEN_BACK, 0), (TWO, 0, 1), (RESIDUAL,), (TWO, 0, 0), (ATTEND, 4), (PRODUCE, 4), (ONE, 2, 0),
    (ONE, 2, 1), (ATTEND, 5), (PRODUCE, 5), (JOIN, 4), (ATTEND, 7), (TWO, 2, 1), (JOIN, 5), (TWO, 2, 0), (ATTEND, 6),
    (TURN, 2), (ONE, 1, 0), (PRODUCE, 6), (ONE, 4, 0), (ONE, 3, 1), (PRODUCE, 7), (PRODUCE, 8), (JOIN, 6),
    (ONE, 4, 1), (JOIN, 8), (LOAD, 8), (LOAD, 9), (ONE, 1, 1), (PRODUCE, 9), (PRODUCE, 10), (ONE, 5, 0), (TWO, 1, 0),
    (ALONG, 4, 0), (PRODUCE, 11), (NARROW, 0), (JOIN, 9), (INWARD, 8), (JOIN, 11), (LOAD, 10), (LOAD, 11),
    (ONE, 5, 1), (ALONG, 4, 1), (INWARD, 9), (ONE, 8, 0), (INWARD, 10), (JOIN, 10), (ONE, 8, 1), (INWARD, 11),
    (JOIN, 7), (ALONG, 5, 0), (ONE, 9, 0), (ONE, 6, 0), (ALONG, 6, 0), (ONE, 9, 1), (TWO, 8, 0), (INPUTS,),
    (TWO, 8, 1), (ALONG, 5, 1), (ONE, 10, 1), (NORM, 0), (ONE, 6, 1), (TWO, 1, 1), (ONE, 10, 0), (ONE, 3, 0),
    (ALONG, 6, 1), (NORM, 1), (TWO, 9, 0), (ONE, 7, 1), (FINISH, 0), (ONE, 11, 1), (ONE, 7, 0), (TWO, 3, 1),
    (ALONG, 8, 0), (TWO, 9, 1), (ONE, 11, 0), (ALONG, 8, 1), (TWO, 10, 1), (LAST, 3, 0), (TWO, 3, 0), (TWO, 10, 0),
    (TWO, 11, 1), (LATENTS,), (NORM, 2), (LAST, 3, 1), (ALONG, 10, 0), (ALONG, 10, 1), (ALONG, 9, 0), (TWO, 11, 0),
    (ALONG, 9, 1), (FINISH, 1), (POINTS,), (FINISH, 2), (NORMS_OUT,), (FINISH, 3),
)
NN = ((1,), (0,))
NT = ((1,), (1,))
TN = ((0,), (0,))


def place():
    dp = lax.axis_index("dp")
    return dp // 4, (dp // 2) % 2, dp % 2, lax.axis_index("mp")


def device(y, x, c, z):
    return (y * 4 + x * 2 + c, z)


def greet(y, x, c, z):
    barrier = pltpu.get_barrier_semaphore()
    partners = [device(1 - y, x, c, z), device(y, 1 - x, c, z), device(y, x, 1 - c, z)]
    partners += [device(y, x, c, (z + d) % PLANES) for d in (1, 2, 3)]
    for partner in partners:
        pl.semaphore_signal(barrier, inc=1, device_id=partner, device_id_type=MESH)
    pl.semaphore_wait(barrier, len(partners))


def arrival(z, k):
    return (z + 1 - 2 * (z % 2), 2 - z // 2, 3 - 3 * (z // 2))[k]


def dot(a, b, contract):
    return lax.dot_general(a, b, (contract, ((), ())), preferred_element_type=jnp.float32)


def tiles(count, size, body):
    def step(n, carry):
        body(pl.ds(pl.multiple_of(n * size, size), size))
        return carry

    lax.fori_loop(0, count, step, 0)


def norm_rows(source, target, gain, shift, strip=64):
    def step(n, carry):
        rows = pl.ds(pl.multiple_of(n * strip, strip), strip)
        target[rows, :] = layer_norm(source[rows, :], gain, shift).astype(target.dtype)
        return carry

    lax.fori_loop(0, ROWS // strip, step, 0)


def step_kernel(*refs):
    f32, bf16 = jnp.float32, jnp.bfloat16
    shards, cotangent_in, (points, members, norms) = refs[0:4], refs[4], refs[5:8]
    outs, norm_out, latents_out, points_out, fulls = refs[8:16], refs[16], refs[17], refs[18], refs[19:23]
    inputs, entering_one, projected, attended, residual, latents = refs[23:29]
    entering_two, cotangent, activated, slope, upward_grad = refs[29:34]
    turned, branch_grad, projected_grad, normed_grad, sent, came = refs[34:40]
    slots, output_full, ring = refs[40:43]
    acc, one_in, two_in, z_in = refs[43:47], refs[47:51], refs[51:55], refs[55:59]
    norm_own, norm_in, norm_planes = refs[59:62]
    load_sem, output_sem, out_sem, swap_send, swap_recv = refs[62:67]
    gz_send, gz_recv, ga_send, ga_recv, gb_send, gb_recv, gc_send, gc_recv = refs[67:75]
    c_send, c_recv, one_send, one_recv, two_send, two_recv, z_send, z_recv = refs[75:83]
    norm_send, norm_recv = refs[83:85]
    residual_grad = residual
    y, x, c, z = place()
    is_mid = jnp.logical_or(z == 1, z == 2)
    is_end = jnp.logical_not(is_mid)
    sibling = device(y, x, 1 - c, z)
    over_x, over_y = device(y, 1 - x, c, z), device(1 - y, x, c, z)
    beside, across = device(y, x, c, arrival(z, 0)), device(y, x, c, 3 - z)
    opposite = device(y, x, c, (z + 2) % PLANES)

    def plane_at(k):
        return z if k is None else arrival(z, k)

    def plane_of(i):
        return z if i == OWN else arrival(z, 2 - i)

    def remote(src, dst, send, recv, target):
        return pltpu.make_async_remote_copy(
            src_ref=src, dst_ref=dst, send_sem=send, recv_sem=recv, device_id=target, device_id_type=MESH
        )

    def rows_of(ref, w, rows):
        return ref.at[:, rows, :] if w == 0 else ref.at[rows, :]

    def view(w, plane, rows):
        return fulls[w].at[rows, :] if w >= 2 else rows_of(fulls[w].at[plane], w, rows)

    def block(w, half, first, count):
        height = SHARDS[w][-2]
        start = pl.multiple_of(half * (height // 2) + first * (height // 16), height // 16)
        return pl.ds(start, count * (height // 16))

    spot = (c * 4 + y * 2 + x, c * 4 + x * 2 + y)
    pair = (c * 4 + y * 2, c * 4 + x * 2)

    def gz_rows(w, half):
        return block(w, half, pair[half], 2) if w in SHORT else block(w, half, spot[half], 1)

    def gz_own(w, half, lane, slot, target):
        rows = gz_rows(w, half)
        send, recv = gz_send.at[w, lane, half], gz_recv.at[w, slot, half]
        return remote(rows_of(shards[w], w, rows), view(w, z, rows), send, recv, target)

    def gz_first(w, half):
        return gz_own(w, half, 0, 0, opposite if w >= 2 else beside)

    def gz_across(w, half):
        return gz_own(w, half, 1, 1, across)

    def gz_foreign(w, k, half, lane, slot, target):
        here = view(w, arrival(z, k), gz_rows(w, half))
        return remote(here, here, gz_send.at[w, lane, half], gz_recv.at[w, slot, half], target)

    def gz_pass(w, k, half):
        lane, target, slot = ((2, across, 2), (3, beside, 1), (4, beside, 2))[k]
        return gz_foreign(w, k, half, lane, slot, target)

    def gz_arrived(w, k, half):
        return gz_foreign(w, k, half, 0, k, beside)

    def ga_copy(w, k, half):
        here = view(w, arrival(z, k), block(w, half, spot[half], 1))
        return remote(here, here, ga_send.at[w, k, half], ga_recv.at[w, k, half], (over_x, over_y)[half])

    def gb_copy(w, k, half):
        here = view(w, arrival(z, k), block(w, half, pair[half], 2))
        return remote(here, here, gb_send.at[w, k, half], gb_recv.at[w, k, half], (over_y, over_x)[half])

    def gc_copy(w, k, half):
        here = view(w, arrival(z, k), block(w, half, c * 4, 4))
        return remote(here, here, gc_send.at[w, k, half], gc_recv.at[w, k, half], sibling)

    def send_own(w):
        for half in HALVES:
            gz_first(w, half).start()
        if w < 2:

            @pl.when(is_mid)
            def _():
                for half in HALVES:
                    gz_across(w, half).start()

    def take(w, k, half):
        gz_arrived(w, k, half).wait_recv()
        (gb_copy if w in SHORT else ga_copy)(w, k, half).start()
        if w < 2:

            @pl.when(is_mid)
            def _():
                gz_pass(w, k, half).start()

    def corner(w, k, half):
        ga_copy(w, k, half).wait_recv()
        gb_copy(w, k, half).start()

    def cross(w, k, half):
        gb_copy(w, k, half).wait_recv()
        gc_copy(w, k, half).start()

    def whole(w, k):
        for half in HALVES:
            gc_copy(w, k, half).wait_recv()
        if w == 1:
            output_load(k).start()

    def loads(n):
        w, k = LOADS[n]
        if w >= 2:
            source = shards[w] if k is None else fulls[w]
            return [pltpu.make_async_copy(source, slots.at[n % SLOTS], load_sem.at[n, 0])]
        source = shards[w] if k is None else fulls[w].at[arrival(z, k)]
        return [
            pltpu.make_async_copy(
                source.at[part], slots.at[n % SLOTS, :, part * 256 : (part + 1) * 256], load_sem.at[n, part]
            )
            for part in range(3)
        ]

    def start_load(n):
        for copy in loads(n):
            copy.start()

    def wait_load(n):
        for copy in loads(n):
            copy.wait()

    def output_load(k):
        source = shards[1] if k is None else fulls[1].at[arrival(z, k)]
        return pltpu.make_async_copy(source, output_full.at[plane_at(k)], output_sem.at[3 if k is None else k])

    mine, theirs = pl.ds(0, ROWS), pl.ds(ROWS, ROWS)

    def swap(n):
        src, dst = (
            (cotangent.at[mine], cotangent.at[theirs]),
            (entering_two.at[mine], entering_two.at[theirs]),
            (sent.at[0], came.at[0]),
            (sent.at[1], came.at[1]),
        )[n]
        return remote(src, dst, swap_send.at[n], swap_recv.at[n], beside)

    cotangent_load = pltpu.make_async_copy(cotangent_in, cotangent.at[mine], out_sem.at[2])

    def send_cotangent():
        cotangent_load.wait()
        swap(0).start()

    def swap_came(n):
        swap(n).wait_recv()

    def enter():
        slot_of = lax.broadcasted_iota(jnp.int32, (ROWS, ROWS), 0) == members[...]
        chosen = slot_of.astype(f32).astype(bf16)

        def pick(columns):
            inputs[:, columns] = dot(chosen, points[:, columns], TN)

        tiles(4, 256, pick)
        norm_rows(inputs, entering_one, norms[0:1, :], norms[1:2, :])
        residual[...] = inputs[...]

    def softmax_parts(plane, span):
        queries, keys_all = projected[plane, 0, :, span], projected[plane, 1, :, span]
        scores = jnp.where(members[...] >= 0, dot(queries, keys_all, NT) * HEAD_DIM ** (-0.5), masked_score)
        exponent = jnp.exp(scores - jnp.max(scores, axis=-1, keepdims=True))
        return queries, keys_all, exponent * (1.0 / jnp.sum(exponent, axis=-1, keepdims=True))

    def project_attend(n):
        wait_load(n)
        plane, slot = plane_at(LOADS[n][1]), n % SLOTS
        for part in range(3):
            right = slots[slot, :, part * 256 : (part + 1) * 256]
            projected[plane, part] = dot(entering_one[...], right, NN).astype(bf16)
        for head in range(2):
            span = slice(head * HEAD_DIM, (head + 1) * HEAD_DIM)
            probs = softmax_parts(plane, span)[2]
            attended[plane, :, span] = dot(probs.astype(bf16), projected[plane, 2, :, span], NN).astype(bf16)

    def branches():
        for k in (None, 0, 1, 2):
            plane = plane_at(k)
            output_load(k).wait()

            def body(columns):
                residual[:, columns] += dot(attended[plane], output_full[plane, :, columns], NN)

            tiles(4, 256, body)
        norm_rows(residual, entering_two, norms[2:3, :], norms[3:4, :])
        swap(1).start()
        latents[...] = residual[...]

    def rows_at(b):
        return theirs if b else mine

    def widen(j, b):
        rows = rows_at(b)

        def body(columns):
            u = dot(entering_two[rows, :], slots[j, :, columns], NN)
            square = u * u
            bend = jnp.tanh(0.7978845608028654 * u * (1.0 + 0.044715 * square))
            activated[j, rows, columns] = (0.5 * u * (1.0 + bend)).astype(bf16)
            slope[j, rows, columns] = 0.5 * (1.0 + bend) + 0.5 * u * (1.0 - bend * bend) * (
                0.7978845608028654 * (1.0 + 3.0 * 0.044715 * square)
            )

        tiles(4, 256, body)

    def narrow_back(j, b):
        rows = rows_at(b)

        def body(columns):
            product = dot(cotangent[rows, :], slots[2 + j, columns, :], NT)
            upward_grad[j, rows, columns] = (product * slope[j, rows, columns]).astype(bf16)

        tiles(4, 256, body)

    def widen_back(b):
        rows = rows_at(b)

        def body(columns):
            total = dot(upward_grad[0, rows, :], slots[0, columns, :], NT)
            total += dot(upward_grad[1, rows, :], slots[1, columns, :], NT)
            if b:
                sent[1, :, columns] = total.astype(bf16)
            else:
                normed_grad[:, columns] = total

        tiles(4, 256, body)
        if b:
            swap(3).start()

    def narrow(b):
        rows = rows_at(b)

        def body(columns):
            total = dot(activated[0, rows, :], slots[2, :, columns], NN)
            total += dot(activated[1, rows, :], slots[3, :, columns], NN)
            if b:
                sent[0, :, columns] = total.astype(bf16)
            else:
                latents[:, columns] += total

        tiles(4, 256, body)
        if b:
            swap(2).start()

    latents_copy = pltpu.make_async_copy(latents, latents_out, out_sem.at[0])

    def add_came(n, target):
        swap_came(2 + n)

        def strip(r, carry):
            rows = pl.ds(pl.multiple_of(r * 32, 32), 32)
            target[rows, :] += came[n, rows, :].astype(f32)
            return carry

        lax.fori_loop(0, ROWS // 32, strip, 0)

    def latents_done():
        add_came(0, latents)
        latents_copy.start()

    def here(t):
        w, i = UNITS[t]
        return acc[w].at[i if w >= 2 else i // OWN]

    def pair_copy(t):
        w = UNITS[t][0]
        return remote(ring.at[t % RING, :, :, :, 0 : WIDTHS[w]], here(t), c_send.at[t], c_recv.at[t], sibling)

    def half_rows(half):
        return pl.ds(half * HALF, HALF)

    def one_in_at(t, half):
        w, i = UNITS[t]
        return one_in[w].at[i if w >= 2 else i // OWN, half]

    def two_in_at(t, half):
        w, i = UNITS[t]
        return two_in[w].at[0 if w in EARLY else i if w >= 2 else i // OWN, half]

    def one_copy(t, half):
        rows = half_rows(half)
        src = here(t).at[1 - y, :, rows] if half == 0 else here(t).at[:, 1 - x, rows]
        send, recv = one_send.at[t, half], one_recv.at[t, half]
        return remote(src, one_in_at(t, half), send, recv, (over_y, over_x)[half])

    def two_copy(t, half):
        rows = half_rows(half)
        src = here(t).at[y, 1 - x, rows] if half == 0 else here(t).at[1 - y, x, rows]
        send, recv = two_send.at[t, half], two_recv.at[t, half]
        return remote(src, two_in_at(t, half), send, recv, (over_x, over_y)[half])

    def z_piece(t, half):
        rows = half_rows(half)
        if UNITS[t][0] in EARLY:
            return here(t).at[y, :, rows] if half == 0 else here(t).at[:, x, rows]
        return here(t).at[y, x, rows]

    def z_copy(t, half, slot, target):
        w = UNITS[t][0]
        send, recv = z_send.at[t, half], z_recv.at[w, slot, half]
        return remote(z_piece(t, half), z_in[w].at[slot, half], send, recv, target)

    def z_add(t, half, slot):
        w = UNITS[t][0]
        z_copy(t, half, slot, beside).wait_recv()
        piece = z_piece(t, half)
        if w in EARLY:
            for k in (0, 1):
                add_rows(piece.at[k], z_in[w].at[slot, half, k])
        else:
            add_rows(piece, z_in[w].at[slot, half])

    def z_first(t, half):
        w, i = UNITS[t]
        if w < 2:
            z_copy(t, half, 0, opposite).start()
            return

        @pl.when(is_end)
        def _():
            z_copy(t, half, 2 - i, beside).start()

    def z_pass(t, half):
        i = UNITS[t][1]

        @pl.when(is_mid)
        def _():
            z_add(t, half, (2, 1, 3)[i])
            z_copy(t, half, (3, 4, 0)[i], (across, across, beside)[i]).start()

    def add_rows(target, source):
        def body(r, carry):
            rows = pl.ds(pl.multiple_of(r * 16, 16), 16)
            target[rows] = (target[rows].astype(f32) + source[rows].astype(f32)).astype(bf16)
            return carry

        lax.fori_loop(0, HALF // 16, body, 0)

    def partial(w, i, parity, columns, n):
        if w < 2:
            right = (activated, upward_grad)[w][1 - i // OWN, :, columns]
            return dot(turned[w, parity], right, NN)
        plane = plane_of(i)
        right = projected_grad[plane, n] if w == 3 else attended[plane, :, columns]
        return dot(turned[TURNED_AT[w], parity, :, 0:ROWS], right, NN)

    def over_tiles(w, body):
        if w == 2:
            body(pl.ds(0, 256), 0)
            return

        def step(n, carry):
            body(pl.ds(pl.multiple_of(n * 256, 256), 256), n)
            return carry

        lax.fori_loop(0, WIDTHS[w] // 256, step, 0)

    def produce(t):
        w, i = UNITS[t]
        if t >= RING:
            pair_copy(t - RING).wait_send()

        def body(columns, n):
            product = partial(w, i, 1 - c, columns, n).astype(bf16)
            for k in range(4):
                ring[t % RING, k // 2, k % 2, :, columns] = product[k * BLOCK : (k + 1) * BLOCK]

        over_tiles(w, body)
        pair_copy(t).start()

    def join(t):
        w, i = UNITS[t]
        at = i if w >= 2 else i // OWN
        pair_copy(t).wait_recv()

        def body(columns, n):
            product = partial(w, i, c, columns, n)
            for k in range(4):
                other = acc[w][at, k // 2, k % 2, :, columns].astype(f32)
                acc[w][at, k // 2, k % 2, :, columns] = (product[k * BLOCK : (k + 1) * BLOCK] + other).astype(bf16)

        over_tiles(w, body)
        for half in HALVES:
            one_copy(t, half).start()

    def after_one(t, half):
        one_copy(t, half).wait()
        rows = half_rows(half)
        for k in (0, 1):
            target = here(t).at[y, k, rows] if half == 0 else here(t).at[k, x, rows]
            add_rows(target, one_in_at(t, half).at[k])
        if UNITS[t][0] not in EARLY:
            two_copy(t, half).start()
        elif UNITS[t][1] < OWN:
            z_first(t, half)

    def after_two(t, half):
        two_copy(t, half).wait()
        add_rows(here(t).at[y, x, half_rows(half)], two_in_at(t, half))
        if UNITS[t][1] < OWN:
            z_first(t, half)

    def own_hop(w, half):
        t = UNITS.index((w, OWN))
        z_add(t, half, 0)
        if w >= 2:

            @pl.when(is_mid)
            def _():
                z_add(t, half, 4)

        two_copy(t, half).start()

    def finish(w):
        t = UNITS.index((w, OWN))
        for half in HALVES:
            if w in EARLY:
                two_copy(t, half).wait()
            else:
                z_copy(t, half, 0, beside).wait_recv()
        if w >= 2 and w not in EARLY:

            @pl.when(is_mid)
            def _():
                for half in HALVES:
                    z_copy(t, half, 4, across).wait_recv()

        def body(n, carry):
            columns = pl.ds(pl.multiple_of(n * 128, 128), 128)
            first = here(t).at[y, x][:, columns].astype(f32)
            if w in EARLY:
                second = [two_in[w][0, half, :, columns] for half in HALVES]
            else:
                second = [z_in[w][0, half, :, columns] for half in HALVES]
            if w >= 2 and w not in EARLY:
                third = [z_in[w][4, half, :, columns] for half in HALVES]
                first += jnp.where(is_mid, jnp.concatenate(third, axis=0).astype(f32), 0.0)
            second = jnp.concatenate(second, axis=0).astype(f32)
            for n_out, value in ((w, first), (4 + w, second)):
                if w in (0, 2):
                    outs[n_out][columns, :] = value.T.astype(outs[n_out].dtype)
                elif w == 1:
                    outs[n_out][:, columns] = value.astype(outs[n_out].dtype)
                else:
                    part_columns = pl.ds(pl.multiple_of((n % 2) * 128, 128), 128)
                    outs[n_out][n // 2, :, part_columns] = value.astype(outs[n_out].dtype)
            return carry

        lax.fori_loop(0, WIDTHS[w] // 128, body, 0)

    def turn(w):
        source = (cotangent, entering_two, branch_grad, entering_one)[w]
        for owner in range(OWNERS):
            columns = slice(owner * BLOCK, (owner + 1) * BLOCK)
            place_at = slice((owner // 2) * BLOCK, (owner // 2 + 1) * BLOCK)
            flat = source[:, columns].T
            if w < 2:
                turned[w, owner % 2, place_at, :] = flat
            else:
                turned[TURNED_AT[w], owner % 2, place_at, 0:ROWS] = flat

    def norm_back(source, gain, row, store):
        norm_own[0, row : row + 2, :] = jnp.zeros((2, D), f32)

        def strip(n, carry):
            rows = pl.ds(pl.multiple_of(n * 32, 32), 32)
            values = source[rows, :]
            center = values - jnp.mean(values, axis=-1, keepdims=True)
            scale = lax.rsqrt(jnp.mean(center * center, axis=-1, keepdims=True) + norm_epsilon)
            hat = center * scale
            grad = normed_grad[rows, :]
            norm_own[0, row : row + 1, :] += jnp.sum(grad * hat, axis=0, keepdims=True)
            norm_own[0, row + 1 : row + 2, :] += jnp.sum(grad, axis=0, keepdims=True)
            grad = grad * gain
            inner = jnp.mean(grad * hat, axis=-1, keepdims=True)
            store(rows, scale * (grad - jnp.mean(grad, axis=-1, keepdims=True) - hat * inner))
            return carry

        lax.fori_loop(0, ROWS // 32, strip, 0)

    def residual_back():
        add_came(1, normed_grad)

        def store(rows, part):
            total = part + cotangent[rows, :].astype(f32)
            residual_grad[rows, :] = total
            branch_grad[rows, :] = total.astype(bf16)

        norm_back(residual, norms[2:3, :], 2, store)

    def attend_back(t):
        plane = plane_of(UNITS[t][1])
        attended_grad = dot(branch_grad[...], output_full[plane], NT).astype(bf16)
        scale = HEAD_DIM ** (-0.5)
        for head in range(2):
            span = slice(head * HEAD_DIM, (head + 1) * HEAD_DIM)
            queries, keys_all, probs = softmax_parts(plane, span)
            grad = attended_grad[:, span]
            projected_grad[plane, 2, :, span] = dot(probs.astype(bf16), grad, TN).astype(bf16)
            prob_grad = dot(grad, projected[plane, 2, :, span], NT)
            inner = jnp.sum(probs * prob_grad, axis=-1, keepdims=True)
            score_grad = (probs * (prob_grad - inner)).astype(bf16)
            projected_grad[plane, 0, :, span] = (dot(score_grad, keys_all, NN) * scale).astype(bf16)
            projected_grad[plane, 1, :, span] = (dot(score_grad, queries, TN) * scale).astype(bf16)

    def project_back(n):
        wait_load(n)
        plane, slot = plane_at(LOADS[n][1]), n % SLOTS
        first = n == 8

        def normed(columns):
            total = dot(projected_grad[plane, 0], slots[slot, columns, 0:256], NT)
            for part in (1, 2):
                total += dot(projected_grad[plane, part], slots[slot, columns, part * 256 : (part + 1) * 256], NT)
            if first:
                normed_grad[:, columns] = total
            else:
                normed_grad[:, columns] += total

        tiles(4, 256, normed)

    def norm_step(k):
        return remote(norm_own.at[k], norm_in.at[k], norm_send.at[k], norm_recv.at[k], (sibling, over_x, over_y)[k])

    def norm_plane(d):
        target = device(y, x, c, (z + d) % PLANES)
        return remote(norm_own.at[3], norm_planes.at[z], norm_send.at[2 + d], norm_recv.at[2 + d], target)

    def inputs_back():
        def store(rows, part):
            residual_grad[rows, :] += part

        norm_back(inputs, norms[0:1, :], 0, store)
        norm_step(0).start()

    def norm_hop(k):
        norm_step(k).wait()
        norm_own[k + 1] = norm_own[k] + norm_in[k]
        if k < 2:
            norm_step(k + 1).start()
        else:
            norm_planes[z] = norm_own[3]
            for d in (1, 2, 3):
                norm_plane(d).start()

    def norms_out():
        for d in (1, 2, 3):
            norm_plane(d).wait()
        norm_out[...] = (norm_planes[0] + norm_planes[1]) + (norm_planes[2] + norm_planes[3])

    points_copy = pltpu.make_async_copy(inputs, points_out, out_sem.at[1])

    def points_back():
        slot_of = lax.broadcasted_iota(jnp.int32, (ROWS, ROWS), 0) == members[...]
        chosen = slot_of.astype(f32).astype(bf16)

        def pick(columns):
            rest = residual_grad[:, columns]
            total = jnp.zeros((ROWS, 256), f32)
            for _ in range(3):
                low = rest.astype(bf16)
                total += dot(chosen, low, NN)
                rest = rest - low.astype(f32)
            inputs[:, columns] = total

        tiles(4, 256, pick)
        points_copy.start()

    steps = (
        send_own, take, corner, cross, whole, start_load, wait_load, enter, project_attend, branches, send_cotangent,
        swap_came, widen, narrow_back, widen_back, narrow, latents_done, residual_back, attend_back, project_back,
        turn, produce, join, after_one, after_two, z_pass, own_hop, finish, inputs_back, norm_hop, norms_out, points_back,
    )
    cotangent_load.start()
    output_load(None).start()
    greet(y, x, c, z)
    for step, *at in SCHEDULE:
        steps[step](*at)
    for w, k in CHUNKS:
        for half in HALVES:
            if w not in SHORT:
                ga_copy(w, k, half).wait_send()
            gb_copy(w, k, half).wait_send()
            gc_copy(w, k, half).wait_send()
    for w in range(4):
        for half in HALVES:
            gz_first(w, half).wait_send()

    @pl.when(is_mid)
    def _():
        for w in (0, 1):
            for half in HALVES:
                gz_across(w, half).wait_send()
                for k in range(3):
                    gz_pass(w, k, half).wait_send()

    for n in range(4):
        swap(n).wait_send()
    for t in range(len(UNITS) - RING, len(UNITS)):
        pair_copy(t).wait_send()
    for t, unit in enumerate(UNITS):
        if unit[1] < OWN:
            for half in HALVES:
                z_copy(t, half, 0, beside).wait_send()
    points_copy.wait()
    latents_copy.wait()


def run_step(shards, points, cotangent, members, layer_norms):
    f32, bf16 = jnp.float32, jnp.bfloat16
    vmem_of = pltpu.VMEM
    blocks = [(WIDTHS[0], BLOCK), (BLOCK, WIDTHS[1]), (WIDTHS[2], BLOCK), (3, BLOCK, 256)]
    out_shape = [jax.ShapeDtypeStruct(blocks[w], bf16 if w < 2 else f32) for w in range(4)]
    out_shape += [jax.ShapeDtypeStruct(s, bf16) for s in blocks]
    out_shape += [jax.ShapeDtypeStruct(s, f32) for s in ((4, D), (ROWS, D), (ROWS, D))]
    out_shape += [jax.ShapeDtypeStruct(((PLANES,) if w < 2 else ()) + SHARDS[w], bf16) for w in range(4)]
    rows_f32, rows_bf16 = vmem_of((ROWS, D), f32), vmem_of((ROWS, D), bf16)
    both_bf16, hidden = vmem_of((2 * ROWS, D), bf16), vmem_of((2, 2 * ROWS, D), bf16)
    parts = vmem_of((PLANES, 3, ROWS, 256), bf16)
    scratch = [rows_f32, rows_bf16, parts, vmem_of((PLANES, ROWS, 256), bf16), rows_f32, rows_f32]
    scratch += [both_bf16, both_bf16, hidden, vmem_of((2, 2 * ROWS, D), f32), hidden]
    scratch += [vmem_of((2, 2, D // 2, 2 * ROWS), bf16), rows_bf16, parts, rows_f32]
    scratch += [vmem_of((2, ROWS, D), bf16)] * 2
    scratch += [vmem_of((SLOTS, D, D), bf16), vmem_of((PLANES, 256, D), bf16), vmem_of((RING, 2, 2, BLOCK, D), bf16)]
    counts = (2, 2, 4, 4)
    scratch += [vmem_of((counts[w], 2, 2, BLOCK, WIDTHS[w]), bf16) for w in range(4)]
    scratch += [vmem_of((counts[w], 2, 2, HALF, WIDTHS[w]), bf16) for w in range(4)]
    scratch += [vmem_of((1 if w in EARLY else counts[w], 2, HALF, WIDTHS[w]), bf16) for w in range(4)]
    scratch += [vmem_of((1 if w < 2 else 5, 2) + ((2,) if w in EARLY else ()) + (HALF, WIDTHS[w]), bf16) for w in range(4)]
    scratch += [vmem_of((n, 4, D), f32) for n in (4, 3, 4)]
    dma = pltpu.SemaphoreType.DMA
    units = len(UNITS)
    scratch += [dma((len(LOADS), 3)), dma((4,)), dma((3,)), dma((4,)), dma((4,)), dma((4, 5, 2))]
    scratch += [dma((4, 3, 2))] * 7
    scratch += [dma((units,))] * 2 + [dma((units, 2))] * 5 + [dma((4, 5, 2))] + [dma((6,))] * 2
    anywhere, vmem = pl.BlockSpec(memory_space=pl.ANY), pl.BlockSpec(memory_space=pltpu.VMEM)
    result = pl.pallas_call(
        step_kernel,
        out_shape=out_shape,
        in_specs=[anywhere] * 5 + [vmem] * 3,
        out_specs=[vmem] * 9 + [anywhere] * 6,
        scratch_shapes=scratch,
        name="step",
        compiler_params=pltpu.CompilerParams(
            collective_id=0, has_side_effects=True, vmem_limit_bytes=60 << 20
        ),
    )(*shards, cotangent, points, members, layer_norms)
    return result[:4], result[4:8], result[8], result[9], result[10]


UPDATES = ((3, D ** (-0.5)), (2, max(1, D * 4 // LAT) ** (-0.5)), (1, D ** (-0.5)), (0, FF ** (-0.5)))
ORDER = (2, 3, 0, 1)


def update_kernel(*refs):
    given, passed, (norm_sum, norms, norm_first, norm_second) = refs[0:20], refs[20:22], refs[22:26]
    passed_out, new_out, norm_out = refs[26:28], refs[28:48], refs[48:52]
    here, rows_here, new, in_sem, out_sem = refs[52:72], refs[72:74], refs[74:94], refs[94], refs[95]
    loads = [pltpu.make_async_copy(a, b, in_sem.at[n]) for n, (a, b) in enumerate(zip(given, here))]
    loads += [pltpu.make_async_copy(a, b, in_sem.at[20 + n]) for n, (a, b) in enumerate(zip(passed, rows_here))]
    stores = [pltpu.make_async_copy(a, b, out_sem.at[n]) for n, (a, b) in enumerate(zip(new, new_out))]
    stores += [pltpu.make_async_copy(a, b, out_sem.at[20 + n]) for n, (a, b) in enumerate(zip(rows_here, passed_out))]
    for n in ORDER:
        for copy in loads[5 * n : 5 * n + 5]:
            copy.start()
    for n in (20, 21):
        loads[n].start()
    columns = pl.ds(pl.multiple_of(lax.axis_index("dp") * BLOCK, BLOCK), BLOCK)
    gradient = norm_sum[:, columns]
    norm_out[0][...] = gradient
    results = adamw_step(norms[:, columns], gradient, norm_first[...], norm_second[...], 0.2)
    for n in range(3):
        norm_out[1 + n][...] = results[n]
    for n in ORDER:
        rate = UPDATES[n][1]
        for copy in loads[5 * n : 5 * n + 5]:
            copy.wait()
        first, second, master, one, two = here[5 * n : 5 * n + 5]
        targets = new[5 * n : 5 * n + 5]
        width = first.shape[-1]
        strip = 16 * D // width
        strip = min(strip, first.shape[-2])

        def update(at, rate=rate, first=first, second=second, master=master, one=one, two=two, targets=targets):
            total = first[at].astype(jnp.float32) + second[at].astype(jnp.float32)
            updated, one_new, two_new = adamw_step(master[at], total, one[at], two[at], rate)
            for target, value in zip(targets, (total, updated, one_new, two_new, updated)):
                target[at] = value.astype(target.dtype)

        def step(r, carry, strip=strip, update=update, parts=first.shape[:-2]):
            rows = pl.ds(pl.multiple_of(r * strip, strip), strip)
            if parts:
                for part in range(parts[0]):
                    update((part, rows, slice(None)))
            else:
                update((rows, slice(None)))
            return carry

        lax.fori_loop(0, first.shape[-2] // strip, step, 0)
        for copy in stores[5 * n : 5 * n + 5]:
            copy.start()
    for n in (20, 21):
        loads[n].wait()
        stores[n].start()
    for copy in stores:
        copy.wait()


def run_update(given, passed, norm_sum, norms, norm_first, norm_second):
    f32, bf16 = jnp.float32, jnp.bfloat16
    vmem_of, dma = pltpu.VMEM, pltpu.SemaphoreType.DMA
    new = [(a.shape, bf16 if n == 4 else f32) for a in given[2::5] for n in range(5)]
    norm_new = [(norm_first.shape, f32)] * 4
    rows_new = [(a.shape, a.dtype) for a in passed]
    anywhere, vmem = pl.BlockSpec(memory_space=pl.ANY), pl.BlockSpec(memory_space=pltpu.VMEM)
    scratch = [vmem_of(a.shape, a.dtype) for a in (*given, *passed)] + [vmem_of(*a) for a in new]
    return pl.pallas_call(
        update_kernel,
        out_shape=[jax.ShapeDtypeStruct(*a) for a in rows_new + new + norm_new],
        in_specs=[anywhere] * 22 + [vmem] * 4,
        out_specs=[anywhere] * 22 + [vmem] * 4,
        scratch_shapes=scratch + [dma((22,)), dma((22,))],
        name="update",
        compiler_params=pltpu.CompilerParams(vmem_limit_bytes=60 << 20),
    )(*given, *passed, norm_sum, norms, norm_first, norm_second)


def on_device_cube(
    points,
    members,
    cotangent,
    project_weight,
    output_weight,
    upward_weight,
    downward_weight,
    layer_norms,
    project_master,
    project_first,
    project_second,
    output_master,
    output_first,
    output_second,
    upward_master,
    upward_first,
    upward_second,
    downward_master,
    downward_first,
    downward_second,
    norm_first,
    norm_second,
):
    firsts, seconds, norm_summed, latents, point_gradient = run_step(
        (jnp.transpose(project_weight, (1, 0, 2)), output_weight, upward_weight, downward_weight),
        points,
        cotangent,
        members,
        layer_norms,
    )
    swap = lambda array: jnp.transpose(array, (1, 0, 2))
    states = {
        3: [swap(a) for a in (project_master, project_first, project_second)],
        2: [output_master, output_first, output_second],
        1: [upward_master, upward_first, upward_second],
        0: [downward_master, downward_first, downward_second],
    }
    given = [array for w, _ in UPDATES for array in (firsts[w], seconds[w], *states[w])]
    results = run_update(given, (latents, point_gradient), norm_summed, layer_norms, norm_first, norm_second)
    return (*results[:2], *[swap(a) for a in results[2:7]], *results[7:])


def solution(mesh):
    return jax.shard_map(
        on_device_cube if dict(mesh.shape) == {"dp": 8, "mp": 4} else on_device_any,
        mesh=mesh,
        in_specs=(
            P(("dp", "mp"), None),
            P(("dp", "mp"), None),
            P(("dp", "mp"), None),
            P(None, None, "mp"),
            P("mp", None),
            P(None, "mp"),
            P("mp", None),
            P(),
            P("dp", None, "mp"),
            P("dp", None, "mp"),
            P("dp", None, "mp"),
            P("mp", "dp"),
            P("mp", "dp"),
            P("mp", "dp"),
            P("dp", "mp"),
            P("dp", "mp"),
            P("dp", "mp"),
            P("mp", "dp"),
            P("mp", "dp"),
            P("mp", "dp"),
            P(None, "dp"),
            P(None, "dp"),
        ),
        out_specs=(
            P(("dp", "mp"), None),
            P(("dp", "mp"), None),
            P("dp", None, "mp"),
            P("dp", None, "mp"),
            P("dp", None, "mp"),
            P("dp", None, "mp"),
            P("dp", None, "mp"),
            P("mp", "dp"),
            P("mp", "dp"),
            P("mp", "dp"),
            P("mp", "dp"),
            P("mp", "dp"),
            P("dp", "mp"),
            P("dp", "mp"),
            P("dp", "mp"),
            P("dp", "mp"),
            P("dp", "mp"),
            P("mp", "dp"),
            P("mp", "dp"),
            P("mp", "dp"),
            P("mp", "dp"),
            P("mp", "dp"),
            P(None, "dp"),
            P(None, "dp"),
            P(None, "dp"),
            P(None, "dp"),
        ),
        check_vma=False,
    )
```
